32 devices in a mesh: seq: 8 (over z, x), exp: 4 (over y, core).
Axes of the slice: x: 2, y: 2, z: 4, core: 2. Of those that a mesh axis runs over, the one named last changes fastest.
Arguments:
- block_in: bfloat16 [16, 2048, 1024], P('exp', 'seq'), may hold values from -6 to 6
- cotangent: bfloat16 [16, 2048, 1024], P('exp', 'seq'), may hold values from -6 to 6
- segment_ids: int32 [16, 2048], P('exp'), may hold values from 0 to 3, never falling along the last dimension, each value on 1 to 1024 neighbouring positions
- expert_routes: int32 [16, 2048, 2], P('exp', 'seq'), may hold values from 0 to 3, all different within a row
- pair_priority: int32 [4, 8, 2048], P('exp', 'seq'), may hold values from 0 to 2047, each once within a row
- gain_attention: float32 [1024], P(('seq', 'exp')), may hold values from 0.5 to 1.5
- w_query: float32 [1024, 1024], P(('seq', 'exp')), may hold values from -0.1875 to 0.1875
- w_key: float32 [1024, 1024], P(('seq', 'exp')), may hold values from -0.1875 to 0.1875
- w_value: float32 [1024, 1024], P(('seq', 'exp')), may hold values from -0.1875 to 0.1875
- w_out: float32 [1024, 1024], P(('seq', 'exp')), may hold values from -2.5 to 2.5
- bias_table: float32 [512], P(('seq', 'exp')), may hold values from -3 to 3
- gain_experts: float32 [1024], P(('seq', 'exp')), may hold values from 0.5 to 1.5
- w_router: float32 [1024, 4], P(('seq', 'exp')), may hold values from -0.09375 to 0.09375
- w_gate: float32 [4, 1024, 2816], P('exp', 'seq'), may hold values from -0.1875 to 0.1875
- w_up: float32 [4, 1024, 2816], P('exp', 'seq'), may hold values from -0.1875 to 0.1875
- w_down: float32 [4, 2816, 1024], P('exp', 'seq'), may hold values from -0.109375 to 0.109375
Outputs:
- block_out: bfloat16 [16, 2048, 1024], P('exp', 'seq')
- block_in_grad: float32 [16, 2048, 1024], P('exp', 'seq')
- gain_attention_grad: float32 [1024], P(('seq', 'exp'))
- query_grad: float32 [1024, 1024], P(('seq', 'exp'))
- key_grad: float32 [1024, 1024], P(('seq', 'exp'))
- value_grad: float32 [1024, 1024], P(('seq', 'exp'))
- out_weight_grad: float32 [1024, 1024], P(('seq', 'exp'))
- bias_grad: float32 [512], P(('seq', 'exp'))
- gain_experts_grad: float32 [1024], P(('seq', 'exp'))
- router_grad: float32 [1024, 4], P(('seq', 'exp'))
- gate_grad: float32 [4, 1024, 2816], P('exp', 'seq')
- up_grad: float32 [4, 1024, 2816], P('exp', 'seq')
- down_grad: float32 [4, 2816, 1024], P('exp', 'seq')
The draws below stay inside these ranges and needn't reach their ends.
Inputs may be any that keep to these rules, and one draw needn't show every extreme that they name: `segment_ids`: document ids never fall along a sequence; no document is longer than 1024 tokens. `expert_routes`: the two experts of a token differ. `pair_priority`: each row is a permutation of the 2048 pairs of one device.
All inputs are finite; a program needn't handle non-finite values.
Results may differ from the reference program's by a relative error of at most 0.017.
The reference program's roundings to bfloat16 on the way count: a program that leaves them out, or rounds other values in their place, can miss the bound.
Values may be sent and summed in bfloat16 or wider, within the bound.
A program may use at most 320 MiB of HBM per device.

```python
import math
import jax
import jax.numpy as jnp
import numpy as np
from jax import lax

D = 1024
HEADS = 16
HEAD_DIM = 64
FF = 2816
BUCKETS = 32
TOP = 2
DOCS = 4
SEQ_GRP = 4
LEN = 2048
HD = 1024
SEQS = 16
TOK_DEV = 1024
EXPERTS = 4
CAP = 640
PAIRS = 2048
N_SEQ = 8
N_EXP = 4


def levels(stream_key, dims, split, smallest, largest):
    level = 1.0
    for axis_at, blocks in split:
        steps = jax.random.uniform(jax.random.fold_in(jax.random.fold_in(stream_key, 6), axis_at), (blocks,), jnp.float32, smallest / len(split), largest / len(split))
        level = level * jnp.repeat(jnp.exp(steps), dims[axis_at] // blocks).reshape((-1,) + (1,) * (len(dims) - 1 - axis_at))
    return level


def choose_distinct(own_key, rows, amount, top, lift):
    ranking = jax.random.permutation(jax.random.fold_in(own_key, 1), amount)
    favour = ranking
    for power in range(3):
        favour = favour * favour // amount
    favour = favour * lift // amount
    tickets = jax.random.randint(jax.random.fold_in(own_key, 2), (rows, amount), 0, 4096) + favour
    sure = jax.random.permutation(jax.random.fold_in(own_key, 3), rows)[jnp.arange(amount) % rows]
    tickets = jnp.where(jnp.arange(rows)[:, None] == sure[None, :], 1 << 14, tickets)
    score = tickets * amount + jnp.arange(amount)
    return lax.top_k(score.astype(jnp.int32), top)[1].astype(jnp.int32)


def split_up(amount, total, bound, slope):
    portions = [(1 << 20) // math.isqrt(rank ** slope) + 1 for rank in range(2, amount + 1)]
    spare, given = total - bound - (amount - 1), [1] * (amount - 1)
    while spare > 0:
        movable = [i for i in range(amount - 1) if given[i] < bound]
        whole, budget = sum([portions[i] for i in movable]), spare
        for i in movable:
            more = min(bound - given[i], max(1, budget * portions[i] // whole), spare)
            given[i] = given[i] + more
            spare = spare - more
    return np.array([bound] + given)


def ragged_sizes(stream_key, count, total, reach, lean):
    if count == 2:
        one = jax.random.randint(stream_key, (), max(1, total - reach), min(reach, total - 1) + 1)
        return jnp.stack([one, total - one])
    lengths = jnp.asarray(split_up(count, total, reach, lean), jnp.int32)
    twos = (count - 1) // 2
    donor, sink = lengths[1:1 + 2 * twos:2], lengths[2:2 + 2 * twos:2]
    margin = jnp.minimum(donor - 1, reach - sink)
    moved = jax.random.randint(jax.random.fold_in(stream_key, 1), (twos,), 0, 1 << 20) % (margin + 1)
    lengths = lengths.at[1:1 + 2 * twos:2].set(donor - moved).at[2:2 + 2 * twos:2].set(sink + moved)
    return lengths[jax.random.permutation(jax.random.fold_in(stream_key, 2), count)]


def gaussian(key, shape, spread, most, cuts=(), kind=jnp.bfloat16):
    values = spread * jax.random.normal(key, shape, jnp.float32)
    if cuts:
        values = values * levels(key, shape, cuts, -0.22, 0.18)
    return jnp.clip(values, -most, most).astype(kind)


def setup_inputs(seed: int = 0) -> dict:
    keys = jax.random.split(jax.random.key(seed), 17)
    return {
        "block_in": gaussian(keys[0], (SEQS, LEN, D), 1.0, 6.0, ((0, 4), (1, 8))),
        "cotangent": gaussian(keys[1], (SEQS, LEN, D), 1.0, 6.0, ((0, 4), (1, 8))),
        "segment_ids": jax.vmap(lambda own: jnp.searchsorted(jnp.cumsum(ragged_sizes(own, DOCS, LEN, LEN // 2, 0)), jnp.arange(LEN), side="right"))(jax.random.split(keys[2], SEQS)).reshape((SEQS, LEN)).astype(jnp.int32),
        "expert_routes": choose_distinct(keys[3], SEQS * LEN, EXPERTS, TOP, 4096).reshape((SEQS, LEN, TOP)),
        "pair_priority": jax.vmap(lambda own: jax.random.permutation(own, PAIRS))(jax.random.split(keys[4], N_EXP * N_SEQ)).reshape((N_EXP, N_SEQ, PAIRS)).astype(jnp.int32),
        "gain_attention": jnp.clip(1.0 + 0.1 * jax.random.normal(keys[5], (D,), jnp.float32), 0.5, 1.5),
        "w_query": gaussian(keys[6], (D, HD), D ** -0.5, 0.1875, ((0, 32),), jnp.float32),
        "w_key": gaussian(keys[7], (D, HD), D ** -0.5, 0.1875, ((0, 32),), jnp.float32),
        "w_value": gaussian(keys[8], (D, HD), D ** -0.5, 0.1875, ((0, 32),), jnp.float32),
        "w_out": gaussian(keys[9], (HD, D), (max(1, 12 * HD // LEN)) ** -0.5, 2.5, ((0, 32),), jnp.float32),
        "bias_table": gaussian(keys[10], (HEADS * BUCKETS,), 0.5, 3.0, ((0, 32),), jnp.float32),
        "gain_experts": jnp.clip(1.0 + 0.1 * jax.random.normal(keys[11], (D,), jnp.float32), 0.5, 1.5),
        "w_router": gaussian(keys[12], (D, EXPERTS), (4 * D) ** -0.5, 0.09375, ((0, 32),), jnp.float32),
        "w_gate": gaussian(keys[13], (EXPERTS, D, FF), D ** -0.5, 0.1875, ((0, 4), (1, 8)), jnp.float32),
        "w_up": gaussian(keys[14], (EXPERTS, D, FF), D ** -0.5, 0.1875, ((0, 4), (1, 8)), jnp.float32),
        "w_down": gaussian(keys[15], (EXPERTS, FF, D), FF ** -0.5, 0.109375, ((0, 4), (1, 8)), jnp.float32),
    }


EPS = 1e-06
NEG = -1e+30
THRESHOLDS = (12, 16, 23, 32, 46, 64, 91)
FULL_PRECISION = lax.Precision.HIGHEST

@jax.custom_vjp
def reduced_precision(v):
    return lax.optimization_barrier(v.astype(jnp.bfloat16)).astype(jnp.float32)

@jax.custom_vjp
def low_back(v):
    return v

def low_keep(v):
    return (reduced_precision(v), None)

def low_pass(kept, grad):
    return (grad,)

def back_keep(v):
    return (v, None)

def back_low(kept, grad):
    return (reduced_precision(grad),)
reduced_precision.defvjp(low_keep, low_pass)
low_back.defvjp(back_keep, back_low)

def bucket_of(offsets):
    distance = jnp.abs(offsets)
    extra = jnp.zeros_like(distance)
    for threshold in THRESHOLDS:
        extra = extra + (distance >= threshold).astype(jnp.int32)
    nearby = jnp.where(distance < 8, distance, 8 + extra)
    return nearby + 16 * (offsets > 0).astype(jnp.int32)

def gelu_tanh(value_entries):
    return 0.5 * value_entries * (1.0 + jnp.tanh(0.7978845608028654 * (value_entries + 0.044715 * value_entries * value_entries * value_entries)))

def rms_scale(value_entries, gain_row):
    return value_entries * lax.rsqrt(lax.optimization_barrier(jnp.mean(value_entries * value_entries, axis=-1, keepdims=True)) + EPS) * gain_row

def gate_values(routes, normed, router):
    logits = jnp.dot(normed, router, precision=FULL_PRECISION)
    row_peak = lax.optimization_barrier(jnp.max(logits, axis=-1, keepdims=True))
    exponent = jnp.exp(logits - row_peak)
    probabilities = exponent / lax.optimization_barrier(jnp.sum(exponent, axis=-1, keepdims=True))
    choose = (routes[..., None] == jnp.arange(router.shape[1], dtype=jnp.int32)).astype(probabilities.dtype)
    chosen = lax.optimization_barrier(jnp.sum(probabilities[..., None, :] * choose, axis=-1))
    return chosen / lax.optimization_barrier(jnp.sum(chosen, axis=-1, keepdims=True))

def head_attention(parts):
    query_rows, key_rows, value_rows, segment_row, table_row = parts
    positions = jnp.arange(LEN, dtype=jnp.int32)
    bucket_ids = bucket_of(positions[None, :] - positions[:, None])
    raw_scores = low_back(jnp.dot(query_rows, key_rows.T, precision=FULL_PRECISION))
    logits = raw_scores * HEAD_DIM ** (-0.5) + table_row[bucket_ids]
    logits = jnp.where(segment_row[:, None] == segment_row[None, :], logits, NEG)
    row_peak = lax.optimization_barrier(jnp.max(logits, axis=-1, keepdims=True))
    exponent = jnp.exp(logits - row_peak)
    probabilities = exponent / lax.optimization_barrier(jnp.sum(exponent, axis=-1, keepdims=True))
    return jnp.dot(reduced_precision(probabilities), value_rows, precision=FULL_PRECISION)

def expert_ffn(parts):
    expert_rows, expert_gate, expert_up, expert_down = parts
    gate_hidden = low_back(jnp.dot(expert_rows, expert_gate, precision=FULL_PRECISION))
    up_hidden = low_back(jnp.dot(expert_rows, expert_up, precision=FULL_PRECISION))
    hidden = reduced_precision(gelu_tanh(gate_hidden) * up_hidden)
    return low_back(reduced_precision(jnp.dot(hidden, expert_down, precision=FULL_PRECISION)))

def slot_positions(parts):
    route_row, priority_row = parts
    same_expert = route_row[:, None] == route_row[None, :]
    earlier = priority_row[None, :] < priority_row[:, None]
    return lax.optimization_barrier(jnp.sum((same_expert & earlier).astype(jnp.int32), axis=1))

def device_view(value_entries):
    shaped = value_entries.reshape((N_EXP, SEQ_GRP, N_SEQ, LEN // N_SEQ) + value_entries.shape[2:])
    shaped = jnp.swapaxes(shaped, 1, 2)
    return shaped.reshape((N_EXP, N_SEQ, TOK_DEV) + value_entries.shape[2:])

def sequence_view(value_entries):
    shaped = value_entries.reshape((N_EXP, N_SEQ, SEQ_GRP, LEN // N_SEQ) + value_entries.shape[3:])
    shaped = jnp.swapaxes(shaped, 1, 2)
    return shaped.reshape((SEQS, LEN) + value_entries.shape[3:])

def per_head(value_entries):
    return jnp.swapaxes(value_entries.reshape(SEQS, LEN, HEADS, HEAD_DIM), 1, 2).reshape(SEQS * HEADS, LEN, HEAD_DIM)

def reference(block_in, cotangent, segment_ids, expert_routes, pair_priority, gain_attention, w_query, w_key, w_value, w_out, bias_table, gain_experts, w_router, w_gate, w_up, w_down):
    pair_expert = device_view(expert_routes).reshape(N_EXP, N_SEQ, PAIRS)
    slots = lax.map(slot_positions, (pair_expert.reshape(N_EXP * N_SEQ, PAIRS), pair_priority.reshape(N_EXP * N_SEQ, PAIRS)))
    slots = slots.reshape(N_EXP, N_SEQ, PAIRS)
    source_exp = jnp.broadcast_to(jnp.arange(N_EXP, dtype=jnp.int32)[:, None, None], (N_EXP, N_SEQ, PAIRS))
    source_seq = jnp.broadcast_to(jnp.arange(N_SEQ, dtype=jnp.int32)[None, :, None], (N_EXP, N_SEQ, PAIRS))
    segments = jnp.repeat(segment_ids, HEADS, axis=0)

    def project(value_entries, weight_factor):
        return jnp.einsum('gyi,iu->gyu', value_entries, reduced_precision(weight_factor), precision=FULL_PRECISION)

    def forward(inputs, gain_one, query_m, key_m, value_m, out_m, table_m, gain_two, router_m, gate_m, up_m, down_m):
        normed_one = reduced_precision(rms_scale(inputs, reduced_precision(gain_one)))
        queries = low_back(reduced_precision(project(normed_one, query_m)))
        key_gathered = low_back(reduced_precision(project(normed_one, key_m)))
        value_all = low_back(reduced_precision(project(normed_one, value_m)))
        tables = jnp.tile(reduced_precision(table_m).reshape(HEADS, BUCKETS), (SEQS, 1))
        context = lax.map(jax.checkpoint(head_attention), (per_head(queries), per_head(key_gathered), per_head(value_all), segments, tables))
        context = jnp.swapaxes(context.reshape(SEQS, HEADS, LEN, HEAD_DIM), 1, 2).reshape(SEQS, LEN, HD)
        context = low_back(reduced_precision(context))
        mid = inputs + low_back(project(context, out_m))
        normed_two = reduced_precision(rms_scale(mid, reduced_precision(gain_two)))
        gates = gate_values(expert_routes, normed_two, reduced_precision(router_m))
        pair_rows = jnp.repeat(device_view(normed_two), 2, axis=2)
        buffer = jnp.zeros((EXPERTS, N_EXP, N_SEQ, CAP, D), jnp.float32)
        buffer = buffer.at[pair_expert, source_exp, source_seq, slots].set(pair_rows, mode='drop')
        buffer = low_back(buffer)
        expert_out = lax.map(jax.checkpoint(expert_ffn), (buffer.reshape(EXPERTS, N_EXP * N_SEQ * CAP, D), reduced_precision(gate_m), reduced_precision(up_m), reduced_precision(down_m)))
        expert_out = expert_out.reshape(EXPERTS, N_EXP, N_SEQ, CAP, D)
        picked = expert_out.at[pair_expert, source_exp, source_seq, slots].get(mode='fill', fill_value=0.0)
        gates_dev = device_view(gates).reshape(N_EXP, N_SEQ, PAIRS)
        mixture = lax.optimization_barrier(jnp.sum((picked * gates_dev[..., None]).reshape(N_EXP, N_SEQ, TOK_DEV, 2, D), axis=3))
        return mid + sequence_view(mixture)
    result, pullback = jax.vjp(forward, block_in.astype(jnp.float32), gain_attention, w_query, w_key, w_value, w_out, bias_table, gain_experts, w_router, w_gate, w_up, w_down)
    grads = pullback(cotangent.astype(jnp.float32))
    return (result.astype(jnp.bfloat16), grads[0], grads[1], grads[2], grads[3], grads[4], grads[5], grads[6], grads[7], grads[8], grads[9], grads[10], grads[11])
```

```python
from functools import partial

import jax
import jax.numpy as jnp
import numpy as np
from jax import lax
from jax.experimental import pallas as pl
from jax.experimental.pallas import tpu as pltpu
from jax.sharding import PartitionSpec as P

HEAD_DIM = 64
BUCKETS = 32
THRESHOLDS = (12, 16, 23, 32, 46, 64, 91)
MASKED = -1e30
TILE = 256
LANES = 128
NT = (((1,), (1,)), ((), ()))


def bucket_of(d):
    a = np.abs(d)
    extra = sum((a >= t).astype(np.int64) for t in THRESHOLDS)
    return np.where(a < 8, a, 8 + extra) + 16 * (d > 0)


def bias_rows(table_rows, tile):
    u = np.arange(2 * tile)
    x = np.where(u < tile, u, u - 2 * tile)
    ids = np.stack([bucket_of(step * tile - x) for step in (-1, 0, 1)])
    hot = (ids.reshape(-1)[None, :] == np.arange(BUCKETS)[:, None]).astype(np.float32)
    rows = jnp.dot(table_rows.astype(jnp.bfloat16), jnp.asarray(hot, jnp.bfloat16), preferred_element_type=jnp.float32)
    return rows.reshape(table_rows.shape[0], 3, 2 * tile)


def tile_ranges(segments, tile):
    blocks = segments.reshape(-1, tile)
    first, last = blocks[:, 0], blocks[:, -1]
    low = jnp.sum((last[None, :] < first[:, None]).astype(jnp.int32), axis=1)
    high = jnp.sum((first[None, :] <= last[:, None]).astype(jnp.int32), axis=1)
    return jnp.stack([low, high])


def segment_columns(segments):
    lane = jnp.arange(LANES, dtype=jnp.int32)[None, :]
    seg = segments[:, None]
    same = seg == lane
    query_side = jnp.where(same & (lane < 4), MASKED, 0.0).astype(jnp.bfloat16)
    key_side = jnp.where(lane < 4, (~same).astype(jnp.float32), (lane < 9).astype(jnp.float32)).astype(jnp.bfloat16)
    return query_side, key_side


def toeplitz(row, tile):
    wide = jnp.broadcast_to(row, (tile, row.shape[1]))
    return pltpu.roll(wide, 0, 1, stride=1, stride_axis=0)[:, :tile]


def fwd_kernel(ranges, ends, q_ref, k_ref, v_ref, qs_ref, ks_ref, rows_ref, o_ref, lse_ref, bias_ref, vt_ref):
    group, qb = pl.program_id(0), pl.program_id(1)
    tile, span = q_ref.shape
    heads = span // HEAD_DIM

    @pl.when(qb == 0)
    def _():
        for h in range(heads):
            for step in range(3):
                bias_ref[h, step] = toeplitz(rows_ref[h, step : step + 1, :], tile)
        for start in range(0, v_ref.shape[0], tile):
            vt_ref[:, start : start + tile] = v_ref[start : start + tile, :].T

    low, high = ranges[0, qb], ranges[1, qb]
    lane = lax.broadcasted_iota(jnp.int32, (tile, LANES), 1)
    q = q_ref[...] * jnp.bfloat16(HEAD_DIM**-0.5)
    qs = qs_ref[...]
    halves = []
    for h in range(heads):
        part = q[:, h // 2 * LANES : (h // 2 + 1) * LANES]
        keep = (lane < HEAD_DIM) if h % 2 == 0 else (lane >= HEAD_DIM)
        halves.append(jnp.where(keep, part, jnp.zeros_like(part)))

    def side(h, which):
        if which == 1:
            extra = qs
        else:
            value = ends[heads * group + h, which // 2].astype(jnp.bfloat16)
            extra = jnp.where(lane == 7, value, qs)
        return jnp.concatenate([halves[h], extra], axis=1)

    def visit(which):
        queries = [side(h, which) for h in range(heads)]

        def step(kb, carry):
            keys = pl.ds(pl.multiple_of(kb * tile, tile), tile)
            ks = ks_ref[keys, :]
            scores = []
            for h in range(heads):
                kx = jnp.concatenate([k_ref[keys, h // 2 * LANES : (h // 2 + 1) * LANES], ks], axis=1)
                scores.append(lax.dot_general(kx, queries[h], NT, preferred_element_type=jnp.float32))
            out = []
            for h in range(heads):
                peak, total, acc = carry[h]
                s = scores[h]
                if which == 1:
                    s = s + bias_ref[h, kb - qb + 1]
                new = jnp.maximum(peak, jnp.max(s, axis=0, keepdims=True))
                p = jnp.exp(s - new)
                scale = jnp.exp(peak - new)
                total = total * scale + jnp.sum(p, axis=0, keepdims=True)
                vt = vt_ref[h * HEAD_DIM : (h + 1) * HEAD_DIM, keys]
                acc = acc * scale + jnp.dot(vt, p.astype(jnp.bfloat16), preferred_element_type=jnp.float32)
                out.append((new, total, acc))
            return tuple(out)

        return step

    start = tuple(
        (
            jnp.full((1, tile), -3e38, jnp.float32),
            jnp.zeros((1, tile), jnp.float32),
            jnp.zeros((HEAD_DIM, tile), jnp.float32),
        )
        for _ in range(heads)
    )
    near_low, near_high = jnp.maximum(low, qb - 1), jnp.minimum(high, qb + 2)
    state = lax.fori_loop(near_low, near_high, visit(1), start)
    state = lax.fori_loop(low, near_low, visit(0), state)
    state = lax.fori_loop(near_high, high, visit(2), state)
    outs = []
    for h in range(heads):
        peak, total, acc = state[h]
        outs.append(acc / total)
        lse_ref[h // 2, h % 2 : h % 2 + 1, :] = peak + jnp.log(total)
    o_ref[...] = jnp.concatenate(outs, axis=0).T.astype(o_ref.dtype)


FWD_PAIRS = 4


def attend_forward(qkv, qs, ks, ranges, rows, ends):
    length, width = qkv.shape[0], qkv.shape[1] // 3
    tile = min(TILE, length)
    pairs = width // LANES
    together = FWD_PAIRS if pairs % FWD_PAIRS == 0 else 1
    span = together * LANES
    tiles = length // tile
    spec = pltpu.PrefetchScalarGridSpec(
        num_scalar_prefetch=2,
        grid=(pairs // together, tiles),
        in_specs=[
            pl.BlockSpec((tile, span), lambda p, i, *_: (i, p)),
            pl.BlockSpec((length, span), lambda p, i, *_: (0, width // span + p)),
            pl.BlockSpec((length, span), lambda p, i, *_: (0, 2 * (width // span) + p)),
            pl.BlockSpec((tile, LANES), lambda p, i, *_: (i, 0)),
            pl.BlockSpec((length, LANES), lambda p, i, *_: (0, 0)),
            pl.BlockSpec((2 * together, 3, 2 * tile), lambda p, i, *_: (p, 0, 0)),
        ],
        out_specs=[
            pl.BlockSpec((tile, span), lambda p, i, *_: (i, p)),
            pl.BlockSpec((together, 2, tile), lambda p, i, *_: (p, 0, i)),
        ],
        scratch_shapes=[
            pltpu.VMEM((2 * together, 3, tile, tile), jnp.float32),
            pltpu.VMEM((span, length), jnp.bfloat16),
        ],
    )
    return pl.pallas_call(
        fwd_kernel,
        name="attend_forward",
        out_shape=(
            jax.ShapeDtypeStruct((length, width), jnp.bfloat16),
            jax.ShapeDtypeStruct((pairs, 2, length), jnp.float32),
        ),
        grid_spec=spec,
        compiler_params=pltpu.CompilerParams(
            dimension_semantics=("arbitrary", "arbitrary"), vmem_limit_bytes=48 << 20
        ),
        cost_estimate=pl.CostEstimate(flops=length * length * width * 4, bytes_accessed=length * width * 8, transcendentals=0),
    )(ranges, ends, qkv, qkv, qkv, qs, ks, rows)


def pieces(row):
    high = row.astype(jnp.bfloat16).astype(jnp.float32)
    mid = (row - high).astype(jnp.bfloat16).astype(jnp.float32)
    return high, mid, row - high - mid


def bwd_kernel(ranges, ends, q_ref, k_ref, v_ref, do_ref, o_ref, lse_ref, qs_ref, ks_ref, rows_ref,
               dq_ref, dk_ref, dv_ref, diag_ref, far_ref,
               qx_ref, dox_ref, kt_ref, bias_ref, dsum_ref, fsum_ref, dqt_ref, dka_ref, dva_ref):
    pair = pl.program_id(0)
    length = q_ref.shape[0]
    tile = bias_ref.shape[2]
    tiles = length // tile
    for h in range(2):
        for step in range(3):
            bias_ref[h, step] = toeplitz(rows_ref[h, step : step + 1, :], tile)
    dsum_ref[...] = jnp.zeros_like(dsum_ref)
    fsum_ref[...] = jnp.zeros_like(fsum_ref)
    dqt_ref[...] = jnp.zeros_like(dqt_ref)
    lane = lax.broadcasted_iota(jnp.int32, (tile, LANES), 1)
    sub = lax.broadcasted_iota(jnp.int32, (LANES, tile), 0)
    pick = (lax.broadcasted_iota(jnp.int32, (8, LANES), 1) // HEAD_DIM == lax.broadcasted_iota(jnp.int32, (8, LANES), 0)).astype(jnp.float32)

    @pl.loop(0, tiles)
    def _(i):
        at = pl.ds(pl.multiple_of(i * tile, tile), tile)
        q = q_ref[at, :] * jnp.bfloat16(HEAD_DIM**-0.5)
        do = do_ref[at, :]
        zero = jnp.zeros_like(q)
        product = do.astype(jnp.float32) * o_ref[at, :].astype(jnp.float32)
        delta = lax.dot_general(pick, product, NT, precision=lax.Precision.HIGHEST, preferred_element_type=jnp.float32)
        kt_ref[:, at] = k_ref[at, :].T
        for h in range(2):
            keep = (lane < HEAD_DIM) if h == 0 else (lane >= HEAD_DIM)
            a, b, c = pieces(-lse_ref[0, h : h + 1, at])
            extra = jnp.where(sub == 4, a, jnp.where(sub == 5, b, jnp.where(sub == 6, c, 0.0)))
            extra = extra.T.astype(jnp.bfloat16) + qs_ref[at, :]
            left, right = ends[2 * pair + h, 0].astype(jnp.bfloat16), ends[2 * pair + h, 1].astype(jnp.bfloat16)
            extra = jnp.where(lane == 7, left, jnp.where(lane == 8, right, extra))
            qx_ref[h, at, :] = jnp.concatenate([jnp.where(keep, q, zero), extra], axis=1)
            a, b, c = pieces(-delta[h : h + 1, :])
            extra = jnp.where(sub == 4, a, jnp.where(sub == 5, b, jnp.where(sub == 6, c, 0.0)))
            dox_ref[h, at, :] = jnp.concatenate([jnp.where(keep, do, zero), extra.T.astype(jnp.bfloat16)], axis=1)

    ones3 = ((lane >= 4) & (lane < 7)).astype(jnp.bfloat16)

    @pl.loop(0, tiles)
    def _(kb):
        low, high = ranges[0, kb], ranges[1, kb]
        keys = pl.ds(pl.multiple_of(kb * tile, tile), tile)
        k, ks = k_ref[keys, :], ks_ref[keys, :]
        vx = jnp.concatenate([v_ref[keys, :], ones3], axis=1)
        nil = jnp.zeros_like(ks)
        dka_ref[...] = jnp.zeros_like(dka_ref)
        dva_ref[...] = jnp.zeros_like(dva_ref)

        def visit(which):
            if which == 0:
                extra = jnp.where(lane == 8, nil, ks)
            elif which == 2:
                extra = jnp.where(lane == 7, nil, ks)
            else:
                extra = jnp.where((lane == 7) | (lane == 8), nil, ks)
            kx = jnp.concatenate([k, extra], axis=1)

            def step(qb, carry):
                at = pl.ds(pl.multiple_of(qb * tile, tile), tile)
                weights, grads = [], []
                for h in range(2):
                    qx, dox = qx_ref[h, at, :], dox_ref[h, at, :]
                    s = lax.dot_general(kx, qx, NT, preferred_element_type=jnp.float32)
                    if which == 1:
                        s = s + bias_ref[h, kb - qb + 1]
                    p = jnp.exp(s)
                    dp = lax.dot_general(vx, dox, NT, preferred_element_type=jnp.float32)
                    ds = p * dp
                    if which == 1:
                        dsum_ref[h, kb - qb + 1] += ds
                    else:
                        fsum_ref[h, which // 2] += jnp.sum(ds.reshape(tile // 8, 8, tile), axis=0)
                    weights.append(p.astype(jnp.bfloat16))
                    grads.append(ds.astype(jnp.bfloat16))
                    rows = slice(h * HEAD_DIM, (h + 1) * HEAD_DIM)
                    dqt_ref[rows, at] += jnp.dot(kt_ref[rows, keys], grads[h], preferred_element_type=jnp.float32)
                both_do = jnp.concatenate([dox_ref[0, at, :LANES], dox_ref[1, at, :LANES]], axis=0)
                both_q = jnp.concatenate([qx_ref[0, at, :LANES], qx_ref[1, at, :LANES]], axis=0)
                dva_ref[...] += jnp.dot(jnp.concatenate(weights, axis=1), both_do, preferred_element_type=jnp.float32)
                dka_ref[...] += jnp.dot(jnp.concatenate(grads, axis=1), both_q, preferred_element_type=jnp.float32)
                return carry

            return step

        near_low, near_high = jnp.maximum(low, kb - 1), jnp.minimum(high, kb + 2)
        lax.fori_loop(near_low, near_high, visit(1), 0)
        lax.fori_loop(near_high, high, visit(0), 0)
        lax.fori_loop(low, near_low, visit(2), 0)
        dk_ref[keys, :] = dka_ref[...].astype(dk_ref.dtype)
        dv_ref[keys, :] = dva_ref[...].astype(dv_ref.dtype)

    @pl.loop(0, tiles)
    def _(i):
        at = pl.ds(pl.multiple_of(i * tile, tile), tile)
        dq_ref[at, :] = (dqt_ref[:, at] * HEAD_DIM**-0.5).T.astype(dq_ref.dtype)

    for h in range(2):
        for step in range(3):
            diag_ref[h, step : step + 1, :] = diagonals(dsum_ref, h, step, tile)
        for step in range(2):
            total = jnp.sum(fsum_ref[h, step], axis=0, keepdims=True)
            far_ref[h, step : step + 1, :] = total


def diagonals(dsum_ref, h, step, tile):
    width = 2 * tile
    acc = jnp.zeros((8, width), jnp.float32)
    for group in range(tile // 8):
        part = dsum_ref[h, step, group * 8 : (group + 1) * 8, :]
        part = jnp.concatenate([part, jnp.zeros((8, tile), jnp.float32)], axis=1)
        acc = acc + (pltpu.roll(part, width - 8 * group, 1) if group else part)
    row = lax.broadcasted_iota(jnp.int32, (8, width), 0)
    for bit in (1, 2, 4):
        acc = jnp.where((row & bit) != 0, pltpu.roll(acc, width - bit, 1), acc)
    return jnp.sum(acc, axis=0, keepdims=True)


def attend_backward(qkv, do, o, lse, qs, ks, ranges, rows, ends):
    length, width = do.shape
    tile = min(TILE, length)
    pairs = width // LANES
    heads = width // HEAD_DIM
    column = pl.BlockSpec((length, LANES), lambda p, *_: (0, p))
    fixed = pl.BlockSpec((length, LANES), lambda p, *_: (0, 0))
    spec = pltpu.PrefetchScalarGridSpec(
        num_scalar_prefetch=2,
        grid=(pairs,),
        in_specs=[
            column,
            pl.BlockSpec((length, LANES), lambda p, *_: (0, pairs + p)),
            pl.BlockSpec((length, LANES), lambda p, *_: (0, 2 * pairs + p)),
            column,
            column,
            pl.BlockSpec((1, 2, length), lambda p, *_: (p, 0, 0)),
            fixed, fixed,
            pl.BlockSpec((2, 3, 2 * tile), lambda p, *_: (p, 0, 0)),
        ],
        out_specs=[
            column, column, column,
            pl.BlockSpec((2, 3, 2 * tile), lambda p, *_: (p, 0, 0)),
            pl.BlockSpec((2, 2, tile), lambda p, *_: (p, 0, 0)),
        ],
        scratch_shapes=[
            pltpu.VMEM((2, length, 2 * LANES), jnp.bfloat16),
            pltpu.VMEM((2, length, 2 * LANES), jnp.bfloat16),
            pltpu.VMEM((LANES, length), jnp.bfloat16),
            pltpu.VMEM((2, 3, tile, tile), jnp.float32),
            pltpu.VMEM((2, 3, tile, tile), jnp.float32),
            pltpu.VMEM((2, 2, 8, tile), jnp.float32),
            pltpu.VMEM((LANES, length), jnp.float32),
            pltpu.VMEM((tile, LANES), jnp.float32),
            pltpu.VMEM((tile, LANES), jnp.float32),
        ],
    )
    low = jax.ShapeDtypeStruct((length, width), jnp.bfloat16)
    return pl.pallas_call(
        bwd_kernel,
        name="attend_backward",
        out_shape=(
            low, low, low,
            jax.ShapeDtypeStruct((heads, 3, 2 * tile), jnp.float32),
            jax.ShapeDtypeStruct((heads, 2, tile), jnp.float32),
        ),
        grid_spec=spec,
        compiler_params=pltpu.CompilerParams(
            dimension_semantics=("arbitrary",), vmem_limit_bytes=40 << 20
        ),
        cost_estimate=pl.CostEstimate(flops=length * length * width * 10, bytes_accessed=length * width * 16, transcendentals=0),
    )(ranges, ends, qkv, qkv, qkv, do, o, lse, qs, ks, rows)


def bucket_sums(diag, far, tile):
    u = np.arange(2 * tile)
    x = np.where(u < tile, u, u - 2 * tile)
    ids = np.stack([bucket_of(step * tile - x) for step in (-1, 0, 1)])
    hot = (ids.reshape(-1)[:, None] == np.arange(BUCKETS)[None, :]).astype(np.float32)
    sums = jnp.dot(diag.reshape(diag.shape[0], -1), jnp.asarray(hot), precision=lax.Precision.HIGHEST)
    outer = jnp.sum(far, axis=2)
    ends = np.zeros((2, BUCKETS), np.float32)
    ends[0, 15] = 1
    ends[1, 31] = 1
    return sums + outer[:, 0:1] * ends[0] + outer[:, 1:2] * ends[1]


EPS = 1e-06
FULL_PRECISION = lax.Precision.HIGHEST


def gelu_tanh(value_entries):
    return (
        0.5
        * value_entries
        * (
            1.0
            + jnp.tanh(
                0.7978845608028654
                * (value_entries + 0.044715 * value_entries * value_entries * value_entries)
            )
        )
    )


def geglu_product(gate_part, up_part):
    return gelu_tanh(gate_part) * up_part


def rms_scale(value_entries, gain_row):
    return (
        value_entries
        * lax.rsqrt(jnp.mean(value_entries * value_entries, axis=-1, keepdims=True) + EPS)
        * gain_row
    )


def gate_values(routes, normed, router):
    logits = jnp.dot(normed, router, precision=FULL_PRECISION)
    row_peak = jnp.max(logits, axis=-1, keepdims=True)
    exponent = jnp.exp(logits - row_peak)
    probabilities = exponent / jnp.sum(exponent, axis=-1, keepdims=True)
    choose = (routes[..., None] == jnp.arange(router.shape[1], dtype=jnp.int32)).astype(
        probabilities.dtype
    )
    chosen = jnp.sum(probabilities[..., None, :] * choose, axis=-1)
    return chosen / jnp.sum(chosen, axis=-1, keepdims=True)


def dot32(a, b):
    return jnp.dot(a, b, preferred_element_type=jnp.float32)


ALL = ("z", "x", "exp")
SEQ = ("z", "x")


def per_device(
    block_in,
    cotangent,
    segment_ids,
    expert_routes,
    pair_priority,
    gain_attention,
    w_query,
    w_key,
    w_value,
    w_out,
    bias_table,
    gain_experts,
    w_router,
    w_gate,
    w_up,
    w_down,
):
    low_type = jnp.bfloat16
    groups, local_len, width = block_in.shape
    tokens = groups * local_len
    rows_own = w_query.shape[0]
    split = lax.axis_size("x")
    exp_count = lax.axis_size("exp")
    seq_count = groups * split
    length = local_len * seq_count
    x_at, z_at = lax.axis_index("x"), lax.axis_index("z")
    head_width = w_query.shape[1] // split
    experts_all = w_router.shape[1]
    bias_own = bias_table.shape[0]

    small = jnp.concatenate(
        [
            gain_attention[:, None],
            gain_experts[:, None],
            jnp.pad(bias_table, (0, rows_own - bias_own))[:, None],
            w_router,
        ],
        axis=1,
    )
    small = jnp.pad(small, ((0, 0), (0, LANES - small.shape[1])))
    packed = jnp.concatenate(
        [part.astype(low_type) for part in (w_query, w_key, w_value, w_out, small)], axis=1
    )
    packed = lax.all_gather(packed, ALL, axis=0, tiled=True)
    gate_w = lax.all_gather(w_gate[0].astype(low_type), SEQ, axis=0, tiled=True)
    up_w = lax.all_gather(w_up[0].astype(low_type), SEQ, axis=0, tiled=True)
    down_w = lax.all_gather(w_down[0].astype(low_type), SEQ, axis=0, tiled=True)

    outgoing = jnp.broadcast_to(block_in[:, None], (groups, split, local_len, width))
    sequence = lax.all_to_all(
        outgoing.reshape(seq_count, local_len, width), SEQ, split_axis=0, concat_axis=0, tiled=True
    ).reshape(length, width)

    hd = w_query.shape[1]
    out_w = packed[:, 3 * hd : 4 * hd]
    small_all = packed[:, 4 * hd :]
    gain_one = small_all[:, 0].astype(jnp.float32)
    gain_two = small_all[:, 1].astype(jnp.float32)
    table_all = small_all[:, 2].reshape(-1, rows_own)[:, :bias_own].reshape(-1, BUCKETS)
    router_w = small_all[:, 3 : 3 + experts_all]
    heads_here = head_width // HEAD_DIM
    qkv_w = [
        lax.dynamic_slice_in_dim(packed, part * hd + x_at * head_width, head_width, 1)
        for part in range(3)
    ]
    qkv_w = jnp.concatenate(qkv_w, axis=1)
    table_rows = lax.dynamic_slice_in_dim(table_all, x_at * heads_here, heads_here, 0)

    normed_one = rms_scale(sequence.astype(jnp.float32), gain_one).astype(low_type)
    qkv = dot32(normed_one, qkv_w).astype(low_type)
    segments = lax.dynamic_index_in_dim(segment_ids, z_at, 0, keepdims=False)
    tile = min(TILE, length)
    query_side, key_side = segment_columns(segments)
    ranges = tile_ranges(segments, tile)
    rows = bias_rows(table_rows, tile)
    ends = jnp.stack([table_rows[:, 15], table_rows[:, 31]], axis=1).astype(jnp.float32)
    contexts, log_totals = attend_forward(qkv, query_side, key_side, ranges, rows, ends)
    context_local = lax.all_to_all(
        contexts.reshape(seq_count, local_len, head_width), SEQ, split_axis=0, concat_axis=0, tiled=True
    )
    context_local = (
        context_local.reshape(groups, split, local_len, head_width)
        .transpose(0, 2, 1, 3)
        .reshape(tokens, hd)
    )
    inputs = block_in.astype(jnp.float32).reshape(tokens, width)
    mid = inputs + dot32(context_local, out_w)
    normed_two_full, norm_two_back = jax.vjp(rms_scale, mid, gain_two)
    normed_two = normed_two_full.astype(low_type)
    routes_local = expert_routes.reshape(tokens, -1)
    top_count = routes_local.shape[1]
    gates, gates_back = jax.vjp(
        partial(gate_values, routes_local),
        normed_two.astype(jnp.float32),
        router_w.astype(jnp.float32),
    )
    pair_experts = routes_local.reshape(-1)
    priority = pair_priority.reshape(-1)
    expert_table = (
        pair_experts[:, None] == jnp.arange(experts_all, dtype=jnp.int32)[None, :]
    ).astype(low_type)
    earlier = (priority[None, :] < priority[:, None]).astype(low_type)
    ahead_counts = dot32(earlier, expert_table)
    slots = jnp.sum(ahead_counts * expert_table, axis=1).astype(jnp.int32)
    capacity = (5 * top_count * tokens + 4 * experts_all - 1) // (4 * experts_all)
    slot_count = experts_all * capacity
    slot_index = jnp.where(slots < capacity, pair_experts * capacity + slots, slot_count)
    slot_table = (
        slot_index[:, None] == jnp.arange(slot_count, dtype=jnp.int32)[None, :]
    ).astype(low_type)
    slot_table = slot_table.reshape(tokens, top_count, slot_count)
    token_table = jnp.sum(slot_table, axis=1, dtype=jnp.float32).astype(low_type)
    buffer = jnp.einsum(
        "ts,td->sd", token_table, normed_two, preferred_element_type=jnp.float32
    ).astype(low_type)

    def swap_experts(rows_):
        return lax.all_to_all(
            rows_.reshape(exp_count, capacity, width), "exp", split_axis=0, concat_axis=0, tiled=True
        ).reshape(slot_count, width)

    arrived = swap_experts(buffer)
    gate_hidden = dot32(arrived, gate_w)
    up_hidden = dot32(arrived, up_w)
    hidden_pair, geglu_back = jax.vjp(geglu_product, gate_hidden, up_hidden)
    hidden = hidden_pair.astype(low_type)
    expert_out = dot32(hidden, down_w).astype(low_type)
    returned = swap_experts(expert_out)
    picked = jnp.einsum("tks,sd->tkd", slot_table, returned, preferred_element_type=jnp.float32)
    mixture = jnp.sum(picked * gates[..., None], axis=1)
    block_out = (mid + mixture).astype(low_type).reshape(groups, local_len, width)

    grad_out = cotangent.astype(jnp.float32).reshape(tokens, width)
    gate_grad_pairs = jnp.sum(picked * grad_out[:, None, :], axis=-1)
    pair_grad = (gates[..., None] * grad_out[:, None, :]).astype(low_type)
    slot_grad = jnp.einsum(
        "tks,tkd->sd", slot_table, pair_grad, preferred_element_type=jnp.float32
    ).astype(low_type)
    expert_grad_in = swap_experts(slot_grad)
    hidden_grad = jnp.einsum("sd,fd->sf", expert_grad_in, down_w, preferred_element_type=jnp.float32)
    gate_hidden_grad, up_hidden_grad = geglu_back(hidden_grad)
    gate_low = gate_hidden_grad.astype(low_type)
    up_low = up_hidden_grad.astype(low_type)
    arrived_grad = jnp.einsum("sf,df->sd", gate_low, gate_w, preferred_element_type=jnp.float32)
    arrived_grad = (
        arrived_grad
        + jnp.einsum("sf,df->sd", up_low, up_w, preferred_element_type=jnp.float32)
    ).astype(low_type)
    back_rows = swap_experts(arrived_grad)

    def summed(a, b):
        return jnp.einsum("sa,sb->ab", a, b, preferred_element_type=jnp.float32)

    def scatter_experts(total):
        return lax.psum_scatter(total.astype(low_type), SEQ, scatter_dimension=0, tiled=True).astype(
            jnp.float32
        )[None]

    down_owned = scatter_experts(summed(hidden, expert_grad_in))
    gate_owned = scatter_experts(summed(arrived, gate_low))
    up_owned = scatter_experts(summed(arrived, up_low))
    row_grad = jnp.einsum("ts,sd->td", token_table, back_rows, preferred_element_type=jnp.float32)
    normed_two_grad, router_sum = gates_back(gate_grad_pairs)
    mid_part, gain_two_sum = norm_two_back(normed_two_grad + row_grad)
    mid_grad = grad_out + mid_part
    attention_grad = mid_grad.astype(low_type)
    out_w_sum = summed(context_local, attention_grad)
    context_grad = jnp.einsum(
        "td,kd->tk", attention_grad, out_w, preferred_element_type=jnp.float32
    ).astype(low_type)
    context_grad = (
        context_grad.reshape(groups, local_len, split, head_width)
        .transpose(0, 2, 1, 3)
        .reshape(seq_count, local_len, head_width)
    )
    context_heads = lax.all_to_all(
        context_grad, SEQ, split_axis=0, concat_axis=0, tiled=True
    ).reshape(length, head_width)
    query_back, key_back, value_back, diag, far = attend_backward(
        qkv, context_heads, contexts, log_totals, query_side, key_side, ranges, rows, ends
    )
    table_local = bucket_sums(diag, far, tile)

    def through(grads, part):
        weight = qkv_w[:, part * head_width : (part + 1) * head_width]
        return jnp.einsum("tk,dk->td", grads, weight, preferred_element_type=jnp.float32)

    normed_part = (through(query_back, 0) + through(key_back, 1) + through(value_back, 2)).astype(low_type)
    normed_parts = lax.all_to_all(
        normed_part.reshape(seq_count, local_len, width), SEQ, split_axis=0, concat_axis=0, tiled=True
    ).reshape(groups, split, local_len, width)
    normed_one_grad = jnp.sum(normed_parts.astype(jnp.float32), axis=1).reshape(tokens, width)
    _, norm_one_back = jax.vjp(rms_scale, inputs, gain_one)
    input_part, gain_one_sum = norm_one_back(normed_one_grad)
    block_in_grad = (mid_grad + input_part).reshape(groups, local_len, width)

    def by_owner(total):
        columns = total.shape[1]
        shaped = total.reshape(groups, split, exp_count, rows_own, columns)
        return shaped.transpose(0, 2, 1, 3, 4).reshape(-1, columns)

    def scatter_rows(total):
        return lax.psum_scatter(
            by_owner(total).astype(low_type), ("z", "exp"), scatter_dimension=0, tiled=True
        ).reshape(split, rows_own, -1)

    out_part = lax.all_to_all(scatter_rows(out_w_sum), "x", split_axis=0, concat_axis=0, tiled=True)
    out_w_out = jnp.sum(out_part.astype(jnp.float32), axis=0)
    qkv_sum = jnp.concatenate(
        [summed(normed_one, grads) for grads in (query_back, key_back, value_back)], axis=1
    )
    qkv_part = lax.all_to_all(scatter_rows(qkv_sum), "x", split_axis=0, concat_axis=0, tiled=True)
    qkv_part = qkv_part.reshape(split, rows_own, 3, head_width).transpose(2, 1, 0, 3)
    qkv_part = qkv_part.reshape(3, rows_own, hd).astype(jnp.float32)

    table_sum = lax.dynamic_update_slice_in_dim(
        jnp.zeros(table_all.shape, jnp.float32), table_local, x_at * heads_here, 0
    ).reshape(-1, bias_own)
    table_sum = jnp.pad(table_sum, ((0, 0), (0, rows_own - bias_own)))[:, None, :]
    little = jnp.concatenate(
        [
            gain_one_sum.reshape(-1, 1, rows_own),
            gain_two_sum.reshape(-1, 1, rows_own),
            table_sum,
            router_sum.reshape(-1, rows_own, experts_all).transpose(0, 2, 1),
        ],
        axis=1,
    )
    little = jnp.sum(lax.all_to_all(little, ALL, split_axis=0, concat_axis=0, tiled=True), axis=0)
    return (
        block_out,
        block_in_grad,
        little[0],
        qkv_part[0],
        qkv_part[1],
        qkv_part[2],
        out_w_out,
        little[2, :bias_own],
        little[1],
        little[3:].T,
        gate_owned,
        up_owned,
        down_owned,
    )


def solution(mesh):
    def run(*args):
        groups = args[0].shape[0] // mesh.shape["exp"]
        seq_count, exp_count = mesh.shape["seq"], mesh.shape["exp"]
        grid = mesh.devices.reshape(groups, seq_count // groups, exp_count)
        fine = jax.sharding.Mesh(grid, ALL)
        placed = P("exp", SEQ, None)
        whole = P(ALL)
        matrix = P(ALL, None)
        return jax.shard_map(
            per_device,
            mesh=fine,
            in_specs=(
                placed, placed, P("exp", None), placed, placed,
                whole, matrix, matrix, matrix, matrix, whole, whole, matrix,
                placed, placed, placed,
            ),
            out_specs=(
                placed, placed, whole, matrix, matrix, matrix, matrix, whole, whole, matrix,
                placed, placed, placed,
            ),
            check_vma=False,
        )(*args)

    return run
```

```python
from functools import partial

import jax
import jax.numpy as jnp
import numpy as np
from jax import lax
from jax.experimental import pallas as pl
from jax.experimental.pallas import tpu as pltpu
from jax.sharding import PartitionSpec as P

HEAD_DIM = 64
BUCKETS = 32
THRESHOLDS = (12, 16, 23, 32, 46, 64, 91)
MASKED = -1e30
TILE = 256
LANES = 128
NT = (((1,), (1,)), ((), ()))


def bucket_of(d):
    a = np.abs(d)
    extra = sum((a >= t).astype(np.int64) for t in THRESHOLDS)
    return np.where(a < 8, a, 8 + extra) + 16 * (d > 0)


def bias_rows(table_rows, tile):
    u = np.arange(2 * tile)
    x = np.where(u < tile, u, u - 2 * tile)
    ids = np.stack([bucket_of(step * tile - x) for step in (-1, 0, 1)])
    hot = (ids.reshape(-1)[None, :] == np.arange(BUCKETS)[:, None]).astype(np.float32)
    rows = jnp.dot(table_rows.astype(jnp.bfloat16), jnp.asarray(hot, jnp.bfloat16), preferred_element_type=jnp.float32)
    return rows.reshape(table_rows.shape[0], 3, 2 * tile)


def tile_ranges(segments, tile):
    blocks = segments.reshape(-1, tile)
    first, last = blocks[:, 0], blocks[:, -1]
    low = jnp.sum((last[None, :] < first[:, None]).astype(jnp.int32), axis=1)
    high = jnp.sum((first[None, :] <= last[:, None]).astype(jnp.int32), axis=1)
    return jnp.stack([low, high])


def segment_columns(segments):
    lane = jnp.arange(LANES, dtype=jnp.int32)[None, :]
    seg = segments[:, None]
    same = seg == lane
    query_side = jnp.where(same & (lane < 4), MASKED, 0.0).astype(jnp.bfloat16)
    key_side = jnp.where(lane < 4, (~same).astype(jnp.float32), (lane < 9).astype(jnp.float32)).astype(jnp.bfloat16)
    return query_side, key_side


def toeplitz(row, tile):
    wide = jnp.broadcast_to(row, (tile, row.shape[1]))
    return pltpu.roll(wide, 0, 1, stride=1, stride_axis=0)[:, :tile]


def block_at(index, own, tile):
    return pl.ds(pl.multiple_of((index ^ own[0]) * tile, tile), tile)


def fwd_kernel(ranges, ends, own, q_ref, k_ref, v_ref, qs_ref, ks_ref, rows_ref, o_ref, lse_ref, bias_ref, vt_ref):
    group, qb = pl.program_id(0), pl.program_id(1)
    tile, span = q_ref.shape
    heads = span // HEAD_DIM

    @pl.when(qb == 0)
    def _():
        for h in range(heads):
            for step in range(3):
                bias_ref[h, step] = toeplitz(rows_ref[h, step : step + 1, :], tile)
        for start in range(0, v_ref.shape[0], tile):
            vt_ref[:, start : start + tile] = v_ref[start : start + tile, :].T

    low, high = ranges[0, qb], ranges[1, qb]
    lane = lax.broadcasted_iota(jnp.int32, (tile, LANES), 1)
    q = q_ref[...] * jnp.bfloat16(HEAD_DIM**-0.5)
    qs = qs_ref[...]
    halves = []
    for h in range(heads):
        part = q[:, h // 2 * LANES : (h // 2 + 1) * LANES]
        keep = (lane < HEAD_DIM) if h % 2 == 0 else (lane >= HEAD_DIM)
        halves.append(jnp.where(keep, part, jnp.zeros_like(part)))

    def side(h, which):
        if which == 1:
            extra = qs
        else:
            value = ends[heads * group + h, which // 2].astype(jnp.bfloat16)
            extra = jnp.where(lane == 7, value, qs)
        return jnp.concatenate([halves[h], extra], axis=1)

    def visit(which):
        queries = [side(h, which) for h in range(heads)]

        def step(kb, carry):
            keys = block_at(kb, own, tile)
            ks = ks_ref[keys, :]
            scores = []
            for h in range(heads):
                kx = jnp.concatenate([k_ref[keys, h // 2 * LANES : (h // 2 + 1) * LANES], ks], axis=1)
                scores.append(lax.dot_general(kx, queries[h], NT, preferred_element_type=jnp.float32))
            out = []
            for h in range(heads):
                peak, total, acc = carry[h]
                s = scores[h]
                if which == 1:
                    s = s + bias_ref[h, kb - qb + 1]
                new = jnp.maximum(peak, jnp.max(s, axis=0, keepdims=True))
                p = jnp.exp(s - new)
                scale = jnp.exp(peak - new)
                total = total * scale + jnp.sum(p, axis=0, keepdims=True)
                vt = vt_ref[h * HEAD_DIM : (h + 1) * HEAD_DIM, keys]
                acc = acc * scale + jnp.dot(vt, p.astype(jnp.bfloat16), preferred_element_type=jnp.float32)
                out.append((new, total, acc))
            return tuple(out)

        return step

    start = tuple(
        (
            jnp.full((1, tile), -3e38, jnp.float32),
            jnp.zeros((1, tile), jnp.float32),
            jnp.zeros((HEAD_DIM, tile), jnp.float32),
        )
        for _ in range(heads)
    )
    near_low, near_high = jnp.maximum(low, qb - 1), jnp.minimum(high, qb + 2)
    state = lax.fori_loop(near_low, near_high, visit(1), start)
    state = lax.fori_loop(low, near_low, visit(0), state)
    state = lax.fori_loop(near_high, high, visit(2), state)
    outs = []
    for h in range(heads):
        peak, total, acc = state[h]
        outs.append(acc / total)
        lse_ref[h // 2, h % 2 : h % 2 + 1, :] = peak + jnp.log(total)
    o_ref[...] = jnp.concatenate(outs, axis=0).T.astype(o_ref.dtype)


FWD_PAIRS = 4


def attend_forward(qkv, qs, ks, ranges, rows, ends, own, tile):
    length, width = qkv.shape[0], qkv.shape[1] // 3
    pairs = width // LANES
    together = FWD_PAIRS if pairs % FWD_PAIRS == 0 else 1
    span = together * LANES
    tiles = length // tile
    spec = pltpu.PrefetchScalarGridSpec(
        num_scalar_prefetch=3,
        grid=(pairs // together, tiles),
        in_specs=[
            pl.BlockSpec((tile, span), lambda p, i, r, e, own: (i ^ own[0], p)),
            pl.BlockSpec((length, span), lambda p, i, *_: (0, width // span + p)),
            pl.BlockSpec((length, span), lambda p, i, *_: (0, 2 * (width // span) + p)),
            pl.BlockSpec((tile, LANES), lambda p, i, r, e, own: (i ^ own[0], 0)),
            pl.BlockSpec((length, LANES), lambda p, i, *_: (0, 0)),
            pl.BlockSpec((2 * together, 3, 2 * tile), lambda p, i, *_: (p, 0, 0)),
        ],
        out_specs=[
            pl.BlockSpec((tile, span), lambda p, i, *_: (i, p)),
            pl.BlockSpec((together, 2, tile), lambda p, i, *_: (p, 0, i)),
        ],
        scratch_shapes=[
            pltpu.VMEM((2 * together, 3, tile, tile), jnp.float32),
            pltpu.VMEM((span, length), jnp.bfloat16),
        ],
    )
    return pl.pallas_call(
        fwd_kernel,
        name="attend_forward",
        out_shape=(
            jax.ShapeDtypeStruct((length, width), jnp.bfloat16),
            jax.ShapeDtypeStruct((pairs, 2, length), jnp.float32),
        ),
        grid_spec=spec,
        compiler_params=pltpu.CompilerParams(
            dimension_semantics=("arbitrary", "arbitrary"), vmem_limit_bytes=48 << 20
        ),
        cost_estimate=pl.CostEstimate(flops=length * length * width * 4, bytes_accessed=length * width * 8, transcendentals=0),
    )(ranges, ends, own, qkv, qkv, qkv, qs, ks, rows)


def pieces(row):
    high = row.astype(jnp.bfloat16).astype(jnp.float32)
    mid = (row - high).astype(jnp.bfloat16).astype(jnp.float32)
    return high, mid, row - high - mid


def bwd_kernel(ranges, ends, own, q_ref, k_ref, v_ref, do_ref, o_ref, lse_ref, qs_ref, ks_ref, rows_ref,
               dq_ref, dk_ref, dv_ref, diag_ref, far_ref,
               qx_ref, dox_ref, kt_ref, bias_ref, dsum_ref, fsum_ref, dqt_ref, dka_ref, dva_ref):
    pair = pl.program_id(0)
    length = q_ref.shape[0]
    tile = bias_ref.shape[2]
    tiles = length // tile
    for h in range(2):
        for step in range(3):
            bias_ref[h, step] = toeplitz(rows_ref[h, step : step + 1, :], tile)
    dsum_ref[...] = jnp.zeros_like(dsum_ref)
    fsum_ref[...] = jnp.zeros_like(fsum_ref)
    dqt_ref[...] = jnp.zeros_like(dqt_ref)
    lane = lax.broadcasted_iota(jnp.int32, (tile, LANES), 1)
    sub = lax.broadcasted_iota(jnp.int32, (LANES, tile), 0)
    pick = (lax.broadcasted_iota(jnp.int32, (8, LANES), 1) // HEAD_DIM == lax.broadcasted_iota(jnp.int32, (8, LANES), 0)).astype(jnp.float32)

    @pl.loop(0, tiles)
    def _(i):
        line = pl.ds(pl.multiple_of(i * tile, tile), tile)
        at = block_at(i, own, tile)
        q = q_ref[at, :] * jnp.bfloat16(HEAD_DIM**-0.5)
        do = do_ref[line, :]
        zero = jnp.zeros_like(q)
        product = do.astype(jnp.float32) * o_ref[line, :].astype(jnp.float32)
        delta = lax.dot_general(pick, product, NT, precision=lax.Precision.HIGHEST, preferred_element_type=jnp.float32)
        kt_ref[:, at] = k_ref[at, :].T
        for h in range(2):
            keep = (lane < HEAD_DIM) if h == 0 else (lane >= HEAD_DIM)
            a, b, c = pieces(-lse_ref[0, h : h + 1, line])
            extra = jnp.where(sub == 4, a, jnp.where(sub == 5, b, jnp.where(sub == 6, c, 0.0)))
            extra = extra.T.astype(jnp.bfloat16) + qs_ref[at, :]
            left, right = ends[2 * pair + h, 0].astype(jnp.bfloat16), ends[2 * pair + h, 1].astype(jnp.bfloat16)
            extra = jnp.where(lane == 7, left, jnp.where(lane == 8, right, extra))
            qx_ref[h, at, :] = jnp.concatenate([jnp.where(keep, q, zero), extra], axis=1)
            a, b, c = pieces(-delta[h : h + 1, :])
            extra = jnp.where(sub == 4, a, jnp.where(sub == 5, b, jnp.where(sub == 6, c, 0.0)))
            dox_ref[h, at, :] = jnp.concatenate([jnp.where(keep, do, zero), extra.T.astype(jnp.bfloat16)], axis=1)

    ones3 = ((lane >= 4) & (lane < 7)).astype(jnp.bfloat16)

    @pl.loop(0, tiles)
    def _(kb):
        low, high = ranges[0, kb], ranges[1, kb]
        keys = block_at(kb, own, tile)
        k, ks = k_ref[keys, :], ks_ref[keys, :]
        vx = jnp.concatenate([v_ref[keys, :], ones3], axis=1)
        nil = jnp.zeros_like(ks)
        dka_ref[...] = jnp.zeros_like(dka_ref)
        dva_ref[...] = jnp.zeros_like(dva_ref)

        def visit(which):
            if which == 0:
                extra = jnp.where(lane == 8, nil, ks)
            elif which == 2:
                extra = jnp.where(lane == 7, nil, ks)
            else:
                extra = jnp.where((lane == 7) | (lane == 8), nil, ks)
            kx = jnp.concatenate([k, extra], axis=1)

            def step(qb, carry):
                at = block_at(qb, own, tile)
                weights, grads = [], []
                for h in range(2):
                    qx, dox = qx_ref[h, at, :], dox_ref[h, at, :]
                    s = lax.dot_general(kx, qx, NT, preferred_element_type=jnp.float32)
                    if which == 1:
                        s = s + bias_ref[h, kb - qb + 1]
                    p = jnp.exp(s)
                    dp = lax.dot_general(vx, dox, NT, preferred_element_type=jnp.float32)
                    ds = p * dp
                    if which == 1:
                        dsum_ref[h, kb - qb + 1] += ds
                    else:
                        fsum_ref[h, which // 2] += jnp.sum(ds.reshape(tile // 8, 8, tile), axis=0)
                    weights.append(p.astype(jnp.bfloat16))
                    grads.append(ds.astype(jnp.bfloat16))
                    rows = slice(h * HEAD_DIM, (h + 1) * HEAD_DIM)
                    dqt_ref[rows, at] += jnp.dot(kt_ref[rows, keys], grads[h], preferred_element_type=jnp.float32)
                both_do = jnp.concatenate([dox_ref[0, at, :LANES], dox_ref[1, at, :LANES]], axis=0)
                both_q = jnp.concatenate([qx_ref[0, at, :LANES], qx_ref[1, at, :LANES]], axis=0)
                dva_ref[...] += jnp.dot(jnp.concatenate(weights, axis=1), both_do, preferred_element_type=jnp.float32)
                dka_ref[...] += jnp.dot(jnp.concatenate(grads, axis=1), both_q, preferred_element_type=jnp.float32)
                return carry

            return step

        near_low, near_high = jnp.maximum(low, kb - 1), jnp.minimum(high, kb + 2)
        lax.fori_loop(near_low, near_high, visit(1), 0)
        lax.fori_loop(near_high, high, visit(0), 0)
        lax.fori_loop(low, near_low, visit(2), 0)
        dk_ref[keys, :] = dka_ref[...].astype(dk_ref.dtype)
        dv_ref[keys, :] = dva_ref[...].astype(dv_ref.dtype)

    @pl.loop(0, tiles)
    def _(i):
        at = pl.ds(pl.multiple_of(i * tile, tile), tile)
        dq_ref[at, :] = (dqt_ref[:, at] * HEAD_DIM**-0.5).T.astype(dq_ref.dtype)

    for h in range(2):
        for step in range(3):
            diag_ref[h, step : step + 1, :] = diagonals(dsum_ref, h, step, tile)
        for step in range(2):
            total = jnp.sum(fsum_ref[h, step], axis=0, keepdims=True)
            far_ref[h, step : step + 1, :] = total


def diagonals(dsum_ref, h, step, tile):
    width = 2 * tile
    acc = jnp.zeros((8, width), jnp.float32)
    for group in range(tile // 8):
        part = dsum_ref[h, step, group * 8 : (group + 1) * 8, :]
        part = jnp.concatenate([part, jnp.zeros((8, tile), jnp.float32)], axis=1)
        acc = acc + (pltpu.roll(part, width - 8 * group, 1) if group else part)
    row = lax.broadcasted_iota(jnp.int32, (8, width), 0)
    for bit in (1, 2, 4):
        acc = jnp.where((row & bit) != 0, pltpu.roll(acc, width - bit, 1), acc)
    return jnp.sum(acc, axis=0, keepdims=True)


def attend_backward(qkv, do, o, lse, qs, ks, ranges, rows, ends, own, tile):
    length, width = do.shape
    pairs = width // LANES
    heads = width // HEAD_DIM
    column = pl.BlockSpec((length, LANES), lambda p, *_: (0, p))
    fixed = pl.BlockSpec((length, LANES), lambda p, *_: (0, 0))
    spec = pltpu.PrefetchScalarGridSpec(
        num_scalar_prefetch=3,
        grid=(pairs,),
        in_specs=[
            column,
            pl.BlockSpec((length, LANES), lambda p, *_: (0, pairs + p)),
            pl.BlockSpec((length, LANES), lambda p, *_: (0, 2 * pairs + p)),
            column,
            column,
            pl.BlockSpec((1, 2, length), lambda p, *_: (p, 0, 0)),
            fixed, fixed,
            pl.BlockSpec((2, 3, 2 * tile), lambda p, *_: (p, 0, 0)),
        ],
        out_specs=[
            column, column, column,
            pl.BlockSpec((2, 3, 2 * tile), lambda p, *_: (p, 0, 0)),
            pl.BlockSpec((2, 2, tile), lambda p, *_: (p, 0, 0)),
        ],
        scratch_shapes=[
            pltpu.VMEM((2, length, 2 * LANES), jnp.bfloat16),
            pltpu.VMEM((2, length, 2 * LANES), jnp.bfloat16),
            pltpu.VMEM((LANES, length), jnp.bfloat16),
            pltpu.VMEM((2, 3, tile, tile), jnp.float32),
            pltpu.VMEM((2, 3, tile, tile), jnp.float32),
            pltpu.VMEM((2, 2, 8, tile), jnp.float32),
            pltpu.VMEM((LANES, length), jnp.float32),
            pltpu.VMEM((tile, LANES), jnp.float32),
            pltpu.VMEM((tile, LANES), jnp.float32),
        ],
    )
    low = jax.ShapeDtypeStruct((length, width), jnp.bfloat16)
    return pl.pallas_call(
        bwd_kernel,
        name="attend_backward",
        out_shape=(
            low, low, low,
            jax.ShapeDtypeStruct((heads, 3, 2 * tile), jnp.float32),
            jax.ShapeDtypeStruct((heads, 2, tile), jnp.float32),
        ),
        grid_spec=spec,
        compiler_params=pltpu.CompilerParams(
            dimension_semantics=("arbitrary",), vmem_limit_bytes=40 << 20
        ),
        cost_estimate=pl.CostEstimate(flops=length * length * width * 10, bytes_accessed=length * width * 16, transcendentals=0),
    )(ranges, ends, own, qkv, qkv, qkv, do, o, lse, qs, ks, rows)


def bucket_sums(diag, far, tile):
    u = np.arange(2 * tile)
    x = np.where(u < tile, u, u - 2 * tile)
    ids = np.stack([bucket_of(step * tile - x) for step in (-1, 0, 1)])
    hot = (ids.reshape(-1)[:, None] == np.arange(BUCKETS)[None, :]).astype(np.float32)
    sums = jnp.dot(diag.reshape(diag.shape[0], -1), jnp.asarray(hot), precision=lax.Precision.HIGHEST)
    outer = jnp.sum(far, axis=2)
    ends = np.zeros((2, BUCKETS), np.float32)
    ends[0, 15] = 1
    ends[1, 31] = 1
    return sums + outer[:, 0:1] * ends[0] + outer[:, 1:2] * ends[1]


GELU_A, GELU_B = 0.7978845608028654, 0.044715
FF_TILE = 256
EXTRA = 16


def expert_kernel(own_ref, x_ref, dy_ref, gate_ref, wg_ref, wu_ref, wd_ref, *refs):
    h_ref, dg_ref, du_ref, dx_ref, part_ref, acc_ref = refs[-6:]
    step = pl.program_id(0)
    rows = gate_ref.shape[0]
    chunk = rows // 2 if rows % 32 == 0 else rows

    @pl.when(step == 0)
    def _():
        acc_ref[...] = jnp.zeros_like(acc_ref)
        part_ref[...] = jnp.zeros_like(part_ref)

    wg, wu, wd = wg_ref[...], wu_ref[...], wd_ref[...]
    for start in range(0, rows, chunk):
        at = slice(start, start + chunk)
        x, dy = x_ref[at, :], dy_ref[at, :]
        g = jnp.dot(x, wg, preferred_element_type=jnp.float32)
        u = jnp.dot(x, wu, preferred_element_type=jnp.float32)
        raw = lax.dot_general(dy, wd, NT, preferred_element_type=jnp.float32)
        square = g * g
        half = 0.5 + 0.5 * jnp.tanh(g * (GELU_A + (GELU_A * GELU_B) * square))
        gelu = g * half
        slope = half + 2.0 * gelu * (1.0 - half) * (GELU_A + (3.0 * GELU_A * GELU_B) * square)
        h = gelu * u
        product = raw * h
        total = product[:, :LANES]
        for column in range(LANES, product.shape[1], LANES):
            total = total + product[:, column : column + LANES]
        part_ref[at, :] += total
        dh = raw * gate_ref[at, :]
        du = (dh * gelu).astype(jnp.bfloat16)
        dg = (dh * u * slope).astype(jnp.bfloat16)
        h_ref[at, :] = h.astype(jnp.bfloat16)
        dg_ref[at, :] = dg
        du_ref[at, :] = du
        acc_ref[at, :] += lax.dot_general(dg, wg, NT, preferred_element_type=jnp.float32) + lax.dot_general(
            du, wu, NT, preferred_element_type=jnp.float32
        )

    @pl.when(step == pl.num_programs(0) - 1)
    def _():
        dx_ref[:rows, :] = acc_ref[...].astype(dx_ref.dtype)
        sums = jnp.sum(part_ref[...].T, axis=0, keepdims=True)
        high = sums.astype(jnp.bfloat16).astype(jnp.float32)
        middle = (sums - high).astype(jnp.bfloat16).astype(jnp.float32)
        line = lax.broadcasted_iota(jnp.int32, (EXTRA, rows), 0)
        lines = jnp.where(line == 0, high, jnp.where(line == 1, middle, jnp.where(line == 2, sums - high - middle, 0.0)))
        dx_ref[rows:, :] = jnp.zeros_like(dx_ref[rows:, :])
        dx_ref[rows:, :rows] = lines.astype(dx_ref.dtype)


def expert_block(at, count, x, dy, gate, wgu, wd, earlier):
    rows, width = gate.shape[0], x.shape[1]
    hidden = wd.shape[0]
    tile = FF_TILE
    whole = jax.ShapeDtypeStruct((count * rows, hidden), jnp.bfloat16)
    fixed = lambda i, *_: (0, 0)
    out_block = pl.BlockSpec((rows, tile), lambda i, *_: (at, i))
    spec = pltpu.PrefetchScalarGridSpec(
        num_scalar_prefetch=1,
        grid=(hidden // tile,),
        in_specs=[
            pl.BlockSpec((rows, width), fixed),
            pl.BlockSpec((rows, width), fixed),
            pl.BlockSpec((rows, 1), fixed),
            pl.BlockSpec((width, tile), lambda i, *_: (0, i)),
            pl.BlockSpec((width, tile), lambda i, *_: (0, hidden // tile + i)),
            pl.BlockSpec((tile, width), lambda i, *_: (i, 0)),
        ]
        + [pl.BlockSpec(memory_space=pl.ANY)] * len(earlier),
        out_specs=[
            out_block,
            out_block,
            out_block,
            pl.BlockSpec((rows + EXTRA, width), fixed),
        ],
        scratch_shapes=[pltpu.VMEM((rows, LANES), jnp.float32), pltpu.VMEM((rows, width), jnp.float32)],
    )
    return pl.pallas_call(
        expert_kernel,
        name="expert_block",
        out_shape=(
            whole,
            whole,
            whole,
            jax.ShapeDtypeStruct((rows + EXTRA, width), jnp.bfloat16),
        ),
        grid_spec=spec,
        input_output_aliases={7 + i: i for i in range(len(earlier))},
        compiler_params=pltpu.CompilerParams(dimension_semantics=("arbitrary",), vmem_limit_bytes=40 << 20),
        cost_estimate=pl.CostEstimate(
            flops=10 * rows * width * hidden, bytes_accessed=6 * width * hidden + 6 * rows * hidden, transcendentals=0
        ),
    )(jnp.zeros((1,), jnp.int32), x, dy, gate, wgu, wgu, wd, *earlier)


EPS = 1e-06
FULL_PRECISION = lax.Precision.HIGHEST
ALL = ("z", "x", "exp")
SEQ = ("z", "x")
LOW = jnp.bfloat16


def dot32(a, b):
    return jnp.dot(a, b, preferred_element_type=jnp.float32)


def dot_nt(a, b):
    return lax.dot_general(a, b, NT, preferred_element_type=jnp.float32)


def dot_tn(a, b):
    return lax.dot_general(a, b, (((0,), (0,)), ((), ())), preferred_element_type=jnp.float32)


def partner(value, axis, offset):
    count = lax.axis_size(axis)
    return lax.ppermute(value, axis, [(i, i ^ offset) for i in range(count)])


def bits_of(count):
    return [1 << b for b in reversed(range(count.bit_length() - 1))]


def reorder(stacked, own):
    count = stacked.shape[0]
    return jnp.stack([lax.dynamic_index_in_dim(stacked, own ^ r, 0, keepdims=False) for r in range(count)])


def gather_double(value, steps):
    for axis, bit in steps:
        other = partner(value, axis, bit)
        high = (lax.axis_index(axis) & bit) != 0
        value = jnp.stack([jnp.where(high, other, value), jnp.where(high, value, other)])
    return value


def scatter_halve(value, steps):
    for axis, bit in steps:
        high = (lax.axis_index(axis) & bit) != 0
        keep = jnp.where(high, value[1], value[0])
        give = jnp.where(high, value[0], value[1])
        value = (keep.astype(jnp.float32) + partner(give, axis, bit).astype(jnp.float32)).astype(LOW)
    return value


def ring_of(groups, split):
    order = []
    for x in range(split):
        line = range(groups) if x % 2 == 0 else reversed(range(groups))
        order += [z * split + x for z in line]
    place = [order.index(s) for s in range(len(order))]
    ahead = [(order[i], order[(i + 1) % len(order)]) for i in range(len(order))]
    return jnp.asarray(order, jnp.int32), jnp.asarray(place, jnp.int32), ahead


def pick(values, index):
    return lax.dynamic_index_in_dim(values, index, 0, keepdims=False)


def ring_gather(piece, groups, split, own):
    order, place, ahead = ring_of(groups, split)
    count = groups * split
    here = pick(place, own)
    rows = piece.shape[0]
    whole = jnp.zeros((count * rows, piece.shape[1]), piece.dtype)
    whole = lax.dynamic_update_slice_in_dim(whole, piece, own * rows, 0)
    forward = backward = piece
    for k in range(1, count // 2 + 1):
        forward = lax.ppermute(forward, SEQ, ahead)
        if k < count - count // 2:
            backward = lax.ppermute(backward, SEQ, [(b, a) for a, b in ahead])
        whole = lax.dynamic_update_slice_in_dim(whole, forward, pick(order, (here - k + count) % count) * rows, 0)
        if k < count - count // 2:
            whole = lax.dynamic_update_slice_in_dim(whole, backward, pick(order, (here + k) % count) * rows, 0)
    return whole


def norm_scale(value):
    return lax.rsqrt(jnp.mean(value * value, axis=-1, keepdims=True) + EPS)


def norm_back(scale, normed, gain, grad):
    scaled = grad * gain
    return scale * (scaled - normed * jnp.mean(scaled * normed, axis=-1, keepdims=True))


def split3(value):
    high = value.astype(LOW)
    rest = value - high.astype(jnp.float32)
    middle = rest.astype(LOW)
    return [high, middle, (rest - middle.astype(jnp.float32)).astype(LOW)]


def per_device(
    block_in,
    cotangent,
    segment_ids,
    expert_routes,
    pair_priority,
    gain_attention,
    w_query,
    w_key,
    w_value,
    w_out,
    bias_table,
    gain_experts,
    w_router,
    w_gate,
    w_up,
    w_down,
):
    groups, local_len, width = block_in.shape
    tokens = groups * local_len
    rows_own, hd = w_query.shape
    split = lax.axis_size("x")
    exp_count = lax.axis_size("exp")
    seq_count = groups * split
    length = local_len * seq_count
    x_at, z_at, e_at = lax.axis_index("x"), lax.axis_index("z"), lax.axis_index("exp")
    s_at = z_at * split + x_at
    head_width = hd // split
    heads_here = head_width // HEAD_DIM
    experts_all = w_router.shape[1]
    bias_own = bias_table.shape[0]
    tile = min(TILE, local_len)
    own = s_at.astype(jnp.int32).reshape(1)
    z_bits, x_bits, e_bits = bits_of(groups), bits_of(split), bits_of(exp_count)

    input_r = reorder(block_in, z_at)

    arrived = [[None] * split for _ in range(groups)]
    for rz in reversed(range(groups)):
        arrived[rz][0] = partner(input_r[rz], "z", rz) if rz else input_r[0]
    for rz in [0] + list(reversed(range(1, groups))):
        for rx in range(1, split):
            arrived[rz][rx] = partner(arrived[rz][0], "x", rx)
    sequence = jnp.stack([block for line in arrived for block in line]).reshape(length, width)

    gate_up_own = jnp.concatenate([w_gate[0].astype(LOW), w_up[0].astype(LOW)], axis=1)
    sequence, gate_up_own, down_own = lax.optimization_barrier((sequence, gate_up_own, w_down[0].astype(LOW)))
    gate_up_w = ring_gather(gate_up_own, groups, split, s_at)
    down_w = lax.all_gather(down_own, SEQ, axis=0, tiled=True)

    small = jnp.concatenate(
        [
            gain_attention[:, None],
            gain_experts[:, None],
            jnp.pad(bias_table, (0, rows_own - bias_own))[:, None],
            w_router,
        ],
        axis=1,
    )
    small = jnp.pad(small, ((0, 0), (0, LANES - small.shape[1]))).astype(LOW)
    share = jnp.stack(
        [part.astype(LOW).reshape(rows_own, split, head_width) for part in (w_query, w_key, w_value)], axis=2
    )
    share = share.reshape(rows_own, split, 3 * head_width).transpose(1, 0, 2)
    share = jnp.concatenate([share, jnp.broadcast_to(small, (split,) + small.shape)], axis=2)
    shares = [lax.dynamic_index_in_dim(share, x_at ^ r, 0, keepdims=False) for r in range(split)]
    shares = [shares[0]] + [partner(shares[r], "x", r) for r in range(1, split)]
    by_x = reorder(jnp.stack(shares), x_at)
    steps = [("z", b) for b in z_bits] + [("exp", b) for b in e_bits]
    packed = gather_double(by_x, steps)
    ne, nz = len(e_bits), len(z_bits)
    packed = packed.transpose(
        tuple(ne + i for i in reversed(range(nz))) + (ne + nz,) + tuple(reversed(range(ne))) + (ne + nz + 1, ne + nz + 2)
    ).reshape(width, 3 * head_width + LANES)
    qkv_w, small_all = packed[:, : 3 * head_width], packed[:, 3 * head_width :]
    out_steps = [("z", b) for b in z_bits] + [("x", b) for b in x_bits] + [("exp", b) for b in e_bits]
    out_w = gather_double(w_out.astype(LOW), out_steps)
    nx = len(x_bits)
    out_w = out_w.transpose(
        tuple(ne + nx + i for i in reversed(range(nz)))
        + tuple(ne + i for i in reversed(range(nx)))
        + tuple(reversed(range(ne)))
        + (ne + nx + nz, ne + nx + nz + 1)
    )
    out_w = out_w.reshape(hd, width)

    gain_one = small_all[:, 0].astype(jnp.float32)
    gain_two = small_all[:, 1].astype(jnp.float32)
    table_all = small_all[:, 2].reshape(-1, rows_own)[:, :bias_own].reshape(-1, BUCKETS)
    router_t = small_all[:, 3 : 3 + experts_all].T
    table_rows = lax.dynamic_slice_in_dim(table_all, x_at * heads_here, heads_here, 0)

    routes = expert_routes.reshape(tokens, -1)
    top_count = routes.shape[1]
    priority = pair_priority.reshape(-1)
    pair_experts = routes.reshape(-1)
    ahead = (pair_experts[None, :] == pair_experts[:, None]) & (priority[None, :] < priority[:, None])
    slots = jnp.sum(ahead.astype(jnp.int32), axis=1)
    capacity = (5 * top_count * tokens + 4 * experts_all - 1) // (4 * experts_all)
    slot_count = experts_all * capacity
    slot_index = jnp.where(slots < capacity, (pair_experts ^ e_at) * capacity + slots, slot_count)
    slot_index = slot_index.reshape(tokens, top_count)
    every_slot = jnp.arange(slot_count, dtype=jnp.int32)[None, :]
    table = sum((slot_index[:, k : k + 1] == every_slot).astype(LOW) for k in range(top_count))
    tables = [table[:, r * capacity : (r + 1) * capacity] for r in range(exp_count)]
    grad_low = cotangent.reshape(tokens, width)
    grad_slots = [dot_tn(part, grad_low).astype(LOW) for part in tables]

    wide = sequence.astype(jnp.float32)
    normed_one = (wide * norm_scale(wide) * gain_one).astype(LOW)
    qkv = dot32(normed_one, qkv_w).astype(LOW)
    qkv, grad_slots = lax.optimization_barrier((qkv, grad_slots))
    grad_slots = [grad_slots[0]] + [partner(grad_slots[r], "exp", r) for r in range(1, exp_count)]
    segments = lax.dynamic_index_in_dim(segment_ids, z_at, 0, keepdims=False)
    ranges = tile_ranges(segments, tile)
    seg_blocks = segments.reshape(seq_count, local_len)
    query_side, key_side = segment_columns(reorder(seg_blocks, s_at).reshape(length))
    rows = bias_rows(table_rows, tile)
    ends = jnp.stack([table_rows[:, 15], table_rows[:, 31]], axis=1).astype(jnp.float32)
    contexts, log_totals = attend_forward(qkv, query_side, key_side, ranges, rows, ends, own, tile)

    def exchange_positions(blocks):
        return lax.all_to_all(blocks, SEQ, split_axis=0, concat_axis=0, tiled=True)

    context_local = exchange_positions(contexts.reshape(seq_count, local_len, head_width))
    context_local = (
        context_local.reshape(groups, split, local_len, head_width).transpose(0, 2, 1, 3).reshape(tokens, hd)
    )
    inputs = block_in.astype(jnp.float32).reshape(tokens, width)
    mid = inputs + dot32(context_local, out_w)
    scale_two = norm_scale(mid)
    normed_two = (mid * scale_two * gain_two).astype(LOW)

    logits = dot_nt(router_t, normed_two)
    exponent = jnp.exp(logits - jnp.max(logits, axis=0, keepdims=True))
    probabilities = exponent / jnp.sum(exponent, axis=0, keepdims=True)
    expert_ids = jnp.arange(experts_all, dtype=jnp.int32)[:, None]
    chosen = sum((routes[:, k][None, :] == expert_ids).astype(jnp.float32) for k in range(top_count))
    chosen_total = jnp.sum(probabilities * chosen, axis=0, keepdims=True)
    gates = probabilities * chosen / chosen_total
    gates_r = reorder(gates, e_at)

    gate_slots = jnp.sum(
        table.astype(jnp.float32).reshape(tokens, exp_count, capacity) * gates_r.T[:, :, None], axis=0
    )
    gate_lines = jnp.pad(jnp.stack(split3(gate_slots), axis=1), ((0, 0), (0, EXTRA - 3), (0, width - capacity)))

    def values_below(rows_):
        return jnp.sum(rows_[capacity : capacity + 3, :capacity].astype(jnp.float32), axis=0)

    sent = [None] * exp_count
    for r in reversed(range(exp_count)):
        sent[r] = jnp.concatenate([dot_tn(tables[r], normed_two).astype(LOW), gate_lines[r]], axis=0)
        if r:
            sent[r] = partner(sent[r], "exp", r)
    sent_gate = [values_below(rows_) for rows_ in sent]

    earlier = ()
    back = [None] * exp_count
    for r in range(exp_count):
        hidden, gate_low, up_low, dx = expert_block(
            r, exp_count, sent[r], grad_slots[r], sent_gate[r][:, None], gate_up_w, down_w, earlier
        )
        earlier = (hidden, gate_low, up_low)
        back[r] = partner(dx, "exp", r) if r else dx

    slot_rows = jnp.concatenate([rows_[:capacity] for rows_ in sent], axis=0)
    slot_gates = jnp.concatenate(sent_gate, axis=0)[:, None]
    slot_grads = (slot_gates * jnp.concatenate(grad_slots, axis=0).astype(jnp.float32)).astype(LOW)
    expert_out = (slot_gates * dot32(hidden, down_w)).astype(LOW)
    down_sum = dot_tn(hidden, slot_grads).astype(LOW)
    gate_sum = dot_tn(slot_rows, gate_low).astype(LOW)
    up_sum = dot_tn(slot_rows, up_low).astype(LOW)

    gate_grad = jnp.sum(
        table.astype(jnp.float32).reshape(tokens, exp_count, capacity) * jnp.stack([values_below(rows_) for rows_ in back])[None], axis=2
    )
    gate_grad = reorder(gate_grad.T, e_at)
    chosen_grad = chosen * (gate_grad - jnp.sum(gates * gate_grad, axis=0, keepdims=True)) / chosen_total
    logit_grad = probabilities * (chosen_grad - jnp.sum(probabilities * chosen_grad, axis=0, keepdims=True))
    logit_pieces = jnp.concatenate(split3(logit_grad), axis=0)
    router_sum = jnp.sum(dot32(logit_pieces, normed_two).reshape(3, experts_all, width), axis=0)
    normed_two_grad = dot_tn(logit_pieces, jnp.concatenate([router_t] * 3, axis=0))
    for r in range(exp_count):
        normed_two_grad = normed_two_grad + dot32(tables[r], back[r][:capacity])
    unit_two = mid * scale_two
    gain_two_sum = jnp.sum(normed_two_grad * unit_two, axis=0)
    grad_out = grad_low.astype(jnp.float32)
    mid_grad = grad_out + norm_back(scale_two, unit_two, gain_two, normed_two_grad)
    attention_grad = mid_grad.astype(LOW)
    context_grad = dot_nt(attention_grad, out_w).astype(LOW)
    context_grad = (
        context_grad.reshape(groups, local_len, split, head_width)
        .transpose(0, 2, 1, 3)
        .reshape(seq_count, local_len, head_width)
    )
    context_heads = exchange_positions(context_grad).reshape(length, head_width)

    def scatter_experts(total):
        return lax.psum_scatter(total, SEQ, scatter_dimension=0, tiled=True).astype(jnp.float32)[None]

    down_owned = scatter_experts(down_sum)
    gate_owned = scatter_experts(gate_sum)
    up_owned = scatter_experts(up_sum)
    context_heads, _, _, _, expert_out = lax.optimization_barrier(
        (context_heads, down_sum[:8], gate_sum[:8], up_sum[:8], expert_out)
    )

    returned = [expert_out[:capacity]] + [
        partner(expert_out[r * capacity : (r + 1) * capacity], "exp", r) for r in range(1, exp_count)
    ]
    block_out = (mid + dot32(table, jnp.concatenate(returned, axis=0))).astype(LOW)

    block_out = block_out.reshape(groups, local_len, width)

    def by_step(total, with_x):
        columns = total.shape[1]
        shaped = total.astype(LOW).reshape((2,) * (nz + nx + ne) + (rows_own, columns))
        z_dims = tuple(reversed(range(nz)))
        x_dims = tuple(nz + i for i in reversed(range(nx)))
        e_dims = tuple(nz + nx + i for i in reversed(range(ne)))
        rest = (nz + nx + ne, nz + nx + ne + 1)
        if with_x:
            return shaped.transpose(e_dims + z_dims + x_dims + rest)
        return shaped.transpose(e_dims + z_dims + tuple(reversed(x_dims)) + rest)

    halving = [("exp", b) for b in reversed(e_bits)] + [("z", b) for b in reversed(z_bits)]
    x_halving = [("x", b) for b in reversed(x_bits)]
    out_w_sum = dot_tn(context_local, attention_grad)
    out_w_out = scatter_halve(by_step(out_w_sum, True), halving + x_halving).astype(jnp.float32)

    query_back, key_back, value_back, diag, far = attend_backward(
        qkv, context_heads, contexts, log_totals, query_side, key_side, ranges, rows, ends, own, tile
    )
    table_local = bucket_sums(diag, far, tile)

    def through(grads, part):
        return dot_nt(grads, qkv_w[:, part * head_width : (part + 1) * head_width])

    normed_part = through(query_back, 0) + through(key_back, 1) + through(value_back, 2)
    normed_part = normed_part.reshape(groups, split, local_len, width)
    pieces_back = [None] * groups
    for rz in list(reversed(range(1, groups))) + [0]:
        total = normed_part[rz, 0]
        for rx in range(1, split):
            total = total + partner(normed_part[rz, rx].astype(LOW), "x", rx).astype(jnp.float32)
        pieces_back[rz] = partner(total.astype(LOW), "z", rz).astype(jnp.float32) if rz else total
    normed_one_grad = reorder(jnp.stack(pieces_back), z_at).reshape(tokens, width)
    scale_one = norm_scale(inputs)
    unit_one = inputs * scale_one
    gain_one_sum = jnp.sum(normed_one_grad * unit_one, axis=0)
    block_in_grad = (mid_grad + norm_back(scale_one, unit_one, gain_one, normed_one_grad)).reshape(groups, local_len, width)

    qkv_sum = jnp.concatenate(
        [dot_tn(normed_one, grads).astype(LOW) for grads in (query_back, key_back, value_back)], axis=1
    )
    qkv_part = scatter_halve(by_step(qkv_sum, False), halving).reshape(split, rows_own, 3 * head_width)
    qkv_own = [lax.dynamic_index_in_dim(qkv_part, x_at ^ r, 0, keepdims=False) for r in range(split)]
    qkv_own = [qkv_own[0]] + [partner(qkv_own[r], "x", r) for r in range(1, split)]
    qkv_own = reorder(jnp.stack(qkv_own), x_at).reshape(split, rows_own, 3, head_width)
    qkv_own = qkv_own.transpose(2, 1, 0, 3).reshape(3, rows_own, hd).astype(jnp.float32)

    table_sum = lax.dynamic_update_slice_in_dim(
        jnp.zeros(table_all.shape, jnp.float32), table_local, x_at * heads_here, 0
    ).reshape(-1, bias_own)
    table_sum = jnp.pad(table_sum, ((0, 0), (0, rows_own - bias_own)))[:, None, :]
    little = jnp.concatenate(
        [
            gain_one_sum.reshape(-1, 1, rows_own),
            gain_two_sum.reshape(-1, 1, rows_own),
            table_sum,
            router_sum.reshape(experts_all, -1, rows_own).transpose(1, 0, 2),
        ],
        axis=1,
    )
    little = jnp.sum(lax.all_to_all(little, ALL, split_axis=0, concat_axis=0, tiled=True), axis=0)
    return (
        block_out,
        block_in_grad,
        little[0],
        qkv_own[0],
        qkv_own[1],
        qkv_own[2],
        out_w_out,
        little[2, :bias_own],
        little[1],
        little[3:].T,
        gate_owned,
        up_owned,
        down_owned,
    )


def solution(mesh):
    def run(*args):
        groups = args[0].shape[0] // mesh.shape["exp"]
        seq_count, exp_count = mesh.shape["seq"], mesh.shape["exp"]
        grid = mesh.devices.reshape(groups, seq_count // groups, exp_count)
        fine = jax.sharding.Mesh(grid, ALL)
        placed = P("exp", SEQ, None)
        whole = P(ALL)
        matrix = P(ALL, None)
        return jax.shard_map(
            per_device,
            mesh=fine,
            in_specs=(
                placed, placed, P("exp", None), placed, placed,
                whole, matrix, matrix, matrix, matrix, whole, whole, matrix,
                placed, placed, placed,
            ),
            out_specs=(
                placed, placed, whole, matrix, matrix, matrix, matrix, whole, whole, matrix,
                placed, placed, placed,
            ),
            check_vma=False,
        )(*args)

    return run
```

```python
from functools import partial

import jax
import jax.numpy as jnp
import numpy as np
from jax import lax
from jax.experimental import pallas as pl
from jax.experimental.pallas import tpu as pltpu
from jax.sharding import PartitionSpec as P

HEAD_DIM = 64
BUCKETS = 32
THRESHOLDS = (12, 16, 23, 32, 46, 64, 91)
MASKED = -1e30
TILE = 256
LANES = 128
NT = (((1,), (1,)), ((), ()))


def bucket_of(d):
    a = np.abs(d)
    extra = sum((a >= t).astype(np.int64) for t in THRESHOLDS)
    return np.where(a < 8, a, 8 + extra) + 16 * (d > 0)


def bias_rows(table_rows, tile):
    u = np.arange(2 * tile)
    x = np.where(u < tile, u, u - 2 * tile)
    ids = np.stack([bucket_of(step * tile - x) for step in (-1, 0, 1)])
    hot = (ids.reshape(-1)[None, :] == np.arange(BUCKETS)[:, None]).astype(np.float32)
    rows = jnp.dot(table_rows.astype(jnp.bfloat16), jnp.asarray(hot, jnp.bfloat16), preferred_element_type=jnp.float32)
    return rows.reshape(table_rows.shape[0], 3, 2 * tile)


def tile_ranges(segments, tile):
    blocks = segments.reshape(-1, tile)
    first, last = blocks[:, 0], blocks[:, -1]
    low = jnp.sum((last[None, :] < first[:, None]).astype(jnp.int32), axis=1)
    high = jnp.sum((first[None, :] <= last[:, None]).astype(jnp.int32), axis=1)
    return jnp.stack([low, high])


def segment_columns(segments):
    lane = jnp.arange(LANES, dtype=jnp.int32)[None, :]
    seg = segments[:, None]
    same = seg == lane
    query_side = jnp.where(same & (lane < 4), MASKED, 0.0).astype(jnp.bfloat16)
    key_side = jnp.where(lane < 4, (~same).astype(jnp.float32), (lane < 9).astype(jnp.float32)).astype(jnp.bfloat16)
    return query_side, key_side


def toeplitz(row, tile):
    wide = jnp.broadcast_to(row, (tile, row.shape[1]))
    return pltpu.roll(wide, 0, 1, stride=1, stride_axis=0)[:, :tile]


def block_at(index, own, tile):
    return pl.ds(pl.multiple_of((index ^ own[0]) * tile, tile), tile)


def fwd_kernel(ranges, ends, own, q_ref, k_ref, v_ref, qs_ref, ks_ref, rows_ref, o_ref, lse_ref, bias_ref, vt_ref):
    group, qb = pl.program_id(0), pl.program_id(1)
    tile, span = q_ref.shape
    heads = span // HEAD_DIM

    @pl.when(qb == 0)
    def _():
        for h in range(heads):
            for step in range(3):
                bias_ref[h, step] = toeplitz(rows_ref[h, step : step + 1, :], tile)
        for start in range(0, v_ref.shape[0], tile):
            vt_ref[:, start : start + tile] = v_ref[start : start + tile, :].T

    low, high = ranges[0, qb], ranges[1, qb]
    lane = lax.broadcasted_iota(jnp.int32, (tile, LANES), 1)
    q = q_ref[...] * jnp.bfloat16(HEAD_DIM**-0.5)
    qs = qs_ref[...]
    halves = []
    for h in range(heads):
        part = q[:, h // 2 * LANES : (h // 2 + 1) * LANES]
        keep = (lane < HEAD_DIM) if h % 2 == 0 else (lane >= HEAD_DIM)
        halves.append(jnp.where(keep, part, jnp.zeros_like(part)))

    def side(h, which):
        if which == 1:
            extra = qs
        else:
            value = ends[heads * group + h, which // 2].astype(jnp.bfloat16)
            extra = jnp.where(lane == 7, value, qs)
        return jnp.concatenate([halves[h], extra], axis=1)

    def visit(which):
        queries = [side(h, which) for h in range(heads)]

        def step(kb, carry):
            keys = block_at(kb, own, tile)
            ks = ks_ref[keys, :]
            scores = []
            for h in range(heads):
                kx = jnp.concatenate([k_ref[keys, h // 2 * LANES : (h // 2 + 1) * LANES], ks], axis=1)
                scores.append(lax.dot_general(kx, queries[h], NT, preferred_element_type=jnp.float32))
            out = []
            for h in range(heads):
                peak, total, acc = carry[h]
                s = scores[h]
                if which == 1:
                    s = s + bias_ref[h, kb - qb + 1]
                new = jnp.maximum(peak, jnp.max(s, axis=0, keepdims=True))
                p = jnp.exp(s - new)
                scale = jnp.exp(peak - new)
                total = total * scale + jnp.sum(p, axis=0, keepdims=True)
                vt = vt_ref[h * HEAD_DIM : (h + 1) * HEAD_DIM, keys]
                acc = acc * scale + jnp.dot(vt, p.astype(jnp.bfloat16), preferred_element_type=jnp.float32)
                out.append((new, total, acc))
            return tuple(out)

        return step

    start = tuple(
        (
            jnp.full((1, tile), -3e38, jnp.float32),
            jnp.zeros((1, tile), jnp.float32),
            jnp.zeros((HEAD_DIM, tile), jnp.float32),
        )
        for _ in range(heads)
    )
    near_low, near_high = jnp.maximum(low, qb - 1), jnp.minimum(high, qb + 2)
    state = lax.fori_loop(near_low, near_high, visit(1), start)
    state = lax.fori_loop(low, near_low, visit(0), state)
    state = lax.fori_loop(near_high, high, visit(2), state)
    outs = []
    for h in range(heads):
        peak, total, acc = state[h]
        outs.append(acc / total)
        lse_ref[h // 2, h % 2 : h % 2 + 1, :] = peak + jnp.log(total)
    o_ref[...] = jnp.concatenate(outs, axis=0).T.astype(o_ref.dtype)


FWD_PAIRS = 4


def attend_forward(qkv, qs, ks, ranges, rows, ends, own, tile):
    length, width = qkv.shape[0], qkv.shape[1] // 3
    pairs = width // LANES
    together = FWD_PAIRS if pairs % FWD_PAIRS == 0 else 1
    span = together * LANES
    tiles = length // tile
    spec = pltpu.PrefetchScalarGridSpec(
        num_scalar_prefetch=3,
        grid=(pairs // together, tiles),
        in_specs=[
            pl.BlockSpec((tile, span), lambda p, i, r, e, own: (i ^ own[0], p)),
            pl.BlockSpec((length, span), lambda p, i, *_: (0, width // span + p)),
            pl.BlockSpec((length, span), lambda p, i, *_: (0, 2 * (width // span) + p)),
            pl.BlockSpec((tile, LANES), lambda p, i, r, e, own: (i ^ own[0], 0)),
            pl.BlockSpec((length, LANES), lambda p, i, *_: (0, 0)),
            pl.BlockSpec((2 * together, 3, 2 * tile), lambda p, i, *_: (p, 0, 0)),
        ],
        out_specs=[
            pl.BlockSpec((tile, span), lambda p, i, *_: (i, p)),
            pl.BlockSpec((together, 2, tile), lambda p, i, *_: (p, 0, i)),
        ],
        scratch_shapes=[
            pltpu.VMEM((2 * together, 3, tile, tile), jnp.float32),
            pltpu.VMEM((span, length), jnp.bfloat16),
        ],
    )
    return pl.pallas_call(
        fwd_kernel,
        name="attend_forward",
        out_shape=(
            jax.ShapeDtypeStruct((length, width), jnp.bfloat16),
            jax.ShapeDtypeStruct((pairs, 2, length), jnp.float32),
        ),
        grid_spec=spec,
        compiler_params=pltpu.CompilerParams(
            dimension_semantics=("arbitrary", "arbitrary"), vmem_limit_bytes=48 << 20
        ),
        cost_estimate=pl.CostEstimate(flops=length * length * width * 4, bytes_accessed=length * width * 8, transcendentals=0),
    )(ranges, ends, own, qkv, qkv, qkv, qs, ks, rows)


def pieces(row):
    high = row.astype(jnp.bfloat16).astype(jnp.float32)
    mid = (row - high).astype(jnp.bfloat16).astype(jnp.float32)
    return high, mid, row - high - mid


def bwd_kernel(ranges, ends, own, q_ref, k_ref, v_ref, do_ref, o_ref, lse_ref, qs_ref, ks_ref, rows_ref,
               dq_ref, dk_ref, dv_ref, diag_ref, far_ref,
               qx_ref, dox_ref, kt_ref, bias_ref, dsum_ref, fsum_ref, dqt_ref, dka_ref, dva_ref):
    pair = pl.program_id(0)
    length = q_ref.shape[0]
    tile = bias_ref.shape[2]
    tiles = length // tile
    for h in range(2):
        for step in range(3):
            bias_ref[h, step] = toeplitz(rows_ref[h, step : step + 1, :], tile)
    dsum_ref[...] = jnp.zeros_like(dsum_ref)
    fsum_ref[...] = jnp.zeros_like(fsum_ref)
    dqt_ref[...] = jnp.zeros_like(dqt_ref)
    lane = lax.broadcasted_iota(jnp.int32, (tile, LANES), 1)
    sub = lax.broadcasted_iota(jnp.int32, (LANES, tile), 0)
    pick = (lax.broadcasted_iota(jnp.int32, (8, LANES), 1) // HEAD_DIM == lax.broadcasted_iota(jnp.int32, (8, LANES), 0)).astype(jnp.float32)

    @pl.loop(0, tiles)
    def _(i):
        line = pl.ds(pl.multiple_of(i * tile, tile), tile)
        at = block_at(i, own, tile)
        q = q_ref[at, :] * jnp.bfloat16(HEAD_DIM**-0.5)
        do = do_ref[line, :]
        zero = jnp.zeros_like(q)
        product = do.astype(jnp.float32) * o_ref[line, :].astype(jnp.float32)
        delta = lax.dot_general(pick, product, NT, precision=lax.Precision.HIGHEST, preferred_element_type=jnp.float32)
        kt_ref[:, at] = k_ref[at, :].T
        for h in range(2):
            keep = (lane < HEAD_DIM) if h == 0 else (lane >= HEAD_DIM)
            a, b, c = pieces(-lse_ref[0, h : h + 1, line])
            extra = jnp.where(sub == 4, a, jnp.where(sub == 5, b, jnp.where(sub == 6, c, 0.0)))
            extra = extra.T.astype(jnp.bfloat16) + qs_ref[at, :]
            left, right = ends[2 * pair + h, 0].astype(jnp.bfloat16), ends[2 * pair + h, 1].astype(jnp.bfloat16)
            extra = jnp.where(lane == 7, left, jnp.where(lane == 8, right, extra))
            qx_ref[h, at, :] = jnp.concatenate([jnp.where(keep, q, zero), extra], axis=1)
            a, b, c = pieces(-delta[h : h + 1, :])
            extra = jnp.where(sub == 4, a, jnp.where(sub == 5, b, jnp.where(sub == 6, c, 0.0)))
            dox_ref[h, at, :] = jnp.concatenate([jnp.where(keep, do, zero), extra.T.astype(jnp.bfloat16)], axis=1)

    ones3 = ((lane >= 4) & (lane < 7)).astype(jnp.bfloat16)

    @pl.loop(0, tiles)
    def _(kb):
        low, high = ranges[0, kb], ranges[1, kb]
        keys = block_at(kb, own, tile)
        k, ks = k_ref[keys, :], ks_ref[keys, :]
        vx = jnp.concatenate([v_ref[keys, :], ones3], axis=1)
        nil = jnp.zeros_like(ks)
        dka_ref[...] = jnp.zeros_like(dka_ref)
        dva_ref[...] = jnp.zeros_like(dva_ref)

        def visit(which):
            if which == 0:
                extra = jnp.where(lane == 8, nil, ks)
            elif which == 2:
                extra = jnp.where(lane == 7, nil, ks)
            else:
                extra = jnp.where((lane == 7) | (lane == 8), nil, ks)
            kx = jnp.concatenate([k, extra], axis=1)

            def step(qb, carry):
                at = block_at(qb, own, tile)
                weights, grads = [], []
                for h in range(2):
                    qx, dox = qx_ref[h, at, :], dox_ref[h, at, :]
                    s = lax.dot_general(kx, qx, NT, preferred_element_type=jnp.float32)
                    if which == 1:
                        s = s + bias_ref[h, kb - qb + 1]
                    p = jnp.exp(s)
                    dp = lax.dot_general(vx, dox, NT, preferred_element_type=jnp.float32)
                    ds = p * dp
                    if which == 1:
                        dsum_ref[h, kb - qb + 1] += ds
                    else:
                        fsum_ref[h, which // 2] += jnp.sum(ds.reshape(tile // 8, 8, tile), axis=0)
                    weights.append(p.astype(jnp.bfloat16))
                    grads.append(ds.astype(jnp.bfloat16))
                    rows = slice(h * HEAD_DIM, (h + 1) * HEAD_DIM)
                    dqt_ref[rows, at] += jnp.dot(kt_ref[rows, keys], grads[h], preferred_element_type=jnp.float32)
                both_do = jnp.concatenate([dox_ref[0, at, :LANES], dox_ref[1, at, :LANES]], axis=0)
                both_q = jnp.concatenate([qx_ref[0, at, :LANES], qx_ref[1, at, :LANES]], axis=0)
                dva_ref[...] += jnp.dot(jnp.concatenate(weights, axis=1), both_do, preferred_element_type=jnp.float32)
                dka_ref[...] += jnp.dot(jnp.concatenate(grads, axis=1), both_q, preferred_element_type=jnp.float32)
                return carry

            return step

        near_low, near_high = jnp.maximum(low, kb - 1), jnp.minimum(high, kb + 2)
        lax.fori_loop(near_low, near_high, visit(1), 0)
        lax.fori_loop(near_high, high, visit(0), 0)
        lax.fori_loop(low, near_low, visit(2), 0)
        dk_ref[keys, :] = dka_ref[...].astype(dk_ref.dtype)
        dv_ref[keys, :] = dva_ref[...].astype(dv_ref.dtype)

    @pl.loop(0, tiles)
    def _(i):
        at = pl.ds(pl.multiple_of(i * tile, tile), tile)
        dq_ref[at, :] = (dqt_ref[:, at] * HEAD_DIM**-0.5).T.astype(dq_ref.dtype)

    for h in range(2):
        for step in range(3):
            diag_ref[h, step : step + 1, :] = diagonals(dsum_ref, h, step, tile)
        for step in range(2):
            total = jnp.sum(fsum_ref[h, step], axis=0, keepdims=True)
            far_ref[h, step : step + 1, :] = total


def diagonals(dsum_ref, h, step, tile):
    width = 2 * tile
    acc = jnp.zeros((8, width), jnp.float32)
    for group in range(tile // 8):
        part = dsum_ref[h, step, group * 8 : (group + 1) * 8, :]
        part = jnp.concatenate([part, jnp.zeros((8, tile), jnp.float32)], axis=1)
        acc = acc + (pltpu.roll(part, width - 8 * group, 1) if group else part)
    row = lax.broadcasted_iota(jnp.int32, (8, width), 0)
    for bit in (1, 2, 4):
        acc = jnp.where((row & bit) != 0, pltpu.roll(acc, width - bit, 1), acc)
    return jnp.sum(acc, axis=0, keepdims=True)


def attend_backward(qkv, do, o, lse, qs, ks, ranges, rows, ends, own, tile):
    length, width = do.shape
    pairs = width // LANES
    heads = width // HEAD_DIM
    column = pl.BlockSpec((length, LANES), lambda p, *_: (0, p))
    fixed = pl.BlockSpec((length, LANES), lambda p, *_: (0, 0))
    spec = pltpu.PrefetchScalarGridSpec(
        num_scalar_prefetch=3,
        grid=(pairs,),
        in_specs=[
            column,
            pl.BlockSpec((length, LANES), lambda p, *_: (0, pairs + p)),
            pl.BlockSpec((length, LANES), lambda p, *_: (0, 2 * pairs + p)),
            column,
            column,
            pl.BlockSpec((1, 2, length), lambda p, *_: (p, 0, 0)),
            fixed, fixed,
            pl.BlockSpec((2, 3, 2 * tile), lambda p, *_: (p, 0, 0)),
        ],
        out_specs=[
            column, column, column,
            pl.BlockSpec((2, 3, 2 * tile), lambda p, *_: (p, 0, 0)),
            pl.BlockSpec((2, 2, tile), lambda p, *_: (p, 0, 0)),
        ],
        scratch_shapes=[
            pltpu.VMEM((2, length, 2 * LANES), jnp.bfloat16),
            pltpu.VMEM((2, length, 2 * LANES), jnp.bfloat16),
            pltpu.VMEM((LANES, length), jnp.bfloat16),
            pltpu.VMEM((2, 3, tile, tile), jnp.float32),
            pltpu.VMEM((2, 3, tile, tile), jnp.float32),
            pltpu.VMEM((2, 2, 8, tile), jnp.float32),
            pltpu.VMEM((LANES, length), jnp.float32),
            pltpu.VMEM((tile, LANES), jnp.float32),
            pltpu.VMEM((tile, LANES), jnp.float32),
        ],
    )
    low = jax.ShapeDtypeStruct((length, width), jnp.bfloat16)
    return pl.pallas_call(
        bwd_kernel,
        name="attend_backward",
        out_shape=(
            low, low, low,
            jax.ShapeDtypeStruct((heads, 3, 2 * tile), jnp.float32),
            jax.ShapeDtypeStruct((heads, 2, tile), jnp.float32),
        ),
        grid_spec=spec,
        compiler_params=pltpu.CompilerParams(
            dimension_semantics=("arbitrary",), vmem_limit_bytes=40 << 20
        ),
        cost_estimate=pl.CostEstimate(flops=length * length * width * 10, bytes_accessed=length * width * 16, transcendentals=0),
    )(ranges, ends, own, qkv, qkv, qkv, do, o, lse, qs, ks, rows)


def bucket_sums(diag, far, tile):
    u = np.arange(2 * tile)
    x = np.where(u < tile, u, u - 2 * tile)
    ids = np.stack([bucket_of(step * tile - x) for step in (-1, 0, 1)])
    hot = (ids.reshape(-1)[:, None] == np.arange(BUCKETS)[None, :]).astype(np.float32)
    sums = jnp.dot(diag.reshape(diag.shape[0], -1), jnp.asarray(hot), precision=lax.Precision.HIGHEST)
    outer = jnp.sum(far, axis=2)
    ends = np.zeros((2, BUCKETS), np.float32)
    ends[0, 15] = 1
    ends[1, 31] = 1
    return sums + outer[:, 0:1] * ends[0] + outer[:, 1:2] * ends[1]


GELU_A, GELU_B = 0.7978845608028654, 0.044715
FF_TILE = 256
EXTRA = 16


def expert_kernel(own_ref, x_ref, dy_ref, wg_ref, wu_ref, wd_ref, *refs):
    h_ref, dg_ref, du_ref, dx_ref, part_ref, acc_ref, gate_ref = refs[-7:]
    step = pl.program_id(0)
    rows = dy_ref.shape[0]
    chunk = rows // 2 if rows % 32 == 0 else rows

    @pl.when(step == 0)
    def _():
        acc_ref[...] = jnp.zeros_like(acc_ref)
        part_ref[...] = jnp.zeros_like(part_ref)
        lines = x_ref[rows:, :rows].astype(jnp.float32)
        gate = jnp.sum(lines, axis=0, keepdims=True)
        gate_ref[...] = jnp.broadcast_to(gate, (LANES, rows)).T

    wg, wu, wd = wg_ref[...], wu_ref[...], wd_ref[...]
    for start in range(0, rows, chunk):
        at = slice(start, start + chunk)
        x, dy = x_ref[at, :], dy_ref[at, :]
        g = jnp.dot(x, wg, preferred_element_type=jnp.float32)
        u = jnp.dot(x, wu, preferred_element_type=jnp.float32)
        raw = lax.dot_general(dy, wd, NT, preferred_element_type=jnp.float32)
        square = g * g
        half = 0.5 + 0.5 * jnp.tanh(g * (GELU_A + (GELU_A * GELU_B) * square))
        gelu = g * half
        slope = half + 2.0 * gelu * (1.0 - half) * (GELU_A + (3.0 * GELU_A * GELU_B) * square)
        h = gelu * u
        product = raw * h
        total = product[:, :LANES]
        for column in range(LANES, product.shape[1], LANES):
            total = total + product[:, column : column + LANES]
        part_ref[at, :] += total
        dh = raw * gate_ref[at, :1]
        du = (dh * gelu).astype(jnp.bfloat16)
        dg = (dh * u * slope).astype(jnp.bfloat16)
        h_ref[at, :] = h.astype(jnp.bfloat16)
        dg_ref[at, :] = dg
        du_ref[at, :] = du
        acc_ref[at, :] += lax.dot_general(dg, wg, NT, preferred_element_type=jnp.float32) + lax.dot_general(
            du, wu, NT, preferred_element_type=jnp.float32
        )

    @pl.when(step == pl.num_programs(0) - 1)
    def _():
        dx_ref[:rows, :] = acc_ref[...].astype(dx_ref.dtype)
        sums = jnp.sum(part_ref[...].T, axis=0, keepdims=True)
        high = sums.astype(jnp.bfloat16).astype(jnp.float32)
        middle = (sums - high).astype(jnp.bfloat16).astype(jnp.float32)
        line = lax.broadcasted_iota(jnp.int32, (EXTRA, rows), 0)
        lines = jnp.where(line == 0, high, jnp.where(line == 1, middle, jnp.where(line == 2, sums - high - middle, 0.0)))
        dx_ref[rows:, :] = jnp.zeros_like(dx_ref[rows:, :])
        dx_ref[rows:, :rows] = lines.astype(dx_ref.dtype)


def expert_block(at, count, x, dy, wgu, wd, earlier):
    rows, width = dy.shape
    hidden = wd.shape[0]
    tile = FF_TILE
    whole = jax.ShapeDtypeStruct((count * rows, hidden), jnp.bfloat16)
    fixed = lambda i, *_: (0, 0)
    out_block = pl.BlockSpec((rows, tile), lambda i, *_: (at, i))
    spec = pltpu.PrefetchScalarGridSpec(
        num_scalar_prefetch=1,
        grid=(hidden // tile,),
        in_specs=[
            pl.BlockSpec((rows + EXTRA, width), fixed),
            pl.BlockSpec((rows, width), fixed),
            pl.BlockSpec((width, tile), lambda i, *_: (0, i)),
            pl.BlockSpec((width, tile), lambda i, *_: (0, hidden // tile + i)),
            pl.BlockSpec((tile, width), lambda i, *_: (i, 0)),
        ]
        + [pl.BlockSpec(memory_space=pl.ANY)] * len(earlier),
        out_specs=[
            out_block,
            out_block,
            out_block,
            pl.BlockSpec((rows + EXTRA, width), fixed),
        ],
        scratch_shapes=[
            pltpu.VMEM((rows, LANES), jnp.float32),
            pltpu.VMEM((rows, width), jnp.float32),
            pltpu.VMEM((rows, LANES), jnp.float32),
        ],
    )
    return pl.pallas_call(
        expert_kernel,
        name="expert_block",
        out_shape=(
            whole,
            whole,
            whole,
            jax.ShapeDtypeStruct((rows + EXTRA, width), jnp.bfloat16),
        ),
        grid_spec=spec,
        input_output_aliases={6 + i: i for i in range(len(earlier))},
        compiler_params=pltpu.CompilerParams(dimension_semantics=("arbitrary",), vmem_limit_bytes=40 << 20),
        cost_estimate=pl.CostEstimate(
            flops=10 * rows * width * hidden, bytes_accessed=6 * width * hidden + 6 * rows * hidden, transcendentals=0
        ),
    )(jnp.zeros((1,), jnp.int32), x, dy, wgu, wgu, wd, *earlier)


EPS = 1e-06
FULL_PRECISION = lax.Precision.HIGHEST
ALL = ("z", "x", "exp")
SEQ = ("z", "x")
LOW = jnp.bfloat16


def dot32(a, b):
    return jnp.dot(a, b, preferred_element_type=jnp.float32)


def dot_nt(a, b):
    return lax.dot_general(a, b, NT, preferred_element_type=jnp.float32)


def dot_tn(a, b):
    return lax.dot_general(a, b, (((0,), (0,)), ((), ())), preferred_element_type=jnp.float32)


def partner(value, axis, offset):
    count = lax.axis_size(axis)
    return lax.ppermute(value, axis, [(i, i ^ offset) for i in range(count)])


def bits_of(count):
    return [1 << b for b in reversed(range(count.bit_length() - 1))]


def reorder(stacked, own):
    count = stacked.shape[0]
    return jnp.stack([lax.dynamic_index_in_dim(stacked, own ^ r, 0, keepdims=False) for r in range(count)])


def gather_double(value, steps):
    for axis, bit in steps:
        other = partner(value, axis, bit)
        high = (lax.axis_index(axis) & bit) != 0
        value = jnp.stack([jnp.where(high, other, value), jnp.where(high, value, other)])
    return value


def scatter_halve(value, steps):
    for axis, bit in steps:
        high = (lax.axis_index(axis) & bit) != 0
        keep = jnp.where(high, value[1], value[0])
        give = jnp.where(high, value[0], value[1])
        value = (keep.astype(jnp.float32) + partner(give, axis, bit).astype(jnp.float32)).astype(LOW)
    return value


def ring_of(groups, split):
    order = []
    for x in range(split):
        line = range(groups) if x % 2 == 0 else reversed(range(groups))
        order += [z * split + x for z in line]
    place = [order.index(s) for s in range(len(order))]
    ahead = [(order[i], order[(i + 1) % len(order)]) for i in range(len(order))]
    return jnp.asarray(order, jnp.int32), jnp.asarray(place, jnp.int32), ahead


def pick(values, index):
    return lax.dynamic_index_in_dim(values, index, 0, keepdims=False)


class RingGather:
    def __init__(self, piece, groups, split, own):
        self.order, place, self.ahead = ring_of(groups, split)
        self.count = groups * split
        self.here = pick(place, own)
        self.rows = piece.shape[0]
        self.whole = jnp.zeros((self.count * self.rows, piece.shape[1]), piece.dtype)
        self.whole = lax.dynamic_update_slice_in_dim(self.whole, piece, own * self.rows, 0)
        self.forward = self.backward = piece
        self.round = 0
        self.waiting = []

    def step(self):
        self.settle()
        self.round += 1
        k = self.round
        self.forward = lax.ppermute(self.forward, SEQ, self.ahead)
        self.waiting.append((self.forward, -k))
        if k < self.count - self.count // 2:
            self.backward = lax.ppermute(self.backward, SEQ, [(b, a) for a, b in self.ahead])
            self.waiting.append((self.backward, k))

    def settle(self):
        for piece, k in self.waiting:
            at = pick(self.order, (self.here + k + self.count) % self.count) * self.rows
            self.whole = lax.dynamic_update_slice_in_dim(self.whole, piece, at, 0)
        self.waiting = []

    def after(self, value):
        value, self.forward, self.backward = lax.optimization_barrier((value, self.forward, self.backward))
        self.waiting = [(self.forward if k < 0 else self.backward, k) for _, k in self.waiting]
        return value

    def finish(self):
        while self.round < self.count // 2:
            self.step()
        self.settle()
        return self.whole


def norm_scale(value):
    return lax.rsqrt(jnp.mean(value * value, axis=-1, keepdims=True) + EPS)


def norm_back(scale, normed, gain, grad):
    scaled = grad * gain
    return scale * (scaled - normed * jnp.mean(scaled * normed, axis=-1, keepdims=True))


def split3(value):
    high = value.astype(LOW)
    rest = value - high.astype(jnp.float32)
    middle = rest.astype(LOW)
    return [high, middle, (rest - middle.astype(jnp.float32)).astype(LOW)]


def per_device(
    block_in,
    cotangent,
    segment_ids,
    expert_routes,
    pair_priority,
    gain_attention,
    w_query,
    w_key,
    w_value,
    w_out,
    bias_table,
    gain_experts,
    w_router,
    w_gate,
    w_up,
    w_down,
):
    groups, local_len, width = block_in.shape
    tokens = groups * local_len
    rows_own, hd = w_query.shape
    split = lax.axis_size("x")
    exp_count = lax.axis_size("exp")
    seq_count = groups * split
    length = local_len * seq_count
    x_at, z_at, e_at = lax.axis_index("x"), lax.axis_index("z"), lax.axis_index("exp")
    s_at = z_at * split + x_at
    head_width = hd // split
    heads_here = head_width // HEAD_DIM
    experts_all = w_router.shape[1]
    bias_own = bias_table.shape[0]
    tile = min(TILE, local_len)
    own = s_at.astype(jnp.int32).reshape(1)
    z_bits, x_bits, e_bits = bits_of(groups), bits_of(split), bits_of(exp_count)

    input_r = reorder(block_in, z_at)

    arrived = [[None] * split for _ in range(groups)]
    for rz in reversed(range(groups)):
        arrived[rz][0] = partner(input_r[rz], "z", rz) if rz else input_r[0]
    for rz in [0] + list(reversed(range(1, groups))):
        for rx in range(1, split):
            arrived[rz][rx] = partner(arrived[rz][0], "x", rx)
    sequence = jnp.stack([block for line in arrived for block in line]).reshape(length, width)

    small = jnp.concatenate(
        [
            gain_attention[:, None],
            gain_experts[:, None],
            jnp.pad(bias_table, (0, rows_own - bias_own))[:, None],
            w_router,
        ],
        axis=1,
    )
    small = jnp.pad(small, ((0, 0), (0, LANES - small.shape[1]))).astype(LOW)
    share = jnp.stack(
        [part.astype(LOW).reshape(rows_own, split, head_width) for part in (w_query, w_key, w_value)], axis=2
    )
    share = share.reshape(rows_own, split, 3 * head_width).transpose(1, 0, 2)
    common = jnp.concatenate([w_out.astype(LOW), small], axis=1)
    share = jnp.concatenate([share, jnp.broadcast_to(common, (split,) + common.shape)], axis=2)
    shares = [lax.dynamic_index_in_dim(share, x_at ^ r, 0, keepdims=False) for r in range(split)]
    shares = [shares[0]] + [partner(shares[r], "x", r) for r in range(1, split)]
    by_x = reorder(jnp.stack(shares), x_at)
    steps = [("z", b) for b in z_bits] + [("exp", b) for b in e_bits]
    packed = gather_double(by_x, steps)
    ne, nz, nx = len(e_bits), len(z_bits), len(x_bits)
    packed = packed.transpose(
        tuple(ne + i for i in reversed(range(nz))) + (ne + nz,) + tuple(reversed(range(ne))) + (ne + nz + 1, ne + nz + 2)
    ).reshape(width, 3 * head_width + width + LANES)
    sequence, packed = lax.optimization_barrier((sequence, packed))
    qkv_w, small_all = packed[:, : 3 * head_width], packed[:, 3 * head_width + width :]
    out_w = packed[:, 3 * head_width : 3 * head_width + width]
    gate_up_own = jnp.concatenate([w_gate[0].astype(LOW), w_up[0].astype(LOW)], axis=1)
    sequence, gate_up_own, down_own = lax.optimization_barrier((sequence, gate_up_own, w_down[0].astype(LOW)))
    gate_up_ring = RingGather(gate_up_own, groups, split, s_at)
    gate_up_ring.step()
    down_w = lax.all_gather(down_own, SEQ, axis=0, tiled=True)

    gain_one = small_all[:, 0].astype(jnp.float32)
    gain_two = small_all[:, 1].astype(jnp.float32)
    table_all = small_all[:, 2].reshape(-1, rows_own)[:, :bias_own].reshape(-1, BUCKETS)
    router_t = small_all[:, 3 : 3 + experts_all].T
    table_rows = lax.dynamic_slice_in_dim(table_all, x_at * heads_here, heads_here, 0)

    routes = expert_routes.reshape(tokens, -1)
    top_count = routes.shape[1]
    priority = pair_priority.reshape(-1)
    pair_experts = routes.reshape(-1)
    ahead = (pair_experts[None, :] == pair_experts[:, None]) & (priority[None, :] < priority[:, None])
    slots = jnp.sum(ahead.astype(jnp.int32), axis=1)
    capacity = (5 * top_count * tokens + 4 * experts_all - 1) // (4 * experts_all)
    slot_count = experts_all * capacity
    slot_index = jnp.where(slots < capacity, (pair_experts ^ e_at) * capacity + slots, slot_count)
    slot_index = slot_index.reshape(tokens, top_count)
    every_slot = jnp.arange(slot_count, dtype=jnp.int32)[None, :]
    table = sum((slot_index[:, k : k + 1] == every_slot).astype(LOW) for k in range(top_count))
    tables = [table[:, r * capacity : (r + 1) * capacity] for r in range(exp_count)]
    grad_low = cotangent.reshape(tokens, width)
    grad_slots = [dot_tn(part, grad_low).astype(LOW) for part in tables]

    wide = sequence.astype(jnp.float32)
    normed_one = (wide * norm_scale(wide) * gain_one).astype(LOW)
    qkv = dot32(normed_one, qkv_w).astype(LOW)
    qkv, grad_slots = lax.optimization_barrier((qkv, grad_slots))
    grad_slots = [grad_slots[0]] + [partner(grad_slots[r], "exp", r) for r in range(1, exp_count)]
    segments = lax.dynamic_index_in_dim(segment_ids, z_at, 0, keepdims=False)
    ranges = tile_ranges(segments, tile)
    seg_blocks = segments.reshape(seq_count, local_len)
    query_side, key_side = segment_columns(reorder(seg_blocks, s_at).reshape(length))
    rows = bias_rows(table_rows, tile)
    ends = jnp.stack([table_rows[:, 15], table_rows[:, 31]], axis=1).astype(jnp.float32)
    contexts, log_totals = attend_forward(qkv, query_side, key_side, ranges, rows, ends, own, tile)
    contexts = gate_up_ring.after(contexts)
    contexts, grad_slots = lax.optimization_barrier((contexts, grad_slots))
    gate_up_w = gate_up_ring.finish()

    def exchange_positions(blocks):
        return lax.all_to_all(blocks, SEQ, split_axis=0, concat_axis=0, tiled=True)

    context_local = exchange_positions(contexts.reshape(seq_count, local_len, head_width))
    context_local = (
        context_local.reshape(groups, split, local_len, head_width).transpose(0, 2, 1, 3).reshape(tokens, hd)
    )
    inputs = block_in.astype(jnp.float32).reshape(tokens, width)
    mid = inputs + dot32(context_local, out_w)
    scale_two = norm_scale(mid)
    normed_two = (mid * scale_two * gain_two).astype(LOW)

    logits = dot_nt(router_t, normed_two)
    exponent = jnp.exp(logits - jnp.max(logits, axis=0, keepdims=True))
    probabilities = exponent / jnp.sum(exponent, axis=0, keepdims=True)
    expert_ids = jnp.arange(experts_all, dtype=jnp.int32)[:, None]
    chosen = sum((routes[:, k][None, :] == expert_ids).astype(jnp.float32) for k in range(top_count))
    chosen_total = jnp.sum(probabilities * chosen, axis=0, keepdims=True)
    gates = probabilities * chosen / chosen_total
    gates_r = reorder(gates, e_at)

    gate_slots = jnp.sum(
        table.astype(jnp.float32).reshape(tokens, exp_count, capacity) * gates_r.T[:, :, None], axis=0
    )
    gate_lines = jnp.pad(jnp.stack(split3(gate_slots), axis=1), ((0, 0), (0, EXTRA - 3), (0, width - capacity)))

    def values_below(rows_):
        return jnp.sum(rows_[capacity : capacity + 3, :capacity].astype(jnp.float32), axis=0)

    sent = [None] * exp_count
    for r in reversed(range(exp_count)):
        sent[r] = jnp.concatenate([dot_tn(tables[r], normed_two).astype(LOW), gate_lines[r]], axis=0)
        if r:
            sent[r] = partner(sent[r], "exp", r)

    earlier = ()
    back = [None] * exp_count
    turns = [0] + list(range(2, exp_count)) + [1]
    for turn, r in enumerate(turns):
        if turn >= 3:
            ready = turns[turn - 2]
            sent[r], back[ready] = lax.optimization_barrier((sent[r], back[ready]))
        hidden, gate_low, up_low, dx = expert_block(
            r, exp_count, sent[r], grad_slots[r], gate_up_w, down_w, earlier
        )
        earlier = (hidden, gate_low, up_low)
        back[r] = partner(dx, "exp", r) if r else dx

    sent, hidden = lax.optimization_barrier((sent, hidden))
    slot_rows = jnp.concatenate([rows_[:capacity] for rows_ in sent], axis=0)
    slot_gates = jnp.concatenate([values_below(rows_) for rows_ in sent], axis=0)[:, None]
    slot_grads = (slot_gates * jnp.concatenate(grad_slots, axis=0).astype(jnp.float32)).astype(LOW)
    down_sum = dot_tn(hidden, slot_grads).astype(LOW)

    gate_grad = jnp.sum(
        table.astype(jnp.float32).reshape(tokens, exp_count, capacity) * jnp.stack([values_below(rows_) for rows_ in back])[None], axis=2
    )
    gate_grad = reorder(gate_grad.T, e_at)
    chosen_grad = chosen * (gate_grad - jnp.sum(gates * gate_grad, axis=0, keepdims=True)) / chosen_total
    logit_grad = probabilities * (chosen_grad - jnp.sum(probabilities * chosen_grad, axis=0, keepdims=True))
    logit_pieces = jnp.concatenate(split3(logit_grad), axis=0)
    router_sum = jnp.sum(dot32(logit_pieces, normed_two).reshape(3, experts_all, width), axis=0)
    normed_two_grad = dot_tn(logit_pieces, jnp.concatenate([router_t] * 3, axis=0))
    for r in range(exp_count):
        normed_two_grad = normed_two_grad + dot32(tables[r], back[r][:capacity])
    unit_two = mid * scale_two
    gain_two_sum = jnp.sum(normed_two_grad * unit_two, axis=0)
    grad_out = grad_low.astype(jnp.float32)
    mid_grad = grad_out + norm_back(scale_two, unit_two, gain_two, normed_two_grad)
    attention_grad = mid_grad.astype(LOW)
    context_grad = dot_nt(attention_grad, out_w).astype(LOW)
    context_grad, gate_low, up_low, hidden, down_sum = lax.optimization_barrier(
        (context_grad, gate_low, up_low, hidden, down_sum)
    )
    gate_sum = dot_tn(slot_rows, gate_low).astype(LOW)
    up_sum = dot_tn(slot_rows, up_low).astype(LOW)
    expert_out = (slot_gates * dot32(hidden, down_w)).astype(LOW)
    context_grad = (
        context_grad.reshape(groups, local_len, split, head_width)
        .transpose(0, 2, 1, 3)
        .reshape(seq_count, local_len, head_width)
    )
    context_heads = exchange_positions(context_grad).reshape(length, head_width)

    def scatter_experts(total):
        return lax.psum_scatter(total, SEQ, scatter_dimension=0, tiled=True).astype(jnp.float32)[None]

    down_owned = scatter_experts(down_sum)
    gate_owned = scatter_experts(gate_sum)
    up_owned = scatter_experts(up_sum)
    context_heads, _, _, expert_out = lax.optimization_barrier(
        (context_heads, gate_sum[:8], up_sum[:8], expert_out)
    )

    returned = [expert_out[:capacity]] + [
        partner(expert_out[r * capacity : (r + 1) * capacity], "exp", r) for r in range(1, exp_count)
    ]
    def by_step(total):
        columns = total.shape[1]
        shaped = total.reshape((2,) * (nz + nx + ne) + (rows_own, columns))
        z_dims = tuple(reversed(range(nz)))
        x_dims = tuple(nz + i for i in range(nx))
        e_dims = tuple(nz + nx + i for i in reversed(range(ne)))
        return shaped.transpose(e_dims + z_dims + x_dims + (nz + nx + ne, nz + nx + ne + 1))

    halving = [("exp", b) for b in reversed(e_bits)] + [("z", b) for b in reversed(z_bits)]

    query_back, key_back, value_back, diag, far = attend_backward(
        qkv, context_heads, contexts, log_totals, query_side, key_side, ranges, rows, ends, own, tile
    )
    query_back, key_back, value_back, returned = lax.optimization_barrier(
        (query_back, key_back, value_back, returned)
    )
    table_local = bucket_sums(diag, far, tile)

    def through(grads, part):
        return dot_nt(grads, qkv_w[:, part * head_width : (part + 1) * head_width])

    normed_part = (through(query_back, 0) + through(key_back, 1) + through(value_back, 2)).astype(LOW)
    normed_part = reorder(normed_part.reshape(seq_count, local_len, width), s_at)
    normed_part, query_back, key_back, value_back = lax.optimization_barrier(
        (normed_part, query_back, key_back, value_back)
    )
    normed_part = exchange_positions(normed_part)
    weight_sum = jnp.concatenate(
        [dot_tn(normed_one, grads).astype(LOW) for grads in (query_back, key_back, value_back)]
        + [dot_tn(context_local, attention_grad).astype(LOW)],
        axis=1,
    )
    weight_part = scatter_halve(by_step(weight_sum), halving).reshape(split, rows_own, 3 * head_width + width)
    weight_own = [lax.dynamic_index_in_dim(weight_part, x_at ^ r, 0, keepdims=False) for r in range(split)]
    weight_own = [weight_own[0]] + [partner(weight_own[r], "x", r) for r in range(1, split)]
    out_w_out = sum(part[:, 3 * head_width :].astype(jnp.float32) for part in weight_own)
    qkv_own = reorder(jnp.stack([part[:, : 3 * head_width] for part in weight_own]), x_at)
    qkv_own = qkv_own.reshape(split, rows_own, 3, head_width)
    qkv_own = qkv_own.transpose(2, 1, 0, 3).reshape(3, rows_own, hd).astype(jnp.float32)
    block_out = (mid + dot32(table, jnp.concatenate(returned, axis=0))).astype(LOW)

    block_out = block_out.reshape(groups, local_len, width)

    normed_one_grad = jnp.sum(
        normed_part.reshape(groups, split, local_len, width).astype(jnp.float32), axis=1
    ).reshape(tokens, width)
    scale_one = norm_scale(inputs)
    unit_one = inputs * scale_one
    gain_one_sum = jnp.sum(normed_one_grad * unit_one, axis=0)
    block_in_grad = (mid_grad + norm_back(scale_one, unit_one, gain_one, normed_one_grad)).reshape(
        groups, local_len, width
    )

    table_sum = lax.dynamic_update_slice_in_dim(
        jnp.zeros(table_all.shape, jnp.float32), table_local, x_at * heads_here, 0
    ).reshape(-1, bias_own)
    table_sum = jnp.pad(table_sum, ((0, 0), (0, rows_own - bias_own)))[:, None, :]
    little = jnp.concatenate(
        [
            gain_one_sum.reshape(-1, 1, rows_own),
            gain_two_sum.reshape(-1, 1, rows_own),
            table_sum,
            router_sum.reshape(experts_all, -1, rows_own).transpose(1, 0, 2),
        ],
        axis=1,
    )
    little = jnp.sum(lax.all_to_all(little, ALL, split_axis=0, concat_axis=0, tiled=True), axis=0)
    return (
        block_out,
        block_in_grad,
        little[0],
        qkv_own[0],
        qkv_own[1],
        qkv_own[2],
        out_w_out,
        little[2, :bias_own],
        little[1],
        little[3:].T,
        gate_owned,
        up_owned,
        down_owned,
    )


def solution(mesh):
    def run(*args):
        groups = args[0].shape[0] // mesh.shape["exp"]
        seq_count, exp_count = mesh.shape["seq"], mesh.shape["exp"]
        grid = mesh.devices.reshape(groups, seq_count // groups, exp_count)
        fine = jax.sharding.Mesh(grid, ALL)
        placed = P("exp", SEQ, None)
        whole = P(ALL)
        matrix = P(ALL, None)
        return jax.shard_map(
            per_device,
            mesh=fine,
            in_specs=(
                placed, placed, P("exp", None), placed, placed,
                whole, matrix, matrix, matrix, matrix, whole, whole, matrix,
                placed, placed, placed,
            ),
            out_specs=(
                placed, placed, whole, matrix, matrix, matrix, matrix, whole, whole, matrix,
                placed, placed, placed,
            ),
            check_vma=False,
        )(*args)

    return run
```

```python
from functools import partial

import jax
import jax.numpy as jnp
import numpy as np
from jax import lax
from jax.experimental import pallas as pl
from jax.experimental.pallas import tpu as pltpu
from jax.sharding import PartitionSpec as P

HEAD_DIM = 64
BUCKETS = 32
THRESHOLDS = (12, 16, 23, 32, 46, 64, 91)
MASKED = -1e30
TILE = 256
LANES = 128
NT = (((1,), (1,)), ((), ()))


def bucket_of(d):
    a = np.abs(d)
    extra = sum((a >= t).astype(np.int64) for t in THRESHOLDS)
    return np.where(a < 8, a, 8 + extra) + 16 * (d > 0)


def bias_rows(table_rows, tile):
    u = np.arange(2 * tile)
    x = np.where(u < tile, u, u - 2 * tile)
    ids = np.stack([bucket_of(step * tile - x) for step in (-1, 0, 1)])
    hot = (ids.reshape(-1)[None, :] == np.arange(BUCKETS)[:, None]).astype(np.float32)
    rows = jnp.dot(table_rows.astype(jnp.bfloat16), jnp.asarray(hot, jnp.bfloat16), preferred_element_type=jnp.float32)
    return rows.reshape(table_rows.shape[0], 3, 2 * tile)


def tile_ranges(segments, tile):
    blocks = segments.reshape(-1, tile)
    first, last = blocks[:, 0], blocks[:, -1]
    low = jnp.sum((last[None, :] < first[:, None]).astype(jnp.int32), axis=1)
    high = jnp.sum((first[None, :] <= last[:, None]).astype(jnp.int32), axis=1)
    return jnp.stack([low, high])


def segment_columns(segments):
    lane = jnp.arange(LANES, dtype=jnp.int32)[None, :]
    seg = segments[:, None]
    same = seg == lane
    query_side = jnp.where(same & (lane < 4), MASKED, 0.0).astype(jnp.bfloat16)
    key_side = jnp.where(lane < 4, (~same).astype(jnp.float32), (lane < 9).astype(jnp.float32)).astype(jnp.bfloat16)
    return query_side, key_side


def toeplitz(row, tile):
    wide = jnp.broadcast_to(row, (tile, row.shape[1]))
    return pltpu.roll(wide, 0, 1, stride=1, stride_axis=0)[:, :tile]


def block_at(index, own, tile):
    return pl.ds(pl.multiple_of((index ^ own[0]) * tile, tile), tile)


def fwd_kernel(ranges, ends, own, q_ref, k_ref, v_ref, qs_ref, ks_ref, rows_ref, o_ref, lse_ref, bias_ref, vt_ref):
    group, qb = pl.program_id(0), pl.program_id(1)
    tile, span = q_ref.shape
    heads = span // HEAD_DIM

    @pl.when(qb == 0)
    def _():
        for h in range(heads):
            for step in range(3):
                bias_ref[h, step] = toeplitz(rows_ref[h, step : step + 1, :], tile)
        for start in range(0, v_ref.shape[0], tile):
            vt_ref[:, start : start + tile] = v_ref[start : start + tile, :].T

    low, high = ranges[0, qb], ranges[1, qb]
    lane = lax.broadcasted_iota(jnp.int32, (tile, LANES), 1)
    q = q_ref[...] * jnp.bfloat16(HEAD_DIM**-0.5)
    qs = qs_ref[...]
    halves = []
    for h in range(heads):
        part = q[:, h // 2 * LANES : (h // 2 + 1) * LANES]
        keep = (lane < HEAD_DIM) if h % 2 == 0 else (lane >= HEAD_DIM)
        halves.append(jnp.where(keep, part, jnp.zeros_like(part)))

    def side(h, which):
        if which == 1:
            extra = qs
        else:
            value = ends[heads * group + h, which // 2].astype(jnp.bfloat16)
            extra = jnp.where(lane == 7, value, qs)
        return jnp.concatenate([halves[h], extra], axis=1)

    def visit(which):
        queries = [side(h, which) for h in range(heads)]

        def step(kb, carry):
            keys = block_at(kb, own, tile)
            ks = ks_ref[keys, :]
            scores = []
            for h in range(heads):
                kx = jnp.concatenate([k_ref[keys, h // 2 * LANES : (h // 2 + 1) * LANES], ks], axis=1)
                scores.append(lax.dot_general(kx, queries[h], NT, preferred_element_type=jnp.float32))
            out = []
            for h in range(heads):
                peak, total, acc = carry[h]
                s = scores[h]
                if which == 1:
                    s = s + bias_ref[h, kb - qb + 1]
                new = jnp.maximum(peak, jnp.max(s, axis=0, keepdims=True))
                p = jnp.exp(s - new)
                scale = jnp.exp(peak - new)
                total = total * scale + jnp.sum(p, axis=0, keepdims=True)
                vt = vt_ref[h * HEAD_DIM : (h + 1) * HEAD_DIM, keys]
                acc = acc * scale + jnp.dot(vt, p.astype(jnp.bfloat16), preferred_element_type=jnp.float32)
                out.append((new, total, acc))
            return tuple(out)

        return step

    start = tuple(
        (
            jnp.full((1, tile), -3e38, jnp.float32),
            jnp.zeros((1, tile), jnp.float32),
            jnp.zeros((HEAD_DIM, tile), jnp.float32),
        )
        for _ in range(heads)
    )
    near_low, near_high = jnp.maximum(low, qb - 1), jnp.minimum(high, qb + 2)
    state = lax.fori_loop(near_low, near_high, visit(1), start)
    state = lax.fori_loop(low, near_low, visit(0), state)
    state = lax.fori_loop(near_high, high, visit(2), state)
    outs = []
    for h in range(heads):
        peak, total, acc = state[h]
        outs.append(acc / total)
        lse_ref[h // 2, h % 2 : h % 2 + 1, :] = peak + jnp.log(total)
    o_ref[...] = jnp.concatenate(outs, axis=0).T.astype(o_ref.dtype)


FWD_PAIRS = 4


def attend_forward(qkv, qs, ks, ranges, rows, ends, own, tile):
    length, width = qkv.shape[0], qkv.shape[1] // 3
    pairs = width // LANES
    together = FWD_PAIRS if pairs % FWD_PAIRS == 0 else 1
    span = together * LANES
    tiles = length // tile
    spec = pltpu.PrefetchScalarGridSpec(
        num_scalar_prefetch=3,
        grid=(pairs // together, tiles),
        in_specs=[
            pl.BlockSpec((tile, span), lambda p, i, r, e, own: (i ^ own[0], p)),
            pl.BlockSpec((length, span), lambda p, i, *_: (0, width // span + p)),
            pl.BlockSpec((length, span), lambda p, i, *_: (0, 2 * (width // span) + p)),
            pl.BlockSpec((tile, LANES), lambda p, i, r, e, own: (i ^ own[0], 0)),
            pl.BlockSpec((length, LANES), lambda p, i, *_: (0, 0)),
            pl.BlockSpec((2 * together, 3, 2 * tile), lambda p, i, *_: (p, 0, 0)),
        ],
        out_specs=[
            pl.BlockSpec((tile, span), lambda p, i, *_: (i, p)),
            pl.BlockSpec((together, 2, tile), lambda p, i, *_: (p, 0, i)),
        ],
        scratch_shapes=[
            pltpu.VMEM((2 * together, 3, tile, tile), jnp.float32),
            pltpu.VMEM((span, length), jnp.bfloat16),
        ],
    )
    return pl.pallas_call(
        fwd_kernel,
        name="attend_forward",
        out_shape=(
            jax.ShapeDtypeStruct((length, width), jnp.bfloat16),
            jax.ShapeDtypeStruct((pairs, 2, length), jnp.float32),
        ),
        grid_spec=spec,
        compiler_params=pltpu.CompilerParams(
            dimension_semantics=("arbitrary", "arbitrary"), vmem_limit_bytes=48 << 20
        ),
        cost_estimate=pl.CostEstimate(flops=length * length * width * 4, bytes_accessed=length * width * 8, transcendentals=0),
    )(ranges, ends, own, qkv, qkv, qkv, qs, ks, rows)


def pieces(row):
    high = row.astype(jnp.bfloat16).astype(jnp.float32)
    mid = (row - high).astype(jnp.bfloat16).astype(jnp.float32)
    return high, mid, row - high - mid


def bwd_kernel(ranges, ends, own, q_ref, k_ref, v_ref, do_ref, o_ref, lse_ref, qs_ref, ks_ref, rows_ref,
               dq_ref, dk_ref, dv_ref, diag_ref, far_ref,
               qx_ref, dox_ref, kt_ref, bias_ref, dsum_ref, fsum_ref, dqt_ref, dka_ref, dva_ref):
    pair = pl.program_id(0)
    length = q_ref.shape[0]
    tile = bias_ref.shape[2]
    tiles = length // tile
    for h in range(2):
        for step in range(3):
            bias_ref[h, step] = toeplitz(rows_ref[h, step : step + 1, :], tile)
    dsum_ref[...] = jnp.zeros_like(dsum_ref)
    fsum_ref[...] = jnp.zeros_like(fsum_ref)
    dqt_ref[...] = jnp.zeros_like(dqt_ref)
    lane = lax.broadcasted_iota(jnp.int32, (tile, LANES), 1)
    sub = lax.broadcasted_iota(jnp.int32, (LANES, tile), 0)
    pick = (lax.broadcasted_iota(jnp.int32, (8, LANES), 1) // HEAD_DIM == lax.broadcasted_iota(jnp.int32, (8, LANES), 0)).astype(jnp.float32)

    @pl.loop(0, tiles)
    def _(i):
        line = pl.ds(pl.multiple_of(i * tile, tile), tile)
        at = block_at(i, own, tile)
        q = q_ref[at, :] * jnp.bfloat16(HEAD_DIM**-0.5)
        do = do_ref[line, :]
        zero = jnp.zeros_like(q)
        product = do.astype(jnp.float32) * o_ref[line, :].astype(jnp.float32)
        delta = lax.dot_general(pick, product, NT, precision=lax.Precision.HIGHEST, preferred_element_type=jnp.float32)
        kt_ref[:, at] = k_ref[at, :].T
        for h in range(2):
            keep = (lane < HEAD_DIM) if h == 0 else (lane >= HEAD_DIM)
            a, b, c = pieces(-lse_ref[0, h : h + 1, line])
            extra = jnp.where(sub == 4, a, jnp.where(sub == 5, b, jnp.where(sub == 6, c, 0.0)))
            extra = extra.T.astype(jnp.bfloat16) + qs_ref[at, :]
            left, right = ends[2 * pair + h, 0].astype(jnp.bfloat16), ends[2 * pair + h, 1].astype(jnp.bfloat16)
            extra = jnp.where(lane == 7, left, jnp.where(lane == 8, right, extra))
            qx_ref[h, at, :] = jnp.concatenate([jnp.where(keep, q, zero), extra], axis=1)
            a, b, c = pieces(-delta[h : h + 1, :])
            extra = jnp.where(sub == 4, a, jnp.where(sub == 5, b, jnp.where(sub == 6, c, 0.0)))
            dox_ref[h, at, :] = jnp.concatenate([jnp.where(keep, do, zero), extra.T.astype(jnp.bfloat16)], axis=1)

    ones3 = ((lane >= 4) & (lane < 7)).astype(jnp.bfloat16)

    @pl.loop(0, tiles)
    def _(kb):
        low, high = ranges[0, kb], ranges[1, kb]
        keys = block_at(kb, own, tile)
        k, ks = k_ref[keys, :], ks_ref[keys, :]
        vx = jnp.concatenate([v_ref[keys, :], ones3], axis=1)
        nil = jnp.zeros_like(ks)
        dka_ref[...] = jnp.zeros_like(dka_ref)
        dva_ref[...] = jnp.zeros_like(dva_ref)

        def visit(which):
            if which == 0:
                extra = jnp.where(lane == 8, nil, ks)
            elif which == 2:
                extra = jnp.where(lane == 7, nil, ks)
            else:
                extra = jnp.where((lane == 7) | (lane == 8), nil, ks)
            kx = jnp.concatenate([k, extra], axis=1)

            def step(qb, carry):
                at = block_at(qb, own, tile)
                weights, grads = [], []
                for h in range(2):
                    qx, dox = qx_ref[h, at, :], dox_ref[h, at, :]
                    s = lax.dot_general(kx, qx, NT, preferred_element_type=jnp.float32)
                    if which == 1:
                        s = s + bias_ref[h, kb - qb + 1]
                    p = jnp.exp(s)
                    dp = lax.dot_general(vx, dox, NT, preferred_element_type=jnp.float32)
                    ds = p * dp
                    if which == 1:
                        dsum_ref[h, kb - qb + 1] += ds
                    else:
                        fsum_ref[h, which // 2] += jnp.sum(ds.reshape(tile // 8, 8, tile), axis=0)
                    weights.append(p.astype(jnp.bfloat16))
                    grads.append(ds.astype(jnp.bfloat16))
                    rows = slice(h * HEAD_DIM, (h + 1) * HEAD_DIM)
                    dqt_ref[rows, at] += jnp.dot(kt_ref[rows, keys], grads[h], preferred_element_type=jnp.float32)
                both_do = jnp.concatenate([dox_ref[0, at, :LANES], dox_ref[1, at, :LANES]], axis=0)
                both_q = jnp.concatenate([qx_ref[0, at, :LANES], qx_ref[1, at, :LANES]], axis=0)
                dva_ref[...] += jnp.dot(jnp.concatenate(weights, axis=1), both_do, preferred_element_type=jnp.float32)
                dka_ref[...] += jnp.dot(jnp.concatenate(grads, axis=1), both_q, preferred_element_type=jnp.float32)
                return carry

            return step

        near_low, near_high = jnp.maximum(low, kb - 1), jnp.minimum(high, kb + 2)
        lax.fori_loop(near_low, near_high, visit(1), 0)
        lax.fori_loop(near_high, high, visit(0), 0)
        lax.fori_loop(low, near_low, visit(2), 0)
        dk_ref[keys, :] = dka_ref[...].astype(dk_ref.dtype)
        dv_ref[keys, :] = dva_ref[...].astype(dv_ref.dtype)

    @pl.loop(0, tiles)
    def _(i):
        at = pl.ds(pl.multiple_of(i * tile, tile), tile)
        dq_ref[at, :] = (dqt_ref[:, at] * HEAD_DIM**-0.5).T.astype(dq_ref.dtype)

    for h in range(2):
        for step in range(3):
            diag_ref[h, step : step + 1, :] = diagonals(dsum_ref, h, step, tile)
        for step in range(2):
            total = jnp.sum(fsum_ref[h, step], axis=0, keepdims=True)
            far_ref[h, step : step + 1, :] = total


def diagonals(dsum_ref, h, step, tile):
    width = 2 * tile
    acc = jnp.zeros((8, width), jnp.float32)
    for group in range(tile // 8):
        part = dsum_ref[h, step, group * 8 : (group + 1) * 8, :]
        part = jnp.concatenate([part, jnp.zeros((8, tile), jnp.float32)], axis=1)
        acc = acc + (pltpu.roll(part, width - 8 * group, 1) if group else part)
    row = lax.broadcasted_iota(jnp.int32, (8, width), 0)
    for bit in (1, 2, 4):
        acc = jnp.where((row & bit) != 0, pltpu.roll(acc, width - bit, 1), acc)
    return jnp.sum(acc, axis=0, keepdims=True)


def attend_backward(qkv, do, o, lse, qs, ks, ranges, rows, ends, own, tile):
    length, width = do.shape
    pairs = width // LANES
    heads = width // HEAD_DIM
    column = pl.BlockSpec((length, LANES), lambda p, *_: (0, p))
    fixed = pl.BlockSpec((length, LANES), lambda p, *_: (0, 0))
    spec = pltpu.PrefetchScalarGridSpec(
        num_scalar_prefetch=3,
        grid=(pairs,),
        in_specs=[
            column,
            pl.BlockSpec((length, LANES), lambda p, *_: (0, pairs + p)),
            pl.BlockSpec((length, LANES), lambda p, *_: (0, 2 * pairs + p)),
            column,
            column,
            pl.BlockSpec((1, 2, length), lambda p, *_: (p, 0, 0)),
            fixed, fixed,
            pl.BlockSpec((2, 3, 2 * tile), lambda p, *_: (p, 0, 0)),
        ],
        out_specs=[
            column, column, column,
            pl.BlockSpec((2, 3, 2 * tile), lambda p, *_: (p, 0, 0)),
            pl.BlockSpec((2, 2, tile), lambda p, *_: (p, 0, 0)),
        ],
        scratch_shapes=[
            pltpu.VMEM((2, length, 2 * LANES), jnp.bfloat16),
            pltpu.VMEM((2, length, 2 * LANES), jnp.bfloat16),
            pltpu.VMEM((LANES, length), jnp.bfloat16),
            pltpu.VMEM((2, 3, tile, tile), jnp.float32),
            pltpu.VMEM((2, 3, tile, tile), jnp.float32),
            pltpu.VMEM((2, 2, 8, tile), jnp.float32),
            pltpu.VMEM((LANES, length), jnp.float32),
            pltpu.VMEM((tile, LANES), jnp.float32),
            pltpu.VMEM((tile, LANES), jnp.float32),
        ],
    )
    low = jax.ShapeDtypeStruct((length, width), jnp.bfloat16)
    return pl.pallas_call(
        bwd_kernel,
        name="attend_backward",
        out_shape=(
            low, low, low,
            jax.ShapeDtypeStruct((heads, 3, 2 * tile), jnp.float32),
            jax.ShapeDtypeStruct((heads, 2, tile), jnp.float32),
        ),
        grid_spec=spec,
        compiler_params=pltpu.CompilerParams(
            dimension_semantics=("arbitrary",), vmem_limit_bytes=40 << 20
        ),
        cost_estimate=pl.CostEstimate(flops=length * length * width * 10, bytes_accessed=length * width * 16, transcendentals=0),
    )(ranges, ends, own, qkv, qkv, qkv, do, o, lse, qs, ks, rows)


def bucket_sums(diag, far, tile):
    u = np.arange(2 * tile)
    x = np.where(u < tile, u, u - 2 * tile)
    ids = np.stack([bucket_of(step * tile - x) for step in (-1, 0, 1)])
    hot = (ids.reshape(-1)[:, None] == np.arange(BUCKETS)[None, :]).astype(np.float32)
    sums = jnp.dot(diag.reshape(diag.shape[0], -1), jnp.asarray(hot), precision=lax.Precision.HIGHEST)
    outer = jnp.sum(far, axis=2)
    ends = np.zeros((2, BUCKETS), np.float32)
    ends[0, 15] = 1
    ends[1, 31] = 1
    return sums + outer[:, 0:1] * ends[0] + outer[:, 1:2] * ends[1]


GELU_A, GELU_B = 0.7978845608028654, 0.044715
FF_TILE = 256
EXTRA = 16


def expert_kernel(own_ref, x_ref, dy_ref, wg_ref, wu_ref, wd_ref, *refs):
    h_ref, dg_ref, du_ref, dx_ref, part_ref, acc_ref, gate_ref = refs[-7:]
    step = pl.program_id(0)
    rows = dy_ref.shape[0]
    chunk = rows // 2 if rows % 32 == 0 else rows

    @pl.when(step == 0)
    def _():
        acc_ref[...] = jnp.zeros_like(acc_ref)
        part_ref[...] = jnp.zeros_like(part_ref)
        lines = x_ref[rows:, :rows].astype(jnp.float32)
        gate = jnp.sum(lines, axis=0, keepdims=True)
        gate_ref[...] = jnp.broadcast_to(gate, (LANES, rows)).T

    wg, wu, wd = wg_ref[...], wu_ref[...], wd_ref[...]
    for start in range(0, rows, chunk):
        at = slice(start, start + chunk)
        x, dy = x_ref[at, :], dy_ref[at, :]
        g = jnp.dot(x, wg, preferred_element_type=jnp.float32)
        u = jnp.dot(x, wu, preferred_element_type=jnp.float32)
        raw = lax.dot_general(dy, wd, NT, preferred_element_type=jnp.float32)
        square = g * g
        half = 0.5 + 0.5 * jnp.tanh(g * (GELU_A + (GELU_A * GELU_B) * square))
        gelu = g * half
        slope = half + 2.0 * gelu * (1.0 - half) * (GELU_A + (3.0 * GELU_A * GELU_B) * square)
        h = gelu * u
        product = raw * h
        total = product[:, :LANES]
        for column in range(LANES, product.shape[1], LANES):
            total = total + product[:, column : column + LANES]
        part_ref[at, :] += total
        dh = raw * gate_ref[at, :1]
        du = (dh * gelu).astype(jnp.bfloat16)
        dg = (dh * u * slope).astype(jnp.bfloat16)
        h_ref[at, :] = h.astype(jnp.bfloat16)
        dg_ref[at, :] = dg
        du_ref[at, :] = du
        acc_ref[at, :] += lax.dot_general(dg, wg, NT, preferred_element_type=jnp.float32) + lax.dot_general(
            du, wu, NT, preferred_element_type=jnp.float32
        )

    @pl.when(step == pl.num_programs(0) - 1)
    def _():
        dx_ref[:rows, :] = acc_ref[...].astype(dx_ref.dtype)
        sums = jnp.sum(part_ref[...].T, axis=0, keepdims=True)
        high = sums.astype(jnp.bfloat16).astype(jnp.float32)
        middle = (sums - high).astype(jnp.bfloat16).astype(jnp.float32)
        line = lax.broadcasted_iota(jnp.int32, (EXTRA, rows), 0)
        lines = jnp.where(line == 0, high, jnp.where(line == 1, middle, jnp.where(line == 2, sums - high - middle, 0.0)))
        dx_ref[rows:, :] = jnp.zeros_like(dx_ref[rows:, :])
        dx_ref[rows:, :rows] = lines.astype(dx_ref.dtype)


def expert_block(at, count, x, dy, wgu, wd, earlier):
    rows, width = dy.shape
    hidden = wd.shape[0]
    tile = FF_TILE
    whole = jax.ShapeDtypeStruct((count * rows, hidden), jnp.bfloat16)
    fixed = lambda i, *_: (0, 0)
    out_block = pl.BlockSpec((rows, tile), lambda i, *_: (at, i))
    spec = pltpu.PrefetchScalarGridSpec(
        num_scalar_prefetch=1,
        grid=(hidden // tile,),
        in_specs=[
            pl.BlockSpec((rows + EXTRA, width), fixed),
            pl.BlockSpec((rows, width), fixed),
            pl.BlockSpec((width, tile), lambda i, *_: (0, i)),
            pl.BlockSpec((width, tile), lambda i, *_: (0, hidden // tile + i)),
            pl.BlockSpec((tile, width), lambda i, *_: (i, 0)),
        ]
        + [pl.BlockSpec(memory_space=pl.ANY)] * len(earlier),
        out_specs=[
            out_block,
            out_block,
            out_block,
            pl.BlockSpec((rows + EXTRA, width), fixed),
        ],
        scratch_shapes=[
            pltpu.VMEM((rows, LANES), jnp.float32),
            pltpu.VMEM((rows, width), jnp.float32),
            pltpu.VMEM((rows, LANES), jnp.float32),
        ],
    )
    return pl.pallas_call(
        expert_kernel,
        name="expert_block",
        out_shape=(
            whole,
            whole,
            whole,
            jax.ShapeDtypeStruct((rows + EXTRA, width), jnp.bfloat16),
        ),
        grid_spec=spec,
        input_output_aliases={6 + i: i for i in range(len(earlier))},
        compiler_params=pltpu.CompilerParams(dimension_semantics=("arbitrary",), vmem_limit_bytes=40 << 20),
        cost_estimate=pl.CostEstimate(
            flops=10 * rows * width * hidden, bytes_accessed=6 * width * hidden + 6 * rows * hidden, transcendentals=0
        ),
    )(jnp.zeros((1,), jnp.int32), x, dy, wgu, wgu, wd, *earlier)


EPS = 1e-06
FULL_PRECISION = lax.Precision.HIGHEST
ALL = ("z", "x", "exp")
SEQ = ("z", "x")
LOW = jnp.bfloat16


def dot32(a, b):
    return jnp.dot(a, b, preferred_element_type=jnp.float32)


def dot_nt(a, b):
    return lax.dot_general(a, b, NT, preferred_element_type=jnp.float32)


def dot_tn(a, b):
    return lax.dot_general(a, b, (((0,), (0,)), ((), ())), preferred_element_type=jnp.float32)


def partner(value, axis, offset):
    count = lax.axis_size(axis)
    return lax.ppermute(value, axis, [(i, i ^ offset) for i in range(count)])


def bits_of(count):
    return [1 << b for b in reversed(range(count.bit_length() - 1))]


def reorder(stacked, own):
    count = stacked.shape[0]
    return jnp.stack([lax.dynamic_index_in_dim(stacked, own ^ r, 0, keepdims=False) for r in range(count)])


def gather_double(value, steps):
    for axis, bit in steps:
        other = partner(value, axis, bit)
        high = (lax.axis_index(axis) & bit) != 0
        value = jnp.stack([jnp.where(high, other, value), jnp.where(high, value, other)])
    return value


def scatter_halve(value, steps):
    gone = []
    for axis, bit, dim in steps:
        at = dim - sum(1 for d in gone if d < dim)
        gone.append(dim)
        high = (lax.axis_index(axis) & bit) != 0
        low_half = lax.index_in_dim(value, 0, at, keepdims=False)
        high_half = lax.index_in_dim(value, 1, at, keepdims=False)
        keep = jnp.where(high, high_half, low_half)
        give = jnp.where(high, low_half, high_half)
        value = (keep.astype(jnp.float32) + partner(give, axis, bit).astype(jnp.float32)).astype(LOW)
    return value


def ring_of(groups, split):
    order = []
    for x in range(split):
        line = range(groups) if x % 2 == 0 else reversed(range(groups))
        order += [z * split + x for z in line]
    place = [order.index(s) for s in range(len(order))]
    ahead = [(order[i], order[(i + 1) % len(order)]) for i in range(len(order))]
    return jnp.asarray(order, jnp.int32), jnp.asarray(place, jnp.int32), ahead


def pick(values, index):
    return lax.dynamic_index_in_dim(values, index, 0, keepdims=False)


class RingGather:
    def __init__(self, piece, groups, split, own):
        self.order, place, self.ahead = ring_of(groups, split)
        self.count = groups * split
        self.here = pick(place, own)
        self.rows = piece.shape[0]
        self.whole = jnp.zeros((self.count * self.rows, piece.shape[1]), piece.dtype)
        self.whole = lax.dynamic_update_slice_in_dim(self.whole, piece, own * self.rows, 0)
        self.forward = self.backward = piece
        self.round = 0
        self.waiting = []

    def step(self):
        self.settle()
        self.round += 1
        k = self.round
        self.forward = lax.ppermute(self.forward, SEQ, self.ahead)
        self.waiting.append((self.forward, -k))
        if k < self.count - self.count // 2:
            self.backward = lax.ppermute(self.backward, SEQ, [(b, a) for a, b in self.ahead])
            self.waiting.append((self.backward, k))

    def settle(self):
        for piece, k in self.waiting:
            at = pick(self.order, (self.here + k + self.count) % self.count) * self.rows
            self.whole = lax.dynamic_update_slice_in_dim(self.whole, piece, at, 0)
        self.waiting = []

    def after(self, value):
        value, self.forward, self.backward = lax.optimization_barrier((value, self.forward, self.backward))
        self.waiting = [(self.forward if k < 0 else self.backward, k) for _, k in self.waiting]
        return value

    def finish(self):
        while self.round < self.count // 2:
            self.step()
        self.settle()
        return self.whole


def norm_scale(value):
    return lax.rsqrt(jnp.mean(value * value, axis=-1, keepdims=True) + EPS)


def norm_back(scale, normed, gain, grad):
    scaled = grad * gain
    return scale * (scaled - normed * jnp.mean(scaled * normed, axis=-1, keepdims=True))


def split3(value):
    high = value.astype(LOW)
    rest = value - high.astype(jnp.float32)
    middle = rest.astype(LOW)
    return [high, middle, (rest - middle.astype(jnp.float32)).astype(LOW)]


def per_device(
    block_in,
    cotangent,
    segment_ids,
    expert_routes,
    pair_priority,
    gain_attention,
    w_query,
    w_key,
    w_value,
    w_out,
    bias_table,
    gain_experts,
    w_router,
    w_gate,
    w_up,
    w_down,
):
    groups, local_len, width = block_in.shape
    tokens = groups * local_len
    rows_own, hd = w_query.shape
    split = lax.axis_size("x")
    exp_count = lax.axis_size("exp")
    seq_count = groups * split
    length = local_len * seq_count
    x_at, z_at, e_at = lax.axis_index("x"), lax.axis_index("z"), lax.axis_index("exp")
    s_at = z_at * split + x_at
    head_width = hd // split
    heads_here = head_width // HEAD_DIM
    experts_all = w_router.shape[1]
    bias_own = bias_table.shape[0]
    tile = min(TILE, local_len)
    own = s_at.astype(jnp.int32).reshape(1)
    z_bits, x_bits, e_bits = bits_of(groups), bits_of(split), bits_of(exp_count)

    input_r = reorder(block_in, z_at)

    arrived = [[None] * split for _ in range(groups)]
    for rz in reversed(range(groups)):
        arrived[rz][0] = partner(input_r[rz], "z", rz) if rz else input_r[0]
    small = jnp.concatenate(
        [
            gain_attention[:, None],
            gain_experts[:, None],
            jnp.pad(bias_table, (0, rows_own - bias_own))[:, None],
            w_router,
        ],
        axis=1,
    )
    small = jnp.pad(small, ((0, 0), (0, LANES - small.shape[1]))).astype(LOW)
    share = jnp.stack(
        [part.astype(LOW).reshape(rows_own, split, head_width) for part in (w_query, w_key, w_value)], axis=2
    )
    share = share.reshape(rows_own, split, 3 * head_width).transpose(1, 0, 2)
    common = jnp.concatenate([w_out.astype(LOW), small], axis=1)
    share = jnp.concatenate([share, jnp.broadcast_to(common, (split,) + common.shape)], axis=2)
    shares = [lax.dynamic_index_in_dim(share, x_at ^ r, 0, keepdims=False) for r in range(split)]
    shares = [shares[0]] + [partner(shares[r], "x", r) for r in range(1, split)]
    by_x = reorder(jnp.stack(shares), x_at)
    for rx in range(1, split):
        arrived[0][rx] = partner(arrived[0][0], "x", rx)
    packed = gather_double(by_x, [("z", b) for b in z_bits])
    near = [arrived[rz][0] for rz in range(1, groups)]
    packed, near = lax.optimization_barrier((packed, near))
    for rz in range(1, groups):
        arrived[rz][0] = near[rz - 1]
        for rx in range(1, split):
            arrived[rz][rx] = partner(arrived[rz][0], "x", rx)
    packed = gather_double(packed, [("exp", b) for b in e_bits[:-1]])
    packed, arrived = lax.optimization_barrier((packed, arrived))
    sequence = jnp.stack([block for line in arrived for block in line]).reshape(length, width)
    packed = gather_double(packed, [("exp", b) for b in e_bits[-1:]])
    ne, nz, nx = len(e_bits), len(z_bits), len(x_bits)
    packed = packed.transpose(
        tuple(ne + i for i in reversed(range(nz))) + (ne + nz,) + tuple(reversed(range(ne))) + (ne + nz + 1, ne + nz + 2)
    ).reshape(width, 3 * head_width + width + LANES)
    sequence, packed = lax.optimization_barrier((sequence, packed))
    qkv_w, small_all = packed[:, : 3 * head_width], packed[:, 3 * head_width + width :]
    out_w = packed[:, 3 * head_width : 3 * head_width + width]
    gate_up_own = jnp.concatenate([w_gate[0].astype(LOW), w_up[0].astype(LOW)], axis=1)
    sequence, gate_up_own = lax.optimization_barrier((sequence, gate_up_own))
    gate_up_ring = RingGather(gate_up_own, groups, split, s_at)
    gate_up_ring.step()
    down_w = lax.all_gather(w_down[0].astype(LOW), SEQ, axis=0, tiled=True)

    gain_one = small_all[:, 0].astype(jnp.float32)
    gain_two = small_all[:, 1].astype(jnp.float32)
    table_all = small_all[:, 2].reshape(-1, rows_own)[:, :bias_own].reshape(-1, BUCKETS)
    router_t = small_all[:, 3 : 3 + experts_all].T
    table_rows = lax.dynamic_slice_in_dim(table_all, x_at * heads_here, heads_here, 0)

    routes = expert_routes.reshape(tokens, -1)
    top_count = routes.shape[1]
    priority = pair_priority.reshape(-1)
    pair_experts = routes.reshape(-1)
    ahead = (pair_experts[None, :] == pair_experts[:, None]) & (priority[None, :] < priority[:, None])
    slots = jnp.sum(ahead.astype(jnp.int32), axis=1)
    capacity = (5 * top_count * tokens + 4 * experts_all - 1) // (4 * experts_all)
    slot_count = experts_all * capacity
    slot_index = jnp.where(slots < capacity, (pair_experts ^ e_at) * capacity + slots, slot_count)
    slot_index = slot_index.reshape(tokens, top_count)
    every_slot = jnp.arange(slot_count, dtype=jnp.int32)[None, :]
    table = sum((slot_index[:, k : k + 1] == every_slot).astype(LOW) for k in range(top_count))
    tables = [table[:, r * capacity : (r + 1) * capacity] for r in range(exp_count)]
    grad_low = cotangent.reshape(tokens, width)
    grad_slots = [dot_tn(part, grad_low).astype(LOW) for part in tables]

    wide = sequence.astype(jnp.float32)
    normed_one = (wide * norm_scale(wide) * gain_one).astype(LOW)
    qkv = dot32(normed_one, qkv_w).astype(LOW)
    qkv, grad_slots = lax.optimization_barrier((qkv, grad_slots))
    grad_slots = [grad_slots[0]] + [partner(grad_slots[r], "exp", r) for r in range(1, exp_count)]
    segments = lax.dynamic_index_in_dim(segment_ids, z_at, 0, keepdims=False)
    ranges = tile_ranges(segments, tile)
    seg_blocks = segments.reshape(seq_count, local_len)
    query_side, key_side = segment_columns(reorder(seg_blocks, s_at).reshape(length))
    rows = bias_rows(table_rows, tile)
    ends = jnp.stack([table_rows[:, 15], table_rows[:, 31]], axis=1).astype(jnp.float32)
    contexts, log_totals = attend_forward(qkv, query_side, key_side, ranges, rows, ends, own, tile)
    contexts = gate_up_ring.after(contexts)
    contexts, grad_slots = lax.optimization_barrier((contexts, grad_slots))
    gate_up_w = gate_up_ring.finish()

    def exchange_positions(blocks):
        return lax.all_to_all(blocks, SEQ, split_axis=0, concat_axis=0, tiled=True)

    context_local = exchange_positions(contexts.reshape(seq_count, local_len, head_width))
    context_local = (
        context_local.reshape(groups, split, local_len, head_width).transpose(0, 2, 1, 3).reshape(tokens, hd)
    )
    inputs = block_in.astype(jnp.float32).reshape(tokens, width)
    mid = inputs + dot32(context_local, out_w)
    scale_two = norm_scale(mid)
    normed_two = (mid * scale_two * gain_two).astype(LOW)

    logits = dot_nt(router_t, normed_two)
    exponent = jnp.exp(logits - jnp.max(logits, axis=0, keepdims=True))
    probabilities = exponent / jnp.sum(exponent, axis=0, keepdims=True)
    expert_ids = jnp.arange(experts_all, dtype=jnp.int32)[:, None]
    chosen = sum((routes[:, k][None, :] == expert_ids).astype(jnp.float32) for k in range(top_count))
    chosen_total = jnp.sum(probabilities * chosen, axis=0, keepdims=True)
    gates = probabilities * chosen / chosen_total
    gates_r = reorder(gates, e_at)

    gate_slots = jnp.sum(
        table.astype(jnp.float32).reshape(tokens, exp_count, capacity) * gates_r.T[:, :, None], axis=0
    )
    gate_lines = jnp.pad(jnp.stack(split3(gate_slots), axis=1), ((0, 0), (0, EXTRA - 3), (0, width - capacity)))

    def values_below(rows_):
        return jnp.sum(rows_[capacity : capacity + 3, :capacity].astype(jnp.float32), axis=0)

    sent = [None] * exp_count
    for r in reversed(range(exp_count)):
        sent[r] = jnp.concatenate([dot_tn(tables[r], normed_two).astype(LOW), gate_lines[r]], axis=0)
        if r:
            sent[r] = partner(sent[r], "exp", r)

    earlier = ()
    back = [None] * exp_count
    turns = [0] + list(range(2, exp_count)) + [1]
    for turn, r in enumerate(turns):
        if turn >= 3:
            ready = turns[turn - 2]
            sent[r], back[ready] = lax.optimization_barrier((sent[r], back[ready]))
        hidden, gate_low, up_low, dx = expert_block(
            r, exp_count, sent[r], grad_slots[r], gate_up_w, down_w, earlier
        )
        earlier = (hidden, gate_low, up_low)
        back[r] = partner(dx, "exp", r) if r else dx

    sent, hidden = lax.optimization_barrier((sent, hidden))
    slot_rows = jnp.concatenate([rows_[:capacity] for rows_ in sent], axis=0)
    slot_gates = jnp.concatenate([values_below(rows_) for rows_ in sent], axis=0)[:, None]
    slot_grads = (slot_gates * jnp.concatenate(grad_slots, axis=0).astype(jnp.float32)).astype(LOW)
    gate_sum = dot_tn(slot_rows, gate_low).astype(LOW)

    gate_grad = jnp.sum(
        table.astype(jnp.float32).reshape(tokens, exp_count, capacity) * jnp.stack([values_below(rows_) for rows_ in back])[None], axis=2
    )
    gate_grad = reorder(gate_grad.T, e_at)
    chosen_grad = chosen * (gate_grad - jnp.sum(gates * gate_grad, axis=0, keepdims=True)) / chosen_total
    logit_grad = probabilities * (chosen_grad - jnp.sum(probabilities * chosen_grad, axis=0, keepdims=True))
    logit_pieces = jnp.concatenate(split3(logit_grad), axis=0)
    router_sum = jnp.sum(dot32(logit_pieces, normed_two).reshape(3, experts_all, width), axis=0)
    normed_two_grad = dot_tn(logit_pieces, jnp.concatenate([router_t] * 3, axis=0))
    for r in range(exp_count):
        normed_two_grad = normed_two_grad + dot32(tables[r], back[r][:capacity])
    unit_two = mid * scale_two
    gain_two_sum = jnp.sum(normed_two_grad * unit_two, axis=0)
    grad_out = grad_low.astype(jnp.float32)
    mid_grad = grad_out + norm_back(scale_two, unit_two, gain_two, normed_two_grad)
    attention_grad = mid_grad.astype(LOW)
    context_grad = dot_nt(attention_grad, out_w).astype(LOW)
    context_grad, up_low, hidden, gate_sum = lax.optimization_barrier((context_grad, up_low, hidden, gate_sum))
    down_sum = dot_tn(hidden, slot_grads).astype(LOW)
    up_sum = dot_tn(slot_rows, up_low).astype(LOW)
    context_grad = (
        context_grad.reshape(groups, local_len, split, head_width)
        .transpose(0, 2, 1, 3)
        .reshape(seq_count, local_len, head_width)
    )
    context_heads = exchange_positions(context_grad).reshape(length, head_width)

    def scatter_experts(total):
        return lax.psum_scatter(total, SEQ, scatter_dimension=0, tiled=True)

    down_owned = scatter_experts(down_sum)
    gate_owned = scatter_experts(gate_sum)
    up_owned = scatter_experts(up_sum)
    context_heads, down_sum, up_sum = lax.optimization_barrier((context_heads, down_sum, up_sum))

    halving = [("exp", b, 1 + nz + nx + ne - 1 - i) for i, b in enumerate(reversed(e_bits))]
    halving += [("z", b, 1 + nz - 1 - i) for i, b in enumerate(reversed(z_bits))]
    out_sum = dot_tn(context_local, attention_grad).astype(LOW)

    query_back, key_back, value_back, diag, far = attend_backward(
        qkv, context_heads, contexts, log_totals, query_side, key_side, ranges, rows, ends, own, tile
    )
    table_local = bucket_sums(diag, far, tile)

    def through(grads, part):
        return dot_nt(grads, qkv_w[:, part * head_width : (part + 1) * head_width])

    out_parts = width // head_width
    weight_sum = jnp.stack(
        [dot_tn(normed_one, grads).astype(LOW) for grads in (query_back, key_back, value_back)]
        + [out_sum[:, i * head_width : (i + 1) * head_width] for i in range(out_parts)]
    )
    weight_sum, query_back, key_back, value_back = lax.optimization_barrier(
        (weight_sum, query_back, key_back, value_back)
    )
    normed_part = (through(query_back, 0) + through(key_back, 1) + through(value_back, 2)).astype(LOW)
    normed_part = reorder(normed_part.reshape(seq_count, local_len, width), s_at)
    half = width // 2
    normed_first = exchange_positions(normed_part[:, :, :half])
    normed_first, hidden, normed_second = lax.optimization_barrier(
        (normed_first, hidden, normed_part[:, :, half:])
    )
    normed_second = exchange_positions(normed_second)
    weight_part = scatter_halve(
        weight_sum.reshape((3 + out_parts,) + (2,) * (nz + nx + ne) + (rows_own, head_width)), halving
    ).reshape(3 + out_parts, split, rows_own, head_width)
    weight_own = [lax.dynamic_index_in_dim(weight_part, x_at ^ r, 1, keepdims=False) for r in range(split)]
    weight_own = [weight_own[0]] + [partner(weight_own[r], "x", r) for r in range(1, split)]
    out_w_out = sum(part[3:].astype(jnp.float32) for part in weight_own)
    out_w_out = out_w_out.transpose(1, 0, 2).reshape(rows_own, width)
    qkv_own = reorder(jnp.stack([part[:3] for part in weight_own]), x_at)
    qkv_own = qkv_own.transpose(1, 2, 0, 3).reshape(3, rows_own, hd).astype(jnp.float32)
    expert_out = (slot_gates * dot32(hidden, down_w)).astype(LOW)
    returned = [expert_out[:capacity]] + [
        partner(expert_out[r * capacity : (r + 1) * capacity], "exp", r) for r in range(1, exp_count)
    ]
    block_out = (mid + dot32(table, jnp.concatenate(returned, axis=0))).astype(LOW)

    block_out = block_out.reshape(groups, local_len, width)

    normed_one_grad = jnp.concatenate(
        [
            jnp.sum(part.reshape(groups, split, local_len, half).astype(jnp.float32), axis=1).reshape(tokens, half)
            for part in (normed_first, normed_second)
        ],
        axis=1,
    )
    scale_one = norm_scale(inputs)
    unit_one = inputs * scale_one
    gain_one_sum = jnp.sum(normed_one_grad * unit_one, axis=0)
    block_in_grad = (mid_grad + norm_back(scale_one, unit_one, gain_one, normed_one_grad)).reshape(
        groups, local_len, width
    )

    table_sum = lax.dynamic_update_slice_in_dim(
        jnp.zeros(table_all.shape, jnp.float32), table_local, x_at * heads_here, 0
    ).reshape(-1, bias_own)
    table_sum = jnp.pad(table_sum, ((0, 0), (0, rows_own - bias_own)))[:, None, :]
    little = jnp.concatenate(
        [
            gain_one_sum.reshape(-1, 1, rows_own),
            gain_two_sum.reshape(-1, 1, rows_own),
            table_sum,
            router_sum.reshape(experts_all, -1, rows_own).transpose(1, 0, 2),
        ],
        axis=1,
    )
    little = jnp.sum(lax.all_to_all(little, ALL, split_axis=0, concat_axis=0, tiled=True), axis=0)
    return (
        block_out,
        block_in_grad,
        little[0],
        qkv_own[0],
        qkv_own[1],
        qkv_own[2],
        out_w_out,
        little[2, :bias_own],
        little[1],
        little[3:].T,
        gate_owned.astype(jnp.float32)[None],
        up_owned.astype(jnp.float32)[None],
        down_owned.astype(jnp.float32)[None],
    )


def solution(mesh):
    def run(*args):
        groups = args[0].shape[0] // mesh.shape["exp"]
        seq_count, exp_count = mesh.shape["seq"], mesh.shape["exp"]
        grid = mesh.devices.reshape(groups, seq_count // groups, exp_count)
        fine = jax.sharding.Mesh(grid, ALL)
        placed = P("exp", SEQ, None)
        whole = P(ALL)
        matrix = P(ALL, None)
        return jax.shard_map(
            per_device,
            mesh=fine,
            in_specs=(
                placed, placed, P("exp", None), placed, placed,
                whole, matrix, matrix, matrix, matrix, whole, whole, matrix,
                placed, placed, placed,
            ),
            out_specs=(
                placed, placed, whole, matrix, matrix, matrix, matrix, whole, whole, matrix,
                placed, placed, placed,
            ),
            check_vma=False,
        )(*args)

    return run
```

```python
from functools import partial

import jax
import jax.numpy as jnp
import numpy as np
from jax import lax
from jax.experimental import pallas as pl
from jax.experimental.pallas import tpu as pltpu
from jax.sharding import PartitionSpec as P

HEAD_DIM = 64
BUCKETS = 32
THRESHOLDS = (12, 16, 23, 32, 46, 64, 91)
MASKED = -1e30
TILE = 256
LANES = 128
NT = (((1,), (1,)), ((), ()))


def bucket_of(d):
    a = np.abs(d)
    extra = sum((a >= t).astype(np.int64) for t in THRESHOLDS)
    return np.where(a < 8, a, 8 + extra) + 16 * (d > 0)


def bias_rows(table_rows, tile):
    u = np.arange(2 * tile)
    x = np.where(u < tile, u, u - 2 * tile)
    ids = np.stack([bucket_of(step * tile - x) for step in (-1, 0, 1)])
    hot = (ids.reshape(-1)[None, :] == np.arange(BUCKETS)[:, None]).astype(np.float32)
    rows = jnp.dot(table_rows.astype(jnp.bfloat16), jnp.asarray(hot, jnp.bfloat16), preferred_element_type=jnp.float32)
    return rows.reshape(table_rows.shape[0], 3, 2 * tile)


def tile_ranges(segments, tile):
    blocks = segments.reshape(-1, tile)
    first, last = blocks[:, 0], blocks[:, -1]
    low = jnp.sum((last[None, :] < first[:, None]).astype(jnp.int32), axis=1)
    high = jnp.sum((first[None, :] <= last[:, None]).astype(jnp.int32), axis=1)
    return jnp.stack([low, high])


def segment_columns(segments):
    lane = jnp.arange(LANES, dtype=jnp.int32)[None, :]
    seg = segments[:, None]
    same = seg == lane
    query_side = jnp.where(same & (lane < 4), MASKED, 0.0).astype(jnp.bfloat16)
    key_side = jnp.where(lane < 4, (~same).astype(jnp.float32), (lane < 9).astype(jnp.float32)).astype(jnp.bfloat16)
    return query_side, key_side


def toeplitz(row, tile):
    wide = jnp.broadcast_to(row, (tile, row.shape[1]))
    return pltpu.roll(wide, 0, 1, stride=1, stride_axis=0)[:, :tile]


def block_at(index, own, tile):
    return pl.ds(pl.multiple_of((index ^ own[0]) * tile, tile), tile)


def fwd_kernel(ranges, ends, own, q_ref, k_ref, v_ref, qs_ref, ks_ref, rows_ref, o_ref, lse_ref, bias_ref, vt_ref):
    group, qb = pl.program_id(0), pl.program_id(1)
    tile, span = q_ref.shape
    heads = span // HEAD_DIM

    @pl.when(qb == 0)
    def _():
        for h in range(heads):
            for step in range(3):
                bias_ref[h, step] = toeplitz(rows_ref[h, step : step + 1, :], tile)
        for start in range(0, v_ref.shape[0], tile):
            vt_ref[:, start : start + tile] = v_ref[start : start + tile, :].T

    low, high = ranges[0, qb], ranges[1, qb]
    lane = lax.broadcasted_iota(jnp.int32, (tile, LANES), 1)
    q = q_ref[...] * jnp.bfloat16(HEAD_DIM**-0.5)
    qs = qs_ref[...]
    halves = []
    for h in range(heads):
        part = q[:, h // 2 * LANES : (h // 2 + 1) * LANES]
        keep = (lane < HEAD_DIM) if h % 2 == 0 else (lane >= HEAD_DIM)
        halves.append(jnp.where(keep, part, jnp.zeros_like(part)))

    def side(h, which):
        if which == 1:
            extra = qs
        else:
            value = ends[heads * group + h, which // 2].astype(jnp.bfloat16)
            extra = jnp.where(lane == 7, value, qs)
        return jnp.concatenate([halves[h], extra], axis=1)

    def visit(which):
        queries = [side(h, which) for h in range(heads)]

        def step(kb, carry):
            keys = block_at(kb, own, tile)
            ks = ks_ref[keys, :]
            scores = []
            for h in range(heads):
                kx = jnp.concatenate([k_ref[keys, h // 2 * LANES : (h // 2 + 1) * LANES], ks], axis=1)
                scores.append(lax.dot_general(kx, queries[h], NT, preferred_element_type=jnp.float32))
            out = []
            for h in range(heads):
                peak, total, acc = carry[h]
                s = scores[h]
                if which == 1:
                    s = s + bias_ref[h, kb - qb + 1]
                new = jnp.maximum(peak, jnp.max(s, axis=0, keepdims=True))
                p = jnp.exp(s - new)
                scale = jnp.exp(peak - new)
                total = total * scale + jnp.sum(p, axis=0, keepdims=True)
                vt = vt_ref[h * HEAD_DIM : (h + 1) * HEAD_DIM, keys]
                acc = acc * scale + jnp.dot(vt, p.astype(jnp.bfloat16), preferred_element_type=jnp.float32)
                out.append((new, total, acc))
            return tuple(out)

        return step

    start = tuple(
        (
            jnp.full((1, tile), -3e38, jnp.float32),
            jnp.zeros((1, tile), jnp.float32),
            jnp.zeros((HEAD_DIM, tile), jnp.float32),
        )
        for _ in range(heads)
    )
    near_low, near_high = jnp.maximum(low, qb - 1), jnp.minimum(high, qb + 2)
    state = lax.fori_loop(near_low, near_high, visit(1), start)
    state = lax.fori_loop(low, near_low, visit(0), state)
    state = lax.fori_loop(near_high, high, visit(2), state)
    outs = []
    for h in range(heads):
        peak, total, acc = state[h]
        outs.append(acc / total)
        lse_ref[h // 2, h % 2 : h % 2 + 1, :] = peak + jnp.log(total)
    o_ref[...] = jnp.concatenate(outs, axis=0).T.astype(o_ref.dtype)


FWD_PAIRS = 4


def attend_forward(qkv, qs, ks, ranges, rows, ends, own, tile):
    length, width = qkv.shape[0], qkv.shape[1] // 3
    pairs = width // LANES
    together = FWD_PAIRS if pairs % FWD_PAIRS == 0 else 1
    span = together * LANES
    tiles = length // tile
    spec = pltpu.PrefetchScalarGridSpec(
        num_scalar_prefetch=3,
        grid=(pairs // together, tiles),
        in_specs=[
            pl.BlockSpec((tile, span), lambda p, i, r, e, own: (i ^ own[0], p)),
            pl.BlockSpec((length, span), lambda p, i, *_: (0, width // span + p)),
            pl.BlockSpec((length, span), lambda p, i, *_: (0, 2 * (width // span) + p)),
            pl.BlockSpec((tile, LANES), lambda p, i, r, e, own: (i ^ own[0], 0)),
            pl.BlockSpec((length, LANES), lambda p, i, *_: (0, 0)),
            pl.BlockSpec((2 * together, 3, 2 * tile), lambda p, i, *_: (p, 0, 0)),
        ],
        out_specs=[
            pl.BlockSpec((tile, span), lambda p, i, *_: (i, p)),
            pl.BlockSpec((together, 2, tile), lambda p, i, *_: (p, 0, i)),
        ],
        scratch_shapes=[
            pltpu.VMEM((2 * together, 3, tile, tile), jnp.float32),
            pltpu.VMEM((span, length), jnp.bfloat16),
        ],
    )
    return pl.pallas_call(
        fwd_kernel,
        name="attend_forward",
        out_shape=(
            jax.ShapeDtypeStruct((length, width), jnp.bfloat16),
            jax.ShapeDtypeStruct((pairs, 2, length), jnp.float32),
        ),
        grid_spec=spec,
        compiler_params=pltpu.CompilerParams(
            dimension_semantics=("arbitrary", "arbitrary"), vmem_limit_bytes=48 << 20
        ),
        cost_estimate=pl.CostEstimate(flops=length * length * width * 4, bytes_accessed=length * width * 8, transcendentals=0),
    )(ranges, ends, own, qkv, qkv, qkv, qs, ks, rows)


def pieces(row):
    high = row.astype(jnp.bfloat16).astype(jnp.float32)
    mid = (row - high).astype(jnp.bfloat16).astype(jnp.float32)
    return high, mid, row - high - mid


def bwd_kernel(ranges, ends, own, q_ref, k_ref, v_ref, do_ref, o_ref, lse_ref, qs_ref, ks_ref, rows_ref, *refs):
    (dq_ref, dk_ref, dv_ref, diag_ref, far_ref,
     qx_ref, dox_ref, kt_ref, bias_ref, dsum_ref, fsum_ref, dqt_ref, dka_ref, dva_ref) = refs[-14:]
    pair = own[1]
    length = q_ref.shape[0]
    tile = bias_ref.shape[2]
    tiles = length // tile
    for h in range(2):
        for step in range(3):
            bias_ref[h, step] = toeplitz(rows_ref[h, step : step + 1, :], tile)
    dsum_ref[...] = jnp.zeros_like(dsum_ref)
    fsum_ref[...] = jnp.zeros_like(fsum_ref)
    dqt_ref[...] = jnp.zeros_like(dqt_ref)
    lane = lax.broadcasted_iota(jnp.int32, (tile, LANES), 1)
    sub = lax.broadcasted_iota(jnp.int32, (LANES, tile), 0)
    pick = (lax.broadcasted_iota(jnp.int32, (8, LANES), 1) // HEAD_DIM == lax.broadcasted_iota(jnp.int32, (8, LANES), 0)).astype(jnp.float32)

    @pl.loop(0, tiles)
    def _(i):
        line = pl.ds(pl.multiple_of(i * tile, tile), tile)
        at = block_at(i, own, tile)
        q = q_ref[at, :] * jnp.bfloat16(HEAD_DIM**-0.5)
        do = do_ref[line, :]
        zero = jnp.zeros_like(q)
        product = do.astype(jnp.float32) * o_ref[line, :].astype(jnp.float32)
        delta = lax.dot_general(pick, product, NT, precision=lax.Precision.HIGHEST, preferred_element_type=jnp.float32)
        kt_ref[:, at] = k_ref[at, :].T
        for h in range(2):
            keep = (lane < HEAD_DIM) if h == 0 else (lane >= HEAD_DIM)
            a, b, c = pieces(-lse_ref[0, h : h + 1, line])
            extra = jnp.where(sub == 4, a, jnp.where(sub == 5, b, jnp.where(sub == 6, c, 0.0)))
            extra = extra.T.astype(jnp.bfloat16) + qs_ref[at, :]
            left, right = ends[2 * pair + h, 0].astype(jnp.bfloat16), ends[2 * pair + h, 1].astype(jnp.bfloat16)
            extra = jnp.where(lane == 7, left, jnp.where(lane == 8, right, extra))
            qx_ref[h, at, :] = jnp.concatenate([jnp.where(keep, q, zero), extra], axis=1)
            a, b, c = pieces(-delta[h : h + 1, :])
            extra = jnp.where(sub == 4, a, jnp.where(sub == 5, b, jnp.where(sub == 6, c, 0.0)))
            dox_ref[h, at, :] = jnp.concatenate([jnp.where(keep, do, zero), extra.T.astype(jnp.bfloat16)], axis=1)

    ones3 = ((lane >= 4) & (lane < 7)).astype(jnp.bfloat16)

    @pl.loop(0, tiles)
    def _(kb):
        low, high = ranges[0, kb], ranges[1, kb]
        keys = block_at(kb, own, tile)
        k, ks = k_ref[keys, :], ks_ref[keys, :]
        vx = jnp.concatenate([v_ref[keys, :], ones3], axis=1)
        nil = jnp.zeros_like(ks)
        dka_ref[...] = jnp.zeros_like(dka_ref)
        dva_ref[...] = jnp.zeros_like(dva_ref)

        def visit(which):
            if which == 0:
                extra = jnp.where(lane == 8, nil, ks)
            elif which == 2:
                extra = jnp.where(lane == 7, nil, ks)
            else:
                extra = jnp.where((lane == 7) | (lane == 8), nil, ks)
            kx = jnp.concatenate([k, extra], axis=1)

            def step(qb, carry):
                at = block_at(qb, own, tile)
                weights, grads = [], []
                for h in range(2):
                    qx, dox = qx_ref[h, at, :], dox_ref[h, at, :]
                    s = lax.dot_general(kx, qx, NT, preferred_element_type=jnp.float32)
                    if which == 1:
                        s = s + bias_ref[h, kb - qb + 1]
                    p = jnp.exp(s)
                    dp = lax.dot_general(vx, dox, NT, preferred_element_type=jnp.float32)
                    ds = p * dp
                    if which == 1:
                        dsum_ref[h, kb - qb + 1] += ds
                    else:
                        fsum_ref[h, which // 2] += jnp.sum(ds.reshape(tile // 8, 8, tile), axis=0)
                    weights.append(p.astype(jnp.bfloat16))
                    grads.append(ds.astype(jnp.bfloat16))
                    rows = slice(h * HEAD_DIM, (h + 1) * HEAD_DIM)
                    dqt_ref[rows, at] += jnp.dot(kt_ref[rows, keys], grads[h], preferred_element_type=jnp.float32)
                both_do = jnp.concatenate([dox_ref[0, at, :LANES], dox_ref[1, at, :LANES]], axis=0)
                both_q = jnp.concatenate([qx_ref[0, at, :LANES], qx_ref[1, at, :LANES]], axis=0)
                dva_ref[...] += jnp.dot(jnp.concatenate(weights, axis=1), both_do, preferred_element_type=jnp.float32)
                dka_ref[...] += jnp.dot(jnp.concatenate(grads, axis=1), both_q, preferred_element_type=jnp.float32)
                return carry

            return step

        near_low, near_high = jnp.maximum(low, kb - 1), jnp.minimum(high, kb + 2)
        lax.fori_loop(near_low, near_high, visit(1), 0)
        lax.fori_loop(near_high, high, visit(0), 0)
        lax.fori_loop(low, near_low, visit(2), 0)
        dk_ref[keys, :] = dka_ref[...].astype(dk_ref.dtype)
        dv_ref[keys, :] = dva_ref[...].astype(dv_ref.dtype)

    @pl.loop(0, tiles)
    def _(i):
        at = pl.ds(pl.multiple_of(i * tile, tile), tile)
        dq_ref[at, :] = (dqt_ref[:, at] * HEAD_DIM**-0.5).T.astype(dq_ref.dtype)

    for h in range(2):
        for step in range(3):
            diag_ref[h, step : step + 1, :] = diagonals(dsum_ref, h, step, tile)
        for step in range(2):
            total = jnp.sum(fsum_ref[h, step], axis=0, keepdims=True)
            far_ref[h, step : step + 1, :] = total


def diagonals(dsum_ref, h, step, tile):
    width = 2 * tile
    acc = jnp.zeros((8, width), jnp.float32)
    for group in range(tile // 8):
        part = dsum_ref[h, step, group * 8 : (group + 1) * 8, :]
        part = jnp.concatenate([part, jnp.zeros((8, tile), jnp.float32)], axis=1)
        acc = acc + (pltpu.roll(part, width - 8 * group, 1) if group else part)
    row = lax.broadcasted_iota(jnp.int32, (8, width), 0)
    for bit in (1, 2, 4):
        acc = jnp.where((row & bit) != 0, pltpu.roll(acc, width - bit, 1), acc)
    return jnp.sum(acc, axis=0, keepdims=True)


def attend_backward(pair, qkv, do, o, lse, qs, ks, ranges, rows, ends, own, tile, earlier):
    length, width = do.shape
    pairs = width // LANES
    own = jnp.concatenate([own, jnp.full((1,), pair, jnp.int32)])
    column = pl.BlockSpec((length, LANES), lambda p, r, e, own: (0, own[1]))
    fixed = pl.BlockSpec((length, LANES), lambda p, *_: (0, 0))
    spec = pltpu.PrefetchScalarGridSpec(
        num_scalar_prefetch=3,
        grid=(1,),
        in_specs=[
            column,
            pl.BlockSpec((length, LANES), lambda p, r, e, own: (0, pairs + own[1])),
            pl.BlockSpec((length, LANES), lambda p, r, e, own: (0, 2 * pairs + own[1])),
            column,
            column,
            pl.BlockSpec((1, 2, length), lambda p, r, e, own: (own[1], 0, 0)),
            fixed, fixed,
            pl.BlockSpec((2, 3, 2 * tile), lambda p, r, e, own: (own[1], 0, 0)),
        ]
        + [pl.BlockSpec(memory_space=pl.ANY)] * len(earlier),
        out_specs=[
            column, column, column,
            pl.BlockSpec((2, 3, 2 * tile), lambda p, *_: (p, 0, 0)),
            pl.BlockSpec((2, 2, tile), lambda p, *_: (p, 0, 0)),
        ],
        scratch_shapes=[
            pltpu.VMEM((2, length, 2 * LANES), jnp.bfloat16),
            pltpu.VMEM((2, length, 2 * LANES), jnp.bfloat16),
            pltpu.VMEM((LANES, length), jnp.bfloat16),
            pltpu.VMEM((2, 3, tile, tile), jnp.float32),
            pltpu.VMEM((2, 3, tile, tile), jnp.float32),
            pltpu.VMEM((2, 2, 8, tile), jnp.float32),
            pltpu.VMEM((LANES, length), jnp.float32),
            pltpu.VMEM((tile, LANES), jnp.float32),
            pltpu.VMEM((tile, LANES), jnp.float32),
        ],
    )
    low = jax.ShapeDtypeStruct((length, width), jnp.bfloat16)
    return pl.pallas_call(
        bwd_kernel,
        name="attend_backward",
        out_shape=(
            low, low, low,
            jax.ShapeDtypeStruct((2, 3, 2 * tile), jnp.float32),
            jax.ShapeDtypeStruct((2, 2, tile), jnp.float32),
        ),
        grid_spec=spec,
        input_output_aliases={12 + i: i for i in range(len(earlier))},
        compiler_params=pltpu.CompilerParams(
            dimension_semantics=("arbitrary",), vmem_limit_bytes=40 << 20
        ),
        cost_estimate=pl.CostEstimate(flops=length * length * LANES * 10, bytes_accessed=length * LANES * 16, transcendentals=0),
    )(ranges, ends, own, qkv, qkv, qkv, do, o, lse, qs, ks, rows, *earlier)


def bucket_sums(diag, far, tile):
    u = np.arange(2 * tile)
    x = np.where(u < tile, u, u - 2 * tile)
    ids = np.stack([bucket_of(step * tile - x) for step in (-1, 0, 1)])
    hot = (ids.reshape(-1)[:, None] == np.arange(BUCKETS)[None, :]).astype(np.float32)
    sums = jnp.dot(diag.reshape(diag.shape[0], -1), jnp.asarray(hot), precision=lax.Precision.HIGHEST)
    outer = jnp.sum(far, axis=2)
    ends = np.zeros((2, BUCKETS), np.float32)
    ends[0, 15] = 1
    ends[1, 31] = 1
    return sums + outer[:, 0:1] * ends[0] + outer[:, 1:2] * ends[1]


GELU_A, GELU_B = 0.7978845608028654, 0.044715
FF_TILE = 256
EXTRA = 16


def expert_kernel(own_ref, x_ref, dy_ref, wg_ref, wu_ref, wd_ref, *refs):
    h_ref, dg_ref, du_ref, dx_ref, part_ref, acc_ref, gate_ref = refs[-7:]
    step = pl.program_id(0)
    rows = dy_ref.shape[0]
    chunk = rows // 2 if rows % 32 == 0 else rows

    @pl.when(step == 0)
    def _():
        acc_ref[...] = jnp.zeros_like(acc_ref)
        part_ref[...] = jnp.zeros_like(part_ref)
        lines = x_ref[rows:, :rows].astype(jnp.float32)
        gate = jnp.sum(lines, axis=0, keepdims=True)
        gate_ref[...] = jnp.broadcast_to(gate, (LANES, rows)).T

    wg, wu, wd = wg_ref[...], wu_ref[...], wd_ref[...]
    for start in range(0, rows, chunk):
        at = slice(start, start + chunk)
        x, dy = x_ref[at, :], dy_ref[at, :]
        g = jnp.dot(x, wg, preferred_element_type=jnp.float32)
        u = jnp.dot(x, wu, preferred_element_type=jnp.float32)
        raw = lax.dot_general(dy, wd, NT, preferred_element_type=jnp.float32)
        square = g * g
        half = 0.5 + 0.5 * jnp.tanh(g * (GELU_A + (GELU_A * GELU_B) * square))
        gelu = g * half
        slope = half + 2.0 * gelu * (1.0 - half) * (GELU_A + (3.0 * GELU_A * GELU_B) * square)
        h = gelu * u
        product = raw * h
        total = product[:, :LANES]
        for column in range(LANES, product.shape[1], LANES):
            total = total + product[:, column : column + LANES]
        part_ref[at, :] += total
        dh = raw * gate_ref[at, :1]
        du = (dh * gelu).astype(jnp.bfloat16)
        dg = (dh * u * slope).astype(jnp.bfloat16)
        h_ref[at, :] = h.astype(jnp.bfloat16)
        dg_ref[at, :] = dg
        du_ref[at, :] = du
        acc_ref[at, :] += lax.dot_general(dg, wg, NT, preferred_element_type=jnp.float32) + lax.dot_general(
            du, wu, NT, preferred_element_type=jnp.float32
        )

    @pl.when(step == pl.num_programs(0) - 1)
    def _():
        dx_ref[:rows, :] = acc_ref[...].astype(dx_ref.dtype)
        sums = jnp.sum(part_ref[...].T, axis=0, keepdims=True)
        high = sums.astype(jnp.bfloat16).astype(jnp.float32)
        middle = (sums - high).astype(jnp.bfloat16).astype(jnp.float32)
        line = lax.broadcasted_iota(jnp.int32, (EXTRA, rows), 0)
        lines = jnp.where(line == 0, high, jnp.where(line == 1, middle, jnp.where(line == 2, sums - high - middle, 0.0)))
        dx_ref[rows:, :] = jnp.zeros_like(dx_ref[rows:, :])
        dx_ref[rows:, :rows] = lines.astype(dx_ref.dtype)


def expert_block(at, count, x, dy, wgu, wd, earlier):
    rows, width = dy.shape
    hidden = wd.shape[0]
    tile = FF_TILE
    whole = jax.ShapeDtypeStruct((count * rows, hidden), jnp.bfloat16)
    fixed = lambda i, *_: (0, 0)
    out_block = pl.BlockSpec((rows, tile), lambda i, *_: (at, i))
    spec = pltpu.PrefetchScalarGridSpec(
        num_scalar_prefetch=1,
        grid=(hidden // tile,),
        in_specs=[
            pl.BlockSpec((rows + EXTRA, width), fixed),
            pl.BlockSpec((rows, width), fixed),
            pl.BlockSpec((width, tile), lambda i, *_: (0, i)),
            pl.BlockSpec((width, tile), lambda i, *_: (0, hidden // tile + i)),
            pl.BlockSpec((tile, width), lambda i, *_: (i, 0)),
        ]
        + [pl.BlockSpec(memory_space=pl.ANY)] * len(earlier),
        out_specs=[
            out_block,
            out_block,
            out_block,
            pl.BlockSpec((rows + EXTRA, width), fixed),
        ],
        scratch_shapes=[
            pltpu.VMEM((rows, LANES), jnp.float32),
            pltpu.VMEM((rows, width), jnp.float32),
            pltpu.VMEM((rows, LANES), jnp.float32),
        ],
    )
    return pl.pallas_call(
        expert_kernel,
        name="expert_block",
        out_shape=(
            whole,
            whole,
            whole,
            jax.ShapeDtypeStruct((rows + EXTRA, width), jnp.bfloat16),
        ),
        grid_spec=spec,
        input_output_aliases={6 + i: i for i in range(len(earlier))},
        compiler_params=pltpu.CompilerParams(dimension_semantics=("arbitrary",), vmem_limit_bytes=40 << 20),
        cost_estimate=pl.CostEstimate(
            flops=10 * rows * width * hidden, bytes_accessed=6 * width * hidden + 6 * rows * hidden, transcendentals=0
        ),
    )(jnp.zeros((1,), jnp.int32), x, dy, wgu, wgu, wd, *earlier)


EPS = 1e-06
FULL_PRECISION = lax.Precision.HIGHEST
ALL = ("z", "x", "exp")
SEQ = ("z", "x")
LOW = jnp.bfloat16


def dot32(a, b):
    return jnp.dot(a, b, preferred_element_type=jnp.float32)


def dot_nt(a, b):
    return lax.dot_general(a, b, NT, preferred_element_type=jnp.float32)


def dot_tn(a, b):
    return lax.dot_general(a, b, (((0,), (0,)), ((), ())), preferred_element_type=jnp.float32)


def partner(value, axis, offset):
    count = lax.axis_size(axis)
    return lax.ppermute(value, axis, [(i, i ^ offset) for i in range(count)])


def bits_of(count):
    return [1 << b for b in reversed(range(count.bit_length() - 1))]


def reorder(stacked, own):
    count = stacked.shape[0]
    return jnp.stack([lax.dynamic_index_in_dim(stacked, own ^ r, 0, keepdims=False) for r in range(count)])


def gather_double(value, steps):
    for axis, bit in steps:
        other = partner(value, axis, bit)
        high = (lax.axis_index(axis) & bit) != 0
        value = jnp.stack([jnp.where(high, other, value), jnp.where(high, value, other)])
    return value


def scatter_halve(value, steps):
    gone = []
    for axis, bit, dim in steps:
        at = dim - sum(1 for d in gone if d < dim)
        gone.append(dim)
        high = (lax.axis_index(axis) & bit) != 0
        low_half = lax.index_in_dim(value, 0, at, keepdims=False)
        high_half = lax.index_in_dim(value, 1, at, keepdims=False)
        keep = jnp.where(high, high_half, low_half)
        give = jnp.where(high, low_half, high_half)
        value = (keep.astype(jnp.float32) + partner(give, axis, bit).astype(jnp.float32)).astype(LOW)
    return value


def ring_of(groups, split):
    order = []
    for x in range(split):
        line = range(groups) if x % 2 == 0 else reversed(range(groups))
        order += [z * split + x for z in line]
    place = [order.index(s) for s in range(len(order))]
    ahead = [(order[i], order[(i + 1) % len(order)]) for i in range(len(order))]
    return jnp.asarray(order, jnp.int32), jnp.asarray(place, jnp.int32), ahead


def pick(values, index):
    return lax.dynamic_index_in_dim(values, index, 0, keepdims=False)


class RingGather:
    def __init__(self, piece, groups, split, own):
        self.order, place, self.ahead = ring_of(groups, split)
        self.count = groups * split
        self.here = pick(place, own)
        self.rows = piece.shape[0]
        self.whole = jnp.zeros((self.count * self.rows, piece.shape[1]), piece.dtype)
        self.whole = lax.dynamic_update_slice_in_dim(self.whole, piece, own * self.rows, 0)
        self.forward = self.backward = piece
        self.round = 0
        self.waiting = []

    def step(self):
        self.settle()
        self.round += 1
        k = self.round
        self.forward = lax.ppermute(self.forward, SEQ, self.ahead)
        self.waiting.append((self.forward, -k))
        if k < self.count - self.count // 2:
            self.backward = lax.ppermute(self.backward, SEQ, [(b, a) for a, b in self.ahead])
            self.waiting.append((self.backward, k))

    def settle(self):
        for piece, k in self.waiting:
            at = pick(self.order, (self.here + k + self.count) % self.count) * self.rows
            self.whole = lax.dynamic_update_slice_in_dim(self.whole, piece, at, 0)
        self.waiting = []

    def after(self, value):
        value, self.forward, self.backward = lax.optimization_barrier((value, self.forward, self.backward))
        self.waiting = [(self.forward if k < 0 else self.backward, k) for _, k in self.waiting]
        return value

    def finish(self):
        while self.round < self.count // 2:
            self.step()
        self.settle()
        return self.whole


class RingScatter:
    def __init__(self, totals, groups, split, own):
        self.order, place, self.ahead = ring_of(groups, split)
        self.count = groups * split
        self.here = pick(place, own)
        self.rows = totals[0].shape[0] // self.count
        self.totals = totals
        self.round = 0
        self.forward = self.backward = None

    def block(self, total, offset):
        at = pick(self.order, (self.here + offset + self.count) % self.count) * self.rows
        return lax.dynamic_slice_in_dim(total, at, self.rows, 0)

    def load(self, coming, offset):
        own = [self.block(total, offset) for total in self.totals]
        if coming is None:
            return own
        return [(a.astype(jnp.float32) + b.astype(jnp.float32)).astype(LOW) for a, b in zip(own, coming)]

    def step(self):
        self.round += 1
        k, far = self.round, self.count // 2
        near = self.count - 1 - far
        if k <= far:
            parts = self.load(self.forward, far - k + 1)
            self.forward = [lax.ppermute(part, SEQ, self.ahead) for part in parts]
        if k <= near:
            parts = self.load(self.backward, k - near - 1)
            self.backward = [lax.ppermute(part, SEQ, [(b, a) for a, b in self.ahead]) for part in parts]

    def after(self, value):
        value, self.forward, self.backward = lax.optimization_barrier((value, self.forward, self.backward))
        return value

    def finish(self):
        while self.round < self.count // 2:
            self.step()
        own = [self.block(total, 0).astype(jnp.float32) for total in self.totals]
        return [
            a + b.astype(jnp.float32) + c.astype(jnp.float32) for a, b, c in zip(own, self.forward, self.backward)
        ]


def norm_scale(value):
    return lax.rsqrt(jnp.mean(value * value, axis=-1, keepdims=True) + EPS)


def norm_back(scale, normed, gain, grad):
    scaled = grad * gain
    return scale * (scaled - normed * jnp.mean(scaled * normed, axis=-1, keepdims=True))


def split3(value):
    high = value.astype(LOW)
    rest = value - high.astype(jnp.float32)
    middle = rest.astype(LOW)
    return [high, middle, (rest - middle.astype(jnp.float32)).astype(LOW)]


def per_device(
    block_in,
    cotangent,
    segment_ids,
    expert_routes,
    pair_priority,
    gain_attention,
    w_query,
    w_key,
    w_value,
    w_out,
    bias_table,
    gain_experts,
    w_router,
    w_gate,
    w_up,
    w_down,
):
    groups, local_len, width = block_in.shape
    tokens = groups * local_len
    rows_own, hd = w_query.shape
    split = lax.axis_size("x")
    exp_count = lax.axis_size("exp")
    seq_count = groups * split
    length = local_len * seq_count
    x_at, z_at, e_at = lax.axis_index("x"), lax.axis_index("z"), lax.axis_index("exp")
    s_at = z_at * split + x_at
    head_width = hd // split
    heads_here = head_width // HEAD_DIM
    experts_all = w_router.shape[1]
    bias_own = bias_table.shape[0]
    tile = min(TILE, local_len)
    own = s_at.astype(jnp.int32).reshape(1)
    z_bits, x_bits, e_bits = bits_of(groups), bits_of(split), bits_of(exp_count)

    input_r = reorder(block_in, z_at)

    arrived = [[None] * split for _ in range(groups)]
    for rz in reversed(range(groups)):
        arrived[rz][0] = partner(input_r[rz], "z", rz) if rz else input_r[0]
    small = jnp.concatenate(
        [
            gain_attention[:, None],
            gain_experts[:, None],
            jnp.pad(bias_table, (0, rows_own - bias_own))[:, None],
            w_router,
        ],
        axis=1,
    )
    small = jnp.pad(small, ((0, 0), (0, LANES - small.shape[1]))).astype(LOW)
    share = jnp.stack(
        [part.astype(LOW).reshape(rows_own, split, head_width) for part in (w_query, w_key, w_value)], axis=2
    )
    share = share.reshape(rows_own, split, 3 * head_width).transpose(1, 0, 2)
    common = jnp.concatenate([w_out.astype(LOW), small], axis=1)
    share = jnp.concatenate([share, jnp.broadcast_to(common, (split,) + common.shape)], axis=2)
    shares = [lax.dynamic_index_in_dim(share, x_at ^ r, 0, keepdims=False) for r in range(split)]
    shares = [shares[0]] + [partner(shares[r], "x", r) for r in range(1, split)]
    by_x = reorder(jnp.stack(shares), x_at)
    for rx in range(1, split):
        arrived[0][rx] = partner(arrived[0][0], "x", rx)
    packed = gather_double(by_x, [("z", b) for b in z_bits])
    near = [arrived[rz][0] for rz in range(1, groups)]
    packed, near = lax.optimization_barrier((packed, near))
    for rz in range(1, groups):
        arrived[rz][0] = near[rz - 1]
        for rx in range(1, split):
            arrived[rz][rx] = partner(arrived[rz][0], "x", rx)
    packed = gather_double(packed, [("exp", b) for b in e_bits[:-1]])
    packed, arrived = lax.optimization_barrier((packed, arrived))
    sequence = jnp.stack([block for line in arrived for block in line]).reshape(length, width)

    gate_up_own = jnp.concatenate([w_gate[0].astype(LOW), w_up[0].astype(LOW)], axis=1)
    sequence, gate_up_own, down_own = lax.optimization_barrier((sequence, gate_up_own, w_down[0].astype(LOW)))
    down_w = lax.all_gather(down_own, SEQ, axis=0, tiled=True)
    gate_up_ring = RingGather(gate_up_own, groups, split, s_at)
    gate_up_ring.step()
    packed = gather_double(packed, [("exp", b) for b in e_bits[-1:]])
    ne, nz, nx = len(e_bits), len(z_bits), len(x_bits)
    packed = packed.transpose(
        tuple(ne + i for i in reversed(range(nz))) + (ne + nz,) + tuple(reversed(range(ne))) + (ne + nz + 1, ne + nz + 2)
    ).reshape(width, 3 * head_width + width + LANES)
    qkv_w, small_all = packed[:, : 3 * head_width], packed[:, 3 * head_width + width :]
    out_w = packed[:, 3 * head_width : 3 * head_width + width]
    gain_one = small_all[:, 0].astype(jnp.float32)
    gain_two = small_all[:, 1].astype(jnp.float32)
    table_all = small_all[:, 2].reshape(-1, rows_own)[:, :bias_own].reshape(-1, BUCKETS)
    router_t = small_all[:, 3 : 3 + experts_all].T
    table_rows = lax.dynamic_slice_in_dim(table_all, x_at * heads_here, heads_here, 0)

    routes = expert_routes.reshape(tokens, -1)
    top_count = routes.shape[1]
    priority = pair_priority.reshape(-1)
    pair_experts = routes.reshape(-1)
    ahead = (pair_experts[None, :] == pair_experts[:, None]) & (priority[None, :] < priority[:, None])
    slots = jnp.sum(ahead.astype(jnp.int32), axis=1)
    capacity = (5 * top_count * tokens + 4 * experts_all - 1) // (4 * experts_all)
    slot_count = experts_all * capacity
    slot_index = jnp.where(slots < capacity, (pair_experts ^ e_at) * capacity + slots, slot_count)
    slot_index = slot_index.reshape(tokens, top_count)
    every_slot = jnp.arange(slot_count, dtype=jnp.int32)[None, :]
    table = sum((slot_index[:, k : k + 1] == every_slot).astype(LOW) for k in range(top_count))
    tables = [table[:, r * capacity : (r + 1) * capacity] for r in range(exp_count)]
    grad_low = cotangent.reshape(tokens, width)
    grad_slots = [dot_tn(part, grad_low).astype(LOW) for part in tables]

    wide = sequence.astype(jnp.float32)
    normed_one = (wide * norm_scale(wide) * gain_one).astype(LOW)
    qkv = dot32(normed_one, qkv_w).astype(LOW)
    qkv, grad_slots = lax.optimization_barrier((qkv, grad_slots))
    qkv = gate_up_ring.after(qkv)
    gate_up_ring.step()
    grad_slots = [grad_slots[0]] + [partner(grad_slots[r], "exp", r) for r in range(1, exp_count)]
    segments = lax.dynamic_index_in_dim(segment_ids, z_at, 0, keepdims=False)
    ranges = tile_ranges(segments, tile)
    seg_blocks = segments.reshape(seq_count, local_len)
    query_side, key_side = segment_columns(reorder(seg_blocks, s_at).reshape(length))
    rows = bias_rows(table_rows, tile)
    ends = jnp.stack([table_rows[:, 15], table_rows[:, 31]], axis=1).astype(jnp.float32)
    contexts, log_totals = attend_forward(qkv, query_side, key_side, ranges, rows, ends, own, tile)
    contexts = gate_up_ring.after(contexts)
    contexts, grad_slots = lax.optimization_barrier((contexts, grad_slots))
    gate_up_w = gate_up_ring.finish()

    def exchange_positions(blocks):
        return lax.all_to_all(blocks, SEQ, split_axis=0, concat_axis=0, tiled=True)

    context_local = exchange_positions(contexts.reshape(seq_count, local_len, head_width))
    context_local = (
        context_local.reshape(groups, split, local_len, head_width).transpose(0, 2, 1, 3).reshape(tokens, hd)
    )
    inputs = block_in.astype(jnp.float32).reshape(tokens, width)
    mid = inputs + dot32(context_local, out_w)
    scale_two = norm_scale(mid)
    normed_two = (mid * scale_two * gain_two).astype(LOW)

    logits = dot_nt(router_t, normed_two)
    exponent = jnp.exp(logits - jnp.max(logits, axis=0, keepdims=True))
    probabilities = exponent / jnp.sum(exponent, axis=0, keepdims=True)
    expert_ids = jnp.arange(experts_all, dtype=jnp.int32)[:, None]
    chosen = sum((routes[:, k][None, :] == expert_ids).astype(jnp.float32) for k in range(top_count))
    chosen_total = jnp.sum(probabilities * chosen, axis=0, keepdims=True)
    gates = probabilities * chosen / chosen_total
    gates_r = reorder(gates, e_at)

    gate_slots = jnp.sum(
        table.astype(jnp.float32).reshape(tokens, exp_count, capacity) * gates_r.T[:, :, None], axis=0
    )
    gate_lines = jnp.pad(jnp.stack(split3(gate_slots), axis=1), ((0, 0), (0, EXTRA - 3), (0, width - capacity)))

    def values_below(rows_):
        return jnp.sum(rows_[capacity : capacity + 3, :capacity].astype(jnp.float32), axis=0)

    sent = [None] * exp_count
    for r in reversed(range(exp_count)):
        sent[r] = jnp.concatenate([dot_tn(tables[r], normed_two).astype(LOW), gate_lines[r]], axis=0)
        if r:
            sent[r] = partner(sent[r], "exp", r)

    earlier = ()
    back = [None] * exp_count
    turns = [0] + list(range(2, exp_count)) + [1]
    for turn, r in enumerate(turns):
        if turn >= 3:
            ready = turns[turn - 2]
            sent[r], back[ready] = lax.optimization_barrier((sent[r], back[ready]))
        hidden, gate_low, up_low, dx = expert_block(
            r, exp_count, sent[r], grad_slots[r], gate_up_w, down_w, earlier
        )
        earlier = (hidden, gate_low, up_low)
        back[r] = partner(dx, "exp", r) if r else dx

    sent, hidden = lax.optimization_barrier((sent, hidden))
    slot_rows = jnp.concatenate([rows_[:capacity] for rows_ in sent], axis=0)
    slot_gates = jnp.concatenate([values_below(rows_) for rows_ in sent], axis=0)[:, None]
    slot_grads = (slot_gates * jnp.concatenate(grad_slots, axis=0).astype(jnp.float32)).astype(LOW)
    down_sum = dot_tn(hidden, slot_grads).astype(LOW)

    gate_grad = jnp.sum(
        table.astype(jnp.float32).reshape(tokens, exp_count, capacity) * jnp.stack([values_below(rows_) for rows_ in back])[None], axis=2
    )
    gate_grad = reorder(gate_grad.T, e_at)
    chosen_grad = chosen * (gate_grad - jnp.sum(gates * gate_grad, axis=0, keepdims=True)) / chosen_total
    logit_grad = probabilities * (chosen_grad - jnp.sum(probabilities * chosen_grad, axis=0, keepdims=True))
    logit_pieces = jnp.concatenate(split3(logit_grad), axis=0)
    router_sum = jnp.sum(dot32(logit_pieces, normed_two).reshape(3, experts_all, width), axis=0)
    normed_two_grad = dot_tn(logit_pieces, jnp.concatenate([router_t] * 3, axis=0))
    for r in range(exp_count):
        normed_two_grad = normed_two_grad + dot32(tables[r], back[r][:capacity])
    unit_two = mid * scale_two
    gain_two_sum = jnp.sum(normed_two_grad * unit_two, axis=0)
    grad_out = grad_low.astype(jnp.float32)
    mid_grad = grad_out + norm_back(scale_two, unit_two, gain_two, normed_two_grad)
    attention_grad = mid_grad.astype(LOW)
    context_grad = dot_nt(attention_grad, out_w).astype(LOW)
    context_grad, up_low, gate_low, hidden, down_sum = lax.optimization_barrier(
        (context_grad, up_low, gate_low, hidden, down_sum)
    )
    gate_sum = dot_tn(slot_rows, gate_low).astype(LOW)
    up_sum = dot_tn(slot_rows, up_low).astype(LOW)
    context_grad = (
        context_grad.reshape(groups, local_len, split, head_width)
        .transpose(0, 2, 1, 3)
        .reshape(seq_count, local_len, head_width)
    )
    context_heads = exchange_positions(context_grad).reshape(length, head_width)

    def scatter_experts(total):
        return lax.psum_scatter(total, SEQ, scatter_dimension=0, tiled=True)

    down_owned = scatter_experts(down_sum)
    context_heads, gate_sum, up_sum = lax.optimization_barrier((context_heads, gate_sum, up_sum))

    halving = [("exp", b, 1 + nz + nx + ne - 1 - i) for i, b in enumerate(reversed(e_bits))]
    halving += [("z", b, 1 + nz - 1 - i) for i, b in enumerate(reversed(z_bits))]
    out_sum = dot_tn(context_local, attention_grad).astype(LOW)

    ring = RingScatter([gate_sum, up_sum], groups, split, s_at)
    grads, diag, far = (), [], []
    pairs = head_width // LANES
    for pair in range(pairs):
        ring.step()
        *grads, pair_diag, pair_far = attend_backward(
            pair, qkv, context_heads, contexts, log_totals, query_side, key_side, ranges, rows, ends, own, tile, tuple(grads)
        )
        grads = ring.after(grads)
        diag.append(pair_diag)
        far.append(pair_far)
    diag, far = jnp.concatenate(diag), jnp.concatenate(far)
    query_back, key_back, value_back, down_owned = lax.optimization_barrier((*grads, down_owned))
    gate_owned, up_owned = ring.finish()
    table_local = bucket_sums(diag, far, tile)

    def through(grads, part):
        return dot_nt(grads, qkv_w[:, part * head_width : (part + 1) * head_width])

    out_parts = width // head_width
    weight_sum = jnp.stack(
        [dot_tn(normed_one, grads).astype(LOW) for grads in (query_back, key_back, value_back)]
        + [out_sum[:, i * head_width : (i + 1) * head_width] for i in range(out_parts)]
    )
    weight_sum, query_back, key_back, value_back = lax.optimization_barrier(
        (weight_sum, query_back, key_back, value_back)
    )
    normed_part = (through(query_back, 0) + through(key_back, 1) + through(value_back, 2)).astype(LOW)
    normed_part = reorder(normed_part.reshape(seq_count, local_len, width), s_at)
    half = width // 2
    normed_first = exchange_positions(normed_part[:, :, :half])
    normed_first, hidden, normed_second = lax.optimization_barrier(
        (normed_first, hidden, normed_part[:, :, half:])
    )
    normed_second = exchange_positions(normed_second)
    weight_part = scatter_halve(
        weight_sum.reshape((3 + out_parts,) + (2,) * (nz + nx + ne) + (rows_own, head_width)), halving
    ).reshape(3 + out_parts, split, rows_own, head_width)
    weight_own = [lax.dynamic_index_in_dim(weight_part, x_at ^ r, 1, keepdims=False) for r in range(split)]
    weight_own = [weight_own[0]] + [partner(weight_own[r], "x", r) for r in range(1, split)]
    out_w_out = sum(part[3:].astype(jnp.float32) for part in weight_own)
    out_w_out = out_w_out.transpose(1, 0, 2).reshape(rows_own, width)
    qkv_own = reorder(jnp.stack([part[:3] for part in weight_own]), x_at)
    qkv_own = qkv_own.transpose(1, 2, 0, 3).reshape(3, rows_own, hd).astype(jnp.float32)
    expert_out = (slot_gates * dot32(hidden, down_w)).astype(LOW)
    returned = [expert_out[:capacity]] + [
        partner(expert_out[r * capacity : (r + 1) * capacity], "exp", r) for r in range(1, exp_count)
    ]
    block_out = (mid + dot32(table, jnp.concatenate(returned, axis=0))).astype(LOW)

    block_out = block_out.reshape(groups, local_len, width)

    normed_one_grad = jnp.concatenate(
        [
            jnp.sum(part.reshape(groups, split, local_len, half).astype(jnp.float32), axis=1).reshape(tokens, half)
            for part in (normed_first, normed_second)
        ],
        axis=1,
    )
    scale_one = norm_scale(inputs)
    unit_one = inputs * scale_one
    gain_one_sum = jnp.sum(normed_one_grad * unit_one, axis=0)
    block_in_grad = (mid_grad + norm_back(scale_one, unit_one, gain_one, normed_one_grad)).reshape(
        groups, local_len, width
    )

    table_sum = lax.dynamic_update_slice_in_dim(
        jnp.zeros(table_all.shape, jnp.float32), table_local, x_at * heads_here, 0
    ).reshape(-1, bias_own)
    table_sum = jnp.pad(table_sum, ((0, 0), (0, rows_own - bias_own)))[:, None, :]
    little = jnp.concatenate(
        [
            gain_one_sum.reshape(-1, 1, rows_own),
            gain_two_sum.reshape(-1, 1, rows_own),
            table_sum,
            router_sum.reshape(experts_all, -1, rows_own).transpose(1, 0, 2),
        ],
        axis=1,
    )
    little = jnp.sum(lax.all_to_all(little, ALL, split_axis=0, concat_axis=0, tiled=True), axis=0)
    return (
        block_out,
        block_in_grad,
        little[0],
        qkv_own[0],
        qkv_own[1],
        qkv_own[2],
        out_w_out,
        little[2, :bias_own],
        little[1],
        little[3:].T,
        gate_owned.astype(jnp.float32)[None],
        up_owned.astype(jnp.float32)[None],
        down_owned.astype(jnp.float32)[None],
    )


def solution(mesh):
    def run(*args):
        groups = args[0].shape[0] // mesh.shape["exp"]
        seq_count, exp_count = mesh.shape["seq"], mesh.shape["exp"]
        grid = mesh.devices.reshape(groups, seq_count // groups, exp_count)
        fine = jax.sharding.Mesh(grid, ALL)
        placed = P("exp", SEQ, None)
        whole = P(ALL)
        matrix = P(ALL, None)
        return jax.shard_map(
            per_device,
            mesh=fine,
            in_specs=(
                placed, placed, P("exp", None), placed, placed,
                whole, matrix, matrix, matrix, matrix, whole, whole, matrix,
                placed, placed, placed,
            ),
            out_specs=(
                placed, placed, whole, matrix, matrix, matrix, matrix, whole, whole, matrix,
                placed, placed, placed,
            ),
            check_vma=False,
        )(*args)

    return run
```

```python
from functools import partial

import jax
import jax.numpy as jnp
import numpy as np
from jax import lax
from jax.experimental import pallas as pl
from jax.experimental.pallas import tpu as pltpu
from jax.sharding import PartitionSpec as P

HEAD_DIM = 64
BUCKETS = 32
THRESHOLDS = (12, 16, 23, 32, 46, 64, 91)
MASKED = -1e30
TILE = 256
LANES = 128
NT = (((1,), (1,)), ((), ()))


def bucket_of(d):
    a = np.abs(d)
    extra = sum((a >= t).astype(np.int64) for t in THRESHOLDS)
    return np.where(a < 8, a, 8 + extra) + 16 * (d > 0)


def bias_rows(table_rows, tile):
    u = np.arange(2 * tile)
    x = np.where(u < tile, u, u - 2 * tile)
    ids = np.stack([bucket_of(step * tile - x) for step in (-1, 0, 1)])
    hot = (ids.reshape(-1)[None, :] == np.arange(BUCKETS)[:, None]).astype(np.float32)
    rows = jnp.dot(table_rows.astype(jnp.bfloat16), jnp.asarray(hot, jnp.bfloat16), preferred_element_type=jnp.float32)
    return rows.reshape(table_rows.shape[0], 3, 2 * tile)


def tile_ranges(segments, tile):
    blocks = segments.reshape(-1, tile)
    first, last = blocks[:, 0], blocks[:, -1]
    low = jnp.sum((last[None, :] < first[:, None]).astype(jnp.int32), axis=1)
    high = jnp.sum((first[None, :] <= last[:, None]).astype(jnp.int32), axis=1)
    return jnp.stack([low, high])


def segment_columns(segments):
    lane = jnp.arange(LANES, dtype=jnp.int32)[None, :]
    seg = segments[:, None]
    same = seg == lane
    query_side = jnp.where(same & (lane < 4), MASKED, 0.0).astype(jnp.bfloat16)
    key_side = jnp.where(lane < 4, (~same).astype(jnp.float32), (lane < 9).astype(jnp.float32)).astype(jnp.bfloat16)
    return query_side, key_side


def toeplitz(row, tile):
    wide = jnp.broadcast_to(row, (tile, row.shape[1]))
    return pltpu.roll(wide, 0, 1, stride=1, stride_axis=0)[:, :tile]


def block_at(index, own, tile):
    return pl.ds(pl.multiple_of((index ^ own[0]) * tile, tile), tile)


def fwd_kernel(ranges, ends, own, q_ref, k_ref, v_ref, qs_ref, ks_ref, rows_ref, o_ref, lse_ref, bias_ref, vt_ref):
    group, qb = pl.program_id(0), pl.program_id(1)
    tile, span = q_ref.shape
    heads = span // HEAD_DIM

    @pl.when(qb == 0)
    def _():
        for h in range(heads):
            for step in range(3):
                bias_ref[h, step] = toeplitz(rows_ref[h, step : step + 1, :], tile)
        for start in range(0, v_ref.shape[0], tile):
            vt_ref[:, start : start + tile] = v_ref[start : start + tile, :].T

    low, high = ranges[0, qb], ranges[1, qb]
    lane = lax.broadcasted_iota(jnp.int32, (tile, LANES), 1)
    q = q_ref[...] * jnp.bfloat16(HEAD_DIM**-0.5)
    qs = qs_ref[...]
    halves = []
    for h in range(heads):
        part = q[:, h // 2 * LANES : (h // 2 + 1) * LANES]
        keep = (lane < HEAD_DIM) if h % 2 == 0 else (lane >= HEAD_DIM)
        halves.append(jnp.where(keep, part, jnp.zeros_like(part)))

    def side(h, which):
        if which == 1:
            extra = qs
        else:
            value = ends[heads * group + h, which // 2].astype(jnp.bfloat16)
            extra = jnp.where(lane == 7, value, qs)
        return jnp.concatenate([halves[h], extra], axis=1)

    def visit(which):
        queries = [side(h, which) for h in range(heads)]

        def step(kb, carry):
            keys = block_at(kb, own, tile)
            ks = ks_ref[keys, :]
            scores = []
            for h in range(heads):
                kx = jnp.concatenate([k_ref[keys, h // 2 * LANES : (h // 2 + 1) * LANES], ks], axis=1)
                scores.append(lax.dot_general(kx, queries[h], NT, preferred_element_type=jnp.float32))
            out = []
            for h in range(heads):
                peak, total, acc = carry[h]
                s = scores[h]
                if which == 1:
                    s = s + bias_ref[h, kb - qb + 1]
                new = jnp.maximum(peak, jnp.max(s, axis=0, keepdims=True))
                p = jnp.exp(s - new)
                scale = jnp.exp(peak - new)
                total = total * scale + jnp.sum(p, axis=0, keepdims=True)
                vt = vt_ref[h * HEAD_DIM : (h + 1) * HEAD_DIM, keys]
                acc = acc * scale + jnp.dot(vt, p.astype(jnp.bfloat16), preferred_element_type=jnp.float32)
                out.append((new, total, acc))
            return tuple(out)

        return step

    start = tuple(
        (
            jnp.full((1, tile), -3e38, jnp.float32),
            jnp.zeros((1, tile), jnp.float32),
            jnp.zeros((HEAD_DIM, tile), jnp.float32),
        )
        for _ in range(heads)
    )
    near_low, near_high = jnp.maximum(low, qb - 1), jnp.minimum(high, qb + 2)
    state = lax.fori_loop(near_low, near_high, visit(1), start)
    state = lax.fori_loop(low, near_low, visit(0), state)
    state = lax.fori_loop(near_high, high, visit(2), state)
    outs = []
    for h in range(heads):
        peak, total, acc = state[h]
        outs.append(acc / total)
        lse_ref[h // 2, h % 2 : h % 2 + 1, :] = peak + jnp.log(total)
    o_ref[...] = jnp.concatenate(outs, axis=0).T.astype(o_ref.dtype)


FWD_PAIRS = 4


def attend_forward(qkv, qs, ks, ranges, rows, ends, own, tile):
    length, width = qkv.shape[0], qkv.shape[1] // 3
    pairs = width // LANES
    together = FWD_PAIRS if pairs % FWD_PAIRS == 0 else 1
    span = together * LANES
    tiles = length // tile
    spec = pltpu.PrefetchScalarGridSpec(
        num_scalar_prefetch=3,
        grid=(pairs // together, tiles),
        in_specs=[
            pl.BlockSpec((tile, span), lambda p, i, r, e, own: (i ^ own[0], p)),
            pl.BlockSpec((length, span), lambda p, i, *_: (0, width // span + p)),
            pl.BlockSpec((length, span), lambda p, i, *_: (0, 2 * (width // span) + p)),
            pl.BlockSpec((tile, LANES), lambda p, i, r, e, own: (i ^ own[0], 0)),
            pl.BlockSpec((length, LANES), lambda p, i, *_: (0, 0)),
            pl.BlockSpec((2 * together, 3, 2 * tile), lambda p, i, *_: (p, 0, 0)),
        ],
        out_specs=[
            pl.BlockSpec((tile, span), lambda p, i, *_: (i, p)),
            pl.BlockSpec((together, 2, tile), lambda p, i, *_: (p, 0, i)),
        ],
        scratch_shapes=[
            pltpu.VMEM((2 * together, 3, tile, tile), jnp.float32),
            pltpu.VMEM((span, length), jnp.bfloat16),
        ],
    )
    return pl.pallas_call(
        fwd_kernel,
        name="attend_forward",
        out_shape=(
            jax.ShapeDtypeStruct((length, width), jnp.bfloat16),
            jax.ShapeDtypeStruct((pairs, 2, length), jnp.float32),
        ),
        grid_spec=spec,
        compiler_params=pltpu.CompilerParams(
            dimension_semantics=("arbitrary", "arbitrary"), vmem_limit_bytes=48 << 20
        ),
        cost_estimate=pl.CostEstimate(flops=length * length * width * 4, bytes_accessed=length * width * 8, transcendentals=0),
    )(ranges, ends, own, qkv, qkv, qkv, qs, ks, rows)


def pieces(row):
    high = row.astype(jnp.bfloat16).astype(jnp.float32)
    mid = (row - high).astype(jnp.bfloat16).astype(jnp.float32)
    return high, mid, row - high - mid


def bwd_kernel(ranges, ends, own, q_ref, k_ref, v_ref, do_ref, o_ref, lse_ref, qs_ref, ks_ref, rows_ref, *refs):
    (dq_ref, dk_ref, dv_ref, diag_ref, far_ref,
     qx_ref, dox_ref, kt_ref, bias_ref, dsum_ref, fsum_ref, dqt_ref, dka_ref, dva_ref) = refs[-14:]
    pair = own[1]
    length = q_ref.shape[0]
    tile = bias_ref.shape[2]
    tiles = length // tile
    for h in range(2):
        for step in range(3):
            bias_ref[h, step] = toeplitz(rows_ref[h, step : step + 1, :], tile)
    dsum_ref[...] = jnp.zeros_like(dsum_ref)
    fsum_ref[...] = jnp.zeros_like(fsum_ref)
    dqt_ref[...] = jnp.zeros_like(dqt_ref)
    lane = lax.broadcasted_iota(jnp.int32, (tile, LANES), 1)
    sub = lax.broadcasted_iota(jnp.int32, (LANES, tile), 0)
    pick = (lax.broadcasted_iota(jnp.int32, (8, LANES), 1) // HEAD_DIM == lax.broadcasted_iota(jnp.int32, (8, LANES), 0)).astype(jnp.float32)

    @pl.loop(0, tiles)
    def _(i):
        line = pl.ds(pl.multiple_of(i * tile, tile), tile)
        at = block_at(i, own, tile)
        q = q_ref[at, :] * jnp.bfloat16(HEAD_DIM**-0.5)
        do = do_ref[line, :]
        zero = jnp.zeros_like(q)
        product = do.astype(jnp.float32) * o_ref[line, :].astype(jnp.float32)
        delta = lax.dot_general(pick, product, NT, precision=lax.Precision.HIGHEST, preferred_element_type=jnp.float32)
        kt_ref[:, at] = k_ref[at, :].T
        for h in range(2):
            keep = (lane < HEAD_DIM) if h == 0 else (lane >= HEAD_DIM)
            a, b, c = pieces(-lse_ref[0, h : h + 1, line])
            extra = jnp.where(sub == 4, a, jnp.where(sub == 5, b, jnp.where(sub == 6, c, 0.0)))
            extra = extra.T.astype(jnp.bfloat16) + qs_ref[at, :]
            left, right = ends[2 * pair + h, 0].astype(jnp.bfloat16), ends[2 * pair + h, 1].astype(jnp.bfloat16)
            extra = jnp.where(lane == 7, left, jnp.where(lane == 8, right, extra))
            qx_ref[h, at, :] = jnp.concatenate([jnp.where(keep, q, zero), extra], axis=1)
            a, b, c = pieces(-delta[h : h + 1, :])
            extra = jnp.where(sub == 4, a, jnp.where(sub == 5, b, jnp.where(sub == 6, c, 0.0)))
            dox_ref[h, at, :] = jnp.concatenate([jnp.where(keep, do, zero), extra.T.astype(jnp.bfloat16)], axis=1)

    ones3 = ((lane >= 4) & (lane < 7)).astype(jnp.bfloat16)

    @pl.loop(0, tiles)
    def _(kb):
        low, high = ranges[0, kb], ranges[1, kb]
        keys = block_at(kb, own, tile)
        k, ks = k_ref[keys, :], ks_ref[keys, :]
        vx = jnp.concatenate([v_ref[keys, :], ones3], axis=1)
        nil = jnp.zeros_like(ks)
        dka_ref[...] = jnp.zeros_like(dka_ref)
        dva_ref[...] = jnp.zeros_like(dva_ref)

        def visit(which):
            if which == 0:
                extra = jnp.where(lane == 8, nil, ks)
            elif which == 2:
                extra = jnp.where(lane == 7, nil, ks)
            else:
                extra = jnp.where((lane == 7) | (lane == 8), nil, ks)
            kx = jnp.concatenate([k, extra], axis=1)

            def step(qb, carry):
                at = block_at(qb, own, tile)
                weights, grads = [], []
                for h in range(2):
                    qx, dox = qx_ref[h, at, :], dox_ref[h, at, :]
                    s = lax.dot_general(kx, qx, NT, preferred_element_type=jnp.float32)
                    if which == 1:
                        s = s + bias_ref[h, kb - qb + 1]
                    p = jnp.exp(s)
                    dp = lax.dot_general(vx, dox, NT, preferred_element_type=jnp.float32)
                    ds = p * dp
                    if which == 1:
                        dsum_ref[h, kb - qb + 1] += ds
                    else:
                        fsum_ref[h, which // 2] += jnp.sum(ds.reshape(tile // 8, 8, tile), axis=0)
                    weights.append(p.astype(jnp.bfloat16))
                    grads.append(ds.astype(jnp.bfloat16))
                    rows = slice(h * HEAD_DIM, (h + 1) * HEAD_DIM)
                    dqt_ref[rows, at] += jnp.dot(kt_ref[rows, keys], grads[h], preferred_element_type=jnp.float32)
                both_do = jnp.concatenate([dox_ref[0, at, :LANES], dox_ref[1, at, :LANES]], axis=0)
                both_q = jnp.concatenate([qx_ref[0, at, :LANES], qx_ref[1, at, :LANES]], axis=0)
                dva_ref[...] += jnp.dot(jnp.concatenate(weights, axis=1), both_do, preferred_element_type=jnp.float32)
                dka_ref[...] += jnp.dot(jnp.concatenate(grads, axis=1), both_q, preferred_element_type=jnp.float32)
                return carry

            return step

        near_low, near_high = jnp.maximum(low, kb - 1), jnp.minimum(high, kb + 2)
        lax.fori_loop(near_low, near_high, visit(1), 0)
        lax.fori_loop(near_high, high, visit(0), 0)
        lax.fori_loop(low, near_low, visit(2), 0)
        dk_ref[keys, :] = dka_ref[...].astype(dk_ref.dtype)
        dv_ref[keys, :] = dva_ref[...].astype(dv_ref.dtype)

    @pl.loop(0, tiles)
    def _(i):
        at = pl.ds(pl.multiple_of(i * tile, tile), tile)
        dq_ref[at, :] = (dqt_ref[:, at] * HEAD_DIM**-0.5).T.astype(dq_ref.dtype)

    for h in range(2):
        for step in range(3):
            diag_ref[h, step : step + 1, :] = diagonals(dsum_ref, h, step, tile)
        for step in range(2):
            total = jnp.sum(fsum_ref[h, step], axis=0, keepdims=True)
            far_ref[h, step : step + 1, :] = total


def diagonals(dsum_ref, h, step, tile):
    width = 2 * tile
    acc = jnp.zeros((8, width), jnp.float32)
    for group in range(tile // 8):
        part = dsum_ref[h, step, group * 8 : (group + 1) * 8, :]
        part = jnp.concatenate([part, jnp.zeros((8, tile), jnp.float32)], axis=1)
        acc = acc + (pltpu.roll(part, width - 8 * group, 1) if group else part)
    row = lax.broadcasted_iota(jnp.int32, (8, width), 0)
    for bit in (1, 2, 4):
        acc = jnp.where((row & bit) != 0, pltpu.roll(acc, width - bit, 1), acc)
    return jnp.sum(acc, axis=0, keepdims=True)


def attend_backward(pair, qkv, do, o, lse, qs, ks, ranges, rows, ends, own, tile, earlier):
    length, width = do.shape
    pairs = width // LANES
    own = jnp.concatenate([own, jnp.full((1,), pair, jnp.int32)])
    column = pl.BlockSpec((length, LANES), lambda p, r, e, own: (0, own[1]))
    fixed = pl.BlockSpec((length, LANES), lambda p, *_: (0, 0))
    spec = pltpu.PrefetchScalarGridSpec(
        num_scalar_prefetch=3,
        grid=(1,),
        in_specs=[
            column,
            pl.BlockSpec((length, LANES), lambda p, r, e, own: (0, pairs + own[1])),
            pl.BlockSpec((length, LANES), lambda p, r, e, own: (0, 2 * pairs + own[1])),
            column,
            column,
            pl.BlockSpec((1, 2, length), lambda p, r, e, own: (own[1], 0, 0)),
            fixed, fixed,
            pl.BlockSpec((2, 3, 2 * tile), lambda p, r, e, own: (own[1], 0, 0)),
        ]
        + [pl.BlockSpec(memory_space=pl.ANY)] * len(earlier),
        out_specs=[
            column, column, column,
            pl.BlockSpec((2, 3, 2 * tile), lambda p, *_: (p, 0, 0)),
            pl.BlockSpec((2, 2, tile), lambda p, *_: (p, 0, 0)),
        ],
        scratch_shapes=[
            pltpu.VMEM((2, length, 2 * LANES), jnp.bfloat16),
            pltpu.VMEM((2, length, 2 * LANES), jnp.bfloat16),
            pltpu.VMEM((LANES, length), jnp.bfloat16),
            pltpu.VMEM((2, 3, tile, tile), jnp.float32),
            pltpu.VMEM((2, 3, tile, tile), jnp.float32),
            pltpu.VMEM((2, 2, 8, tile), jnp.float32),
            pltpu.VMEM((LANES, length), jnp.float32),
            pltpu.VMEM((tile, LANES), jnp.float32),
            pltpu.VMEM((tile, LANES), jnp.float32),
        ],
    )
    low = jax.ShapeDtypeStruct((length, width), jnp.bfloat16)
    return pl.pallas_call(
        bwd_kernel,
        name="attend_backward",
        out_shape=(
            low, low, low,
            jax.ShapeDtypeStruct((2, 3, 2 * tile), jnp.float32),
            jax.ShapeDtypeStruct((2, 2, tile), jnp.float32),
        ),
        grid_spec=spec,
        input_output_aliases={12 + i: i for i in range(len(earlier))},
        compiler_params=pltpu.CompilerParams(
            dimension_semantics=("arbitrary",), vmem_limit_bytes=40 << 20
        ),
        cost_estimate=pl.CostEstimate(flops=length * length * LANES * 10, bytes_accessed=length * LANES * 16, transcendentals=0),
    )(ranges, ends, own, qkv, qkv, qkv, do, o, lse, qs, ks, rows, *earlier)


def bucket_sums(diag, far, tile):
    u = np.arange(2 * tile)
    x = np.where(u < tile, u, u - 2 * tile)
    ids = np.stack([bucket_of(step * tile - x) for step in (-1, 0, 1)])
    hot = (ids.reshape(-1)[:, None] == np.arange(BUCKETS)[None, :]).astype(np.float32)
    sums = jnp.dot(diag.reshape(diag.shape[0], -1), jnp.asarray(hot), precision=lax.Precision.HIGHEST)
    outer = jnp.sum(far, axis=2)
    ends = np.zeros((2, BUCKETS), np.float32)
    ends[0, 15] = 1
    ends[1, 31] = 1
    return sums + outer[:, 0:1] * ends[0] + outer[:, 1:2] * ends[1]


GELU_A, GELU_B = 0.7978845608028654, 0.044715
FF_TILE = 256
EXTRA = 16


def expert_kernel(own_ref, x_ref, dy_ref, wg_ref, wu_ref, wd_ref, *refs):
    h_ref, dg_ref, du_ref, dx_ref, part_ref, acc_ref, gate_ref = refs[-7:]
    step = pl.program_id(0)
    rows = dy_ref.shape[0]
    chunk = rows // 2 if rows % 32 == 0 else rows

    @pl.when(step == 0)
    def _():
        acc_ref[...] = jnp.zeros_like(acc_ref)
        part_ref[...] = jnp.zeros_like(part_ref)
        lines = x_ref[rows:, :rows].astype(jnp.float32)
        gate = jnp.sum(lines, axis=0, keepdims=True)
        gate_ref[...] = jnp.broadcast_to(gate, (LANES, rows)).T

    wg, wu, wd = wg_ref[...], wu_ref[...], wd_ref[...]
    for start in range(0, rows, chunk):
        at = slice(start, start + chunk)
        x, dy = x_ref[at, :], dy_ref[at, :]
        g = jnp.dot(x, wg, preferred_element_type=jnp.float32)
        u = jnp.dot(x, wu, preferred_element_type=jnp.float32)
        raw = lax.dot_general(dy, wd, NT, preferred_element_type=jnp.float32)
        square = g * g
        half = 0.5 + 0.5 * jnp.tanh(g * (GELU_A + (GELU_A * GELU_B) * square))
        gelu = g * half
        slope = half + 2.0 * gelu * (1.0 - half) * (GELU_A + (3.0 * GELU_A * GELU_B) * square)
        h = gelu * u
        product = raw * h
        total = product[:, :LANES]
        for column in range(LANES, product.shape[1], LANES):
            total = total + product[:, column : column + LANES]
        part_ref[at, :] += total
        dh = raw * gate_ref[at, :1]
        du = (dh * gelu).astype(jnp.bfloat16)
        dg = (dh * u * slope).astype(jnp.bfloat16)
        h_ref[at, :] = h.astype(jnp.bfloat16)
        dg_ref[at, :] = dg
        du_ref[at, :] = du
        acc_ref[at, :] += lax.dot_general(dg, wg, NT, preferred_element_type=jnp.float32) + lax.dot_general(
            du, wu, NT, preferred_element_type=jnp.float32
        )

    @pl.when(step == pl.num_programs(0) - 1)
    def _():
        dx_ref[:rows, :] = acc_ref[...].astype(dx_ref.dtype)
        sums = jnp.sum(part_ref[...].T, axis=0, keepdims=True)
        high = sums.astype(jnp.bfloat16).astype(jnp.float32)
        middle = (sums - high).astype(jnp.bfloat16).astype(jnp.float32)
        line = lax.broadcasted_iota(jnp.int32, (EXTRA, rows), 0)
        lines = jnp.where(line == 0, high, jnp.where(line == 1, middle, jnp.where(line == 2, sums - high - middle, 0.0)))
        dx_ref[rows:, :] = jnp.zeros_like(dx_ref[rows:, :])
        dx_ref[rows:, :rows] = lines.astype(dx_ref.dtype)


def expert_block(at, count, x, dy, wgu, wd, earlier):
    rows, width = dy.shape
    hidden = wd.shape[0]
    tile = FF_TILE
    whole = jax.ShapeDtypeStruct((count * rows, hidden), jnp.bfloat16)
    fixed = lambda i, *_: (0, 0)
    out_block = pl.BlockSpec((rows, tile), lambda i, *_: (at, i))
    spec = pltpu.PrefetchScalarGridSpec(
        num_scalar_prefetch=1,
        grid=(hidden // tile,),
        in_specs=[
            pl.BlockSpec((rows + EXTRA, width), fixed),
            pl.BlockSpec((rows, width), fixed),
            pl.BlockSpec((width, tile), lambda i, *_: (0, i)),
            pl.BlockSpec((width, tile), lambda i, *_: (0, hidden // tile + i)),
            pl.BlockSpec((tile, width), lambda i, *_: (i, 0)),
        ]
        + [pl.BlockSpec(memory_space=pl.ANY)] * len(earlier),
        out_specs=[
            out_block,
            out_block,
            out_block,
            pl.BlockSpec((rows + EXTRA, width), fixed),
        ],
        scratch_shapes=[
            pltpu.VMEM((rows, LANES), jnp.float32),
            pltpu.VMEM((rows, width), jnp.float32),
            pltpu.VMEM((rows, LANES), jnp.float32),
        ],
    )
    return pl.pallas_call(
        expert_kernel,
        name="expert_block",
        out_shape=(
            whole,
            whole,
            whole,
            jax.ShapeDtypeStruct((rows + EXTRA, width), jnp.bfloat16),
        ),
        grid_spec=spec,
        input_output_aliases={6 + i: i for i in range(len(earlier))},
        compiler_params=pltpu.CompilerParams(dimension_semantics=("arbitrary",), vmem_limit_bytes=40 << 20),
        cost_estimate=pl.CostEstimate(
            flops=10 * rows * width * hidden, bytes_accessed=6 * width * hidden + 6 * rows * hidden, transcendentals=0
        ),
    )(jnp.zeros((1,), jnp.int32), x, dy, wgu, wgu, wd, *earlier)


EPS = 1e-06
FULL_PRECISION = lax.Precision.HIGHEST
ALL = ("z", "x", "exp")
SEQ = ("z", "x")
LOW = jnp.bfloat16


def dot32(a, b):
    return jnp.dot(a, b, preferred_element_type=jnp.float32)


def dot_nt(a, b):
    return lax.dot_general(a, b, NT, preferred_element_type=jnp.float32)


def dot_tn(a, b):
    return lax.dot_general(a, b, (((0,), (0,)), ((), ())), preferred_element_type=jnp.float32)


def partner(value, axis, offset):
    count = lax.axis_size(axis)
    return lax.ppermute(value, axis, [(i, i ^ offset) for i in range(count)])


def bits_of(count):
    return [1 << b for b in reversed(range(count.bit_length() - 1))]


def reorder(stacked, own):
    count = stacked.shape[0]
    return jnp.stack([lax.dynamic_index_in_dim(stacked, own ^ r, 0, keepdims=False) for r in range(count)])


def gather_double(value, steps):
    for axis, bit in steps:
        other = partner(value, axis, bit)
        high = (lax.axis_index(axis) & bit) != 0
        value = jnp.stack([jnp.where(high, other, value), jnp.where(high, value, other)])
    return value


def scatter_halve(value, steps):
    gone = []
    for axis, bit, dim in steps:
        at = dim - sum(1 for d in gone if d < dim)
        gone.append(dim)
        high = (lax.axis_index(axis) & bit) != 0
        low_half = lax.index_in_dim(value, 0, at, keepdims=False)
        high_half = lax.index_in_dim(value, 1, at, keepdims=False)
        keep = jnp.where(high, high_half, low_half)
        give = jnp.where(high, low_half, high_half)
        value = (keep.astype(jnp.float32) + partner(give, axis, bit).astype(jnp.float32)).astype(LOW)
    return value


def ring_of(groups, split):
    order = []
    for x in range(split):
        line = range(groups) if x % 2 == 0 else reversed(range(groups))
        order += [z * split + x for z in line]
    place = [order.index(s) for s in range(len(order))]
    ahead = [(order[i], order[(i + 1) % len(order)]) for i in range(len(order))]
    return jnp.asarray(order, jnp.int32), jnp.asarray(place, jnp.int32), ahead


def pick(values, index):
    return lax.dynamic_index_in_dim(values, index, 0, keepdims=False)


class RingGather:
    def __init__(self, piece, groups, split, own):
        self.order, place, self.ahead = ring_of(groups, split)
        self.count = groups * split
        self.here = pick(place, own)
        self.rows = piece.shape[0]
        self.whole = jnp.zeros((self.count * self.rows, piece.shape[1]), piece.dtype)
        self.whole = lax.dynamic_update_slice_in_dim(self.whole, piece, own * self.rows, 0)
        self.forward = self.backward = piece
        self.round = 0
        self.waiting = []

    def step(self):
        self.settle()
        self.round += 1
        k = self.round
        self.forward = lax.ppermute(self.forward, SEQ, self.ahead)
        self.waiting.append((self.forward, -k))
        if k < self.count - self.count // 2:
            self.backward = lax.ppermute(self.backward, SEQ, [(b, a) for a, b in self.ahead])
            self.waiting.append((self.backward, k))

    def settle(self):
        for piece, k in self.waiting:
            at = pick(self.order, (self.here + k + self.count) % self.count) * self.rows
            self.whole = lax.dynamic_update_slice_in_dim(self.whole, piece, at, 0)
        self.waiting = []

    def after(self, value):
        value, self.forward, self.backward = lax.optimization_barrier((value, self.forward, self.backward))
        self.waiting = [(self.forward if k < 0 else self.backward, k) for _, k in self.waiting]
        return value

    def finish(self):
        while self.round < self.count // 2:
            self.step()
        self.settle()
        return self.whole


class RingScatter:
    def __init__(self, totals, groups, split, own):
        self.order, place, self.ahead = ring_of(groups, split)
        self.count = groups * split
        self.here = pick(place, own)
        self.rows = totals[0].shape[0] // self.count
        self.totals = totals
        self.round = 0
        self.forward = self.backward = None

    def block(self, total, offset):
        at = pick(self.order, (self.here + offset + self.count) % self.count) * self.rows
        return lax.dynamic_slice_in_dim(total, at, self.rows, 0)

    def load(self, coming, offset):
        own = [self.block(total, offset) for total in self.totals]
        if coming is None:
            return own
        return [(a.astype(jnp.float32) + b.astype(jnp.float32)).astype(LOW) for a, b in zip(own, coming)]

    def step(self):
        self.round += 1
        k, far = self.round, self.count // 2
        near = self.count - 1 - far
        if k <= far:
            parts = self.load(self.forward, far - k + 1)
            self.forward = [lax.ppermute(part, SEQ, self.ahead) for part in parts]
        if k <= near:
            parts = self.load(self.backward, k - near - 1)
            self.backward = [lax.ppermute(part, SEQ, [(b, a) for a, b in self.ahead]) for part in parts]

    def after(self, value):
        value, self.forward, self.backward = lax.optimization_barrier((value, self.forward, self.backward))
        return value

    def finish(self):
        while self.round < self.count // 2:
            self.step()
        own = [self.block(total, 0).astype(jnp.float32) for total in self.totals]
        return [
            a + b.astype(jnp.float32) + c.astype(jnp.float32) for a, b, c in zip(own, self.forward, self.backward)
        ]


def norm_scale(value):
    return lax.rsqrt(jnp.mean(value * value, axis=-1, keepdims=True) + EPS)


def norm_back(scale, normed, gain, grad):
    scaled = grad * gain
    return scale * (scaled - normed * jnp.mean(scaled * normed, axis=-1, keepdims=True))


def split3(value):
    high = value.astype(LOW)
    rest = value - high.astype(jnp.float32)
    middle = rest.astype(LOW)
    return [high, middle, (rest - middle.astype(jnp.float32)).astype(LOW)]


def per_device(
    block_in,
    cotangent,
    segment_ids,
    expert_routes,
    pair_priority,
    gain_attention,
    w_query,
    w_key,
    w_value,
    w_out,
    bias_table,
    gain_experts,
    w_router,
    w_gate,
    w_up,
    w_down,
):
    groups, local_len, width = block_in.shape
    tokens = groups * local_len
    rows_own, hd = w_query.shape
    split = lax.axis_size("x")
    exp_count = lax.axis_size("exp")
    seq_count = groups * split
    length = local_len * seq_count
    x_at, z_at, e_at = lax.axis_index("x"), lax.axis_index("z"), lax.axis_index("exp")
    s_at = z_at * split + x_at
    head_width = hd // split
    heads_here = head_width // HEAD_DIM
    experts_all = w_router.shape[1]
    bias_own = bias_table.shape[0]
    tile = min(TILE, local_len)
    own = s_at.astype(jnp.int32).reshape(1)
    z_bits, x_bits, e_bits = bits_of(groups), bits_of(split), bits_of(exp_count)

    input_r = reorder(block_in, z_at)

    small = jnp.concatenate(
        [
            gain_attention[:, None],
            gain_experts[:, None],
            jnp.pad(bias_table, (0, rows_own - bias_own))[:, None],
            w_router,
        ],
        axis=1,
    )
    small = jnp.pad(small, ((0, 0), (0, LANES - small.shape[1]))).astype(LOW)
    share = jnp.stack(
        [part.astype(LOW).reshape(rows_own, split, head_width) for part in (w_query, w_key, w_value)], axis=2
    )
    share = share.reshape(rows_own, split, 3 * head_width).transpose(1, 0, 2)
    common = jnp.concatenate([w_out.astype(LOW), small], axis=1)
    share = jnp.concatenate([share, jnp.broadcast_to(common, (split,) + common.shape)], axis=2)
    shares = [lax.dynamic_index_in_dim(share, x_at ^ r, 0, keepdims=False) for r in range(split)]
    shares = [shares[0]] + [partner(shares[r], "x", r) for r in range(1, split)]
    by_x = reorder(jnp.stack(shares), x_at)
    packed = gather_double(by_x, [("z", b) for b in z_bits[:1]])

    packed, input_r = lax.optimization_barrier((packed, input_r))
    arrived = [[input_r[rz]] + [None] * (split - 1) for rz in range(groups)]
    for rz in reversed(range(1, groups)):
        arrived[rz][0] = partner(input_r[rz], "z", rz)
    for rx in range(1, split):
        arrived[0][rx] = partner(arrived[0][0], "x", rx)
    packed = gather_double(packed, [("z", b) for b in z_bits[1:]] + [("exp", b) for b in e_bits[:-1]])
    near = [arrived[rz][0] for rz in range(1, groups)]
    packed, near = lax.optimization_barrier((packed, near))
    for rz in range(1, groups):
        arrived[rz][0] = near[rz - 1]
        for rx in range(1, split):
            arrived[rz][rx] = partner(arrived[rz][0], "x", rx)
    sequence = jnp.stack([block for line in arrived for block in line]).reshape(length, width)

    gate_up_own = jnp.concatenate([w_gate[0].astype(LOW), w_up[0].astype(LOW)], axis=1)
    sequence, gate_up_own, down_own = lax.optimization_barrier((sequence, gate_up_own, w_down[0].astype(LOW)))
    down_w = lax.all_gather(down_own, SEQ, axis=0, tiled=True)
    gate_up_ring = RingGather(gate_up_own, groups, split, s_at)
    gate_up_ring.step()
    packed = gather_double(packed, [("exp", b) for b in e_bits[-1:]])
    ne, nz, nx = len(e_bits), len(z_bits), len(x_bits)
    packed = packed.transpose(
        tuple(ne + i for i in reversed(range(nz))) + (ne + nz,) + tuple(reversed(range(ne))) + (ne + nz + 1, ne + nz + 2)
    ).reshape(width, 3 * head_width + width + LANES)
    qkv_w, small_all = packed[:, : 3 * head_width], packed[:, 3 * head_width + width :]
    out_w = packed[:, 3 * head_width : 3 * head_width + width]
    gain_one = small_all[:, 0].astype(jnp.float32)
    gain_two = small_all[:, 1].astype(jnp.float32)
    table_all = small_all[:, 2].reshape(-1, rows_own)[:, :bias_own].reshape(-1, BUCKETS)
    router_t = small_all[:, 3 : 3 + experts_all].T
    table_rows = lax.dynamic_slice_in_dim(table_all, x_at * heads_here, heads_here, 0)

    routes = expert_routes.reshape(tokens, -1)
    top_count = routes.shape[1]
    priority = pair_priority.reshape(-1)
    pair_experts = routes.reshape(-1)
    ahead = (pair_experts[None, :] == pair_experts[:, None]) & (priority[None, :] < priority[:, None])
    slots = jnp.sum(ahead.astype(jnp.int32), axis=1)
    capacity = (5 * top_count * tokens + 4 * experts_all - 1) // (4 * experts_all)
    slot_count = experts_all * capacity
    slot_index = jnp.where(slots < capacity, (pair_experts ^ e_at) * capacity + slots, slot_count)
    slot_index = slot_index.reshape(tokens, top_count)
    every_slot = jnp.arange(slot_count, dtype=jnp.int32)[None, :]
    table = sum((slot_index[:, k : k + 1] == every_slot).astype(LOW) for k in range(top_count))
    tables = [table[:, r * capacity : (r + 1) * capacity] for r in range(exp_count)]
    grad_low = cotangent.reshape(tokens, width)
    grad_slots = [dot_tn(part, grad_low).astype(LOW) for part in tables]

    wide = sequence.astype(jnp.float32)
    normed_one = (wide * norm_scale(wide) * gain_one).astype(LOW)
    qkv = dot32(normed_one, qkv_w).astype(LOW)
    qkv, grad_slots = lax.optimization_barrier((qkv, grad_slots))
    qkv = gate_up_ring.after(qkv)
    gate_up_ring.step()
    grad_slots = [grad_slots[0]] + [partner(grad_slots[r], "exp", r) for r in range(1, exp_count)]
    segments = lax.dynamic_index_in_dim(segment_ids, z_at, 0, keepdims=False)
    ranges = tile_ranges(segments, tile)
    seg_blocks = segments.reshape(seq_count, local_len)
    query_side, key_side = segment_columns(reorder(seg_blocks, s_at).reshape(length))
    rows = bias_rows(table_rows, tile)
    ends = jnp.stack([table_rows[:, 15], table_rows[:, 31]], axis=1).astype(jnp.float32)
    contexts, log_totals = attend_forward(qkv, query_side, key_side, ranges, rows, ends, own, tile)
    contexts = gate_up_ring.after(contexts)
    contexts, grad_slots = lax.optimization_barrier((contexts, grad_slots))
    gate_up_w = gate_up_ring.finish()

    def exchange_positions(blocks):
        return lax.all_to_all(blocks, SEQ, split_axis=0, concat_axis=0, tiled=True)

    context_local = exchange_positions(contexts.reshape(seq_count, local_len, head_width))
    context_local = (
        context_local.reshape(groups, split, local_len, head_width).transpose(0, 2, 1, 3).reshape(tokens, hd)
    )
    inputs = block_in.astype(jnp.float32).reshape(tokens, width)
    mid = inputs + dot32(context_local, out_w)
    scale_two = norm_scale(mid)
    normed_two = (mid * scale_two * gain_two).astype(LOW)

    logits = dot_nt(router_t, normed_two)
    exponent = jnp.exp(logits - jnp.max(logits, axis=0, keepdims=True))
    probabilities = exponent / jnp.sum(exponent, axis=0, keepdims=True)
    expert_ids = jnp.arange(experts_all, dtype=jnp.int32)[:, None]
    chosen = sum((routes[:, k][None, :] == expert_ids).astype(jnp.float32) for k in range(top_count))
    chosen_total = jnp.sum(probabilities * chosen, axis=0, keepdims=True)
    gates = probabilities * chosen / chosen_total
    gates_r = reorder(gates, e_at)

    gate_slots = jnp.sum(
        table.astype(jnp.float32).reshape(tokens, exp_count, capacity) * gates_r.T[:, :, None], axis=0
    )
    gate_lines = jnp.pad(jnp.stack(split3(gate_slots), axis=1), ((0, 0), (0, EXTRA - 3), (0, width - capacity)))

    def values_below(rows_):
        return jnp.sum(rows_[capacity : capacity + 3, :capacity].astype(jnp.float32), axis=0)

    sent = [None] * exp_count
    for r in reversed(range(exp_count)):
        sent[r] = jnp.concatenate([dot_tn(tables[r], normed_two).astype(LOW), gate_lines[r]], axis=0)
        if r:
            sent[r] = partner(sent[r], "exp", r)

    earlier = ()
    back = [None] * exp_count
    turns = [0] + list(range(2, exp_count)) + [1]
    for turn, r in enumerate(turns):
        if turn >= 3:
            ready = turns[turn - 2]
            sent[r], back[ready] = lax.optimization_barrier((sent[r], back[ready]))
        hidden, gate_low, up_low, dx = expert_block(
            r, exp_count, sent[r], grad_slots[r], gate_up_w, down_w, earlier
        )
        earlier = (hidden, gate_low, up_low)
        back[r] = partner(dx, "exp", r) if r else dx

    sent, hidden = lax.optimization_barrier((sent, hidden))
    slot_rows = jnp.concatenate([rows_[:capacity] for rows_ in sent], axis=0)
    slot_gates = jnp.concatenate([values_below(rows_) for rows_ in sent], axis=0)[:, None]
    slot_grads = (slot_gates * jnp.concatenate(grad_slots, axis=0).astype(jnp.float32)).astype(LOW)

    gate_grad = jnp.sum(
        table.astype(jnp.float32).reshape(tokens, exp_count, capacity) * jnp.stack([values_below(rows_) for rows_ in back])[None], axis=2
    )
    gate_grad = reorder(gate_grad.T, e_at)
    chosen_grad = chosen * (gate_grad - jnp.sum(gates * gate_grad, axis=0, keepdims=True)) / chosen_total
    logit_grad = probabilities * (chosen_grad - jnp.sum(probabilities * chosen_grad, axis=0, keepdims=True))
    logit_pieces = jnp.concatenate(split3(logit_grad), axis=0)
    router_sum = jnp.sum(dot32(logit_pieces, normed_two).reshape(3, experts_all, width), axis=0)
    normed_two_grad = dot_tn(logit_pieces, jnp.concatenate([router_t] * 3, axis=0))
    for r in range(exp_count):
        normed_two_grad = normed_two_grad + dot32(tables[r], back[r][:capacity])
    unit_two = mid * scale_two
    gain_two_sum = jnp.sum(normed_two_grad * unit_two, axis=0)
    grad_out = grad_low.astype(jnp.float32)
    mid_grad = grad_out + norm_back(scale_two, unit_two, gain_two, normed_two_grad)
    attention_grad = mid_grad.astype(LOW)
    context_grad = dot_nt(attention_grad, out_w).astype(LOW)
    context_grad, up_low, gate_low, hidden = lax.optimization_barrier((context_grad, up_low, gate_low, hidden))
    down_sum = dot_tn(hidden, slot_grads).astype(LOW)
    gate_sum = dot_tn(slot_rows, gate_low).astype(LOW)
    up_sum = dot_tn(slot_rows, up_low).astype(LOW)
    context_grad = (
        context_grad.reshape(groups, local_len, split, head_width)
        .transpose(0, 2, 1, 3)
        .reshape(seq_count, local_len, head_width)
    )
    context_heads = exchange_positions(context_grad).reshape(length, head_width)

    def scatter_experts(total):
        return lax.psum_scatter(total, SEQ, scatter_dimension=0, tiled=True)

    context_heads, gate_sum, up_sum, down_sum = lax.optimization_barrier(
        (context_heads, gate_sum, up_sum, down_sum)
    )
    down_owned = scatter_experts(down_sum)

    halving = [("exp", b, 1 + nz + nx + ne - 1 - i) for i, b in enumerate(reversed(e_bits))]
    halving += [("z", b, 1 + nz - 1 - i) for i, b in enumerate(reversed(z_bits))]
    out_sum = dot_tn(context_local, attention_grad).astype(LOW)

    ring = RingScatter([gate_sum, up_sum], groups, split, s_at)
    grads, diag, far = (), [], []
    pairs = head_width // LANES
    for pair in range(pairs):
        ring.step()
        *grads, pair_diag, pair_far = attend_backward(
            pair, qkv, context_heads, contexts, log_totals, query_side, key_side, ranges, rows, ends, own, tile, tuple(grads)
        )
        grads = ring.after(grads)
        diag.append(pair_diag)
        far.append(pair_far)
    diag, far = jnp.concatenate(diag), jnp.concatenate(far)
    query_back, key_back, value_back, down_owned = lax.optimization_barrier((*grads, down_owned))
    gate_owned, up_owned = ring.finish()
    table_local = bucket_sums(diag, far, tile)

    def through(grads, part):
        return dot_nt(grads, qkv_w[:, part * head_width : (part + 1) * head_width])

    out_parts = width // head_width
    weight_sum = jnp.stack(
        [dot_tn(normed_one, grads).astype(LOW) for grads in (query_back, key_back, value_back)]
        + [out_sum[:, i * head_width : (i + 1) * head_width] for i in range(out_parts)]
    )
    weight_sum, query_back, key_back, value_back = lax.optimization_barrier(
        (weight_sum, query_back, key_back, value_back)
    )
    normed_part = through(query_back, 0) + through(key_back, 1) + through(value_back, 2)
    half = width // 2
    normed_part = normed_part.reshape(groups, split, local_len, width)

    sides = [normed_part[:, rx].astype(LOW) for rx in range(1, split)]
    first = [partner(side[:, :, :half], "x", rx) for rx, side in enumerate(sides, 1)]
    first, hidden, rest = lax.optimization_barrier((first, hidden, [side[:, :, half:] for side in sides]))

    def send_back(own_part, coming):
        total = own_part + sum(part.astype(jnp.float32) for part in coming)
        total = reorder(total.astype(LOW), z_at)
        return lax.all_to_all(total, "z", split_axis=0, concat_axis=0, tiled=True)

    normed_first = send_back(normed_part[:, 0, :, :half], first)
    rest = [partner(side, "x", rx) for rx, side in enumerate(rest, 1)]
    normed_second = send_back(normed_part[:, 0, :, half:], rest)
    expert_out = (slot_gates * dot32(hidden, down_w)).astype(LOW)
    weight_part = scatter_halve(
        weight_sum.reshape((3 + out_parts,) + (2,) * (nz + nx + ne) + (rows_own, head_width)), halving[:ne]
    )
    weight_part, expert_out = lax.optimization_barrier((weight_part, expert_out))
    weight_part = scatter_halve(weight_part, halving[ne:]).reshape(3 + out_parts, split, rows_own, head_width)
    weight_own = [lax.dynamic_index_in_dim(weight_part, x_at ^ r, 1, keepdims=False) for r in range(split)]
    weight_own = [weight_own[0]] + [partner(weight_own[r], "x", r) for r in range(1, split)]
    returned = [expert_out[:capacity]] + [
        partner(expert_out[r * capacity : (r + 1) * capacity], "exp", r) for r in range(1, exp_count)
    ]
    normed_second, returned, weight_own = lax.optimization_barrier((normed_second, returned, weight_own))
    block_out = (mid + dot32(table, jnp.concatenate(returned, axis=0))).astype(LOW)

    block_out = block_out.reshape(groups, local_len, width)
    out_w_out = sum(part[3:].astype(jnp.float32) for part in weight_own)
    out_w_out = out_w_out.transpose(1, 0, 2).reshape(rows_own, width)
    qkv_own = reorder(jnp.stack([part[:3] for part in weight_own]), x_at)
    qkv_own = qkv_own.transpose(1, 2, 0, 3).reshape(3, rows_own, hd).astype(jnp.float32)

    normed_one_grad = jnp.concatenate([normed_first, normed_second], axis=2).astype(jnp.float32).reshape(tokens, width)
    scale_one = norm_scale(inputs)
    unit_one = inputs * scale_one
    gain_one_sum = jnp.sum(normed_one_grad * unit_one, axis=0)
    block_in_grad = (mid_grad + norm_back(scale_one, unit_one, gain_one, normed_one_grad)).reshape(
        groups, local_len, width
    )

    table_sum = lax.dynamic_update_slice_in_dim(
        jnp.zeros(table_all.shape, jnp.float32), table_local, x_at * heads_here, 0
    ).reshape(-1, bias_own)
    table_sum = jnp.pad(table_sum, ((0, 0), (0, rows_own - bias_own)))[:, None, :]
    little = jnp.concatenate(
        [
            gain_one_sum.reshape(-1, 1, rows_own),
            gain_two_sum.reshape(-1, 1, rows_own),
            table_sum,
            router_sum.reshape(experts_all, -1, rows_own).transpose(1, 0, 2),
        ],
        axis=1,
    )
    little = jnp.sum(lax.all_to_all(little, ALL, split_axis=0, concat_axis=0, tiled=True), axis=0)
    return (
        block_out,
        block_in_grad,
        little[0],
        qkv_own[0],
        qkv_own[1],
        qkv_own[2],
        out_w_out,
        little[2, :bias_own],
        little[1],
        little[3:].T,
        gate_owned.astype(jnp.float32)[None],
        up_owned.astype(jnp.float32)[None],
        down_owned.astype(jnp.float32)[None],
    )


def solution(mesh):
    def run(*args):
        groups = args[0].shape[0] // mesh.shape["exp"]
        seq_count, exp_count = mesh.shape["seq"], mesh.shape["exp"]
        grid = mesh.devices.reshape(groups, seq_count // groups, exp_count)
        fine = jax.sharding.Mesh(grid, ALL)
        placed = P("exp", SEQ, None)
        whole = P(ALL)
        matrix = P(ALL, None)
        return jax.shard_map(
            per_device,
            mesh=fine,
            in_specs=(
                placed, placed, P("exp", None), placed, placed,
                whole, matrix, matrix, matrix, matrix, whole, whole, matrix,
                placed, placed, placed,
            ),
            out_specs=(
                placed, placed, whole, matrix, matrix, matrix, matrix, whole, whole, matrix,
                placed, placed, placed,
            ),
            check_vma=False,
        )(*args)

    return run
```

```python
from functools import partial

import jax
import jax.numpy as jnp
import numpy as np
from jax import lax
from jax.experimental import pallas as pl
from jax.experimental.pallas import tpu as pltpu
from jax.sharding import PartitionSpec as P

HEAD_DIM = 64
BUCKETS = 32
THRESHOLDS = (12, 16, 23, 32, 46, 64, 91)
MASKED = -1e30
TILE = 256
LANES = 128
NT = (((1,), (1,)), ((), ()))


def bucket_of(d):
    a = np.abs(d)
    extra = sum((a >= t).astype(np.int64) for t in THRESHOLDS)
    return np.where(a < 8, a, 8 + extra) + 16 * (d > 0)


def bias_rows(table_rows, tile):
    u = np.arange(2 * tile)
    x = np.where(u < tile, u, u - 2 * tile)
    ids = np.stack([bucket_of(step * tile - x) for step in (-1, 0, 1)])
    hot = (ids.reshape(-1)[None, :] == np.arange(BUCKETS)[:, None]).astype(np.float32)
    rows = jnp.dot(table_rows.astype(jnp.bfloat16), jnp.asarray(hot, jnp.bfloat16), preferred_element_type=jnp.float32)
    return rows.reshape(table_rows.shape[0], 3, 2 * tile)


def tile_ranges(segments, tile):
    blocks = segments.reshape(-1, tile)
    first, last = blocks[:, 0], blocks[:, -1]
    low = jnp.sum((last[None, :] < first[:, None]).astype(jnp.int32), axis=1)
    high = jnp.sum((first[None, :] <= last[:, None]).astype(jnp.int32), axis=1)
    return jnp.stack([low, high])


def segment_columns(segments):
    lane = jnp.arange(LANES, dtype=jnp.int32)[None, :]
    seg = segments[:, None]
    same = seg == lane
    query_side = jnp.where(same & (lane < 4), MASKED, 0.0).astype(jnp.bfloat16)
    key_side = jnp.where(lane < 4, (~same).astype(jnp.float32), (lane < 9).astype(jnp.float32)).astype(jnp.bfloat16)
    return query_side, key_side


def toeplitz(row, tile):
    wide = jnp.broadcast_to(row, (tile, row.shape[1]))
    return pltpu.roll(wide, 0, 1, stride=1, stride_axis=0)[:, :tile]


def block_at(index, own, tile):
    return pl.ds(pl.multiple_of((index ^ own[0]) * tile, tile), tile)


def fwd_kernel(ranges, ends, own, q_ref, k_ref, v_ref, qs_ref, ks_ref, rows_ref, o_ref, lse_ref, bias_ref, vt_ref):
    group, qb = pl.program_id(0), pl.program_id(1)
    tile, span = q_ref.shape
    heads = span // HEAD_DIM

    @pl.when(qb == 0)
    def _():
        for h in range(heads):
            for step in range(3):
                bias_ref[h, step] = toeplitz(rows_ref[h, step : step + 1, :], tile)
        for start in range(0, v_ref.shape[0], tile):
            vt_ref[:, start : start + tile] = v_ref[start : start + tile, :].T

    low, high = ranges[0, qb], ranges[1, qb]
    lane = lax.broadcasted_iota(jnp.int32, (tile, LANES), 1)
    q = q_ref[...] * jnp.bfloat16(HEAD_DIM**-0.5)
    qs = qs_ref[...]
    halves = []
    for h in range(heads):
        part = q[:, h // 2 * LANES : (h // 2 + 1) * LANES]
        keep = (lane < HEAD_DIM) if h % 2 == 0 else (lane >= HEAD_DIM)
        halves.append(jnp.where(keep, part, jnp.zeros_like(part)))

    def side(h, which):
        if which == 1:
            extra = qs
        else:
            value = ends[heads * group + h, which // 2].astype(jnp.bfloat16)
            extra = jnp.where(lane == 7, value, qs)
        return jnp.concatenate([halves[h], extra], axis=1)

    def visit(which):
        queries = [side(h, which) for h in range(heads)]

        def step(kb, carry):
            keys = block_at(kb, own, tile)
            ks = ks_ref[keys, :]
            scores = []
            for h in range(heads):
                kx = jnp.concatenate([k_ref[keys, h // 2 * LANES : (h // 2 + 1) * LANES], ks], axis=1)
                scores.append(lax.dot_general(kx, queries[h], NT, preferred_element_type=jnp.float32))
            out = []
            for h in range(heads):
                peak, total, acc = carry[h]
                s = scores[h]
                if which == 1:
                    s = s + bias_ref[h, kb - qb + 1]
                new = jnp.maximum(peak, jnp.max(s, axis=0, keepdims=True))
                p = jnp.exp(s - new)
                scale = jnp.exp(peak - new)
                total = total * scale + jnp.sum(p, axis=0, keepdims=True)
                vt = vt_ref[h * HEAD_DIM : (h + 1) * HEAD_DIM, keys]
                acc = acc * scale + jnp.dot(vt, p.astype(jnp.bfloat16), preferred_element_type=jnp.float32)
                out.append((new, total, acc))
            return tuple(out)

        return step

    start = tuple(
        (
            jnp.full((1, tile), -3e38, jnp.float32),
            jnp.zeros((1, tile), jnp.float32),
            jnp.zeros((HEAD_DIM, tile), jnp.float32),
        )
        for _ in range(heads)
    )
    near_low, near_high = jnp.maximum(low, qb - 1), jnp.minimum(high, qb + 2)
    state = lax.fori_loop(near_low, near_high, visit(1), start)
    state = lax.fori_loop(low, near_low, visit(0), state)
    state = lax.fori_loop(near_high, high, visit(2), state)
    outs = []
    for h in range(heads):
        peak, total, acc = state[h]
        outs.append(acc / total)
        lse_ref[h // 2, h % 2 : h % 2 + 1, :] = peak + jnp.log(total)
    o_ref[...] = jnp.concatenate(outs, axis=0).T.astype(o_ref.dtype)


FWD_PAIRS = 4


def attend_forward(qkv, qs, ks, ranges, rows, ends, own, tile):
    length, width = qkv.shape[0], qkv.shape[1] // 3
    pairs = width // LANES
    together = FWD_PAIRS if pairs % FWD_PAIRS == 0 else 1
    span = together * LANES
    tiles = length // tile
    spec = pltpu.PrefetchScalarGridSpec(
        num_scalar_prefetch=3,
        grid=(pairs // together, tiles),
        in_specs=[
            pl.BlockSpec((tile, span), lambda p, i, r, e, own: (i ^ own[0], p)),
            pl.BlockSpec((length, span), lambda p, i, *_: (0, width // span + p)),
            pl.BlockSpec((length, span), lambda p, i, *_: (0, 2 * (width // span) + p)),
            pl.BlockSpec((tile, LANES), lambda p, i, r, e, own: (i ^ own[0], 0)),
            pl.BlockSpec((length, LANES), lambda p, i, *_: (0, 0)),
            pl.BlockSpec((2 * together, 3, 2 * tile), lambda p, i, *_: (p, 0, 0)),
        ],
        out_specs=[
            pl.BlockSpec((tile, span), lambda p, i, *_: (i, p)),
            pl.BlockSpec((together, 2, tile), lambda p, i, *_: (p, 0, i)),
        ],
        scratch_shapes=[
            pltpu.VMEM((2 * together, 3, tile, tile), jnp.float32),
            pltpu.VMEM((span, length), jnp.bfloat16),
        ],
    )
    return pl.pallas_call(
        fwd_kernel,
        name="attend_forward",
        out_shape=(
            jax.ShapeDtypeStruct((length, width), jnp.bfloat16),
            jax.ShapeDtypeStruct((pairs, 2, length), jnp.float32),
        ),
        grid_spec=spec,
        compiler_params=pltpu.CompilerParams(
            dimension_semantics=("arbitrary", "arbitrary"), vmem_limit_bytes=48 << 20
        ),
        cost_estimate=pl.CostEstimate(flops=length * length * width * 4, bytes_accessed=length * width * 8, transcendentals=0),
    )(ranges, ends, own, qkv, qkv, qkv, qs, ks, rows)


def pieces(row):
    high = row.astype(jnp.bfloat16).astype(jnp.float32)
    mid = (row - high).astype(jnp.bfloat16).astype(jnp.float32)
    return high, mid, row - high - mid


def bwd_kernel(ranges, ends, own, q_ref, k_ref, v_ref, do_ref, o_ref, lse_ref, qs_ref, ks_ref, rows_ref, *refs):
    (dq_ref, dk_ref, dv_ref, diag_ref, far_ref,
     qx_ref, dox_ref, kt_ref, bias_ref, dsum_ref, fsum_ref, dqt_ref, dka_ref, dva_ref) = refs[-14:]
    pair = own[1]
    length = q_ref.shape[0]
    tile = bias_ref.shape[2]
    tiles = length // tile
    for h in range(2):
        for step in range(3):
            bias_ref[h, step] = toeplitz(rows_ref[h, step : step + 1, :], tile)
    dsum_ref[...] = jnp.zeros_like(dsum_ref)
    fsum_ref[...] = jnp.zeros_like(fsum_ref)
    dqt_ref[...] = jnp.zeros_like(dqt_ref)
    lane = lax.broadcasted_iota(jnp.int32, (tile, LANES), 1)
    sub = lax.broadcasted_iota(jnp.int32, (LANES, tile), 0)
    pick = (lax.broadcasted_iota(jnp.int32, (8, LANES), 1) // HEAD_DIM == lax.broadcasted_iota(jnp.int32, (8, LANES), 0)).astype(jnp.float32)

    @pl.loop(0, tiles)
    def _(i):
        line = pl.ds(pl.multiple_of(i * tile, tile), tile)
        at = block_at(i, own, tile)
        q = q_ref[at, :] * jnp.bfloat16(HEAD_DIM**-0.5)
        do = do_ref[line, :]
        zero = jnp.zeros_like(q)
        product = do.astype(jnp.float32) * o_ref[line, :].astype(jnp.float32)
        delta = lax.dot_general(pick, product, NT, precision=lax.Precision.HIGHEST, preferred_element_type=jnp.float32)
        kt_ref[:, at] = k_ref[at, :].T
        for h in range(2):
            keep = (lane < HEAD_DIM) if h == 0 else (lane >= HEAD_DIM)
            a, b, c = pieces(-lse_ref[0, h : h + 1, line])
            extra = jnp.where(sub == 4, a, jnp.where(sub == 5, b, jnp.where(sub == 6, c, 0.0)))
            extra = extra.T.astype(jnp.bfloat16) + qs_ref[at, :]
            left, right = ends[2 * pair + h, 0].astype(jnp.bfloat16), ends[2 * pair + h, 1].astype(jnp.bfloat16)
            extra = jnp.where(lane == 7, left, jnp.where(lane == 8, right, extra))
            qx_ref[h, at, :] = jnp.concatenate([jnp.where(keep, q, zero), extra], axis=1)
            a, b, c = pieces(-delta[h : h + 1, :])
            extra = jnp.where(sub == 4, a, jnp.where(sub == 5, b, jnp.where(sub == 6, c, 0.0)))
            dox_ref[h, at, :] = jnp.concatenate([jnp.where(keep, do, zero), extra.T.astype(jnp.bfloat16)], axis=1)

    ones3 = ((lane >= 4) & (lane < 7)).astype(jnp.bfloat16)

    @pl.loop(0, tiles)
    def _(kb):
        low, high = ranges[0, kb], ranges[1, kb]
        keys = block_at(kb, own, tile)
        k, ks = k_ref[keys, :], ks_ref[keys, :]
        vx = jnp.concatenate([v_ref[keys, :], ones3], axis=1)
        nil = jnp.zeros_like(ks)
        dka_ref[...] = jnp.zeros_like(dka_ref)
        dva_ref[...] = jnp.zeros_like(dva_ref)

        def visit(which):
            if which == 0:
                extra = jnp.where(lane == 8, nil, ks)
            elif which == 2:
                extra = jnp.where(lane == 7, nil, ks)
            else:
                extra = jnp.where((lane == 7) | (lane == 8), nil, ks)
            kx = jnp.concatenate([k, extra], axis=1)

            def step(qb, carry):
                at = block_at(qb, own, tile)
                weights, grads = [], []
                for h in range(2):
                    qx, dox = qx_ref[h, at, :], dox_ref[h, at, :]
                    s = lax.dot_general(kx, qx, NT, preferred_element_type=jnp.float32)
                    if which == 1:
                        s = s + bias_ref[h, kb - qb + 1]
                    p = jnp.exp(s)
                    dp = lax.dot_general(vx, dox, NT, preferred_element_type=jnp.float32)
                    ds = p * dp
                    if which == 1:
                        dsum_ref[h, kb - qb + 1] += ds
                    else:
                        fsum_ref[h, which // 2] += jnp.sum(ds.reshape(tile // 8, 8, tile), axis=0)
                    weights.append(p.astype(jnp.bfloat16))
                    grads.append(ds.astype(jnp.bfloat16))
                    rows = slice(h * HEAD_DIM, (h + 1) * HEAD_DIM)
                    dqt_ref[rows, at] += jnp.dot(kt_ref[rows, keys], grads[h], preferred_element_type=jnp.float32)
                both_do = jnp.concatenate([dox_ref[0, at, :LANES], dox_ref[1, at, :LANES]], axis=0)
                both_q = jnp.concatenate([qx_ref[0, at, :LANES], qx_ref[1, at, :LANES]], axis=0)
                dva_ref[...] += jnp.dot(jnp.concatenate(weights, axis=1), both_do, preferred_element_type=jnp.float32)
                dka_ref[...] += jnp.dot(jnp.concatenate(grads, axis=1), both_q, preferred_element_type=jnp.float32)
                return carry

            return step

        near_low, near_high = jnp.maximum(low, kb - 1), jnp.minimum(high, kb + 2)
        lax.fori_loop(near_low, near_high, visit(1), 0)
        lax.fori_loop(near_high, high, visit(0), 0)
        lax.fori_loop(low, near_low, visit(2), 0)
        dk_ref[keys, :] = dka_ref[...].astype(dk_ref.dtype)
        dv_ref[keys, :] = dva_ref[...].astype(dv_ref.dtype)

    @pl.loop(0, tiles)
    def _(i):
        at = pl.ds(pl.multiple_of(i * tile, tile), tile)
        dq_ref[at, :] = (dqt_ref[:, at] * HEAD_DIM**-0.5).T.astype(dq_ref.dtype)

    for h in range(2):
        for step in range(3):
            diag_ref[h, step : step + 1, :] = diagonals(dsum_ref, h, step, tile)
        for step in range(2):
            total = jnp.sum(fsum_ref[h, step], axis=0, keepdims=True)
            far_ref[h, step : step + 1, :] = total


def diagonals(dsum_ref, h, step, tile):
    width = 2 * tile
    acc = jnp.zeros((8, width), jnp.float32)
    for group in range(tile // 8):
        part = dsum_ref[h, step, group * 8 : (group + 1) * 8, :]
        part = jnp.concatenate([part, jnp.zeros((8, tile), jnp.float32)], axis=1)
        acc = acc + (pltpu.roll(part, width - 8 * group, 1) if group else part)
    row = lax.broadcasted_iota(jnp.int32, (8, width), 0)
    for bit in (1, 2, 4):
        acc = jnp.where((row & bit) != 0, pltpu.roll(acc, width - bit, 1), acc)
    return jnp.sum(acc, axis=0, keepdims=True)


def attend_backward(pair, qkv, do, o, lse, qs, ks, ranges, rows, ends, own, tile, earlier):
    length, width = do.shape
    pairs = width // LANES
    own = jnp.concatenate([own, jnp.full((1,), pair, jnp.int32)])
    column = pl.BlockSpec((length, LANES), lambda p, r, e, own: (0, own[1]))
    fixed = pl.BlockSpec((length, LANES), lambda p, *_: (0, 0))
    spec = pltpu.PrefetchScalarGridSpec(
        num_scalar_prefetch=3,
        grid=(1,),
        in_specs=[
            column,
            pl.BlockSpec((length, LANES), lambda p, r, e, own: (0, pairs + own[1])),
            pl.BlockSpec((length, LANES), lambda p, r, e, own: (0, 2 * pairs + own[1])),
            column,
            column,
            pl.BlockSpec((1, 2, length), lambda p, r, e, own: (own[1], 0, 0)),
            fixed, fixed,
            pl.BlockSpec((2, 3, 2 * tile), lambda p, r, e, own: (own[1], 0, 0)),
        ]
        + [pl.BlockSpec(memory_space=pl.ANY)] * len(earlier),
        out_specs=[
            column, column, column,
            pl.BlockSpec((2, 3, 2 * tile), lambda p, *_: (p, 0, 0)),
            pl.BlockSpec((2, 2, tile), lambda p, *_: (p, 0, 0)),
        ],
        scratch_shapes=[
            pltpu.VMEM((2, length, 2 * LANES), jnp.bfloat16),
            pltpu.VMEM((2, length, 2 * LANES), jnp.bfloat16),
            pltpu.VMEM((LANES, length), jnp.bfloat16),
            pltpu.VMEM((2, 3, tile, tile), jnp.float32),
            pltpu.VMEM((2, 3, tile, tile), jnp.float32),
            pltpu.VMEM((2, 2, 8, tile), jnp.float32),
            pltpu.VMEM((LANES, length), jnp.float32),
            pltpu.VMEM((tile, LANES), jnp.float32),
            pltpu.VMEM((tile, LANES), jnp.float32),
        ],
    )
    low = jax.ShapeDtypeStruct((length, width), jnp.bfloat16)
    return pl.pallas_call(
        bwd_kernel,
        name="attend_backward",
        out_shape=(
            low, low, low,
            jax.ShapeDtypeStruct((2, 3, 2 * tile), jnp.float32),
            jax.ShapeDtypeStruct((2, 2, tile), jnp.float32),
        ),
        grid_spec=spec,
        input_output_aliases={12 + i: i for i in range(len(earlier))},
        compiler_params=pltpu.CompilerParams(
            dimension_semantics=("arbitrary",), vmem_limit_bytes=40 << 20
        ),
        cost_estimate=pl.CostEstimate(flops=length * length * LANES * 10, bytes_accessed=length * LANES * 16, transcendentals=0),
    )(ranges, ends, own, qkv, qkv, qkv, do, o, lse, qs, ks, rows, *earlier)


def bucket_sums(diag, far, tile):
    u = np.arange(2 * tile)
    x = np.where(u < tile, u, u - 2 * tile)
    ids = np.stack([bucket_of(step * tile - x) for step in (-1, 0, 1)])
    hot = (ids.reshape(-1)[:, None] == np.arange(BUCKETS)[None, :]).astype(np.float32)
    sums = jnp.dot(diag.reshape(diag.shape[0], -1), jnp.asarray(hot), precision=lax.Precision.HIGHEST)
    outer = jnp.sum(far, axis=2)
    ends = np.zeros((2, BUCKETS), np.float32)
    ends[0, 15] = 1
    ends[1, 31] = 1
    return sums + outer[:, 0:1] * ends[0] + outer[:, 1:2] * ends[1]


GELU_A, GELU_B = 0.7978845608028654, 0.044715
FF_TILE = 256
EXTRA = 16


def expert_kernel(own_ref, x_ref, dy_ref, wg_ref, wu_ref, wd_ref, *refs):
    h_ref, dg_ref, du_ref, dx_ref, part_ref, acc_ref, gate_ref = refs[-7:]
    step = pl.program_id(0)
    rows = dy_ref.shape[0]
    chunk = rows // 2 if rows % 32 == 0 else rows

    @pl.when(step == 0)
    def _():
        acc_ref[...] = jnp.zeros_like(acc_ref)
        part_ref[...] = jnp.zeros_like(part_ref)
        lines = x_ref[rows:, :rows].astype(jnp.float32)
        gate = jnp.sum(lines, axis=0, keepdims=True)
        gate_ref[...] = jnp.broadcast_to(gate, (LANES, rows)).T

    wg, wu, wd = wg_ref[...], wu_ref[...], wd_ref[...]
    for start in range(0, rows, chunk):
        at = slice(start, start + chunk)
        x, dy = x_ref[at, :], dy_ref[at, :]
        g = jnp.dot(x, wg, preferred_element_type=jnp.float32)
        u = jnp.dot(x, wu, preferred_element_type=jnp.float32)
        raw = lax.dot_general(dy, wd, NT, preferred_element_type=jnp.float32)
        square = g * g
        half = 0.5 + 0.5 * jnp.tanh(g * (GELU_A + (GELU_A * GELU_B) * square))
        gelu = g * half
        slope = half + 2.0 * gelu * (1.0 - half) * (GELU_A + (3.0 * GELU_A * GELU_B) * square)
        h = gelu * u
        product = raw * h
        total = product[:, :LANES]
        for column in range(LANES, product.shape[1], LANES):
            total = total + product[:, column : column + LANES]
        part_ref[at, :] += total
        dh = raw * gate_ref[at, :1]
        du = (dh * gelu).astype(jnp.bfloat16)
        dg = (dh * u * slope).astype(jnp.bfloat16)
        h_ref[at, :] = h.astype(jnp.bfloat16)
        dg_ref[at, :] = dg
        du_ref[at, :] = du
        acc_ref[at, :] += lax.dot_general(dg, wg, NT, preferred_element_type=jnp.float32) + lax.dot_general(
            du, wu, NT, preferred_element_type=jnp.float32
        )

    @pl.when(step == pl.num_programs(0) - 1)
    def _():
        dx_ref[:rows, :] = acc_ref[...].astype(dx_ref.dtype)
        sums = jnp.sum(part_ref[...].T, axis=0, keepdims=True)
        high = sums.astype(jnp.bfloat16).astype(jnp.float32)
        middle = (sums - high).astype(jnp.bfloat16).astype(jnp.float32)
        line = lax.broadcasted_iota(jnp.int32, (EXTRA, rows), 0)
        lines = jnp.where(line == 0, high, jnp.where(line == 1, middle, jnp.where(line == 2, sums - high - middle, 0.0)))
        dx_ref[rows:, :] = jnp.zeros_like(dx_ref[rows:, :])
        dx_ref[rows:, :rows] = lines.astype(dx_ref.dtype)


def expert_block(at, count, x, dy, wgu, wd, earlier):
    rows, width = dy.shape
    hidden = wd.shape[0]
    tile = FF_TILE
    whole = jax.ShapeDtypeStruct((count * rows, hidden), jnp.bfloat16)
    fixed = lambda i, *_: (0, 0)
    out_block = pl.BlockSpec((rows, tile), lambda i, *_: (at, i))
    spec = pltpu.PrefetchScalarGridSpec(
        num_scalar_prefetch=1,
        grid=(hidden // tile,),
        in_specs=[
            pl.BlockSpec((rows + EXTRA, width), fixed),
            pl.BlockSpec((rows, width), fixed),
            pl.BlockSpec((width, tile), lambda i, *_: (0, i)),
            pl.BlockSpec((width, tile), lambda i, *_: (0, hidden // tile + i)),
            pl.BlockSpec((tile, width), lambda i, *_: (i, 0)),
        ]
        + [pl.BlockSpec(memory_space=pl.ANY)] * len(earlier),
        out_specs=[
            out_block,
            out_block,
            out_block,
            pl.BlockSpec((rows + EXTRA, width), fixed),
        ],
        scratch_shapes=[
            pltpu.VMEM((rows, LANES), jnp.float32),
            pltpu.VMEM((rows, width), jnp.float32),
            pltpu.VMEM((rows, LANES), jnp.float32),
        ],
    )
    return pl.pallas_call(
        expert_kernel,
        name="expert_block",
        out_shape=(
            whole,
            whole,
            whole,
            jax.ShapeDtypeStruct((rows + EXTRA, width), jnp.bfloat16),
        ),
        grid_spec=spec,
        input_output_aliases={6 + i: i for i in range(len(earlier))},
        compiler_params=pltpu.CompilerParams(dimension_semantics=("arbitrary",), vmem_limit_bytes=40 << 20),
        cost_estimate=pl.CostEstimate(
            flops=10 * rows * width * hidden, bytes_accessed=6 * width * hidden + 6 * rows * hidden, transcendentals=0
        ),
    )(jnp.zeros((1,), jnp.int32), x, dy, wgu, wgu, wd, *earlier)


EPS = 1e-06
FULL_PRECISION = lax.Precision.HIGHEST
ALL = ("z", "x", "exp")
SEQ = ("z", "x")
LOW = jnp.bfloat16


def dot32(a, b):
    return jnp.dot(a, b, preferred_element_type=jnp.float32)


def dot_nt(a, b):
    return lax.dot_general(a, b, NT, preferred_element_type=jnp.float32)


def dot_tn(a, b):
    return lax.dot_general(a, b, (((0,), (0,)), ((), ())), preferred_element_type=jnp.float32)


def partner(value, axis, offset):
    count = lax.axis_size(axis)
    return lax.ppermute(value, axis, [(i, i ^ offset) for i in range(count)])


def bits_of(count):
    return [1 << b for b in reversed(range(count.bit_length() - 1))]


def reorder(stacked, own):
    count = stacked.shape[0]
    return jnp.stack([lax.dynamic_index_in_dim(stacked, own ^ r, 0, keepdims=False) for r in range(count)])


def gather_double(value, steps):
    for axis, bit in steps:
        other = partner(value, axis, bit)
        high = (lax.axis_index(axis) & bit) != 0
        value = jnp.stack([jnp.where(high, other, value), jnp.where(high, value, other)])
    return value


def scatter_halve(value, steps):
    gone = []
    for axis, bit, dim in steps:
        at = dim - sum(1 for d in gone if d < dim)
        gone.append(dim)
        high = (lax.axis_index(axis) & bit) != 0
        low_half = lax.index_in_dim(value, 0, at, keepdims=False)
        high_half = lax.index_in_dim(value, 1, at, keepdims=False)
        keep = jnp.where(high, high_half, low_half)
        give = jnp.where(high, low_half, high_half)
        value = (keep.astype(jnp.float32) + partner(give, axis, bit).astype(jnp.float32)).astype(LOW)
    return value


def ring_of(groups, split):
    order = []
    for x in range(split):
        line = range(groups) if x % 2 == 0 else reversed(range(groups))
        order += [z * split + x for z in line]
    place = [order.index(s) for s in range(len(order))]
    ahead = [(order[i], order[(i + 1) % len(order)]) for i in range(len(order))]
    return jnp.asarray(order, jnp.int32), jnp.asarray(place, jnp.int32), ahead


def pick(values, index):
    return lax.dynamic_index_in_dim(values, index, 0, keepdims=False)


class RingGather:
    def __init__(self, piece, groups, split, own):
        self.order, place, self.ahead = ring_of(groups, split)
        self.count = groups * split
        self.here = pick(place, own)
        self.rows = piece.shape[0]
        self.whole = jnp.zeros((self.count * self.rows, piece.shape[1]), piece.dtype)
        self.whole = lax.dynamic_update_slice_in_dim(self.whole, piece, own * self.rows, 0)
        self.forward = self.backward = piece
        self.round = 0
        self.waiting = []

    def step(self):
        self.settle()
        self.round += 1
        k = self.round
        self.forward = lax.ppermute(self.forward, SEQ, self.ahead)
        self.waiting.append((self.forward, -k))
        if k < self.count - self.count // 2:
            self.backward = lax.ppermute(self.backward, SEQ, [(b, a) for a, b in self.ahead])
            self.waiting.append((self.backward, k))

    def settle(self):
        for piece, k in self.waiting:
            at = pick(self.order, (self.here + k + self.count) % self.count) * self.rows
            self.whole = lax.dynamic_update_slice_in_dim(self.whole, piece, at, 0)
        self.waiting = []

    def after(self, value):
        value, self.forward, self.backward = lax.optimization_barrier((value, self.forward, self.backward))
        self.waiting = [(self.forward if k < 0 else self.backward, k) for _, k in self.waiting]
        return value

    def finish(self):
        while self.round < self.count // 2:
            self.step()
        self.settle()
        return self.whole


class RingScatter:
    def __init__(self, totals, groups, split, own):
        self.order, place, self.ahead = ring_of(groups, split)
        self.count = groups * split
        self.here = pick(place, own)
        self.rows = totals[0].shape[0] // self.count
        self.totals = totals
        self.round = 0
        self.forward = self.backward = None

    def block(self, total, offset):
        at = pick(self.order, (self.here + offset + self.count) % self.count) * self.rows
        return lax.dynamic_slice_in_dim(total, at, self.rows, 0)

    def load(self, coming, offset):
        own = [self.block(total, offset) for total in self.totals]
        if coming is None:
            return own
        return [(a.astype(jnp.float32) + b.astype(jnp.float32)).astype(LOW) for a, b in zip(own, coming)]

    def step(self):
        self.round += 1
        k, far = self.round, self.count // 2
        near = self.count - 1 - far
        if k <= far:
            parts = self.load(self.forward, far - k + 1)
            self.forward = [lax.ppermute(part, SEQ, self.ahead) for part in parts]
        if k <= near:
            parts = self.load(self.backward, k - near - 1)
            self.backward = [lax.ppermute(part, SEQ, [(b, a) for a, b in self.ahead]) for part in parts]

    def after(self, value):
        value, self.forward, self.backward = lax.optimization_barrier((value, self.forward, self.backward))
        return value

    def finish(self):
        while self.round < self.count // 2:
            self.step()
        own = [self.block(total, 0).astype(jnp.float32) for total in self.totals]
        return [
            a + b.astype(jnp.float32) + c.astype(jnp.float32) for a, b, c in zip(own, self.forward, self.backward)
        ]


def norm_scale(value):
    return lax.rsqrt(jnp.mean(value * value, axis=-1, keepdims=True) + EPS)


def norm_back(scale, normed, gain, grad):
    scaled = grad * gain
    return scale * (scaled - normed * jnp.mean(scaled * normed, axis=-1, keepdims=True))


def split3(value):
    high = value.astype(LOW)
    rest = value - high.astype(jnp.float32)
    middle = rest.astype(LOW)
    return [high, middle, (rest - middle.astype(jnp.float32)).astype(LOW)]


def per_device(
    block_in,
    cotangent,
    segment_ids,
    expert_routes,
    pair_priority,
    gain_attention,
    w_query,
    w_key,
    w_value,
    w_out,
    bias_table,
    gain_experts,
    w_router,
    w_gate,
    w_up,
    w_down,
):
    groups, local_len, width = block_in.shape
    tokens = groups * local_len
    rows_own, hd = w_query.shape
    split = lax.axis_size("x")
    exp_count = lax.axis_size("exp")
    seq_count = groups * split
    length = local_len * seq_count
    x_at, z_at, e_at = lax.axis_index("x"), lax.axis_index("z"), lax.axis_index("exp")
    s_at = z_at * split + x_at
    head_width = hd // split
    heads_here = head_width // HEAD_DIM
    experts_all = w_router.shape[1]
    bias_own = bias_table.shape[0]
    tile = min(TILE, local_len)
    own = s_at.astype(jnp.int32).reshape(1)
    z_bits, x_bits, e_bits = bits_of(groups), bits_of(split), bits_of(exp_count)

    input_r = reorder(block_in, z_at)

    arrived = [[None] * split for _ in range(groups)]
    for rz in reversed(range(groups)):
        arrived[rz][0] = partner(input_r[rz], "z", rz) if rz else input_r[0]
    small = jnp.concatenate(
        [
            gain_attention[:, None],
            gain_experts[:, None],
            jnp.pad(bias_table, (0, rows_own - bias_own))[:, None],
            w_router,
        ],
        axis=1,
    )
    small = jnp.pad(small, ((0, 0), (0, LANES - small.shape[1]))).astype(LOW)
    share = jnp.stack(
        [part.astype(LOW).reshape(rows_own, split, head_width) for part in (w_query, w_key, w_value)], axis=2
    )
    share = share.reshape(rows_own, split, 3 * head_width).transpose(1, 0, 2)
    common = jnp.concatenate([w_out.astype(LOW), small], axis=1)
    share = jnp.concatenate([share, jnp.broadcast_to(common, (split,) + common.shape)], axis=2)
    shares = [lax.dynamic_index_in_dim(share, x_at ^ r, 0, keepdims=False) for r in range(split)]
    shares = [shares[0]] + [partner(shares[r], "x", r) for r in range(1, split)]
    by_x = reorder(jnp.stack(shares), x_at)
    for rx in range(1, split):
        arrived[0][rx] = partner(arrived[0][0], "x", rx)
    packed = gather_double(by_x, [("z", b) for b in z_bits])
    near = [arrived[rz][0] for rz in range(1, groups)]
    packed, near = lax.optimization_barrier((packed, near))
    for rz in range(1, groups):
        arrived[rz][0] = near[rz - 1]
        for rx in range(1, split):
            arrived[rz][rx] = partner(arrived[rz][0], "x", rx)
    packed = gather_double(packed, [("exp", b) for b in e_bits[:-1]])
    packed, arrived = lax.optimization_barrier((packed, arrived))
    sequence = jnp.stack([block for line in arrived for block in line]).reshape(length, width)

    gate_up_own = jnp.concatenate([w_gate[0].astype(LOW), w_up[0].astype(LOW)], axis=1)
    sequence, gate_up_own, down_own = lax.optimization_barrier((sequence, gate_up_own, w_down[0].astype(LOW)))
    down_w = lax.all_gather(down_own, SEQ, axis=0, tiled=True)
    gate_up_ring = RingGather(gate_up_own, groups, split, s_at)
    gate_up_ring.step()
    packed = gather_double(packed, [("exp", b) for b in e_bits[-1:]])
    ne, nz, nx = len(e_bits), len(z_bits), len(x_bits)
    packed = packed.transpose(
        tuple(ne + i for i in reversed(range(nz))) + (ne + nz,) + tuple(reversed(range(ne))) + (ne + nz + 1, ne + nz + 2)
    ).reshape(width, 3 * head_width + width + LANES)
    qkv_w, small_all = packed[:, : 3 * head_width], packed[:, 3 * head_width + width :]
    out_w = packed[:, 3 * head_width : 3 * head_width + width]
    gain_one = small_all[:, 0].astype(jnp.float32)
    gain_two = small_all[:, 1].astype(jnp.float32)
    table_all = small_all[:, 2].reshape(-1, rows_own)[:, :bias_own].reshape(-1, BUCKETS)
    router_t = small_all[:, 3 : 3 + experts_all].T
    table_rows = lax.dynamic_slice_in_dim(table_all, x_at * heads_here, heads_here, 0)

    routes = expert_routes.reshape(tokens, -1)
    top_count = routes.shape[1]
    priority = pair_priority.reshape(-1)
    pair_experts = routes.reshape(-1)
    ahead = (pair_experts[None, :] == pair_experts[:, None]) & (priority[None, :] < priority[:, None])
    slots = jnp.sum(ahead.astype(jnp.int32), axis=1)
    capacity = (5 * top_count * tokens + 4 * experts_all - 1) // (4 * experts_all)
    slot_count = experts_all * capacity
    slot_index = jnp.where(slots < capacity, (pair_experts ^ e_at) * capacity + slots, slot_count)
    slot_index = slot_index.reshape(tokens, top_count)
    every_slot = jnp.arange(slot_count, dtype=jnp.int32)[None, :]
    table = sum((slot_index[:, k : k + 1] == every_slot).astype(LOW) for k in range(top_count))
    tables = [table[:, r * capacity : (r + 1) * capacity] for r in range(exp_count)]
    grad_low = cotangent.reshape(tokens, width)
    grad_slots = [dot_tn(part, grad_low).astype(LOW) for part in tables]

    wide = sequence.astype(jnp.float32)
    normed_one = (wide * norm_scale(wide) * gain_one).astype(LOW)
    qkv = dot32(normed_one, qkv_w).astype(LOW)
    qkv, grad_slots = lax.optimization_barrier((qkv, grad_slots))
    qkv = gate_up_ring.after(qkv)
    gate_up_ring.step()
    grad_slots = [grad_slots[0]] + [partner(grad_slots[r], "exp", r) for r in range(1, exp_count)]
    segments = lax.dynamic_index_in_dim(segment_ids, z_at, 0, keepdims=False)
    ranges = tile_ranges(segments, tile)
    seg_blocks = segments.reshape(seq_count, local_len)
    query_side, key_side = segment_columns(reorder(seg_blocks, s_at).reshape(length))
    rows = bias_rows(table_rows, tile)
    ends = jnp.stack([table_rows[:, 15], table_rows[:, 31]], axis=1).astype(jnp.float32)
    contexts, log_totals = attend_forward(qkv, query_side, key_side, ranges, rows, ends, own, tile)
    contexts = gate_up_ring.after(contexts)
    contexts, grad_slots = lax.optimization_barrier((contexts, grad_slots))
    gate_up_w = gate_up_ring.finish()

    def exchange_positions(blocks):
        return lax.all_to_all(blocks, SEQ, split_axis=0, concat_axis=0, tiled=True)

    context_local = exchange_positions(contexts.reshape(seq_count, local_len, head_width))
    context_local = (
        context_local.reshape(groups, split, local_len, head_width).transpose(0, 2, 1, 3).reshape(tokens, hd)
    )
    inputs = block_in.astype(jnp.float32).reshape(tokens, width)
    mid = inputs + dot32(context_local, out_w)
    scale_two = norm_scale(mid)
    normed_two = (mid * scale_two * gain_two).astype(LOW)

    logits = dot_nt(router_t, normed_two)
    exponent = jnp.exp(logits - jnp.max(logits, axis=0, keepdims=True))
    probabilities = exponent / jnp.sum(exponent, axis=0, keepdims=True)
    expert_ids = jnp.arange(experts_all, dtype=jnp.int32)[:, None]
    chosen = sum((routes[:, k][None, :] == expert_ids).astype(jnp.float32) for k in range(top_count))
    chosen_total = jnp.sum(probabilities * chosen, axis=0, keepdims=True)
    gates = probabilities * chosen / chosen_total
    gates_r = reorder(gates, e_at)

    gate_slots = jnp.sum(
        table.astype(jnp.float32).reshape(tokens, exp_count, capacity) * gates_r.T[:, :, None], axis=0
    )
    gate_lines = jnp.pad(jnp.stack(split3(gate_slots), axis=1), ((0, 0), (0, EXTRA - 3), (0, width - capacity)))

    def values_below(rows_):
        return jnp.sum(rows_[capacity : capacity + 3, :capacity].astype(jnp.float32), axis=0)

    sent = [None] * exp_count
    for r in reversed(range(exp_count)):
        sent[r] = jnp.concatenate([dot_tn(tables[r], normed_two).astype(LOW), gate_lines[r]], axis=0)
        if r:
            sent[r] = partner(sent[r], "exp", r)

    earlier = ()
    back = [None] * exp_count
    turns = [0] + list(range(2, exp_count)) + [1]
    for turn, r in enumerate(turns):
        if turn >= 3:
            ready = turns[turn - 2]
            sent[r], back[ready] = lax.optimization_barrier((sent[r], back[ready]))
        hidden, gate_low, up_low, dx = expert_block(
            r, exp_count, sent[r], grad_slots[r], gate_up_w, down_w, earlier
        )
        earlier = (hidden, gate_low, up_low)
        back[r] = partner(dx, "exp", r) if r else dx

    sent, hidden = lax.optimization_barrier((sent, hidden))
    slot_rows = jnp.concatenate([rows_[:capacity] for rows_ in sent], axis=0)
    slot_gates = jnp.concatenate([values_below(rows_) for rows_ in sent], axis=0)[:, None]
    slot_grads = (slot_gates * jnp.concatenate(grad_slots, axis=0).astype(jnp.float32)).astype(LOW)

    gate_grad = jnp.sum(
        table.astype(jnp.float32).reshape(tokens, exp_count, capacity) * jnp.stack([values_below(rows_) for rows_ in back])[None], axis=2
    )
    gate_grad = reorder(gate_grad.T, e_at)
    chosen_grad = chosen * (gate_grad - jnp.sum(gates * gate_grad, axis=0, keepdims=True)) / chosen_total
    logit_grad = probabilities * (chosen_grad - jnp.sum(probabilities * chosen_grad, axis=0, keepdims=True))
    logit_pieces = jnp.concatenate(split3(logit_grad), axis=0)
    router_sum = jnp.sum(dot32(logit_pieces, normed_two).reshape(3, experts_all, width), axis=0)
    normed_two_grad = dot_tn(logit_pieces, jnp.concatenate([router_t] * 3, axis=0))
    for r in range(exp_count):
        normed_two_grad = normed_two_grad + dot32(tables[r], back[r][:capacity])
    unit_two = mid * scale_two
    gain_two_sum = jnp.sum(normed_two_grad * unit_two, axis=0)
    grad_out = grad_low.astype(jnp.float32)
    mid_grad = grad_out + norm_back(scale_two, unit_two, gain_two, normed_two_grad)
    attention_grad = mid_grad.astype(LOW)
    context_grad = dot_nt(attention_grad, out_w).astype(LOW)
    context_grad, up_low, gate_low, hidden = lax.optimization_barrier((context_grad, up_low, gate_low, hidden))
    down_sum = dot_tn(hidden, slot_grads).astype(LOW)
    gate_sum = dot_tn(slot_rows, gate_low).astype(LOW)
    up_sum = dot_tn(slot_rows, up_low).astype(LOW)
    context_grad = (
        context_grad.reshape(groups, local_len, split, head_width)
        .transpose(0, 2, 1, 3)
        .reshape(seq_count, local_len, head_width)
    )
    context_heads = exchange_positions(context_grad).reshape(length, head_width)

    def scatter_experts(total):
        return lax.psum_scatter(total, SEQ, scatter_dimension=0, tiled=True)

    context_heads, gate_sum, up_sum, down_sum = lax.optimization_barrier(
        (context_heads, gate_sum, up_sum, down_sum)
    )
    down_owned = scatter_experts(down_sum)

    halving = [("exp", b, 1 + nz + nx + ne - 1 - i) for i, b in enumerate(reversed(e_bits))]
    halving += [("z", b, 1 + nz - 1 - i) for i, b in enumerate(reversed(z_bits))]
    out_sum = dot_tn(context_local, attention_grad).astype(LOW)

    ring = RingScatter([gate_sum, up_sum], groups, split, s_at)
    grads, diag, far = (), [], []
    pairs = head_width // LANES
    for pair in range(pairs):
        ring.step()
        *grads, pair_diag, pair_far = attend_backward(
            pair, qkv, context_heads, contexts, log_totals, query_side, key_side, ranges, rows, ends, own, tile, tuple(grads)
        )
        grads = ring.after(grads)
        if pair == 0:
            grads, hidden = lax.optimization_barrier((grads, hidden))
            expert_out = (slot_gates * dot32(hidden, down_w)).astype(LOW)
            expert_out = reorder(expert_out.reshape(exp_count, capacity, width), e_at)
            returned = lax.all_to_all(expert_out, "exp", split_axis=0, concat_axis=0, tiled=True)
        if pair == min(1, pairs - 1):
            grads, expert_out = lax.optimization_barrier((grads, expert_out))
        if pair == pairs - 1:
            grads, returned = lax.optimization_barrier((grads, returned))
        diag.append(pair_diag)
        far.append(pair_far)
    diag, far = jnp.concatenate(diag), jnp.concatenate(far)
    query_back, key_back, value_back, down_owned = lax.optimization_barrier((*grads, down_owned))
    gate_owned, up_owned = ring.finish()
    table_local = bucket_sums(diag, far, tile)

    def through(grads, part):
        return dot_nt(grads, qkv_w[:, part * head_width : (part + 1) * head_width])

    out_parts = width // head_width
    weight_sum = jnp.stack(
        [dot_tn(normed_one, grads).astype(LOW) for grads in (query_back, key_back, value_back)]
        + [out_sum[:, i * head_width : (i + 1) * head_width] for i in range(out_parts)]
    )
    weight_sum, query_back, key_back, value_back = lax.optimization_barrier(
        (weight_sum, query_back, key_back, value_back)
    )
    normed_part = through(query_back, 0) + through(key_back, 1) + through(value_back, 2)
    half = width // 2
    normed_part = normed_part.reshape(groups, split, local_len, width)

    sides = [normed_part[:, rx].astype(LOW) for rx in range(1, split)]
    first = [partner(side[:, :, :half], "x", rx) for rx, side in enumerate(sides, 1)]
    first, rest = lax.optimization_barrier((first, [side[:, :, half:] for side in sides]))

    def send_back(own_part, coming):
        total = own_part + sum(part.astype(jnp.float32) for part in coming)
        total = reorder(total.astype(LOW), z_at)
        return lax.all_to_all(total, "z", split_axis=0, concat_axis=0, tiled=True)

    normed_first = send_back(normed_part[:, 0, :, :half], first)
    rest = [partner(side, "x", rx) for rx, side in enumerate(rest, 1)]
    normed_second = send_back(normed_part[:, 0, :, half:], rest)
    weight_part = scatter_halve(
        weight_sum.reshape((3 + out_parts,) + (2,) * (nz + nx + ne) + (rows_own, head_width)), halving[:ne]
    )
    weight_part = scatter_halve(weight_part, halving[ne:]).reshape(3 + out_parts, split, rows_own, head_width)
    weight_own = [lax.dynamic_index_in_dim(weight_part, x_at ^ r, 1, keepdims=False) for r in range(split)]
    weight_own = [weight_own[0]] + [partner(weight_own[r], "x", r) for r in range(1, split)]
    normed_second, weight_own = lax.optimization_barrier((normed_second, weight_own))
    block_out = (mid + dot32(table, reorder(returned, e_at).reshape(slot_count, width))).astype(LOW)

    block_out = block_out.reshape(groups, local_len, width)
    out_w_out = sum(part[3:].astype(jnp.float32) for part in weight_own)
    out_w_out = out_w_out.transpose(1, 0, 2).reshape(rows_own, width)
    qkv_own = reorder(jnp.stack([part[:3] for part in weight_own]), x_at)
    qkv_own = qkv_own.transpose(1, 2, 0, 3).reshape(3, rows_own, hd).astype(jnp.float32)

    normed_one_grad = jnp.concatenate([normed_first, normed_second], axis=2).astype(jnp.float32).reshape(tokens, width)
    scale_one = norm_scale(inputs)
    unit_one = inputs * scale_one
    gain_one_sum = jnp.sum(normed_one_grad * unit_one, axis=0)
    block_in_grad = (mid_grad + norm_back(scale_one, unit_one, gain_one, normed_one_grad)).reshape(
        groups, local_len, width
    )

    table_sum = lax.dynamic_update_slice_in_dim(
        jnp.zeros(table_all.shape, jnp.float32), table_local, x_at * heads_here, 0
    ).reshape(-1, bias_own)
    table_sum = jnp.pad(table_sum, ((0, 0), (0, rows_own - bias_own)))[:, None, :]
    little = jnp.concatenate(
        [
            gain_one_sum.reshape(-1, 1, rows_own),
            gain_two_sum.reshape(-1, 1, rows_own),
            table_sum,
            router_sum.reshape(experts_all, -1, rows_own).transpose(1, 0, 2),
        ],
        axis=1,
    )
    little = jnp.sum(lax.all_to_all(little, ALL, split_axis=0, concat_axis=0, tiled=True), axis=0)
    return (
        block_out,
        block_in_grad,
        little[0],
        qkv_own[0],
        qkv_own[1],
        qkv_own[2],
        out_w_out,
        little[2, :bias_own],
        little[1],
        little[3:].T,
        gate_owned.astype(jnp.float32)[None],
        up_owned.astype(jnp.float32)[None],
        down_owned.astype(jnp.float32)[None],
    )


def solution(mesh):
    def run(*args):
        groups = args[0].shape[0] // mesh.shape["exp"]
        seq_count, exp_count = mesh.shape["seq"], mesh.shape["exp"]
        grid = mesh.devices.reshape(groups, seq_count // groups, exp_count)
        fine = jax.sharding.Mesh(grid, ALL)
        placed = P("exp", SEQ, None)
        whole = P(ALL)
        matrix = P(ALL, None)
        return jax.shard_map(
            per_device,
            mesh=fine,
            in_specs=(
                placed, placed, P("exp", None), placed, placed,
                whole, matrix, matrix, matrix, matrix, whole, whole, matrix,
                placed, placed, placed,
            ),
            out_specs=(
                placed, placed, whole, matrix, matrix, matrix, matrix, whole, whole, matrix,
                placed, placed, placed,
            ),
            check_vma=False,
        )(*args)

    return run
```

```python
from functools import partial

import jax
import jax.numpy as jnp
import numpy as np
from jax import lax
from jax.experimental import pallas as pl
from jax.experimental.pallas import tpu as pltpu
from jax.sharding import PartitionSpec as P

HEAD_DIM = 64
BUCKETS = 32
THRESHOLDS = (12, 16, 23, 32, 46, 64, 91)
MASKED = -1e30
TILE = 256
LANES = 128
NT = (((1,), (1,)), ((), ()))


def bucket_of(d):
    a = np.abs(d)
    extra = sum((a >= t).astype(np.int64) for t in THRESHOLDS)
    return np.where(a < 8, a, 8 + extra) + 16 * (d > 0)


def bias_rows(table_rows, tile):
    u = np.arange(2 * tile)
    x = np.where(u < tile, u, u - 2 * tile)
    ids = np.stack([bucket_of(step * tile - x) for step in (-1, 0, 1)])
    hot = (ids.reshape(-1)[None, :] == np.arange(BUCKETS)[:, None]).astype(np.float32)
    rows = jnp.dot(table_rows.astype(jnp.bfloat16), jnp.asarray(hot, jnp.bfloat16), preferred_element_type=jnp.float32)
    return rows.reshape(table_rows.shape[0], 3, 2 * tile)


def tile_ranges(segments, tile):
    blocks = segments.reshape(-1, tile)
    first, last = blocks[:, 0], blocks[:, -1]
    low = jnp.sum((last[None, :] < first[:, None]).astype(jnp.int32), axis=1)
    high = jnp.sum((first[None, :] <= last[:, None]).astype(jnp.int32), axis=1)
    return jnp.stack([low, high])


def segment_columns(segments):
    lane = jnp.arange(LANES, dtype=jnp.int32)[None, :]
    seg = segments[:, None]
    same = seg == lane
    query_side = jnp.where(same & (lane < 4), MASKED, 0.0).astype(jnp.bfloat16)
    key_side = jnp.where(lane < 4, (~same).astype(jnp.float32), (lane < 9).astype(jnp.float32)).astype(jnp.bfloat16)
    return query_side, key_side


def toeplitz(row, tile):
    wide = jnp.broadcast_to(row, (tile, row.shape[1]))
    return pltpu.roll(wide, 0, 1, stride=1, stride_axis=0)[:, :tile]


def block_at(index, own, tile):
    return pl.ds(pl.multiple_of((index ^ own[0]) * tile, tile), tile)


def fwd_kernel(ranges, ends, own, q_ref, k_ref, v_ref, qs_ref, ks_ref, rows_ref, o_ref, lse_ref, bias_ref, vt_ref):
    group, qb = pl.program_id(0), pl.program_id(1)
    tile, span = q_ref.shape
    heads = span // HEAD_DIM

    @pl.when(qb == 0)
    def _():
        for h in range(heads):
            for step in range(3):
                bias_ref[h, step] = toeplitz(rows_ref[h, step : step + 1, :], tile)
        for start in range(0, v_ref.shape[0], tile):
            vt_ref[:, start : start + tile] = v_ref[start : start + tile, :].T

    low, high = ranges[0, qb], ranges[1, qb]
    lane = lax.broadcasted_iota(jnp.int32, (tile, LANES), 1)
    q = q_ref[...] * jnp.bfloat16(HEAD_DIM**-0.5)
    qs = qs_ref[...]
    halves = []
    for h in range(heads):
        part = q[:, h // 2 * LANES : (h // 2 + 1) * LANES]
        keep = (lane < HEAD_DIM) if h % 2 == 0 else (lane >= HEAD_DIM)
        halves.append(jnp.where(keep, part, jnp.zeros_like(part)))

    def side(h, which):
        if which == 1:
            extra = qs
        else:
            value = ends[heads * group + h, which // 2].astype(jnp.bfloat16)
            extra = jnp.where(lane == 7, value, qs)
        return jnp.concatenate([halves[h], extra], axis=1)

    def visit(which):
        queries = [side(h, which) for h in range(heads)]

        def step(kb, carry):
            keys = block_at(kb, own, tile)
            ks = ks_ref[keys, :]
            scores = []
            for h in range(heads):
                kx = jnp.concatenate([k_ref[keys, h // 2 * LANES : (h // 2 + 1) * LANES], ks], axis=1)
                scores.append(lax.dot_general(kx, queries[h], NT, preferred_element_type=jnp.float32))
            out = []
            for h in range(heads):
                peak, total, acc = carry[h]
                s = scores[h]
                if which == 1:
                    s = s + bias_ref[h, kb - qb + 1]
                new = jnp.maximum(peak, jnp.max(s, axis=0, keepdims=True))
                p = jnp.exp(s - new)
                scale = jnp.exp(peak - new)
                total = total * scale + jnp.sum(p, axis=0, keepdims=True)
                vt = vt_ref[h * HEAD_DIM : (h + 1) * HEAD_DIM, keys]
                acc = acc * scale + jnp.dot(vt, p.astype(jnp.bfloat16), preferred_element_type=jnp.float32)
                out.append((new, total, acc))
            return tuple(out)

        return step

    start = tuple(
        (
            jnp.full((1, tile), -3e38, jnp.float32),
            jnp.zeros((1, tile), jnp.float32),
            jnp.zeros((HEAD_DIM, tile), jnp.float32),
        )
        for _ in range(heads)
    )
    near_low, near_high = jnp.maximum(low, qb - 1), jnp.minimum(high, qb + 2)
    state = lax.fori_loop(near_low, near_high, visit(1), start)
    state = lax.fori_loop(low, near_low, visit(0), state)
    state = lax.fori_loop(near_high, high, visit(2), state)
    outs = []
    for h in range(heads):
        peak, total, acc = state[h]
        outs.append(acc / total)
        lse_ref[h // 2, h % 2 : h % 2 + 1, :] = peak + jnp.log(total)
    o_ref[...] = jnp.concatenate(outs, axis=0).T.astype(o_ref.dtype)


FWD_PAIRS = 4


def attend_forward(qkv, qs, ks, ranges, rows, ends, own, tile):
    length, width = qkv.shape[0], qkv.shape[1] // 3
    pairs = width // LANES
    together = FWD_PAIRS if pairs % FWD_PAIRS == 0 else 1
    span = together * LANES
    tiles = length // tile
    spec = pltpu.PrefetchScalarGridSpec(
        num_scalar_prefetch=3,
        grid=(pairs // together, tiles),
        in_specs=[
            pl.BlockSpec((tile, span), lambda p, i, r, e, own: (i ^ own[0], p)),
            pl.BlockSpec((length, span), lambda p, i, *_: (0, width // span + p)),
            pl.BlockSpec((length, span), lambda p, i, *_: (0, 2 * (width // span) + p)),
            pl.BlockSpec((tile, LANES), lambda p, i, r, e, own: (i ^ own[0], 0)),
            pl.BlockSpec((length, LANES), lambda p, i, *_: (0, 0)),
            pl.BlockSpec((2 * together, 3, 2 * tile), lambda p, i, *_: (p, 0, 0)),
        ],
        out_specs=[
            pl.BlockSpec((tile, span), lambda p, i, *_: (i, p)),
            pl.BlockSpec((together, 2, tile), lambda p, i, *_: (p, 0, i)),
        ],
        scratch_shapes=[
            pltpu.VMEM((2 * together, 3, tile, tile), jnp.float32),
            pltpu.VMEM((span, length), jnp.bfloat16),
        ],
    )
    return pl.pallas_call(
        fwd_kernel,
        name="attend_forward",
        out_shape=(
            jax.ShapeDtypeStruct((length, width), jnp.bfloat16),
            jax.ShapeDtypeStruct((pairs, 2, length), jnp.float32),
        ),
        grid_spec=spec,
        compiler_params=pltpu.CompilerParams(
            dimension_semantics=("arbitrary", "arbitrary"), vmem_limit_bytes=48 << 20
        ),
        cost_estimate=pl.CostEstimate(flops=length * length * width * 4, bytes_accessed=length * width * 8, transcendentals=0),
    )(ranges, ends, own, qkv, qkv, qkv, qs, ks, rows)


def pieces(row):
    high = row.astype(jnp.bfloat16).astype(jnp.float32)
    mid = (row - high).astype(jnp.bfloat16).astype(jnp.float32)
    return high, mid, row - high - mid


def bwd_kernel(ranges, ends, own, q_ref, k_ref, v_ref, do_ref, o_ref, lse_ref, qs_ref, ks_ref, rows_ref, *refs):
    (dq_ref, dk_ref, dv_ref, diag_ref, far_ref,
     qx_ref, dox_ref, kt_ref, bias_ref, dsum_ref, fsum_ref, dqt_ref, dka_ref, dva_ref) = refs[-14:]
    pair = own[1]
    length = q_ref.shape[0]
    tile = bias_ref.shape[2]
    tiles = length // tile
    for h in range(2):
        for step in range(3):
            bias_ref[h, step] = toeplitz(rows_ref[h, step : step + 1, :], tile)
    dsum_ref[...] = jnp.zeros_like(dsum_ref)
    fsum_ref[...] = jnp.zeros_like(fsum_ref)
    dqt_ref[...] = jnp.zeros_like(dqt_ref)
    lane = lax.broadcasted_iota(jnp.int32, (tile, LANES), 1)
    sub = lax.broadcasted_iota(jnp.int32, (LANES, tile), 0)
    pick = (lax.broadcasted_iota(jnp.int32, (8, LANES), 1) // HEAD_DIM == lax.broadcasted_iota(jnp.int32, (8, LANES), 0)).astype(jnp.float32)

    @pl.loop(0, tiles)
    def _(i):
        line = pl.ds(pl.multiple_of(i * tile, tile), tile)
        at = block_at(i, own, tile)
        q = q_ref[at, :] * jnp.bfloat16(HEAD_DIM**-0.5)
        do = do_ref[line, :]
        zero = jnp.zeros_like(q)
        product = do.astype(jnp.float32) * o_ref[line, :].astype(jnp.float32)
        delta = lax.dot_general(pick, product, NT, precision=lax.Precision.HIGHEST, preferred_element_type=jnp.float32)
        kt_ref[:, at] = k_ref[at, :].T
        for h in range(2):
            keep = (lane < HEAD_DIM) if h == 0 else (lane >= HEAD_DIM)
            a, b, c = pieces(-lse_ref[0, h : h + 1, line])
            extra = jnp.where(sub == 4, a, jnp.where(sub == 5, b, jnp.where(sub == 6, c, 0.0)))
            extra = extra.T.astype(jnp.bfloat16) + qs_ref[at, :]
            left, right = ends[2 * pair + h, 0].astype(jnp.bfloat16), ends[2 * pair + h, 1].astype(jnp.bfloat16)
            extra = jnp.where(lane == 7, left, jnp.where(lane == 8, right, extra))
            qx_ref[h, at, :] = jnp.concatenate([jnp.where(keep, q, zero), extra], axis=1)
            a, b, c = pieces(-delta[h : h + 1, :])
            extra = jnp.where(sub == 4, a, jnp.where(sub == 5, b, jnp.where(sub == 6, c, 0.0)))
            dox_ref[h, at, :] = jnp.concatenate([jnp.where(keep, do, zero), extra.T.astype(jnp.bfloat16)], axis=1)

    ones3 = ((lane >= 4) & (lane < 7)).astype(jnp.bfloat16)

    @pl.loop(0, tiles)
    def _(kb):
        low, high = ranges[0, kb], ranges[1, kb]
        keys = block_at(kb, own, tile)
        k, ks = k_ref[keys, :], ks_ref[keys, :]
        vx = jnp.concatenate([v_ref[keys, :], ones3], axis=1)
        nil = jnp.zeros_like(ks)
        dka_ref[...] = jnp.zeros_like(dka_ref)
        dva_ref[...] = jnp.zeros_like(dva_ref)

        def visit(which):
            if which == 0:
                extra = jnp.where(lane == 8, nil, ks)
            elif which == 2:
                extra = jnp.where(lane == 7, nil, ks)
            else:
                extra = jnp.where((lane == 7) | (lane == 8), nil, ks)
            kx = jnp.concatenate([k, extra], axis=1)

            def step(qb, carry):
                at = block_at(qb, own, tile)
                weights, grads = [], []
                for h in range(2):
                    qx, dox = qx_ref[h, at, :], dox_ref[h, at, :]
                    s = lax.dot_general(kx, qx, NT, preferred_element_type=jnp.float32)
                    if which == 1:
                        s = s + bias_ref[h, kb - qb + 1]
                    p = jnp.exp(s)
                    dp = lax.dot_general(vx, dox, NT, preferred_element_type=jnp.float32)
                    ds = p * dp
                    if which == 1:
                        dsum_ref[h, kb - qb + 1] += ds
                    else:
                        fsum_ref[h, which // 2] += jnp.sum(ds.reshape(tile // 8, 8, tile), axis=0)
                    weights.append(p.astype(jnp.bfloat16))
                    grads.append(ds.astype(jnp.bfloat16))
                    rows = slice(h * HEAD_DIM, (h + 1) * HEAD_DIM)
                    dqt_ref[rows, at] += jnp.dot(kt_ref[rows, keys], grads[h], preferred_element_type=jnp.float32)
                both_do = jnp.concatenate([dox_ref[0, at, :LANES], dox_ref[1, at, :LANES]], axis=0)
                both_q = jnp.concatenate([qx_ref[0, at, :LANES], qx_ref[1, at, :LANES]], axis=0)
                dva_ref[...] += jnp.dot(jnp.concatenate(weights, axis=1), both_do, preferred_element_type=jnp.float32)
                dka_ref[...] += jnp.dot(jnp.concatenate(grads, axis=1), both_q, preferred_element_type=jnp.float32)
                return carry

            return step

        near_low, near_high = jnp.maximum(low, kb - 1), jnp.minimum(high, kb + 2)
        lax.fori_loop(near_low, near_high, visit(1), 0)
        lax.fori_loop(near_high, high, visit(0), 0)
        lax.fori_loop(low, near_low, visit(2), 0)
        dk_ref[keys, :] = dka_ref[...].astype(dk_ref.dtype)
        dv_ref[keys, :] = dva_ref[...].astype(dv_ref.dtype)

    @pl.loop(0, tiles)
    def _(i):
        at = pl.ds(pl.multiple_of(i * tile, tile), tile)
        dq_ref[at, :] = (dqt_ref[:, at] * HEAD_DIM**-0.5).T.astype(dq_ref.dtype)

    for h in range(2):
        for step in range(3):
            diag_ref[h, step : step + 1, :] = diagonals(dsum_ref, h, step, tile)
        for step in range(2):
            total = jnp.sum(fsum_ref[h, step], axis=0, keepdims=True)
            far_ref[h, step : step + 1, :] = total


def diagonals(dsum_ref, h, step, tile):
    width = 2 * tile
    acc = jnp.zeros((8, width), jnp.float32)
    for group in range(tile // 8):
        part = dsum_ref[h, step, group * 8 : (group + 1) * 8, :]
        part = jnp.concatenate([part, jnp.zeros((8, tile), jnp.float32)], axis=1)
        acc = acc + (pltpu.roll(part, width - 8 * group, 1) if group else part)
    row = lax.broadcasted_iota(jnp.int32, (8, width), 0)
    for bit in (1, 2, 4):
        acc = jnp.where((row & bit) != 0, pltpu.roll(acc, width - bit, 1), acc)
    return jnp.sum(acc, axis=0, keepdims=True)


def attend_backward(pair, qkv, do, o, lse, qs, ks, ranges, rows, ends, own, tile, earlier):
    length, width = do.shape
    pairs = width // LANES
    own = jnp.concatenate([own, jnp.full((1,), pair, jnp.int32)])
    column = pl.BlockSpec((length, LANES), lambda p, r, e, own: (0, own[1]))
    fixed = pl.BlockSpec((length, LANES), lambda p, *_: (0, 0))
    spec = pltpu.PrefetchScalarGridSpec(
        num_scalar_prefetch=3,
        grid=(1,),
        in_specs=[
            column,
            pl.BlockSpec((length, LANES), lambda p, r, e, own: (0, pairs + own[1])),
            pl.BlockSpec((length, LANES), lambda p, r, e, own: (0, 2 * pairs + own[1])),
            column,
            column,
            pl.BlockSpec((1, 2, length), lambda p, r, e, own: (own[1], 0, 0)),
            fixed, fixed,
            pl.BlockSpec((2, 3, 2 * tile), lambda p, r, e, own: (own[1], 0, 0)),
        ]
        + [pl.BlockSpec(memory_space=pl.ANY)] * len(earlier),
        out_specs=[
            column, column, column,
            pl.BlockSpec((2, 3, 2 * tile), lambda p, *_: (p, 0, 0)),
            pl.BlockSpec((2, 2, tile), lambda p, *_: (p, 0, 0)),
        ],
        scratch_shapes=[
            pltpu.VMEM((2, length, 2 * LANES), jnp.bfloat16),
            pltpu.VMEM((2, length, 2 * LANES), jnp.bfloat16),
            pltpu.VMEM((LANES, length), jnp.bfloat16),
            pltpu.VMEM((2, 3, tile, tile), jnp.float32),
            pltpu.VMEM((2, 3, tile, tile), jnp.float32),
            pltpu.VMEM((2, 2, 8, tile), jnp.float32),
            pltpu.VMEM((LANES, length), jnp.float32),
            pltpu.VMEM((tile, LANES), jnp.float32),
            pltpu.VMEM((tile, LANES), jnp.float32),
        ],
    )
    low = jax.ShapeDtypeStruct((length, width), jnp.bfloat16)
    return pl.pallas_call(
        bwd_kernel,
        name="attend_backward",
        out_shape=(
            low, low, low,
            jax.ShapeDtypeStruct((2, 3, 2 * tile), jnp.float32),
            jax.ShapeDtypeStruct((2, 2, tile), jnp.float32),
        ),
        grid_spec=spec,
        input_output_aliases={12 + i: i for i in range(len(earlier))},
        compiler_params=pltpu.CompilerParams(
            dimension_semantics=("arbitrary",), vmem_limit_bytes=40 << 20
        ),
        cost_estimate=pl.CostEstimate(flops=length * length * LANES * 10, bytes_accessed=length * LANES * 16, transcendentals=0),
    )(ranges, ends, own, qkv, qkv, qkv, do, o, lse, qs, ks, rows, *earlier)


def bucket_sums(diag, far, tile):
    u = np.arange(2 * tile)
    x = np.where(u < tile, u, u - 2 * tile)
    ids = np.stack([bucket_of(step * tile - x) for step in (-1, 0, 1)])
    hot = (ids.reshape(-1)[:, None] == np.arange(BUCKETS)[None, :]).astype(np.float32)
    sums = jnp.dot(diag.reshape(diag.shape[0], -1), jnp.asarray(hot), precision=lax.Precision.HIGHEST)
    outer = jnp.sum(far, axis=2)
    ends = np.zeros((2, BUCKETS), np.float32)
    ends[0, 15] = 1
    ends[1, 31] = 1
    return sums + outer[:, 0:1] * ends[0] + outer[:, 1:2] * ends[1]


GELU_A, GELU_B = 0.7978845608028654, 0.044715
FF_TILE = 256
EXTRA = 16


def expert_kernel(own_ref, x_ref, dy_ref, wg_ref, wu_ref, wd_ref, *refs):
    h_ref, dg_ref, du_ref, dx_ref, part_ref, acc_ref, gate_ref = refs[-7:]
    step = pl.program_id(0)
    rows = dy_ref.shape[0]
    chunk = rows // 2 if rows % 32 == 0 else rows

    @pl.when(step == 0)
    def _():
        acc_ref[...] = jnp.zeros_like(acc_ref)
        part_ref[...] = jnp.zeros_like(part_ref)
        lines = x_ref[rows:, :rows].astype(jnp.float32)
        gate = jnp.sum(lines, axis=0, keepdims=True)
        gate_ref[...] = jnp.broadcast_to(gate, (LANES, rows)).T

    wg, wu, wd = wg_ref[...], wu_ref[...], wd_ref[...]
    kept = []
    for start in range(0, rows, chunk):
        at = slice(start, start + chunk)
        x, dy = x_ref[at, :], dy_ref[at, :]
        g = jnp.dot(x, wg, preferred_element_type=jnp.float32)
        u = jnp.dot(x, wu, preferred_element_type=jnp.float32)
        raw = lax.dot_general(dy, wd, NT, preferred_element_type=jnp.float32)
        square = g * g
        half = 0.5 + 0.5 * jnp.tanh(g * (GELU_A + (GELU_A * GELU_B) * square))
        gelu = g * half
        slope = half + 2.0 * gelu * (1.0 - half) * (GELU_A + (3.0 * GELU_A * GELU_B) * square)
        h = gelu * u
        product = raw * h
        total = product[:, :LANES]
        for column in range(LANES, product.shape[1], LANES):
            total = total + product[:, column : column + LANES]
        part_ref[at, :] += total
        dh = raw * gate_ref[at, :1]
        du = (dh * gelu).astype(jnp.bfloat16)
        dg = (dh * u * slope).astype(jnp.bfloat16)
        h_ref[at, :] = h.astype(jnp.bfloat16)
        dg_ref[at, :] = dg
        du_ref[at, :] = du
        kept.append((at, dg, du))
    for at, dg, du in kept:
        acc_ref[at, :] += lax.dot_general(dg, wg, NT, preferred_element_type=jnp.float32) + lax.dot_general(
            du, wu, NT, preferred_element_type=jnp.float32
        )

    @pl.when(step == pl.num_programs(0) - 1)
    def _():
        dx_ref[:rows, :] = acc_ref[...].astype(dx_ref.dtype)
        sums = jnp.sum(part_ref[...].T, axis=0, keepdims=True)
        high = sums.astype(jnp.bfloat16).astype(jnp.float32)
        middle = (sums - high).astype(jnp.bfloat16).astype(jnp.float32)
        line = lax.broadcasted_iota(jnp.int32, (EXTRA, rows), 0)
        lines = jnp.where(line == 0, high, jnp.where(line == 1, middle, jnp.where(line == 2, sums - high - middle, 0.0)))
        dx_ref[rows:, :] = jnp.zeros_like(dx_ref[rows:, :])
        dx_ref[rows:, :rows] = lines.astype(dx_ref.dtype)


def expert_block(at, count, x, dy, wgu, wd, earlier):
    rows, width = dy.shape
    hidden = wd.shape[0]
    tile = FF_TILE
    whole = jax.ShapeDtypeStruct((count * rows, hidden), jnp.bfloat16)
    fixed = lambda i, *_: (0, 0)
    out_block = pl.BlockSpec((rows, tile), lambda i, *_: (at, i))
    spec = pltpu.PrefetchScalarGridSpec(
        num_scalar_prefetch=1,
        grid=(hidden // tile,),
        in_specs=[
            pl.BlockSpec((rows + EXTRA, width), fixed),
            pl.BlockSpec((rows, width), fixed),
            pl.BlockSpec((width, tile), lambda i, *_: (0, i)),
            pl.BlockSpec((width, tile), lambda i, *_: (0, hidden // tile + i)),
            pl.BlockSpec((tile, width), lambda i, *_: (i, 0)),
        ]
        + [pl.BlockSpec(memory_space=pl.ANY)] * len(earlier),
        out_specs=[
            out_block,
            out_block,
            out_block,
            pl.BlockSpec((rows + EXTRA, width), fixed),
        ],
        scratch_shapes=[
            pltpu.VMEM((rows, LANES), jnp.float32),
            pltpu.VMEM((rows, width), jnp.float32),
            pltpu.VMEM((rows, LANES), jnp.float32),
        ],
    )
    return pl.pallas_call(
        expert_kernel,
        name="expert_block",
        out_shape=(
            whole,
            whole,
            whole,
            jax.ShapeDtypeStruct((rows + EXTRA, width), jnp.bfloat16),
        ),
        grid_spec=spec,
        input_output_aliases={6 + i: i for i in range(len(earlier))},
        compiler_params=pltpu.CompilerParams(dimension_semantics=("arbitrary",), vmem_limit_bytes=40 << 20),
        cost_estimate=pl.CostEstimate(
            flops=10 * rows * width * hidden, bytes_accessed=6 * width * hidden + 6 * rows * hidden, transcendentals=0
        ),
    )(jnp.zeros((1,), jnp.int32), x, dy, wgu, wgu, wd, *earlier)


EPS = 1e-06
FULL_PRECISION = lax.Precision.HIGHEST
ALL = ("z", "x", "exp")
SEQ = ("z", "x")
LOW = jnp.bfloat16


def dot32(a, b):
    return jnp.dot(a, b, preferred_element_type=jnp.float32)


def dot_nt(a, b):
    return lax.dot_general(a, b, NT, preferred_element_type=jnp.float32)


def dot_tn(a, b):
    return lax.dot_general(a, b, (((0,), (0,)), ((), ())), preferred_element_type=jnp.float32)


def partner(value, axis, offset):
    count = lax.axis_size(axis)
    return lax.ppermute(value, axis, [(i, i ^ offset) for i in range(count)])


def bits_of(count):
    return [1 << b for b in reversed(range(count.bit_length() - 1))]


def reorder(stacked, own):
    count = stacked.shape[0]
    return jnp.stack([lax.dynamic_index_in_dim(stacked, own ^ r, 0, keepdims=False) for r in range(count)])


def gather_double(value, steps):
    for axis, bit in steps:
        other = partner(value, axis, bit)
        high = (lax.axis_index(axis) & bit) != 0
        value = jnp.stack([jnp.where(high, other, value), jnp.where(high, value, other)])
    return value


def scatter_halve(value, steps):
    gone = []
    for axis, bit, dim in steps:
        at = dim - sum(1 for d in gone if d < dim)
        gone.append(dim)
        high = (lax.axis_index(axis) & bit) != 0
        low_half = lax.index_in_dim(value, 0, at, keepdims=False)
        high_half = lax.index_in_dim(value, 1, at, keepdims=False)
        keep = jnp.where(high, high_half, low_half)
        give = jnp.where(high, low_half, high_half)
        value = (keep.astype(jnp.float32) + partner(give, axis, bit).astype(jnp.float32)).astype(LOW)
    return value


def ring_of(groups, split):
    order = []
    for x in range(split):
        line = range(groups) if x % 2 == 0 else reversed(range(groups))
        order += [z * split + x for z in line]
    place = [order.index(s) for s in range(len(order))]
    ahead = [(order[i], order[(i + 1) % len(order)]) for i in range(len(order))]
    return jnp.asarray(order, jnp.int32), jnp.asarray(place, jnp.int32), ahead


def pick(values, index):
    return lax.dynamic_index_in_dim(values, index, 0, keepdims=False)


def unwritten(shape, dtype):
    return pl.pallas_call(
        lambda out_ref: None,
        name="unwritten",
        out_shape=jax.ShapeDtypeStruct(shape, dtype),
        out_specs=pl.BlockSpec(memory_space=pl.ANY),
    )()


class RingGather:
    def __init__(self, piece, groups, split, own):
        self.order, place, self.ahead = ring_of(groups, split)
        self.count = groups * split
        self.here = pick(place, own)
        self.rows = piece.shape[0]
        self.whole = unwritten((self.count * self.rows, piece.shape[1]), piece.dtype)
        self.whole = lax.dynamic_update_slice_in_dim(self.whole, piece, own * self.rows, 0)
        self.forward = self.backward = piece
        self.round = 0
        self.waiting = []

    def step(self):
        self.settle()
        self.round += 1
        k = self.round
        self.forward = lax.ppermute(self.forward, SEQ, self.ahead)
        self.waiting.append((self.forward, -k))
        if k < self.count - self.count // 2:
            self.backward = lax.ppermute(self.backward, SEQ, [(b, a) for a, b in self.ahead])
            self.waiting.append((self.backward, k))

    def settle(self):
        for piece, k in self.waiting:
            at = pick(self.order, (self.here + k + self.count) % self.count) * self.rows
            self.whole = lax.dynamic_update_slice_in_dim(self.whole, piece, at, 0)
        self.waiting = []

    def after(self, value):
        value, self.forward, self.backward = lax.optimization_barrier((value, self.forward, self.backward))
        self.waiting = [(self.forward if k < 0 else self.backward, k) for _, k in self.waiting]
        return value

    def finish(self):
        while self.round < self.count // 2:
            self.step()
        self.settle()
        return self.whole


class RingScatter:
    def __init__(self, totals, groups, split, own):
        self.order, place, self.ahead = ring_of(groups, split)
        self.count = groups * split
        self.here = pick(place, own)
        self.rows = totals[0].shape[0] // self.count
        self.totals = totals
        self.round = 0
        self.forward = self.backward = None

    def block(self, total, offset):
        at = pick(self.order, (self.here + offset + self.count) % self.count) * self.rows
        return lax.dynamic_slice_in_dim(total, at, self.rows, 0)

    def load(self, coming, offset):
        own = [self.block(total, offset) for total in self.totals]
        if coming is None:
            return own
        return [(a.astype(jnp.float32) + b.astype(jnp.float32)).astype(LOW) for a, b in zip(own, coming)]

    def step(self):
        self.round += 1
        k, far = self.round, self.count // 2
        near = self.count - 1 - far
        if k <= far:
            parts = self.load(self.forward, far - k + 1)
            self.forward = [lax.ppermute(part, SEQ, self.ahead) for part in parts]
        if k <= near:
            parts = self.load(self.backward, k - near - 1)
            self.backward = [lax.ppermute(part, SEQ, [(b, a) for a, b in self.ahead]) for part in parts]

    def after(self, value):
        value, self.forward, self.backward = lax.optimization_barrier((value, self.forward, self.backward))
        return value

    def finish(self):
        while self.round < self.count // 2:
            self.step()
        own = [self.block(total, 0).astype(jnp.float32) for total in self.totals]
        return [
            a + b.astype(jnp.float32) + c.astype(jnp.float32) for a, b, c in zip(own, self.forward, self.backward)
        ]


def norm_scale(value):
    return lax.rsqrt(jnp.mean(value * value, axis=-1, keepdims=True) + EPS)


def norm_back(scale, normed, gain, grad):
    scaled = grad * gain
    return scale * (scaled - normed * jnp.mean(scaled * normed, axis=-1, keepdims=True))


def split3(value):
    high = value.astype(LOW)
    rest = value - high.astype(jnp.float32)
    middle = rest.astype(LOW)
    return [high, middle, (rest - middle.astype(jnp.float32)).astype(LOW)]


def per_device(
    block_in,
    cotangent,
    segment_ids,
    expert_routes,
    pair_priority,
    gain_attention,
    w_query,
    w_key,
    w_value,
    w_out,
    bias_table,
    gain_experts,
    w_router,
    w_gate,
    w_up,
    w_down,
):
    groups, local_len, width = block_in.shape
    tokens = groups * local_len
    rows_own, hd = w_query.shape
    split = lax.axis_size("x")
    exp_count = lax.axis_size("exp")
    seq_count = groups * split
    length = local_len * seq_count
    x_at, z_at, e_at = lax.axis_index("x"), lax.axis_index("z"), lax.axis_index("exp")
    s_at = z_at * split + x_at
    head_width = hd // split
    heads_here = head_width // HEAD_DIM
    experts_all = w_router.shape[1]
    bias_own = bias_table.shape[0]
    tile = min(TILE, local_len)
    own = s_at.astype(jnp.int32).reshape(1)
    z_bits, x_bits, e_bits = bits_of(groups), bits_of(split), bits_of(exp_count)

    input_r = reorder(block_in, z_at)

    arrived = [[None] * split for _ in range(groups)]
    for rz in reversed(range(groups)):
        arrived[rz][0] = partner(input_r[rz], "z", rz) if rz else input_r[0]
    small = jnp.concatenate(
        [
            gain_attention[:, None],
            gain_experts[:, None],
            jnp.pad(bias_table, (0, rows_own - bias_own))[:, None],
            w_router,
        ],
        axis=1,
    )
    small = jnp.pad(small, ((0, 0), (0, LANES - small.shape[1]))).astype(LOW)
    share = jnp.stack(
        [part.astype(LOW).reshape(rows_own, split, head_width) for part in (w_query, w_key, w_value)], axis=2
    )
    share = share.reshape(rows_own, split, 3 * head_width).transpose(1, 0, 2)
    common = jnp.concatenate([w_out.astype(LOW), small], axis=1)
    share = jnp.concatenate([share, jnp.broadcast_to(common, (split,) + common.shape)], axis=2)
    shares = [lax.dynamic_index_in_dim(share, x_at ^ r, 0, keepdims=False) for r in range(split)]
    shares = [shares[0]] + [partner(shares[r], "x", r) for r in range(1, split)]
    by_x = reorder(jnp.stack(shares), x_at)
    for rx in range(1, split):
        arrived[0][rx] = partner(arrived[0][0], "x", rx)
    packed = gather_double(by_x, [("z", b) for b in z_bits])
    near = [arrived[rz][0] for rz in range(1, groups)]
    packed, near = lax.optimization_barrier((packed, near))
    for rz in range(1, groups):
        arrived[rz][0] = near[rz - 1]
        for rx in range(1, split):
            arrived[rz][rx] = partner(arrived[rz][0], "x", rx)
    packed = gather_double(packed, [("exp", b) for b in e_bits[:-1]])
    packed, arrived = lax.optimization_barrier((packed, arrived))
    sequence = jnp.stack([block for line in arrived for block in line]).reshape(length, width)

    gate_up_own = jnp.concatenate([w_gate[0].astype(LOW), w_up[0].astype(LOW)], axis=1)
    sequence, gate_up_own, down_own = lax.optimization_barrier((sequence, gate_up_own, w_down[0].astype(LOW)))
    down_w = lax.all_gather(down_own, SEQ, axis=0, tiled=True)
    gate_up_ring = RingGather(gate_up_own, groups, split, s_at)
    gate_up_ring.step()
    packed = gather_double(packed, [("exp", b) for b in e_bits[-1:]])
    ne, nz, nx = len(e_bits), len(z_bits), len(x_bits)
    packed = packed.transpose(
        tuple(ne + i for i in reversed(range(nz))) + (ne + nz,) + tuple(reversed(range(ne))) + (ne + nz + 1, ne + nz + 2)
    ).reshape(width, 3 * head_width + width + LANES)
    qkv_w, small_all = packed[:, : 3 * head_width], packed[:, 3 * head_width + width :]
    out_w = packed[:, 3 * head_width : 3 * head_width + width]
    gain_one = small_all[:, 0].astype(jnp.float32)
    gain_two = small_all[:, 1].astype(jnp.float32)
    table_all = small_all[:, 2].reshape(-1, rows_own)[:, :bias_own].reshape(-1, BUCKETS)
    router_t = small_all[:, 3 : 3 + experts_all].T
    table_rows = lax.dynamic_slice_in_dim(table_all, x_at * heads_here, heads_here, 0)

    routes = expert_routes.reshape(tokens, -1)
    top_count = routes.shape[1]
    priority = pair_priority.reshape(-1)
    pair_experts = routes.reshape(-1)
    ahead = (pair_experts[None, :] == pair_experts[:, None]) & (priority[None, :] < priority[:, None])
    slots = jnp.sum(ahead.astype(jnp.int32), axis=1)
    capacity = (5 * top_count * tokens + 4 * experts_all - 1) // (4 * experts_all)
    slot_count = experts_all * capacity
    slot_index = jnp.where(slots < capacity, (pair_experts ^ e_at) * capacity + slots, slot_count)
    slot_index = slot_index.reshape(tokens, top_count)
    every_slot = jnp.arange(slot_count, dtype=jnp.int32)[None, :]
    table = sum((slot_index[:, k : k + 1] == every_slot).astype(LOW) for k in range(top_count))
    tables = [table[:, r * capacity : (r + 1) * capacity] for r in range(exp_count)]
    grad_low = cotangent.reshape(tokens, width)
    grad_slots = [dot_tn(part, grad_low).astype(LOW) for part in tables]

    wide = sequence.astype(jnp.float32)
    normed_one = (wide * norm_scale(wide) * gain_one).astype(LOW)
    qkv = dot32(normed_one, qkv_w).astype(LOW)
    qkv, grad_slots = lax.optimization_barrier((qkv, grad_slots))
    qkv = gate_up_ring.after(qkv)
    gate_up_ring.step()
    grad_slots = [grad_slots[0]] + [partner(grad_slots[r], "exp", r) for r in range(1, exp_count)]
    segments = lax.dynamic_index_in_dim(segment_ids, z_at, 0, keepdims=False)
    ranges = tile_ranges(segments, tile)
    seg_blocks = segments.reshape(seq_count, local_len)
    query_side, key_side = segment_columns(reorder(seg_blocks, s_at).reshape(length))
    rows = bias_rows(table_rows, tile)
    ends = jnp.stack([table_rows[:, 15], table_rows[:, 31]], axis=1).astype(jnp.float32)
    contexts, log_totals = attend_forward(qkv, query_side, key_side, ranges, rows, ends, own, tile)
    contexts = gate_up_ring.after(contexts)
    contexts, grad_slots = lax.optimization_barrier((contexts, grad_slots))
    gate_up_w = gate_up_ring.finish()

    def exchange_positions(blocks):
        return lax.all_to_all(blocks, SEQ, split_axis=0, concat_axis=0, tiled=True)

    context_local = exchange_positions(contexts.reshape(seq_count, local_len, head_width))
    context_local = (
        context_local.reshape(groups, split, local_len, head_width).transpose(0, 2, 1, 3).reshape(tokens, hd)
    )
    inputs = block_in.astype(jnp.float32).reshape(tokens, width)
    mid = inputs + dot32(context_local, out_w)
    scale_two = norm_scale(mid)
    normed_two = (mid * scale_two * gain_two).astype(LOW)

    logits = dot_nt(router_t, normed_two)
    exponent = jnp.exp(logits - jnp.max(logits, axis=0, keepdims=True))
    probabilities = exponent / jnp.sum(exponent, axis=0, keepdims=True)
    expert_ids = jnp.arange(experts_all, dtype=jnp.int32)[:, None]
    chosen = sum((routes[:, k][None, :] == expert_ids).astype(jnp.float32) for k in range(top_count))
    chosen_total = jnp.sum(probabilities * chosen, axis=0, keepdims=True)
    gates = probabilities * chosen / chosen_total
    gates_r = reorder(gates, e_at)

    gate_slots = jnp.sum(
        table.astype(jnp.float32).reshape(tokens, exp_count, capacity) * gates_r.T[:, :, None], axis=0
    )
    gate_lines = jnp.pad(jnp.stack(split3(gate_slots), axis=1), ((0, 0), (0, EXTRA - 3), (0, width - capacity)))

    def values_below(rows_):
        return jnp.sum(rows_[capacity : capacity + 3, :capacity].astype(jnp.float32), axis=0)

    sent = [None] * exp_count
    for r in reversed(range(exp_count)):
        sent[r] = jnp.concatenate([dot_tn(tables[r], normed_two).astype(LOW), gate_lines[r]], axis=0)
        if r:
            sent[r] = partner(sent[r], "exp", r)

    earlier = ()
    back = [None] * exp_count
    turns = [0] + list(range(2, exp_count)) + [1]
    for turn, r in enumerate(turns):
        if turn >= 3:
            ready = turns[turn - 2]
            sent[r], back[ready] = lax.optimization_barrier((sent[r], back[ready]))
        hidden, gate_low, up_low, dx = expert_block(
            r, exp_count, sent[r], grad_slots[r], gate_up_w, down_w, earlier
        )
        earlier = (hidden, gate_low, up_low)
        back[r] = partner(dx, "exp", r) if r else dx

    sent, hidden = lax.optimization_barrier((sent, hidden))
    slot_rows = jnp.concatenate([rows_[:capacity] for rows_ in sent], axis=0)
    slot_gates = jnp.concatenate([values_below(rows_) for rows_ in sent], axis=0)[:, None]
    slot_grads = (slot_gates * jnp.concatenate(grad_slots, axis=0).astype(jnp.float32)).astype(LOW)

    gate_grad = jnp.sum(
        table.astype(jnp.float32).reshape(tokens, exp_count, capacity) * jnp.stack([values_below(rows_) for rows_ in back])[None], axis=2
    )
    gate_grad = reorder(gate_grad.T, e_at)
    chosen_grad = chosen * (gate_grad - jnp.sum(gates * gate_grad, axis=0, keepdims=True)) / chosen_total
    logit_grad = probabilities * (chosen_grad - jnp.sum(probabilities * chosen_grad, axis=0, keepdims=True))
    logit_pieces = jnp.concatenate(split3(logit_grad), axis=0)
    router_sum = jnp.sum(dot32(logit_pieces, normed_two).reshape(3, experts_all, width), axis=0)
    normed_two_grad = dot_tn(logit_pieces, jnp.concatenate([router_t] * 3, axis=0))
    for r in range(exp_count):
        normed_two_grad = normed_two_grad + dot32(tables[r], back[r][:capacity])
    unit_two = mid * scale_two
    gain_two_sum = jnp.sum(normed_two_grad * unit_two, axis=0)
    grad_out = grad_low.astype(jnp.float32)
    mid_grad = grad_out + norm_back(scale_two, unit_two, gain_two, normed_two_grad)
    attention_grad = mid_grad.astype(LOW)
    context_grad = dot_nt(attention_grad, out_w).astype(LOW)
    context_grad, up_low, gate_low = lax.optimization_barrier((context_grad, up_low, gate_low))
    gate_sum = dot_tn(slot_rows, gate_low).astype(LOW)
    up_sum = dot_tn(slot_rows, up_low).astype(LOW)
    context_grad = (
        context_grad.reshape(groups, local_len, split, head_width)
        .transpose(0, 2, 1, 3)
        .reshape(seq_count, local_len, head_width)
    )
    context_heads = exchange_positions(context_grad).reshape(length, head_width)

    def scatter_experts(total):
        return lax.psum_scatter(total, SEQ, scatter_dimension=0, tiled=True)

    context_heads, gate_sum, up_sum = lax.optimization_barrier((context_heads, gate_sum, up_sum))

    halving = [("exp", b, 1 + nz + nx + ne - 1 - i) for i, b in enumerate(reversed(e_bits))]
    halving += [("z", b, 1 + nz - 1 - i) for i, b in enumerate(reversed(z_bits))]
    out_sum = dot_tn(context_local, attention_grad).astype(LOW)

    ring = RingScatter([gate_sum, up_sum], groups, split, s_at)
    grads, diag, far = (), [], []
    pairs = head_width // LANES
    for pair in range(pairs):
        ring.step()
        *grads, pair_diag, pair_far = attend_backward(
            pair, qkv, context_heads, contexts, log_totals, query_side, key_side, ranges, rows, ends, own, tile, tuple(grads)
        )
        grads = ring.after(grads)
        if pair == 0:
            grads, hidden = lax.optimization_barrier((grads, hidden))
            down_sum = dot_tn(hidden, slot_grads).astype(LOW)
            down_owned = scatter_experts(down_sum)
        if pair == min(1, pairs - 1):
            grads, hidden, down_sum = lax.optimization_barrier((grads, hidden, down_sum))
            expert_out = (slot_gates * dot32(hidden, down_w)).astype(LOW)
            expert_out = reorder(expert_out.reshape(exp_count, capacity, width), e_at)
            returned = lax.all_to_all(expert_out, "exp", split_axis=0, concat_axis=0, tiled=True)
        if pair == min(2, pairs - 1):
            grads, expert_out = lax.optimization_barrier((grads, expert_out))
        if pair == pairs - 1:
            grads, returned = lax.optimization_barrier((grads, returned))
        diag.append(pair_diag)
        far.append(pair_far)
    diag, far = jnp.concatenate(diag), jnp.concatenate(far)
    query_back, key_back, value_back, down_owned = lax.optimization_barrier((*grads, down_owned))
    gate_owned, up_owned = ring.finish()
    table_local = bucket_sums(diag, far, tile)

    def through(grads, part):
        return dot_nt(grads, qkv_w[:, part * head_width : (part + 1) * head_width])

    out_parts = width // head_width
    weight_sum = jnp.stack(
        [dot_tn(normed_one, grads).astype(LOW) for grads in (query_back, key_back, value_back)]
        + [out_sum[:, i * head_width : (i + 1) * head_width] for i in range(out_parts)]
    )
    weight_sum, query_back, key_back, value_back = lax.optimization_barrier(
        (weight_sum, query_back, key_back, value_back)
    )
    normed_part = through(query_back, 0) + through(key_back, 1) + through(value_back, 2)
    half = width // 2
    normed_part = normed_part.reshape(groups, split, local_len, width)

    sides = [normed_part[:, rx].astype(LOW) for rx in range(1, split)]
    first = [partner(side[:, :, :half], "x", rx) for rx, side in enumerate(sides, 1)]
    first, rest = lax.optimization_barrier((first, [side[:, :, half:] for side in sides]))

    def send_back(own_part, coming):
        total = own_part + sum(part.astype(jnp.float32) for part in coming)
        total = reorder(total.astype(LOW), z_at)
        return lax.all_to_all(total, "z", split_axis=0, concat_axis=0, tiled=True)

    normed_first = send_back(normed_part[:, 0, :, :half], first)
    rest = [partner(side, "x", rx) for rx, side in enumerate(rest, 1)]
    normed_second = send_back(normed_part[:, 0, :, half:], rest)
    weight_part = scatter_halve(
        weight_sum.reshape((3 + out_parts,) + (2,) * (nz + nx + ne) + (rows_own, head_width)), halving[:ne]
    )
    weight_part = scatter_halve(weight_part, halving[ne:]).reshape(3 + out_parts, split, rows_own, head_width)
    weight_own = [lax.dynamic_index_in_dim(weight_part, x_at ^ r, 1, keepdims=False) for r in range(split)]
    weight_own = [weight_own[0]] + [partner(weight_own[r], "x", r) for r in range(1, split)]
    normed_second, weight_own = lax.optimization_barrier((normed_second, weight_own))
    block_out = (mid + dot32(table, reorder(returned, e_at).reshape(slot_count, width))).astype(LOW)

    block_out = block_out.reshape(groups, local_len, width)
    out_w_out = sum(part[3:].astype(jnp.float32) for part in weight_own)
    out_w_out = out_w_out.transpose(1, 0, 2).reshape(rows_own, width)
    qkv_own = reorder(jnp.stack([part[:3] for part in weight_own]), x_at)
    qkv_own = qkv_own.transpose(1, 2, 0, 3).reshape(3, rows_own, hd).astype(jnp.float32)

    normed_one_grad = jnp.concatenate([normed_first, normed_second], axis=2).astype(jnp.float32).reshape(tokens, width)
    scale_one = norm_scale(inputs)
    unit_one = inputs * scale_one
    gain_one_sum = jnp.sum(normed_one_grad * unit_one, axis=0)
    block_in_grad = (mid_grad + norm_back(scale_one, unit_one, gain_one, normed_one_grad)).reshape(
        groups, local_len, width
    )

    table_sum = lax.dynamic_update_slice_in_dim(
        jnp.zeros(table_all.shape, jnp.float32), table_local, x_at * heads_here, 0
    ).reshape(-1, bias_own)
    table_sum = jnp.pad(table_sum, ((0, 0), (0, rows_own - bias_own)))[:, None, :]
    little = jnp.concatenate(
        [
            gain_one_sum.reshape(-1, 1, rows_own),
            gain_two_sum.reshape(-1, 1, rows_own),
            table_sum,
            router_sum.reshape(experts_all, -1, rows_own).transpose(1, 0, 2),
        ],
        axis=1,
    )
    little = jnp.sum(lax.all_to_all(little, ALL, split_axis=0, concat_axis=0, tiled=True), axis=0)
    return (
        block_out,
        block_in_grad,
        little[0],
        qkv_own[0],
        qkv_own[1],
        qkv_own[2],
        out_w_out,
        little[2, :bias_own],
        little[1],
        little[3:].T,
        gate_owned.astype(jnp.float32)[None],
        up_owned.astype(jnp.float32)[None],
        down_owned.astype(jnp.float32)[None],
    )


def solution(mesh):
    def run(*args):
        groups = args[0].shape[0] // mesh.shape["exp"]
        seq_count, exp_count = mesh.shape["seq"], mesh.shape["exp"]
        grid = mesh.devices.reshape(groups, seq_count // groups, exp_count)
        fine = jax.sharding.Mesh(grid, ALL)
        placed = P("exp", SEQ, None)
        whole = P(ALL)
        matrix = P(ALL, None)
        return jax.shard_map(
            per_device,
            mesh=fine,
            in_specs=(
                placed, placed, P("exp", None), placed, placed,
                whole, matrix, matrix, matrix, matrix, whole, whole, matrix,
                placed, placed, placed,
            ),
            out_specs=(
                placed, placed, whole, matrix, matrix, matrix, matrix, whole, whole, matrix,
                placed, placed, placed,
            ),
            check_vma=False,
        )(*args)

    return run
```

```python
from functools import partial

import jax
import jax.numpy as jnp
import numpy as np
from jax import lax
from jax.experimental import pallas as pl
from jax.experimental.pallas import tpu as pltpu
from jax.sharding import PartitionSpec as P

HEAD_DIM = 64
BUCKETS = 32
THRESHOLDS = (12, 16, 23, 32, 46, 64, 91)
MASKED = -1e30
TILE = 256
LANES = 128
NT = (((1,), (1,)), ((), ()))


def bucket_of(d):
    a = np.abs(d)
    extra = sum((a >= t).astype(np.int64) for t in THRESHOLDS)
    return np.where(a < 8, a, 8 + extra) + 16 * (d > 0)


def bias_rows(table_rows, tile):
    u = np.arange(2 * tile)
    x = np.where(u < tile, u, u - 2 * tile)
    ids = np.stack([bucket_of(step * tile - x) for step in (-1, 0, 1)])
    hot = (ids.reshape(-1)[None, :] == np.arange(BUCKETS)[:, None]).astype(np.float32)
    rows = jnp.dot(table_rows.astype(jnp.bfloat16), jnp.asarray(hot, jnp.bfloat16), preferred_element_type=jnp.float32)
    return rows.reshape(table_rows.shape[0], 3, 2 * tile)


def tile_ranges(segments, tile):
    blocks = segments.reshape(-1, tile)
    first, last = blocks[:, 0], blocks[:, -1]
    low = jnp.sum((last[None, :] < first[:, None]).astype(jnp.int32), axis=1)
    high = jnp.sum((first[None, :] <= last[:, None]).astype(jnp.int32), axis=1)
    return jnp.stack([low, high])


def segment_columns(segments):
    lane = jnp.arange(LANES, dtype=jnp.int32)[None, :]
    seg = segments[:, None]
    same = seg == lane
    query_side = jnp.where(same & (lane < 4), MASKED, 0.0).astype(jnp.bfloat16)
    key_side = jnp.where(lane < 4, (~same).astype(jnp.float32), (lane < 9).astype(jnp.float32)).astype(jnp.bfloat16)
    return query_side, key_side


def toeplitz(row, tile):
    wide = jnp.broadcast_to(row, (tile, row.shape[1]))
    return pltpu.roll(wide, 0, 1, stride=1, stride_axis=0)[:, :tile]


def block_at(index, own, tile):
    return pl.ds(pl.multiple_of((index ^ own[0]) * tile, tile), tile)


def fwd_kernel(ranges, ends, own, q_ref, k_ref, v_ref, qs_ref, ks_ref, rows_ref, o_ref, lse_ref, bias_ref, vt_ref):
    group, qb = pl.program_id(0), pl.program_id(1)
    tile, span = q_ref.shape
    heads = span // HEAD_DIM

    @pl.when(qb == 0)
    def _():
        for h in range(heads):
            for step in range(3):
                bias_ref[h, step] = toeplitz(rows_ref[h, step : step + 1, :], tile)
        for start in range(0, v_ref.shape[0], tile):
            vt_ref[:, start : start + tile] = v_ref[start : start + tile, :].T

    low, high = ranges[0, qb], ranges[1, qb]
    lane = lax.broadcasted_iota(jnp.int32, (tile, LANES), 1)
    q = q_ref[...] * jnp.bfloat16(HEAD_DIM**-0.5)
    qs = qs_ref[...]
    halves = []
    for h in range(heads):
        part = q[:, h // 2 * LANES : (h // 2 + 1) * LANES]
        keep = (lane < HEAD_DIM) if h % 2 == 0 else (lane >= HEAD_DIM)
        halves.append(jnp.where(keep, part, jnp.zeros_like(part)))

    def side(h, which):
        if which == 1:
            extra = qs
        else:
            value = ends[heads * group + h, which // 2].astype(jnp.bfloat16)
            extra = jnp.where(lane == 7, value, qs)
        return jnp.concatenate([halves[h], extra], axis=1)

    def visit(which):
        queries = [side(h, which) for h in range(heads)]

        def step(kb, carry):
            keys = block_at(kb, own, tile)
            ks = ks_ref[keys, :]
            scores = []
            for h in range(heads):
                kx = jnp.concatenate([k_ref[keys, h // 2 * LANES : (h // 2 + 1) * LANES], ks], axis=1)
                scores.append(lax.dot_general(kx, queries[h], NT, preferred_element_type=jnp.float32))
            out = []
            for h in range(heads):
                peak, total, acc = carry[h]
                s = scores[h]
                if which == 1:
                    s = s + bias_ref[h, kb - qb + 1]
                new = jnp.maximum(peak, jnp.max(s, axis=0, keepdims=True))
                p = jnp.exp(s - new)
                scale = jnp.exp(peak - new)
                total = total * scale + jnp.sum(p, axis=0, keepdims=True)
                vt = vt_ref[h * HEAD_DIM : (h + 1) * HEAD_DIM, keys]
                acc = acc * scale + jnp.dot(vt, p.astype(jnp.bfloat16), preferred_element_type=jnp.float32)
                out.append((new, total, acc))
            return tuple(out)

        return step

    start = tuple(
        (
            jnp.full((1, tile), -3e38, jnp.float32),
            jnp.zeros((1, tile), jnp.float32),
            jnp.zeros((HEAD_DIM, tile), jnp.float32),
        )
        for _ in range(heads)
    )
    near_low, near_high = jnp.maximum(low, qb - 1), jnp.minimum(high, qb + 2)
    state = lax.fori_loop(near_low, near_high, visit(1), start)
    state = lax.fori_loop(low, near_low, visit(0), state)
    state = lax.fori_loop(near_high, high, visit(2), state)
    outs = []
    for h in range(heads):
        peak, total, acc = state[h]
        outs.append(acc / total)
        lse_ref[h // 2, h % 2 : h % 2 + 1, :] = peak + jnp.log(total)
    o_ref[...] = jnp.concatenate(outs, axis=0).T.astype(o_ref.dtype)


FWD_PAIRS = 4


def attend_forward(qkv, qs, ks, ranges, rows, ends, own, tile):
    length, width = qkv.shape[0], qkv.shape[1] // 3
    pairs = width // LANES
    together = FWD_PAIRS if pairs % FWD_PAIRS == 0 else 1
    span = together * LANES
    tiles = length // tile
    spec = pltpu.PrefetchScalarGridSpec(
        num_scalar_prefetch=3,
        grid=(pairs // together, tiles),
        in_specs=[
            pl.BlockSpec((tile, span), lambda p, i, r, e, own: (i ^ own[0], p)),
            pl.BlockSpec((length, span), lambda p, i, *_: (0, width // span + p)),
            pl.BlockSpec((length, span), lambda p, i, *_: (0, 2 * (width // span) + p)),
            pl.BlockSpec((tile, LANES), lambda p, i, r, e, own: (i ^ own[0], 0)),
            pl.BlockSpec((length, LANES), lambda p, i, *_: (0, 0)),
            pl.BlockSpec((2 * together, 3, 2 * tile), lambda p, i, *_: (p, 0, 0)),
        ],
        out_specs=[
            pl.BlockSpec((tile, span), lambda p, i, *_: (i, p)),
            pl.BlockSpec((together, 2, tile), lambda p, i, *_: (p, 0, i)),
        ],
        scratch_shapes=[
            pltpu.VMEM((2 * together, 3, tile, tile), jnp.float32),
            pltpu.VMEM((span, length), jnp.bfloat16),
        ],
    )
    return pl.pallas_call(
        fwd_kernel,
        name="attend_forward",
        out_shape=(
            jax.ShapeDtypeStruct((length, width), jnp.bfloat16),
            jax.ShapeDtypeStruct((pairs, 2, length), jnp.float32),
        ),
        grid_spec=spec,
        compiler_params=pltpu.CompilerParams(
            dimension_semantics=("arbitrary", "arbitrary"), vmem_limit_bytes=48 << 20
        ),
        cost_estimate=pl.CostEstimate(flops=length * length * width * 4, bytes_accessed=length * width * 8, transcendentals=0),
    )(ranges, ends, own, qkv, qkv, qkv, qs, ks, rows)


def pieces(row):
    high = row.astype(jnp.bfloat16).astype(jnp.float32)
    mid = (row - high).astype(jnp.bfloat16).astype(jnp.float32)
    return high, mid, row - high - mid


def bwd_kernel(ranges, ends, own, q_ref, k_ref, v_ref, do_ref, o_ref, lse_ref, qs_ref, ks_ref, rows_ref, *refs):
    (dq_ref, dk_ref, dv_ref, diag_ref, far_ref,
     qx_ref, dox_ref, kt_ref, bias_ref, dsum_ref, fsum_ref, dqt_ref, dka_ref, dva_ref) = refs[-14:]
    pair = own[1]
    length = q_ref.shape[0]
    tile = bias_ref.shape[2]
    tiles = length // tile
    for h in range(2):
        for step in range(3):
            bias_ref[h, step] = toeplitz(rows_ref[h, step : step + 1, :], tile)
    dsum_ref[...] = jnp.zeros_like(dsum_ref)
    fsum_ref[...] = jnp.zeros_like(fsum_ref)
    dqt_ref[...] = jnp.zeros_like(dqt_ref)
    lane = lax.broadcasted_iota(jnp.int32, (tile, LANES), 1)
    sub = lax.broadcasted_iota(jnp.int32, (LANES, tile), 0)
    pick = (lax.broadcasted_iota(jnp.int32, (8, LANES), 1) // HEAD_DIM == lax.broadcasted_iota(jnp.int32, (8, LANES), 0)).astype(jnp.float32)

    @pl.loop(0, tiles)
    def _(i):
        line = pl.ds(pl.multiple_of(i * tile, tile), tile)
        at = block_at(i, own, tile)
        q = q_ref[at, :] * jnp.bfloat16(HEAD_DIM**-0.5)
        do = do_ref[line, :]
        zero = jnp.zeros_like(q)
        product = do.astype(jnp.float32) * o_ref[line, :].astype(jnp.float32)
        delta = lax.dot_general(pick, product, NT, precision=lax.Precision.HIGHEST, preferred_element_type=jnp.float32)
        kt_ref[:, at] = k_ref[at, :].T
        for h in range(2):
            keep = (lane < HEAD_DIM) if h == 0 else (lane >= HEAD_DIM)
            a, b, c = pieces(-lse_ref[0, h : h + 1, line])
            extra = jnp.where(sub == 4, a, jnp.where(sub == 5, b, jnp.where(sub == 6, c, 0.0)))
            extra = extra.T.astype(jnp.bfloat16) + qs_ref[at, :]
            left, right = ends[2 * pair + h, 0].astype(jnp.bfloat16), ends[2 * pair + h, 1].astype(jnp.bfloat16)
            extra = jnp.where(lane == 7, left, jnp.where(lane == 8, right, extra))
            qx_ref[h, at, :] = jnp.concatenate([jnp.where(keep, q, zero), extra], axis=1)
            a, b, c = pieces(-delta[h : h + 1, :])
            extra = jnp.where(sub == 4, a, jnp.where(sub == 5, b, jnp.where(sub == 6, c, 0.0)))
            dox_ref[h, at, :] = jnp.concatenate([jnp.where(keep, do, zero), extra.T.astype(jnp.bfloat16)], axis=1)

    ones3 = ((lane >= 4) & (lane < 7)).astype(jnp.bfloat16)

    @pl.loop(0, tiles)
    def _(kb):
        low, high = ranges[0, kb], ranges[1, kb]
        keys = block_at(kb, own, tile)
        k, ks = k_ref[keys, :], ks_ref[keys, :]
        vx = jnp.concatenate([v_ref[keys, :], ones3], axis=1)
        nil = jnp.zeros_like(ks)
        dka_ref[...] = jnp.zeros_like(dka_ref)
        dva_ref[...] = jnp.zeros_like(dva_ref)

        def visit(which):
            if which == 0:
                extra = jnp.where(lane == 8, nil, ks)
            elif which == 2:
                extra = jnp.where(lane == 7, nil, ks)
            else:
                extra = jnp.where((lane == 7) | (lane == 8), nil, ks)
            kx = jnp.concatenate([k, extra], axis=1)

            def step(qb, carry):
                at = block_at(qb, own, tile)
                weights, grads = [], []
                for h in range(2):
                    qx, dox = qx_ref[h, at, :], dox_ref[h, at, :]
                    s = lax.dot_general(kx, qx, NT, preferred_element_type=jnp.float32)
                    if which == 1:
                        s = s + bias_ref[h, kb - qb + 1]
                    p = jnp.exp(s)
                    dp = lax.dot_general(vx, dox, NT, preferred_element_type=jnp.float32)
                    ds = p * dp
                    if which == 1:
                        dsum_ref[h, kb - qb + 1] += ds
                    else:
                        fsum_ref[h, which // 2] += jnp.sum(ds.reshape(tile // 8, 8, tile), axis=0)
                    weights.append(p.astype(jnp.bfloat16))
                    grads.append(ds.astype(jnp.bfloat16))
                    rows = slice(h * HEAD_DIM, (h + 1) * HEAD_DIM)
                    dqt_ref[rows, at] += jnp.dot(kt_ref[rows, keys], grads[h], preferred_element_type=jnp.float32)
                both_do = jnp.concatenate([dox_ref[0, at, :LANES], dox_ref[1, at, :LANES]], axis=0)
                both_q = jnp.concatenate([qx_ref[0, at, :LANES], qx_ref[1, at, :LANES]], axis=0)
                dva_ref[...] += jnp.dot(jnp.concatenate(weights, axis=1), both_do, preferred_element_type=jnp.float32)
                dka_ref[...] += jnp.dot(jnp.concatenate(grads, axis=1), both_q, preferred_element_type=jnp.float32)
                return carry

            return step

        near_low, near_high = jnp.maximum(low, kb - 1), jnp.minimum(high, kb + 2)
        lax.fori_loop(near_low, near_high, visit(1), 0)
        lax.fori_loop(near_high, high, visit(0), 0)
        lax.fori_loop(low, near_low, visit(2), 0)
        dk_ref[keys, :] = dka_ref[...].astype(dk_ref.dtype)
        dv_ref[keys, :] = dva_ref[...].astype(dv_ref.dtype)

    @pl.loop(0, tiles)
    def _(i):
        at = pl.ds(pl.multiple_of(i * tile, tile), tile)
        dq_ref[at, :] = (dqt_ref[:, at] * HEAD_DIM**-0.5).T.astype(dq_ref.dtype)

    for h in range(2):
        for step in range(3):
            diag_ref[h, step : step + 1, :] = diagonals(dsum_ref, h, step, tile)
        for step in range(2):
            total = jnp.sum(fsum_ref[h, step], axis=0, keepdims=True)
            far_ref[h, step : step + 1, :] = total


def diagonals(dsum_ref, h, step, tile):
    width = 2 * tile
    acc = jnp.zeros((8, width), jnp.float32)
    for group in range(tile // 8):
        part = dsum_ref[h, step, group * 8 : (group + 1) * 8, :]
        part = jnp.concatenate([part, jnp.zeros((8, tile), jnp.float32)], axis=1)
        acc = acc + (pltpu.roll(part, width - 8 * group, 1) if group else part)
    row = lax.broadcasted_iota(jnp.int32, (8, width), 0)
    for bit in (1, 2, 4):
        acc = jnp.where((row & bit) != 0, pltpu.roll(acc, width - bit, 1), acc)
    return jnp.sum(acc, axis=0, keepdims=True)


def attend_backward(pair, qkv, do, o, lse, qs, ks, ranges, rows, ends, own, tile, earlier):
    length, width = do.shape
    pairs = width // LANES
    own = jnp.concatenate([own, jnp.full((1,), pair, jnp.int32)])
    column = pl.BlockSpec((length, LANES), lambda p, r, e, own: (0, own[1]))
    fixed = pl.BlockSpec((length, LANES), lambda p, *_: (0, 0))
    spec = pltpu.PrefetchScalarGridSpec(
        num_scalar_prefetch=3,
        grid=(1,),
        in_specs=[
            column,
            pl.BlockSpec((length, LANES), lambda p, r, e, own: (0, pairs + own[1])),
            pl.BlockSpec((length, LANES), lambda p, r, e, own: (0, 2 * pairs + own[1])),
            column,
            column,
            pl.BlockSpec((1, 2, length), lambda p, r, e, own: (own[1], 0, 0)),
            fixed, fixed,
            pl.BlockSpec((2, 3, 2 * tile), lambda p, r, e, own: (own[1], 0, 0)),
        ]
        + [pl.BlockSpec(memory_space=pl.ANY)] * len(earlier),
        out_specs=[
            column, column, column,
            pl.BlockSpec((2, 3, 2 * tile), lambda p, *_: (p, 0, 0)),
            pl.BlockSpec((2, 2, tile), lambda p, *_: (p, 0, 0)),
        ],
        scratch_shapes=[
            pltpu.VMEM((2, length, 2 * LANES), jnp.bfloat16),
            pltpu.VMEM((2, length, 2 * LANES), jnp.bfloat16),
            pltpu.VMEM((LANES, length), jnp.bfloat16),
            pltpu.VMEM((2, 3, tile, tile), jnp.float32),
            pltpu.VMEM((2, 3, tile, tile), jnp.float32),
            pltpu.VMEM((2, 2, 8, tile), jnp.float32),
            pltpu.VMEM((LANES, length), jnp.float32),
            pltpu.VMEM((tile, LANES), jnp.float32),
            pltpu.VMEM((tile, LANES), jnp.float32),
        ],
    )
    low = jax.ShapeDtypeStruct((length, width), jnp.bfloat16)
    return pl.pallas_call(
        bwd_kernel,
        name="attend_backward",
        out_shape=(
            low, low, low,
            jax.ShapeDtypeStruct((2, 3, 2 * tile), jnp.float32),
            jax.ShapeDtypeStruct((2, 2, tile), jnp.float32),
        ),
        grid_spec=spec,
        input_output_aliases={12 + i: i for i in range(len(earlier))},
        compiler_params=pltpu.CompilerParams(
            dimension_semantics=("arbitrary",), vmem_limit_bytes=40 << 20
        ),
        cost_estimate=pl.CostEstimate(flops=length * length * LANES * 10, bytes_accessed=length * LANES * 16, transcendentals=0),
    )(ranges, ends, own, qkv, qkv, qkv, do, o, lse, qs, ks, rows, *earlier)


def bucket_sums(diag, far, tile):
    u = np.arange(2 * tile)
    x = np.where(u < tile, u, u - 2 * tile)
    ids = np.stack([bucket_of(step * tile - x) for step in (-1, 0, 1)])
    hot = (ids.reshape(-1)[:, None] == np.arange(BUCKETS)[None, :]).astype(np.float32)
    sums = jnp.dot(diag.reshape(diag.shape[0], -1), jnp.asarray(hot), precision=lax.Precision.HIGHEST)
    outer = jnp.sum(far, axis=2)
    ends = np.zeros((2, BUCKETS), np.float32)
    ends[0, 15] = 1
    ends[1, 31] = 1
    return sums + outer[:, 0:1] * ends[0] + outer[:, 1:2] * ends[1]


GELU_A, GELU_B = 0.7978845608028654, 0.044715
FF_TILE = 256
EXTRA = 16


def expert_kernel(own_ref, x_ref, dy_ref, wg_ref, wu_ref, wd_ref, *refs):
    h_ref, dg_ref, du_ref, dx_ref, part_ref, acc_ref, gate_ref = refs[-7:]
    step = pl.program_id(0)
    rows = dy_ref.shape[0]
    chunk = rows // 2 if rows % 32 == 0 else rows

    @pl.when(step == 0)
    def _():
        acc_ref[...] = jnp.zeros_like(acc_ref)
        part_ref[...] = jnp.zeros_like(part_ref)
        lines = x_ref[rows:, :rows].astype(jnp.float32)
        gate = jnp.sum(lines, axis=0, keepdims=True)
        gate_ref[...] = jnp.broadcast_to(gate, (LANES, rows)).T

    wg, wu, wd = wg_ref[...], wu_ref[...], wd_ref[...]
    kept = []
    for start in range(0, rows, chunk):
        at = slice(start, start + chunk)
        x, dy = x_ref[at, :], dy_ref[at, :]
        g = jnp.dot(x, wg, preferred_element_type=jnp.float32)
        u = jnp.dot(x, wu, preferred_element_type=jnp.float32)
        raw = lax.dot_general(dy, wd, NT, preferred_element_type=jnp.float32)
        square = g * g
        half = 0.5 + 0.5 * jnp.tanh(g * (GELU_A + (GELU_A * GELU_B) * square))
        gelu = g * half
        slope = half + 2.0 * gelu * (1.0 - half) * (GELU_A + (3.0 * GELU_A * GELU_B) * square)
        h = gelu * u
        product = raw * h
        total = product[:, :LANES]
        for column in range(LANES, product.shape[1], LANES):
            total = total + product[:, column : column + LANES]
        part_ref[at, :] += total
        dh = raw * gate_ref[at, :1]
        du = (dh * gelu).astype(jnp.bfloat16)
        dg = (dh * u * slope).astype(jnp.bfloat16)
        h_ref[at, :] = h.astype(jnp.bfloat16)
        dg_ref[at, :] = dg
        du_ref[at, :] = du
        kept.append((at, dg, du))
    for at, dg, du in kept:
        acc_ref[at, :] += lax.dot_general(dg, wg, NT, preferred_element_type=jnp.float32) + lax.dot_general(
            du, wu, NT, preferred_element_type=jnp.float32
        )

    @pl.when(step == pl.num_programs(0) - 1)
    def _():
        dx_ref[:rows, :] = acc_ref[...].astype(dx_ref.dtype)
        sums = jnp.sum(part_ref[...].T, axis=0, keepdims=True)
        high = sums.astype(jnp.bfloat16).astype(jnp.float32)
        middle = (sums - high).astype(jnp.bfloat16).astype(jnp.float32)
        line = lax.broadcasted_iota(jnp.int32, (EXTRA, rows), 0)
        lines = jnp.where(line == 0, high, jnp.where(line == 1, middle, jnp.where(line == 2, sums - high - middle, 0.0)))
        dx_ref[rows:, :] = jnp.zeros_like(dx_ref[rows:, :])
        dx_ref[rows:, :rows] = lines.astype(dx_ref.dtype)


def expert_block(at, count, x, dy, wgu, wd, earlier):
    rows, width = dy.shape
    hidden = wd.shape[0]
    tile = FF_TILE
    whole = jax.ShapeDtypeStruct((count * rows, hidden), jnp.bfloat16)
    fixed = lambda i, *_: (0, 0)
    out_block = pl.BlockSpec((rows, tile), lambda i, *_: (at, i))
    spec = pltpu.PrefetchScalarGridSpec(
        num_scalar_prefetch=1,
        grid=(hidden // tile,),
        in_specs=[
            pl.BlockSpec((rows + EXTRA, width), fixed),
            pl.BlockSpec((rows, width), fixed),
            pl.BlockSpec((width, tile), lambda i, *_: (0, i)),
            pl.BlockSpec((width, tile), lambda i, *_: (0, hidden // tile + i)),
            pl.BlockSpec((tile, width), lambda i, *_: (i, 0)),
        ]
        + [pl.BlockSpec(memory_space=pl.ANY)] * len(earlier),
        out_specs=[
            out_block,
            out_block,
            out_block,
            pl.BlockSpec((rows + EXTRA, width), fixed),
        ],
        scratch_shapes=[
            pltpu.VMEM((rows, LANES), jnp.float32),
            pltpu.VMEM((rows, width), jnp.float32),
            pltpu.VMEM((rows, LANES), jnp.float32),
        ],
    )
    return pl.pallas_call(
        expert_kernel,
        name="expert_block",
        out_shape=(
            whole,
            whole,
            whole,
            jax.ShapeDtypeStruct((rows + EXTRA, width), jnp.bfloat16),
        ),
        grid_spec=spec,
        input_output_aliases={6 + i: i for i in range(len(earlier))},
        compiler_params=pltpu.CompilerParams(dimension_semantics=("arbitrary",), vmem_limit_bytes=40 << 20),
        cost_estimate=pl.CostEstimate(
            flops=10 * rows * width * hidden, bytes_accessed=6 * width * hidden + 6 * rows * hidden, transcendentals=0
        ),
    )(jnp.zeros((1,), jnp.int32), x, dy, wgu, wgu, wd, *earlier)


EPS = 1e-06
FULL_PRECISION = lax.Precision.HIGHEST
ALL = ("z", "x", "exp")
SEQ = ("z", "x")
LOW = jnp.bfloat16


def dot32(a, b):
    return jnp.dot(a, b, preferred_element_type=jnp.float32)


def dot_nt(a, b):
    return lax.dot_general(a, b, NT, preferred_element_type=jnp.float32)


def dot_tn(a, b):
    return lax.dot_general(a, b, (((0,), (0,)), ((), ())), preferred_element_type=jnp.float32)


def partner(value, axis, offset):
    count = lax.axis_size(axis)
    return lax.ppermute(value, axis, [(i, i ^ offset) for i in range(count)])


def bits_of(count):
    return [1 << b for b in reversed(range(count.bit_length() - 1))]


def reorder(stacked, own):
    count = stacked.shape[0]
    return jnp.stack([lax.dynamic_index_in_dim(stacked, own ^ r, 0, keepdims=False) for r in range(count)])


def gather_double(value, steps):
    for axis, bit in steps:
        other = partner(value, axis, bit)
        high = (lax.axis_index(axis) & bit) != 0
        value = jnp.stack([jnp.where(high, other, value), jnp.where(high, value, other)])
    return value


def scatter_halve(value, steps):
    gone = []
    for axis, bit, dim in steps:
        at = dim - sum(1 for d in gone if d < dim)
        gone.append(dim)
        high = (lax.axis_index(axis) & bit) != 0
        low_half = lax.index_in_dim(value, 0, at, keepdims=False)
        high_half = lax.index_in_dim(value, 1, at, keepdims=False)
        keep = jnp.where(high, high_half, low_half)
        give = jnp.where(high, low_half, high_half)
        value = (keep.astype(jnp.float32) + partner(give, axis, bit).astype(jnp.float32)).astype(LOW)
    return value


def ring_of(groups, split):
    order = []
    for x in range(split):
        line = range(groups) if x % 2 == 0 else reversed(range(groups))
        order += [z * split + x for z in line]
    place = [order.index(s) for s in range(len(order))]
    ahead = [(order[i], order[(i + 1) % len(order)]) for i in range(len(order))]
    return jnp.asarray(order, jnp.int32), jnp.asarray(place, jnp.int32), ahead


def pick(values, index):
    return lax.dynamic_index_in_dim(values, index, 0, keepdims=False)


def unwritten(shape, dtype):
    return pl.pallas_call(
        lambda out_ref: None,
        name="unwritten",
        out_shape=jax.ShapeDtypeStruct(shape, dtype),
        out_specs=pl.BlockSpec(memory_space=pl.ANY),
    )()


class RingGather:
    def __init__(self, piece, groups, split, own):
        self.order, place, self.ahead = ring_of(groups, split)
        self.count = groups * split
        self.here = pick(place, own)
        self.rows = piece.shape[0]
        self.whole = unwritten((self.count * self.rows, piece.shape[1]), piece.dtype)
        self.whole = lax.dynamic_update_slice_in_dim(self.whole, piece, own * self.rows, 0)
        self.forward = self.backward = piece
        self.round = 0
        self.waiting = []

    def step(self):
        self.settle()
        self.round += 1
        k = self.round
        self.forward = lax.ppermute(self.forward, SEQ, self.ahead)
        self.waiting.append((self.forward, -k))
        if k < self.count - self.count // 2:
            self.backward = lax.ppermute(self.backward, SEQ, [(b, a) for a, b in self.ahead])
            self.waiting.append((self.backward, k))

    def settle(self):
        for piece, k in self.waiting:
            at = pick(self.order, (self.here + k + self.count) % self.count) * self.rows
            self.whole = lax.dynamic_update_slice_in_dim(self.whole, piece, at, 0)
        self.waiting = []

    def after(self, value):
        value, self.forward, self.backward = lax.optimization_barrier((value, self.forward, self.backward))
        self.waiting = [(self.forward if k < 0 else self.backward, k) for _, k in self.waiting]
        return value

    def finish(self):
        while self.round < self.count // 2:
            self.step()
        self.settle()
        return self.whole


class RingScatter:
    def __init__(self, totals, groups, split, own):
        self.order, place, self.ahead = ring_of(groups, split)
        self.count = groups * split
        self.here = pick(place, own)
        self.rows = totals[0].shape[0] // self.count
        self.totals = totals
        self.round = 0
        self.forward = self.backward = None

    def block(self, total, offset):
        at = pick(self.order, (self.here + offset + self.count) % self.count) * self.rows
        return lax.dynamic_slice_in_dim(total, at, self.rows, 0)

    def load(self, coming, offset):
        own = [self.block(total, offset) for total in self.totals]
        if coming is None:
            return own
        return [(a.astype(jnp.float32) + b.astype(jnp.float32)).astype(LOW) for a, b in zip(own, coming)]

    def step(self):
        self.round += 1
        k, far = self.round, self.count // 2
        near = self.count - 1 - far
        if k <= far:
            parts = self.load(self.forward, far - k + 1)
            self.forward = [lax.ppermute(part, SEQ, self.ahead) for part in parts]
        if k <= near:
            parts = self.load(self.backward, k - near - 1)
            self.backward = [lax.ppermute(part, SEQ, [(b, a) for a, b in self.ahead]) for part in parts]

    def after(self, value):
        value, self.forward, self.backward = lax.optimization_barrier((value, self.forward, self.backward))
        return value

    def finish(self):
        while self.round < self.count // 2:
            self.step()
        own = [self.block(total, 0).astype(jnp.float32) for total in self.totals]
        return [
            a + b.astype(jnp.float32) + c.astype(jnp.float32) for a, b, c in zip(own, self.forward, self.backward)
        ]


def norm_scale(value):
    return lax.rsqrt(jnp.mean(value * value, axis=-1, keepdims=True) + EPS)


def norm_back(scale, normed, gain, grad):
    scaled = grad * gain
    return scale * (scaled - normed * jnp.mean(scaled * normed, axis=-1, keepdims=True))


def split3(value):
    high = value.astype(LOW)
    rest = value - high.astype(jnp.float32)
    middle = rest.astype(LOW)
    return [high, middle, (rest - middle.astype(jnp.float32)).astype(LOW)]


def per_device(
    block_in,
    cotangent,
    segment_ids,
    expert_routes,
    pair_priority,
    gain_attention,
    w_query,
    w_key,
    w_value,
    w_out,
    bias_table,
    gain_experts,
    w_router,
    w_gate,
    w_up,
    w_down,
):
    groups, local_len, width = block_in.shape
    tokens = groups * local_len
    rows_own, hd = w_query.shape
    split = lax.axis_size("x")
    exp_count = lax.axis_size("exp")
    seq_count = groups * split
    length = local_len * seq_count
    x_at, z_at, e_at = lax.axis_index("x"), lax.axis_index("z"), lax.axis_index("exp")
    s_at = z_at * split + x_at
    head_width = hd // split
    heads_here = head_width // HEAD_DIM
    experts_all = w_router.shape[1]
    bias_own = bias_table.shape[0]
    tile = min(TILE, local_len)
    own = s_at.astype(jnp.int32).reshape(1)
    z_bits, x_bits, e_bits = bits_of(groups), bits_of(split), bits_of(exp_count)

    input_r = reorder(block_in, z_at)

    arrived = [[None] * split for _ in range(groups)]
    for rz in reversed(range(groups)):
        arrived[rz][0] = partner(input_r[rz], "z", rz) if rz else input_r[0]
    small = jnp.concatenate(
        [
            gain_attention[:, None],
            gain_experts[:, None],
            jnp.pad(bias_table, (0, rows_own - bias_own))[:, None],
            w_router,
        ],
        axis=1,
    )
    small = jnp.pad(small, ((0, 0), (0, LANES - small.shape[1]))).astype(LOW)
    share = jnp.stack(
        [part.astype(LOW).reshape(rows_own, split, head_width) for part in (w_query, w_key, w_value)], axis=2
    )
    share = share.reshape(rows_own, split, 3 * head_width).transpose(1, 0, 2)
    common = jnp.concatenate([w_out.astype(LOW), small], axis=1)
    share = jnp.concatenate([share, jnp.broadcast_to(common, (split,) + common.shape)], axis=2)
    shares = [lax.dynamic_index_in_dim(share, x_at ^ r, 0, keepdims=False) for r in range(split)]
    shares = [shares[0]] + [partner(shares[r], "x", r) for r in range(1, split)]
    by_x = reorder(jnp.stack(shares), x_at)
    for rx in range(1, split):
        arrived[0][rx] = partner(arrived[0][0], "x", rx)
    packed = gather_double(by_x, [("z", b) for b in z_bits])
    near = [arrived[rz][0] for rz in range(1, groups)]
    packed, near = lax.optimization_barrier((packed, near))
    for rz in range(1, groups):
        arrived[rz][0] = near[rz - 1]
        for rx in range(1, split):
            arrived[rz][rx] = partner(arrived[rz][0], "x", rx)
    packed = gather_double(packed, [("exp", b) for b in e_bits[:-1]])
    packed, arrived = lax.optimization_barrier((packed, arrived))
    sequence = jnp.stack([block for line in arrived for block in line]).reshape(length, width)

    gate_up_own = jnp.concatenate([w_gate[0].astype(LOW), w_up[0].astype(LOW)], axis=1)
    sequence, gate_up_own, down_own = lax.optimization_barrier((sequence, gate_up_own, w_down[0].astype(LOW)))
    down_w = lax.all_gather(down_own, SEQ, axis=0, tiled=True)
    gate_up_ring = RingGather(gate_up_own, groups, split, s_at)
    gate_up_ring.step()
    packed = gather_double(packed, [("exp", b) for b in e_bits[-1:]])
    ne, nz, nx = len(e_bits), len(z_bits), len(x_bits)
    packed = packed.transpose(
        tuple(ne + i for i in reversed(range(nz))) + (ne + nz,) + tuple(reversed(range(ne))) + (ne + nz + 1, ne + nz + 2)
    ).reshape(width, 3 * head_width + width + LANES)
    qkv_w, small_all = packed[:, : 3 * head_width], packed[:, 3 * head_width + width :]
    out_w = packed[:, 3 * head_width : 3 * head_width + width]
    gain_one = small_all[:, 0].astype(jnp.float32)
    gain_two = small_all[:, 1].astype(jnp.float32)
    table_all = small_all[:, 2].reshape(-1, rows_own)[:, :bias_own].reshape(-1, BUCKETS)
    router_t = small_all[:, 3 : 3 + experts_all].T
    table_rows = lax.dynamic_slice_in_dim(table_all, x_at * heads_here, heads_here, 0)

    routes = expert_routes.reshape(tokens, -1)
    top_count = routes.shape[1]
    priority = pair_priority.reshape(-1)
    pair_experts = routes.reshape(-1)
    ahead = (pair_experts[None, :] == pair_experts[:, None]) & (priority[None, :] < priority[:, None])
    slots = jnp.sum(ahead.astype(jnp.int32), axis=1)
    capacity = (5 * top_count * tokens + 4 * experts_all - 1) // (4 * experts_all)
    slot_count = experts_all * capacity
    slot_index = jnp.where(slots < capacity, (pair_experts ^ e_at) * capacity + slots, slot_count)
    slot_index = slot_index.reshape(tokens, top_count)
    every_slot = jnp.arange(slot_count, dtype=jnp.int32)[None, :]
    table = sum((slot_index[:, k : k + 1] == every_slot).astype(LOW) for k in range(top_count))
    tables = [table[:, r * capacity : (r + 1) * capacity] for r in range(exp_count)]
    grad_low = cotangent.reshape(tokens, width)
    grad_slots = [dot_tn(part, grad_low).astype(LOW) for part in tables]

    wide = sequence.astype(jnp.float32)
    normed_one = (wide * norm_scale(wide) * gain_one).astype(LOW)
    qkv = dot32(normed_one, qkv_w).astype(LOW)
    qkv, grad_slots = lax.optimization_barrier((qkv, grad_slots))
    qkv = gate_up_ring.after(qkv)
    gate_up_ring.step()
    grad_slots = [grad_slots[0]] + [partner(grad_slots[r], "exp", r) for r in range(1, exp_count)]
    segments = lax.dynamic_index_in_dim(segment_ids, z_at, 0, keepdims=False)
    ranges = tile_ranges(segments, tile)
    seg_blocks = segments.reshape(seq_count, local_len)
    query_side, key_side = segment_columns(reorder(seg_blocks, s_at).reshape(length))
    rows = bias_rows(table_rows, tile)
    ends = jnp.stack([table_rows[:, 15], table_rows[:, 31]], axis=1).astype(jnp.float32)
    contexts, log_totals = attend_forward(qkv, query_side, key_side, ranges, rows, ends, own, tile)
    contexts = gate_up_ring.after(contexts)
    contexts, grad_slots = lax.optimization_barrier((contexts, grad_slots))
    gate_up_w = gate_up_ring.finish()

    def exchange_positions(blocks):
        return lax.all_to_all(blocks, SEQ, split_axis=0, concat_axis=0, tiled=True)

    context_local = exchange_positions(contexts.reshape(seq_count, local_len, head_width))
    context_local = (
        context_local.reshape(groups, split, local_len, head_width).transpose(0, 2, 1, 3).reshape(tokens, hd)
    )
    inputs = block_in.astype(jnp.float32).reshape(tokens, width)
    mid = inputs + dot32(context_local, out_w)
    scale_two = norm_scale(mid)
    normed_two = (mid * scale_two * gain_two).astype(LOW)

    logits = dot_nt(router_t, normed_two)
    exponent = jnp.exp(logits - jnp.max(logits, axis=0, keepdims=True))
    probabilities = exponent / jnp.sum(exponent, axis=0, keepdims=True)
    expert_ids = jnp.arange(experts_all, dtype=jnp.int32)[:, None]
    chosen = sum((routes[:, k][None, :] == expert_ids).astype(jnp.float32) for k in range(top_count))
    chosen_total = jnp.sum(probabilities * chosen, axis=0, keepdims=True)
    gates = probabilities * chosen / chosen_total
    gates_r = reorder(gates, e_at)

    gate_slots = jnp.sum(
        table.astype(jnp.float32).reshape(tokens, exp_count, capacity) * gates_r.T[:, :, None], axis=0
    )
    gate_lines = jnp.pad(jnp.stack(split3(gate_slots), axis=1), ((0, 0), (0, EXTRA - 3), (0, width - capacity)))

    def values_below(rows_):
        return jnp.sum(rows_[capacity : capacity + 3, :capacity].astype(jnp.float32), axis=0)

    sent = [None] * exp_count
    for r in reversed(range(exp_count)):
        sent[r] = jnp.concatenate([dot_tn(tables[r], normed_two).astype(LOW), gate_lines[r]], axis=0)
        if r:
            sent[r] = partner(sent[r], "exp", r)

    earlier = ()
    back = [None] * exp_count
    turns = [0] + list(range(2, exp_count)) + [1]
    for turn, r in enumerate(turns):
        if turn >= 3:
            ready = turns[turn - 2]
            sent[r], back[ready] = lax.optimization_barrier((sent[r], back[ready]))
        hidden, gate_low, up_low, dx = expert_block(
            r, exp_count, sent[r], grad_slots[r], gate_up_w, down_w, earlier
        )
        earlier = (hidden, gate_low, up_low)
        back[r] = partner(dx, "exp", r) if r else dx

    sent, hidden = lax.optimization_barrier((sent, hidden))
    slot_rows = jnp.concatenate([rows_[:capacity] for rows_ in sent], axis=0)
    slot_gates = jnp.concatenate([values_below(rows_) for rows_ in sent], axis=0)[:, None]
    slot_grads = (slot_gates * jnp.concatenate(grad_slots, axis=0).astype(jnp.float32)).astype(LOW)

    gate_grad = jnp.sum(
        table.astype(jnp.float32).reshape(tokens, exp_count, capacity) * jnp.stack([values_below(rows_) for rows_ in back])[None], axis=2
    )
    gate_grad = reorder(gate_grad.T, e_at)
    chosen_grad = chosen * (gate_grad - jnp.sum(gates * gate_grad, axis=0, keepdims=True)) / chosen_total
    logit_grad = probabilities * (chosen_grad - jnp.sum(probabilities * chosen_grad, axis=0, keepdims=True))
    logit_pieces = jnp.concatenate(split3(logit_grad), axis=0)
    router_sum = jnp.sum(dot32(logit_pieces, normed_two).reshape(3, experts_all, width), axis=0)
    normed_two_grad = dot_tn(logit_pieces, jnp.concatenate([router_t] * 3, axis=0))
    for r in range(exp_count):
        normed_two_grad = normed_two_grad + dot32(tables[r], back[r][:capacity])
    unit_two = mid * scale_two
    gain_two_sum = jnp.sum(normed_two_grad * unit_two, axis=0)
    grad_out = grad_low.astype(jnp.float32)
    mid_grad = grad_out + norm_back(scale_two, unit_two, gain_two, normed_two_grad)
    attention_grad = mid_grad.astype(LOW)
    context_grad = dot_nt(attention_grad, out_w).astype(LOW)
    context_grad, up_low, gate_low = lax.optimization_barrier((context_grad, up_low, gate_low))
    gate_sum = dot_tn(slot_rows, gate_low).astype(LOW)
    up_sum = dot_tn(slot_rows, up_low).astype(LOW)
    context_grad = (
        context_grad.reshape(groups, local_len, split, head_width)
        .transpose(0, 2, 1, 3)
        .reshape(seq_count, local_len, head_width)
    )
    context_heads = exchange_positions(context_grad).reshape(length, head_width)

    def scatter_experts(total):
        return lax.psum_scatter(total, SEQ, scatter_dimension=0, tiled=True)

    context_heads, gate_sum, up_sum = lax.optimization_barrier((context_heads, gate_sum, up_sum))

    halving = [("exp", b, 1 + nz + nx + ne - 1 - i) for i, b in enumerate(reversed(e_bits))]
    halving += [("z", b, 1 + nz - 1 - i) for i, b in enumerate(reversed(z_bits))]
    out_sum = dot_tn(context_local, attention_grad).astype(LOW)

    ring = RingScatter([gate_sum, up_sum], groups, split, s_at)
    grads, diag, far = (), [], []
    pairs = head_width // LANES
    for pair in range(pairs):
        ring.step()
        *grads, pair_diag, pair_far = attend_backward(
            pair, qkv, context_heads, contexts, log_totals, query_side, key_side, ranges, rows, ends, own, tile, tuple(grads)
        )
        grads = ring.after(grads)
        if pair == 0:
            grads, hidden = lax.optimization_barrier((grads, hidden))
            down_sum = dot_tn(hidden, slot_grads).astype(LOW)
            down_owned = scatter_experts(down_sum)
        if pair == min(1, pairs - 1):
            grads, hidden, down_sum = lax.optimization_barrier((grads, hidden, down_sum))
            expert_out = (slot_gates * dot32(hidden, down_w)).astype(LOW)
            expert_out = reorder(expert_out.reshape(exp_count, capacity, width), e_at)
            returned = lax.all_to_all(expert_out, "exp", split_axis=0, concat_axis=0, tiled=True)
        if pair == min(2, pairs - 1):
            grads, expert_out = lax.optimization_barrier((grads, expert_out))
        if pair == pairs - 1:
            grads, returned = lax.optimization_barrier((grads, returned))
        diag.append(pair_diag)
        far.append(pair_far)
    diag, far = jnp.concatenate(diag), jnp.concatenate(far)
    query_back, key_back, value_back, down_owned = lax.optimization_barrier((*grads, down_owned))
    gate_owned, up_owned = ring.finish()
    table_local = bucket_sums(diag, far, tile)

    def through(grads, part):
        return dot_nt(grads, qkv_w[:, part * head_width : (part + 1) * head_width])

    normed_part = through(query_back, 0) + through(key_back, 1) + through(value_back, 2)
    normed_part = normed_part.reshape(groups, split, local_len, width)
    sides = [normed_part[:, rx].astype(LOW) for rx in range(1, split)]
    sides, query_back, key_back, value_back = lax.optimization_barrier((sides, query_back, key_back, value_back))
    sides = [partner(side, "x", rx) for rx, side in enumerate(sides, 1)]
    out_parts = width // head_width
    weight_sum = jnp.stack(
        [dot_tn(normed_one, grads).astype(LOW) for grads in (query_back, key_back, value_back)]
        + [out_sum[:, i * head_width : (i + 1) * head_width] for i in range(out_parts)]
    )
    weight_part = scatter_halve(
        weight_sum.reshape((3 + out_parts,) + (2,) * (nz + nx + ne) + (rows_own, head_width)), halving[:1]
    )
    normed_back = normed_part[:, 0] + sum(side.astype(jnp.float32) for side in sides)
    normed_back = lax.all_to_all(
        reorder(normed_back.astype(LOW), z_at), "z", split_axis=0, concat_axis=0, tiled=True
    )
    weight_part = scatter_halve(weight_part, halving[1:]).reshape(3 + out_parts, split, rows_own, head_width)
    weight_own = [lax.dynamic_index_in_dim(weight_part, x_at ^ r, 1, keepdims=False) for r in range(split)]
    weight_own = [weight_own[0]] + [partner(weight_own[r], "x", r) for r in range(1, split)]
    normed_back, weight_own = lax.optimization_barrier((normed_back, weight_own))
    block_out = (mid + dot32(table, reorder(returned, e_at).reshape(slot_count, width))).astype(LOW)

    block_out = block_out.reshape(groups, local_len, width)
    out_w_out = sum(part[3:].astype(jnp.float32) for part in weight_own)
    out_w_out = out_w_out.transpose(1, 0, 2).reshape(rows_own, width)
    qkv_own = reorder(jnp.stack([part[:3] for part in weight_own]), x_at)
    qkv_own = qkv_own.transpose(1, 2, 0, 3).reshape(3, rows_own, hd).astype(jnp.float32)

    normed_one_grad = normed_back.astype(jnp.float32).reshape(tokens, width)
    scale_one = norm_scale(inputs)
    unit_one = inputs * scale_one
    gain_one_sum = jnp.sum(normed_one_grad * unit_one, axis=0)
    block_in_grad = (mid_grad + norm_back(scale_one, unit_one, gain_one, normed_one_grad)).reshape(
        groups, local_len, width
    )

    table_sum = lax.dynamic_update_slice_in_dim(
        jnp.zeros(table_all.shape, jnp.float32), table_local, x_at * heads_here, 0
    ).reshape(-1, bias_own)
    table_sum = jnp.pad(table_sum, ((0, 0), (0, rows_own - bias_own)))[:, None, :]
    little = jnp.concatenate(
        [
            gain_one_sum.reshape(-1, 1, rows_own),
            gain_two_sum.reshape(-1, 1, rows_own),
            table_sum,
            router_sum.reshape(experts_all, -1, rows_own).transpose(1, 0, 2),
        ],
        axis=1,
    )
    little = jnp.sum(lax.all_to_all(little, ALL, split_axis=0, concat_axis=0, tiled=True), axis=0)
    return (
        block_out,
        block_in_grad,
        little[0],
        qkv_own[0],
        qkv_own[1],
        qkv_own[2],
        out_w_out,
        little[2, :bias_own],
        little[1],
        little[3:].T,
        gate_owned.astype(jnp.float32)[None],
        up_owned.astype(jnp.float32)[None],
        down_owned.astype(jnp.float32)[None],
    )


def solution(mesh):
    def run(*args):
        groups = args[0].shape[0] // mesh.shape["exp"]
        seq_count, exp_count = mesh.shape["seq"], mesh.shape["exp"]
        grid = mesh.devices.reshape(groups, seq_count // groups, exp_count)
        fine = jax.sharding.Mesh(grid, ALL)
        placed = P("exp", SEQ, None)
        whole = P(ALL)
        matrix = P(ALL, None)
        return jax.shard_map(
            per_device,
            mesh=fine,
            in_specs=(
                placed, placed, P("exp", None), placed, placed,
                whole, matrix, matrix, matrix, matrix, whole, whole, matrix,
                placed, placed, placed,
            ),
            out_specs=(
                placed, placed, whole, matrix, matrix, matrix, matrix, whole, whole, matrix,
                placed, placed, placed,
            ),
            check_vma=False,
        )(*args)

    return run
```

```python
from functools import partial

import jax
import jax.numpy as jnp
import numpy as np
from jax import lax
from jax.experimental import pallas as pl
from jax.experimental.pallas import tpu as pltpu
from jax.sharding import PartitionSpec as P

HEAD_DIM = 64
BUCKETS = 32
THRESHOLDS = (12, 16, 23, 32, 46, 64, 91)
MASKED = -1e30
TILE = 256
LANES = 128
NT = (((1,), (1,)), ((), ()))


def bucket_of(d):
    a = np.abs(d)
    extra = sum((a >= t).astype(np.int64) for t in THRESHOLDS)
    return np.where(a < 8, a, 8 + extra) + 16 * (d > 0)


def bias_rows(table_rows, tile):
    u = np.arange(2 * tile)
    x = np.where(u < tile, u, u - 2 * tile)
    ids = np.stack([bucket_of(step * tile - x) for step in (-1, 0, 1)])
    hot = (ids.reshape(-1)[None, :] == np.arange(BUCKETS)[:, None]).astype(np.float32)
    rows = jnp.dot(table_rows.astype(jnp.bfloat16), jnp.asarray(hot, jnp.bfloat16), preferred_element_type=jnp.float32)
    return rows.reshape(table_rows.shape[0], 3, 2 * tile)


def tile_ranges(segments, tile):
    blocks = segments.reshape(-1, tile)
    first, last = blocks[:, 0], blocks[:, -1]
    low = jnp.sum((last[None, :] < first[:, None]).astype(jnp.int32), axis=1)
    high = jnp.sum((first[None, :] <= last[:, None]).astype(jnp.int32), axis=1)
    return jnp.stack([low, high])


def segment_columns(segments):
    lane = jnp.arange(LANES, dtype=jnp.int32)[None, :]
    seg = segments[:, None]
    same = seg == lane
    query_side = jnp.where(same & (lane < 4), MASKED, 0.0).astype(jnp.bfloat16)
    key_side = jnp.where(lane < 4, (~same).astype(jnp.float32), (lane < 9).astype(jnp.float32)).astype(jnp.bfloat16)
    return query_side, key_side


def toeplitz(row, tile):
    wide = jnp.broadcast_to(row, (tile, row.shape[1]))
    return pltpu.roll(wide, 0, 1, stride=1, stride_axis=0)[:, :tile]


def block_at(index, own, tile):
    return pl.ds(pl.multiple_of((index ^ own[0]) * tile, tile), tile)


def fwd_kernel(ranges, ends, own, q_ref, k_ref, v_ref, qs_ref, ks_ref, rows_ref, o_ref, lse_ref, bias_ref, vt_ref):
    group, qb = pl.program_id(0), pl.program_id(1)
    tile, span = q_ref.shape
    heads = span // HEAD_DIM

    @pl.when(qb == 0)
    def _():
        for h in range(heads):
            for step in range(3):
                bias_ref[h, step] = toeplitz(rows_ref[h, step : step + 1, :], tile)
        for start in range(0, v_ref.shape[0], tile):
            vt_ref[:, start : start + tile] = v_ref[start : start + tile, :].T

    low, high = ranges[0, qb], ranges[1, qb]
    lane = lax.broadcasted_iota(jnp.int32, (tile, LANES), 1)
    q = q_ref[...] * jnp.bfloat16(HEAD_DIM**-0.5)
    qs = qs_ref[...]
    halves = []
    for h in range(heads):
        part = q[:, h // 2 * LANES : (h // 2 + 1) * LANES]
        keep = (lane < HEAD_DIM) if h % 2 == 0 else (lane >= HEAD_DIM)
        halves.append(jnp.where(keep, part, jnp.zeros_like(part)))

    def side(h, which):
        if which == 1:
            extra = qs
        else:
            value = ends[heads * group + h, which // 2].astype(jnp.bfloat16)
            extra = jnp.where(lane == 7, value, qs)
        return jnp.concatenate([halves[h], extra], axis=1)

    def visit(which):
        queries = [side(h, which) for h in range(heads)]

        def step(kb, carry):
            keys = block_at(kb, own, tile)
            ks = ks_ref[keys, :]
            scores = []
            for h in range(heads):
                kx = jnp.concatenate([k_ref[keys, h // 2 * LANES : (h // 2 + 1) * LANES], ks], axis=1)
                scores.append(lax.dot_general(kx, queries[h], NT, preferred_element_type=jnp.float32))
            kept = []
            for h in range(heads):
                peak, total, acc = carry[h]
                s = scores[h]
                if which == 1:
                    s = s + bias_ref[h, kb - qb + 1]
                new = jnp.maximum(peak, jnp.max(s, axis=0, keepdims=True))
                p = jnp.exp(s - new)
                scale = jnp.exp(peak - new)
                total = total * scale + jnp.sum(p, axis=0, keepdims=True)
                kept.append((new, total, acc, scale, p.astype(jnp.bfloat16)))
            out = []
            for h in range(heads):
                new, total, acc, scale, p = kept[h]
                vt = vt_ref[h * HEAD_DIM : (h + 1) * HEAD_DIM, keys]
                acc = acc * scale + jnp.dot(vt, p, preferred_element_type=jnp.float32)
                out.append((new, total, acc))
            return tuple(out)

        return step

    start = tuple(
        (
            jnp.full((1, tile), -3e38, jnp.float32),
            jnp.zeros((1, tile), jnp.float32),
            jnp.zeros((HEAD_DIM, tile), jnp.float32),
        )
        for _ in range(heads)
    )
    near_low, near_high = jnp.maximum(low, qb - 1), jnp.minimum(high, qb + 2)
    state = lax.fori_loop(near_low, near_high, visit(1), start)
    state = lax.fori_loop(low, near_low, visit(0), state)
    state = lax.fori_loop(near_high, high, visit(2), state)
    outs = []
    for h in range(heads):
        peak, total, acc = state[h]
        outs.append(acc / total)
        lse_ref[h // 2, h % 2 : h % 2 + 1, :] = peak + jnp.log(total)
    o_ref[...] = jnp.concatenate(outs, axis=0).T.astype(o_ref.dtype)


FWD_PAIRS = 4


def attend_forward(qkv, qs, ks, ranges, rows, ends, own, tile):
    length, width = qkv.shape[0], qkv.shape[1] // 3
    pairs = width // LANES
    together = FWD_PAIRS if pairs % FWD_PAIRS == 0 else 1
    span = together * LANES
    tiles = length // tile
    spec = pltpu.PrefetchScalarGridSpec(
        num_scalar_prefetch=3,
        grid=(pairs // together, tiles),
        in_specs=[
            pl.BlockSpec((tile, span), lambda p, i, r, e, own: (i ^ own[0], p)),
            pl.BlockSpec((length, span), lambda p, i, *_: (0, width // span + p)),
            pl.BlockSpec((length, span), lambda p, i, *_: (0, 2 * (width // span) + p)),
            pl.BlockSpec((tile, LANES), lambda p, i, r, e, own: (i ^ own[0], 0)),
            pl.BlockSpec((length, LANES), lambda p, i, *_: (0, 0)),
            pl.BlockSpec((2 * together, 3, 2 * tile), lambda p, i, *_: (p, 0, 0)),
        ],
        out_specs=[
            pl.BlockSpec((tile, span), lambda p, i, *_: (i, p)),
            pl.BlockSpec((together, 2, tile), lambda p, i, *_: (p, 0, i)),
        ],
        scratch_shapes=[
            pltpu.VMEM((2 * together, 3, tile, tile), jnp.float32),
            pltpu.VMEM((span, length), jnp.bfloat16),
        ],
    )
    return pl.pallas_call(
        fwd_kernel,
        name="attend_forward",
        out_shape=(
            jax.ShapeDtypeStruct((length, width), jnp.bfloat16),
            jax.ShapeDtypeStruct((pairs, 2, length), jnp.float32),
        ),
        grid_spec=spec,
        compiler_params=pltpu.CompilerParams(
            dimension_semantics=("arbitrary", "arbitrary"), vmem_limit_bytes=48 << 20
        ),
        cost_estimate=pl.CostEstimate(flops=length * length * width * 4, bytes_accessed=length * width * 8, transcendentals=0),
    )(ranges, ends, own, qkv, qkv, qkv, qs, ks, rows)


def pieces(row):
    high = row.astype(jnp.bfloat16).astype(jnp.float32)
    mid = (row - high).astype(jnp.bfloat16).astype(jnp.float32)
    return high, mid, row - high - mid


def bwd_kernel(ranges, ends, own, q_ref, k_ref, v_ref, do_ref, o_ref, lse_ref, qs_ref, ks_ref, rows_ref, *refs):
    (dq_ref, dk_ref, dv_ref, diag_ref, far_ref,
     qx_ref, dox_ref, kt_ref, bias_ref, dsum_ref, fsum_ref, dqt_ref, dka_ref, dva_ref) = refs[-14:]
    pair = own[1]
    length = q_ref.shape[0]
    tile = bias_ref.shape[2]
    tiles = length // tile
    for h in range(2):
        for step in range(3):
            bias_ref[h, step] = toeplitz(rows_ref[h, step : step + 1, :], tile)
    dsum_ref[...] = jnp.zeros_like(dsum_ref)
    fsum_ref[...] = jnp.zeros_like(fsum_ref)
    dqt_ref[...] = jnp.zeros_like(dqt_ref)
    lane = lax.broadcasted_iota(jnp.int32, (tile, LANES), 1)
    sub = lax.broadcasted_iota(jnp.int32, (LANES, tile), 0)
    pick = (lax.broadcasted_iota(jnp.int32, (8, LANES), 1) // HEAD_DIM == lax.broadcasted_iota(jnp.int32, (8, LANES), 0)).astype(jnp.float32)

    @pl.loop(0, tiles)
    def _(i):
        line = pl.ds(pl.multiple_of(i * tile, tile), tile)
        at = block_at(i, own, tile)
        q = q_ref[at, :] * jnp.bfloat16(HEAD_DIM**-0.5)
        do = do_ref[line, :]
        zero = jnp.zeros_like(q)
        product = do.astype(jnp.float32) * o_ref[line, :].astype(jnp.float32)
        delta = lax.dot_general(pick, product, NT, precision=lax.Precision.HIGHEST, preferred_element_type=jnp.float32)
        kt_ref[:, at] = k_ref[at, :].T
        for h in range(2):
            keep = (lane < HEAD_DIM) if h == 0 else (lane >= HEAD_DIM)
            a, b, c = pieces(-lse_ref[0, h : h + 1, line])
            extra = jnp.where(sub == 4, a, jnp.where(sub == 5, b, jnp.where(sub == 6, c, 0.0)))
            extra = extra.T.astype(jnp.bfloat16) + qs_ref[at, :]
            left, right = ends[2 * pair + h, 0].astype(jnp.bfloat16), ends[2 * pair + h, 1].astype(jnp.bfloat16)
            extra = jnp.where(lane == 7, left, jnp.where(lane == 8, right, extra))
            qx_ref[h, at, :] = jnp.concatenate([jnp.where(keep, q, zero), extra], axis=1)
            a, b, c = pieces(-delta[h : h + 1, :])
            extra = jnp.where(sub == 4, a, jnp.where(sub == 5, b, jnp.where(sub == 6, c, 0.0)))
            dox_ref[h, at, :] = jnp.concatenate([jnp.where(keep, do, zero), extra.T.astype(jnp.bfloat16)], axis=1)

    ones3 = ((lane >= 4) & (lane < 7)).astype(jnp.bfloat16)

    @pl.loop(0, tiles)
    def _(kb):
        low, high = ranges[0, kb], ranges[1, kb]
        keys = block_at(kb, own, tile)
        k, ks = k_ref[keys, :], ks_ref[keys, :]
        vx = jnp.concatenate([v_ref[keys, :], ones3], axis=1)
        nil = jnp.zeros_like(ks)
        dka_ref[...] = jnp.zeros_like(dka_ref)
        dva_ref[...] = jnp.zeros_like(dva_ref)

        def visit(which):
            if which == 0:
                extra = jnp.where(lane == 8, nil, ks)
            elif which == 2:
                extra = jnp.where(lane == 7, nil, ks)
            else:
                extra = jnp.where((lane == 7) | (lane == 8), nil, ks)
            kx = jnp.concatenate([k, extra], axis=1)

            def step(qb, carry):
                at = block_at(qb, own, tile)
                weights, grads, scores, products = [], [], [], []
                for h in range(2):
                    scores.append(lax.dot_general(kx, qx_ref[h, at, :], NT, preferred_element_type=jnp.float32))
                    products.append(lax.dot_general(vx, dox_ref[h, at, :], NT, preferred_element_type=jnp.float32))
                for h in range(2):
                    s = scores[h]
                    if which == 1:
                        s = s + bias_ref[h, kb - qb + 1]
                    p = jnp.exp(s)
                    ds = p * products[h]
                    if which == 1:
                        dsum_ref[h, kb - qb + 1] += ds
                    else:
                        fsum_ref[h, which // 2] += jnp.sum(ds.reshape(tile // 8, 8, tile), axis=0)
                    weights.append(p.astype(jnp.bfloat16))
                    grads.append(ds.astype(jnp.bfloat16))
                both_do = jnp.concatenate([dox_ref[0, at, :LANES], dox_ref[1, at, :LANES]], axis=0)
                both_q = jnp.concatenate([qx_ref[0, at, :LANES], qx_ref[1, at, :LANES]], axis=0)
                dva_ref[...] += jnp.dot(jnp.concatenate(weights, axis=1), both_do, preferred_element_type=jnp.float32)
                dka_ref[...] += jnp.dot(jnp.concatenate(grads, axis=1), both_q, preferred_element_type=jnp.float32)
                for h in range(2):
                    part = slice(h * HEAD_DIM, (h + 1) * HEAD_DIM)
                    dqt_ref[part, at] += jnp.dot(kt_ref[part, keys], grads[h], preferred_element_type=jnp.float32)
                return carry

            return step

        near_low, near_high = jnp.maximum(low, kb - 1), jnp.minimum(high, kb + 2)
        lax.fori_loop(near_low, near_high, visit(1), 0)
        lax.fori_loop(near_high, high, visit(0), 0)
        lax.fori_loop(low, near_low, visit(2), 0)
        dk_ref[keys, :] = dka_ref[...].astype(dk_ref.dtype)
        dv_ref[keys, :] = dva_ref[...].astype(dv_ref.dtype)

    @pl.loop(0, tiles)
    def _(i):
        at = pl.ds(pl.multiple_of(i * tile, tile), tile)
        dq_ref[at, :] = (dqt_ref[:, at] * HEAD_DIM**-0.5).T.astype(dq_ref.dtype)

    for h in range(2):
        for step in range(3):
            diag_ref[h, step : step + 1, :] = diagonals(dsum_ref, h, step, tile)
        for step in range(2):
            total = jnp.sum(fsum_ref[h, step], axis=0, keepdims=True)
            far_ref[h, step : step + 1, :] = total


def diagonals(dsum_ref, h, step, tile):
    width = 2 * tile
    acc = jnp.zeros((8, width), jnp.float32)
    for group in range(tile // 8):
        part = dsum_ref[h, step, group * 8 : (group + 1) * 8, :]
        part = jnp.concatenate([part, jnp.zeros((8, tile), jnp.float32)], axis=1)
        acc = acc + (pltpu.roll(part, width - 8 * group, 1) if group else part)
    row = lax.broadcasted_iota(jnp.int32, (8, width), 0)
    for bit in (1, 2, 4):
        acc = jnp.where((row & bit) != 0, pltpu.roll(acc, width - bit, 1), acc)
    return jnp.sum(acc, axis=0, keepdims=True)


def attend_backward(pair, qkv, do, o, lse, qs, ks, ranges, rows, ends, own, tile, earlier):
    length, width = do.shape
    pairs = width // LANES
    own = jnp.concatenate([own, jnp.full((1,), pair, jnp.int32)])
    column = pl.BlockSpec((length, LANES), lambda p, r, e, own: (0, own[1]))
    fixed = pl.BlockSpec((length, LANES), lambda p, *_: (0, 0))
    spec = pltpu.PrefetchScalarGridSpec(
        num_scalar_prefetch=3,
        grid=(1,),
        in_specs=[
            column,
            pl.BlockSpec((length, LANES), lambda p, r, e, own: (0, pairs + own[1])),
            pl.BlockSpec((length, LANES), lambda p, r, e, own: (0, 2 * pairs + own[1])),
            column,
            column,
            pl.BlockSpec((1, 2, length), lambda p, r, e, own: (own[1], 0, 0)),
            fixed, fixed,
            pl.BlockSpec((2, 3, 2 * tile), lambda p, r, e, own: (own[1], 0, 0)),
        ]
        + [pl.BlockSpec(memory_space=pl.ANY)] * len(earlier),
        out_specs=[
            column, column, column,
            pl.BlockSpec((2, 3, 2 * tile), lambda p, *_: (p, 0, 0)),
            pl.BlockSpec((2, 2, tile), lambda p, *_: (p, 0, 0)),
        ],
        scratch_shapes=[
            pltpu.VMEM((2, length, 2 * LANES), jnp.bfloat16),
            pltpu.VMEM((2, length, 2 * LANES), jnp.bfloat16),
            pltpu.VMEM((LANES, length), jnp.bfloat16),
            pltpu.VMEM((2, 3, tile, tile), jnp.float32),
            pltpu.VMEM((2, 3, tile, tile), jnp.float32),
            pltpu.VMEM((2, 2, 8, tile), jnp.float32),
            pltpu.VMEM((LANES, length), jnp.float32),
            pltpu.VMEM((tile, LANES), jnp.float32),
            pltpu.VMEM((tile, LANES), jnp.float32),
        ],
    )
    low = jax.ShapeDtypeStruct((length, width), jnp.bfloat16)
    return pl.pallas_call(
        bwd_kernel,
        name="attend_backward",
        out_shape=(
            low, low, low,
            jax.ShapeDtypeStruct((2, 3, 2 * tile), jnp.float32),
            jax.ShapeDtypeStruct((2, 2, tile), jnp.float32),
        ),
        grid_spec=spec,
        input_output_aliases={12 + i: i for i in range(len(earlier))},
        compiler_params=pltpu.CompilerParams(
            dimension_semantics=("arbitrary",), vmem_limit_bytes=40 << 20
        ),
        cost_estimate=pl.CostEstimate(flops=length * length * LANES * 10, bytes_accessed=length * LANES * 16, transcendentals=0),
    )(ranges, ends, own, qkv, qkv, qkv, do, o, lse, qs, ks, rows, *earlier)


def bucket_sums(diag, far, tile):
    u = np.arange(2 * tile)
    x = np.where(u < tile, u, u - 2 * tile)
    ids = np.stack([bucket_of(step * tile - x) for step in (-1, 0, 1)])
    hot = (ids.reshape(-1)[:, None] == np.arange(BUCKETS)[None, :]).astype(np.float32)
    sums = jnp.dot(diag.reshape(diag.shape[0], -1), jnp.asarray(hot), precision=lax.Precision.HIGHEST)
    outer = jnp.sum(far, axis=2)
    ends = np.zeros((2, BUCKETS), np.float32)
    ends[0, 15] = 1
    ends[1, 31] = 1
    return sums + outer[:, 0:1] * ends[0] + outer[:, 1:2] * ends[1]


GELU_A, GELU_B = 0.7978845608028654, 0.044715
FF_TILE = 256
EXTRA = 16


def expert_kernel(own_ref, x_ref, dy_ref, wg_ref, wu_ref, wd_ref, *refs):
    h_ref, dg_ref, du_ref, dx_ref, part_ref, acc_ref, gate_ref = refs[-7:]
    step = pl.program_id(0)
    rows = dy_ref.shape[0]
    chunk = rows // 2 if rows % 32 == 0 else rows

    @pl.when(step == 0)
    def _():
        acc_ref[...] = jnp.zeros_like(acc_ref)
        part_ref[...] = jnp.zeros_like(part_ref)
        lines = x_ref[rows:, :rows].astype(jnp.float32)
        gate = jnp.sum(lines, axis=0, keepdims=True)
        gate_ref[...] = jnp.broadcast_to(gate, (LANES, rows)).T

    wg, wu, wd = wg_ref[...], wu_ref[...], wd_ref[...]
    kept = []
    for start in range(0, rows, chunk):
        at = slice(start, start + chunk)
        x, dy = x_ref[at, :], dy_ref[at, :]
        g = jnp.dot(x, wg, preferred_element_type=jnp.float32)
        u = jnp.dot(x, wu, preferred_element_type=jnp.float32)
        raw = lax.dot_general(dy, wd, NT, preferred_element_type=jnp.float32)
        square = g * g
        half = 0.5 + 0.5 * jnp.tanh(g * (GELU_A + (GELU_A * GELU_B) * square))
        gelu = g * half
        slope = half + 2.0 * gelu * (1.0 - half) * (GELU_A + (3.0 * GELU_A * GELU_B) * square)
        h = gelu * u
        product = raw * h
        total = product[:, :LANES]
        for column in range(LANES, product.shape[1], LANES):
            total = total + product[:, column : column + LANES]
        part_ref[at, :] += total
        dh = raw * gate_ref[at, :1]
        du = (dh * gelu).astype(jnp.bfloat16)
        dg = (dh * u * slope).astype(jnp.bfloat16)
        h_ref[at, :] = h.astype(jnp.bfloat16)
        dg_ref[at, :] = dg
        du_ref[at, :] = du
        kept.append((at, dg, du))
    for at, dg, du in kept:
        acc_ref[at, :] += lax.dot_general(dg, wg, NT, preferred_element_type=jnp.float32) + lax.dot_general(
            du, wu, NT, preferred_element_type=jnp.float32
        )

    @pl.when(step == pl.num_programs(0) - 1)
    def _():
        dx_ref[:rows, :] = acc_ref[...].astype(dx_ref.dtype)
        sums = jnp.sum(part_ref[...].T, axis=0, keepdims=True)
        high = sums.astype(jnp.bfloat16).astype(jnp.float32)
        middle = (sums - high).astype(jnp.bfloat16).astype(jnp.float32)
        line = lax.broadcasted_iota(jnp.int32, (EXTRA, rows), 0)
        lines = jnp.where(line == 0, high, jnp.where(line == 1, middle, jnp.where(line == 2, sums - high - middle, 0.0)))
        dx_ref[rows:, :] = jnp.zeros_like(dx_ref[rows:, :])
        dx_ref[rows:, :rows] = lines.astype(dx_ref.dtype)


def expert_block(at, count, x, dy, wgu, wd, earlier):
    rows, width = dy.shape
    hidden = wd.shape[0]
    tile = FF_TILE
    whole = jax.ShapeDtypeStruct((count * rows, hidden), jnp.bfloat16)
    fixed = lambda i, *_: (0, 0)
    out_block = pl.BlockSpec((rows, tile), lambda i, *_: (at, i))
    spec = pltpu.PrefetchScalarGridSpec(
        num_scalar_prefetch=1,
        grid=(hidden // tile,),
        in_specs=[
            pl.BlockSpec((rows + EXTRA, width), fixed),
            pl.BlockSpec((rows, width), fixed),
            pl.BlockSpec((width, tile), lambda i, *_: (0, i)),
            pl.BlockSpec((width, tile), lambda i, *_: (0, hidden // tile + i)),
            pl.BlockSpec((tile, width), lambda i, *_: (i, 0)),
        ]
        + [pl.BlockSpec(memory_space=pl.ANY)] * len(earlier),
        out_specs=[
            out_block,
            out_block,
            out_block,
            pl.BlockSpec((rows + EXTRA, width), fixed),
        ],
        scratch_shapes=[
            pltpu.VMEM((rows, LANES), jnp.float32),
            pltpu.VMEM((rows, width), jnp.float32),
            pltpu.VMEM((rows, LANES), jnp.float32),
        ],
    )
    return pl.pallas_call(
        expert_kernel,
        name="expert_block",
        out_shape=(
            whole,
            whole,
            whole,
            jax.ShapeDtypeStruct((rows + EXTRA, width), jnp.bfloat16),
        ),
        grid_spec=spec,
        input_output_aliases={6 + i: i for i in range(len(earlier))},
        compiler_params=pltpu.CompilerParams(dimension_semantics=("arbitrary",), vmem_limit_bytes=40 << 20),
        cost_estimate=pl.CostEstimate(
            flops=10 * rows * width * hidden, bytes_accessed=6 * width * hidden + 6 * rows * hidden, transcendentals=0
        ),
    )(jnp.zeros((1,), jnp.int32), x, dy, wgu, wgu, wd, *earlier)


EPS = 1e-06
FULL_PRECISION = lax.Precision.HIGHEST
ALL = ("z", "x", "exp")
SEQ = ("z", "x")
LOW = jnp.bfloat16


def dot32(a, b):
    return jnp.dot(a, b, preferred_element_type=jnp.float32)


def dot_nt(a, b):
    return lax.dot_general(a, b, NT, preferred_element_type=jnp.float32)


def dot_tn(a, b):
    return lax.dot_general(a, b, (((0,), (0,)), ((), ())), preferred_element_type=jnp.float32)


def partner(value, axis, offset):
    count = lax.axis_size(axis)
    return lax.ppermute(value, axis, [(i, i ^ offset) for i in range(count)])


def bits_of(count):
    return [1 << b for b in reversed(range(count.bit_length() - 1))]


def reorder(stacked, own):
    count = stacked.shape[0]
    return jnp.stack([lax.dynamic_index_in_dim(stacked, own ^ r, 0, keepdims=False) for r in range(count)])


def gather_double(value, steps):
    for axis, bit in steps:
        other = partner(value, axis, bit)
        high = (lax.axis_index(axis) & bit) != 0
        value = jnp.stack([jnp.where(high, other, value), jnp.where(high, value, other)])
    return value


def scatter_halve(value, steps):
    gone = []
    for axis, bit, dim in steps:
        at = dim - sum(1 for d in gone if d < dim)
        gone.append(dim)
        high = (lax.axis_index(axis) & bit) != 0
        low_half = lax.index_in_dim(value, 0, at, keepdims=False)
        high_half = lax.index_in_dim(value, 1, at, keepdims=False)
        keep = jnp.where(high, high_half, low_half)
        give = jnp.where(high, low_half, high_half)
        value = (keep.astype(jnp.float32) + partner(give, axis, bit).astype(jnp.float32)).astype(LOW)
    return value


def ring_of(groups, split):
    order = []
    for x in range(split):
        line = range(groups) if x % 2 == 0 else reversed(range(groups))
        order += [z * split + x for z in line]
    place = [order.index(s) for s in range(len(order))]
    ahead = [(order[i], order[(i + 1) % len(order)]) for i in range(len(order))]
    return jnp.asarray(order, jnp.int32), jnp.asarray(place, jnp.int32), ahead


def pick(values, index):
    return lax.dynamic_index_in_dim(values, index, 0, keepdims=False)


def unwritten(shape, dtype):
    return pl.pallas_call(
        lambda out_ref: None,
        name="unwritten",
        out_shape=jax.ShapeDtypeStruct(shape, dtype),
        out_specs=pl.BlockSpec(memory_space=pl.ANY),
    )()


class RingGather:
    def __init__(self, piece, groups, split, own):
        self.order, place, self.ahead = ring_of(groups, split)
        self.count = groups * split
        self.here = pick(place, own)
        self.rows = piece.shape[0]
        self.whole = unwritten((self.count * self.rows, piece.shape[1]), piece.dtype)
        self.whole = lax.dynamic_update_slice_in_dim(self.whole, piece, own * self.rows, 0)
        self.forward = self.backward = piece
        self.round = 0
        self.waiting = []

    def step(self):
        self.settle()
        self.round += 1
        k = self.round
        self.forward = lax.ppermute(self.forward, SEQ, self.ahead)
        self.waiting.append((self.forward, -k))
        if k < self.count - self.count // 2:
            self.backward = lax.ppermute(self.backward, SEQ, [(b, a) for a, b in self.ahead])
            self.waiting.append((self.backward, k))

    def settle(self):
        for piece, k in self.waiting:
            at = pick(self.order, (self.here + k + self.count) % self.count) * self.rows
            self.whole = lax.dynamic_update_slice_in_dim(self.whole, piece, at, 0)
        self.waiting = []

    def after(self, value):
        value, self.forward, self.backward = lax.optimization_barrier((value, self.forward, self.backward))
        self.waiting = [(self.forward if k < 0 else self.backward, k) for _, k in self.waiting]
        return value

    def finish(self):
        while self.round < self.count // 2:
            self.step()
        self.settle()
        return self.whole


class RingScatter:
    def __init__(self, totals, groups, split, own):
        self.order, place, self.ahead = ring_of(groups, split)
        self.count = groups * split
        self.here = pick(place, own)
        self.rows = totals[0].shape[0] // self.count
        self.totals = totals
        self.round = 0
        self.forward = self.backward = None

    def block(self, total, offset):
        at = pick(self.order, (self.here + offset + self.count) % self.count) * self.rows
        return lax.dynamic_slice_in_dim(total, at, self.rows, 0)

    def load(self, coming, offset):
        own = [self.block(total, offset) for total in self.totals]
        if coming is None:
            return own
        return [(a.astype(jnp.float32) + b.astype(jnp.float32)).astype(LOW) for a, b in zip(own, coming)]

    def step(self):
        self.round += 1
        k, far = self.round, self.count // 2
        near = self.count - 1 - far
        if k <= far:
            parts = self.load(self.forward, far - k + 1)
            self.forward = [lax.ppermute(part, SEQ, self.ahead) for part in parts]
        if k <= near:
            parts = self.load(self.backward, k - near - 1)
            self.backward = [lax.ppermute(part, SEQ, [(b, a) for a, b in self.ahead]) for part in parts]

    def after(self, value):
        value, self.forward, self.backward = lax.optimization_barrier((value, self.forward, self.backward))
        return value

    def finish(self):
        while self.round < self.count // 2:
            self.step()
        own = [self.block(total, 0).astype(jnp.float32) for total in self.totals]
        return [
            a + b.astype(jnp.float32) + c.astype(jnp.float32) for a, b, c in zip(own, self.forward, self.backward)
        ]


def norm_scale(value):
    return lax.rsqrt(jnp.mean(value * value, axis=-1, keepdims=True) + EPS)


def norm_back(scale, normed, gain, grad):
    scaled = grad * gain
    return scale * (scaled - normed * jnp.mean(scaled * normed, axis=-1, keepdims=True))


def split3(value):
    high = value.astype(LOW)
    rest = value - high.astype(jnp.float32)
    middle = rest.astype(LOW)
    return [high, middle, (rest - middle.astype(jnp.float32)).astype(LOW)]


def per_device(
    block_in,
    cotangent,
    segment_ids,
    expert_routes,
    pair_priority,
    gain_attention,
    w_query,
    w_key,
    w_value,
    w_out,
    bias_table,
    gain_experts,
    w_router,
    w_gate,
    w_up,
    w_down,
):
    groups, local_len, width = block_in.shape
    tokens = groups * local_len
    rows_own, hd = w_query.shape
    split = lax.axis_size("x")
    exp_count = lax.axis_size("exp")
    seq_count = groups * split
    length = local_len * seq_count
    x_at, z_at, e_at = lax.axis_index("x"), lax.axis_index("z"), lax.axis_index("exp")
    s_at = z_at * split + x_at
    head_width = hd // split
    heads_here = head_width // HEAD_DIM
    experts_all = w_router.shape[1]
    bias_own = bias_table.shape[0]
    tile = min(TILE, local_len)
    own = s_at.astype(jnp.int32).reshape(1)
    z_bits, x_bits, e_bits = bits_of(groups), bits_of(split), bits_of(exp_count)

    input_r = reorder(block_in, z_at)

    arrived = [[None] * split for _ in range(groups)]
    for rz in reversed(range(groups)):
        arrived[rz][0] = partner(input_r[rz], "z", rz) if rz else input_r[0]
    small = jnp.concatenate(
        [
            gain_attention[:, None],
            gain_experts[:, None],
            jnp.pad(bias_table, (0, rows_own - bias_own))[:, None],
            w_router,
        ],
        axis=1,
    )
    small = jnp.pad(small, ((0, 0), (0, LANES - small.shape[1]))).astype(LOW)
    share = jnp.stack(
        [part.astype(LOW).reshape(rows_own, split, head_width) for part in (w_query, w_key, w_value)], axis=2
    )
    share = share.reshape(rows_own, split, 3 * head_width).transpose(1, 0, 2)
    common = jnp.concatenate([w_out.astype(LOW), small], axis=1)
    share = jnp.concatenate([share, jnp.broadcast_to(common, (split,) + common.shape)], axis=2)
    shares = [lax.dynamic_index_in_dim(share, x_at ^ r, 0, keepdims=False) for r in range(split)]
    shares = [shares[0]] + [partner(shares[r], "x", r) for r in range(1, split)]
    by_x = reorder(jnp.stack(shares), x_at)
    for rx in range(1, split):
        arrived[0][rx] = partner(arrived[0][0], "x", rx)
    packed = gather_double(by_x, [("z", b) for b in z_bits])
    near = [arrived[rz][0] for rz in range(1, groups)]
    packed, near = lax.optimization_barrier((packed, near))
    for rz in range(1, groups):
        arrived[rz][0] = near[rz - 1]
        for rx in range(1, split):
            arrived[rz][rx] = partner(arrived[rz][0], "x", rx)
    packed = gather_double(packed, [("exp", b) for b in e_bits[:-1]])
    packed, arrived = lax.optimization_barrier((packed, arrived))
    sequence = jnp.stack([block for line in arrived for block in line]).reshape(length, width)

    gate_up_own = jnp.concatenate([w_gate[0].astype(LOW), w_up[0].astype(LOW)], axis=1)
    sequence, gate_up_own, down_own = lax.optimization_barrier((sequence, gate_up_own, w_down[0].astype(LOW)))
    down_w = lax.all_gather(down_own, SEQ, axis=0, tiled=True)
    gate_up_ring = RingGather(gate_up_own, groups, split, s_at)
    gate_up_ring.step()
    packed = gather_double(packed, [("exp", b) for b in e_bits[-1:]])
    ne, nz, nx = len(e_bits), len(z_bits), len(x_bits)
    packed = packed.transpose(
        tuple(ne + i for i in reversed(range(nz))) + (ne + nz,) + tuple(reversed(range(ne))) + (ne + nz + 1, ne + nz + 2)
    ).reshape(width, 3 * head_width + width + LANES)
    qkv_w, small_all = packed[:, : 3 * head_width], packed[:, 3 * head_width + width :]
    out_w = packed[:, 3 * head_width : 3 * head_width + width]
    gain_one = small_all[:, 0].astype(jnp.float32)
    gain_two = small_all[:, 1].astype(jnp.float32)
    table_all = small_all[:, 2].reshape(-1, rows_own)[:, :bias_own].reshape(-1, BUCKETS)
    router_t = small_all[:, 3 : 3 + experts_all].T
    table_rows = lax.dynamic_slice_in_dim(table_all, x_at * heads_here, heads_here, 0)

    routes = expert_routes.reshape(tokens, -1)
    top_count = routes.shape[1]
    priority = pair_priority.reshape(-1)
    pair_experts = routes.reshape(-1)
    ahead = (pair_experts[None, :] == pair_experts[:, None]) & (priority[None, :] < priority[:, None])
    slots = jnp.sum(ahead.astype(jnp.int32), axis=1)
    capacity = (5 * top_count * tokens + 4 * experts_all - 1) // (4 * experts_all)
    slot_count = experts_all * capacity
    slot_index = jnp.where(slots < capacity, (pair_experts ^ e_at) * capacity + slots, slot_count)
    slot_index = slot_index.reshape(tokens, top_count)
    every_slot = jnp.arange(slot_count, dtype=jnp.int32)[None, :]
    table = sum((slot_index[:, k : k + 1] == every_slot).astype(LOW) for k in range(top_count))
    tables = [table[:, r * capacity : (r + 1) * capacity] for r in range(exp_count)]
    grad_low = cotangent.reshape(tokens, width)
    grad_slots = [dot_tn(part, grad_low).astype(LOW) for part in tables]

    wide = sequence.astype(jnp.float32)
    normed_one = (wide * norm_scale(wide) * gain_one).astype(LOW)
    qkv = dot32(normed_one, qkv_w).astype(LOW)
    qkv, grad_slots = lax.optimization_barrier((qkv, grad_slots))
    qkv = gate_up_ring.after(qkv)
    gate_up_ring.step()
    grad_slots = [grad_slots[0]] + [partner(grad_slots[r], "exp", r) for r in range(1, exp_count)]
    segments = lax.dynamic_index_in_dim(segment_ids, z_at, 0, keepdims=False)
    ranges = tile_ranges(segments, tile)
    seg_blocks = segments.reshape(seq_count, local_len)
    query_side, key_side = segment_columns(reorder(seg_blocks, s_at).reshape(length))
    rows = bias_rows(table_rows, tile)
    ends = jnp.stack([table_rows[:, 15], table_rows[:, 31]], axis=1).astype(jnp.float32)
    contexts, log_totals = attend_forward(qkv, query_side, key_side, ranges, rows, ends, own, tile)
    contexts = gate_up_ring.after(contexts)
    contexts, grad_slots = lax.optimization_barrier((contexts, grad_slots))
    gate_up_w = gate_up_ring.finish()

    def exchange_positions(blocks):
        return lax.all_to_all(blocks, SEQ, split_axis=0, concat_axis=0, tiled=True)

    context_local = exchange_positions(contexts.reshape(seq_count, local_len, head_width))
    context_local = (
        context_local.reshape(groups, split, local_len, head_width).transpose(0, 2, 1, 3).reshape(tokens, hd)
    )
    inputs = block_in.astype(jnp.float32).reshape(tokens, width)
    mid = inputs + dot32(context_local, out_w)
    scale_two = norm_scale(mid)
    normed_two = (mid * scale_two * gain_two).astype(LOW)

    logits = dot_nt(router_t, normed_two)
    exponent = jnp.exp(logits - jnp.max(logits, axis=0, keepdims=True))
    probabilities = exponent / jnp.sum(exponent, axis=0, keepdims=True)
    expert_ids = jnp.arange(experts_all, dtype=jnp.int32)[:, None]
    chosen = sum((routes[:, k][None, :] == expert_ids).astype(jnp.float32) for k in range(top_count))
    chosen_total = jnp.sum(probabilities * chosen, axis=0, keepdims=True)
    gates = probabilities * chosen / chosen_total
    gates_r = reorder(gates, e_at)

    gate_slots = jnp.sum(
        table.astype(jnp.float32).reshape(tokens, exp_count, capacity) * gates_r.T[:, :, None], axis=0
    )
    gate_lines = jnp.pad(jnp.stack(split3(gate_slots), axis=1), ((0, 0), (0, EXTRA - 3), (0, width - capacity)))

    def values_below(rows_):
        return jnp.sum(rows_[capacity : capacity + 3, :capacity].astype(jnp.float32), axis=0)

    sent = [None] * exp_count
    for r in reversed(range(exp_count)):
        sent[r] = jnp.concatenate([dot_tn(tables[r], normed_two).astype(LOW), gate_lines[r]], axis=0)
        if r:
            sent[r] = partner(sent[r], "exp", r)

    earlier = ()
    back = [None] * exp_count
    turns = [0] + list(range(2, exp_count)) + [1]
    for turn, r in enumerate(turns):
        if turn >= 3:
            ready = turns[turn - 2]
            sent[r], back[ready] = lax.optimization_barrier((sent[r], back[ready]))
        hidden, gate_low, up_low, dx = expert_block(
            r, exp_count, sent[r], grad_slots[r], gate_up_w, down_w, earlier
        )
        earlier = (hidden, gate_low, up_low)
        back[r] = partner(dx, "exp", r) if r else dx

    sent, hidden = lax.optimization_barrier((sent, hidden))
    slot_rows = jnp.concatenate([rows_[:capacity] for rows_ in sent], axis=0)
    slot_gates = jnp.concatenate([values_below(rows_) for rows_ in sent], axis=0)[:, None]
    slot_grads = (slot_gates * jnp.concatenate(grad_slots, axis=0).astype(jnp.float32)).astype(LOW)

    gate_grad = jnp.sum(
        table.astype(jnp.float32).reshape(tokens, exp_count, capacity) * jnp.stack([values_below(rows_) for rows_ in back])[None], axis=2
    )
    gate_grad = reorder(gate_grad.T, e_at)
    chosen_grad = chosen * (gate_grad - jnp.sum(gates * gate_grad, axis=0, keepdims=True)) / chosen_total
    logit_grad = probabilities * (chosen_grad - jnp.sum(probabilities * chosen_grad, axis=0, keepdims=True))
    logit_pieces = jnp.concatenate(split3(logit_grad), axis=0)
    router_sum = jnp.sum(dot32(logit_pieces, normed_two).reshape(3, experts_all, width), axis=0)
    normed_two_grad = dot_tn(logit_pieces, jnp.concatenate([router_t] * 3, axis=0))
    for r in range(exp_count):
        normed_two_grad = normed_two_grad + dot32(tables[r], back[r][:capacity])
    unit_two = mid * scale_two
    gain_two_sum = jnp.sum(normed_two_grad * unit_two, axis=0)
    grad_out = grad_low.astype(jnp.float32)
    mid_grad = grad_out + norm_back(scale_two, unit_two, gain_two, normed_two_grad)
    attention_grad = mid_grad.astype(LOW)
    context_grad = dot_nt(attention_grad, out_w).astype(LOW)
    context_grad, up_low, gate_low = lax.optimization_barrier((context_grad, up_low, gate_low))
    gate_sum = dot_tn(slot_rows, gate_low).astype(LOW)
    up_sum = dot_tn(slot_rows, up_low).astype(LOW)
    context_grad = (
        context_grad.reshape(groups, local_len, split, head_width)
        .transpose(0, 2, 1, 3)
        .reshape(seq_count, local_len, head_width)
    )
    context_heads = exchange_positions(context_grad).reshape(length, head_width)

    def scatter_experts(total):
        return lax.psum_scatter(total, SEQ, scatter_dimension=0, tiled=True)

    context_heads, gate_sum, up_sum = lax.optimization_barrier((context_heads, gate_sum, up_sum))

    halving = [("exp", b, 1 + nz + nx + ne - 1 - i) for i, b in enumerate(reversed(e_bits))]
    halving += [("z", b, 1 + nz - 1 - i) for i, b in enumerate(reversed(z_bits))]
    out_sum = dot_tn(context_local, attention_grad).astype(LOW)

    ring = RingScatter([gate_sum, up_sum], groups, split, s_at)
    grads, diag, far = (), [], []
    pairs = head_width // LANES
    for pair in range(pairs):
        ring.step()
        *grads, pair_diag, pair_far = attend_backward(
            pair, qkv, context_heads, contexts, log_totals, query_side, key_side, ranges, rows, ends, own, tile, tuple(grads)
        )
        grads = ring.after(grads)
        if pair == 0:
            grads, hidden = lax.optimization_barrier((grads, hidden))
            down_sum = dot_tn(hidden, slot_grads).astype(LOW)
            down_owned = scatter_experts(down_sum)
        if pair == min(1, pairs - 1):
            grads, hidden, down_sum = lax.optimization_barrier((grads, hidden, down_sum))
            expert_out = (slot_gates * dot32(hidden, down_w)).astype(LOW)
            expert_out = reorder(expert_out.reshape(exp_count, capacity, width), e_at)
            returned = lax.all_to_all(expert_out, "exp", split_axis=0, concat_axis=0, tiled=True)
        if pair == min(2, pairs - 1):
            grads, expert_out = lax.optimization_barrier((grads, expert_out))
        if pair == pairs - 1:
            grads, returned = lax.optimization_barrier((grads, returned))
        diag.append(pair_diag)
        far.append(pair_far)
    diag, far = jnp.concatenate(diag), jnp.concatenate(far)
    query_back, key_back, value_back, down_owned = lax.optimization_barrier((*grads, down_owned))
    gate_owned, up_owned = ring.finish()
    table_local = bucket_sums(diag, far, tile)

    def through(grads, part):
        return dot_nt(grads, qkv_w[:, part * head_width : (part + 1) * head_width])

    out_parts = width // head_width
    weight_sum = jnp.stack(
        [dot_tn(normed_one, grads).astype(LOW) for grads in (query_back, key_back, value_back)]
        + [out_sum[:, i * head_width : (i + 1) * head_width] for i in range(out_parts)]
    )
    weight_sum, query_back, key_back, value_back = lax.optimization_barrier(
        (weight_sum, query_back, key_back, value_back)
    )
    normed_part = through(query_back, 0) + through(key_back, 1) + through(value_back, 2)
    half = width // 2
    normed_part = normed_part.reshape(groups, split, local_len, width)

    sides = [normed_part[:, rx].astype(LOW) for rx in range(1, split)]
    first = [partner(side[:, :, :half], "x", rx) for rx, side in enumerate(sides, 1)]
    first, rest = lax.optimization_barrier((first, [side[:, :, half:] for side in sides]))

    def send_back(own_part, coming):
        total = own_part + sum(part.astype(jnp.float32) for part in coming)
        total = reorder(total.astype(LOW), z_at)
        return lax.all_to_all(total, "z", split_axis=0, concat_axis=0, tiled=True)

    normed_first = send_back(normed_part[:, 0, :, :half], first)
    rest = [partner(side, "x", rx) for rx, side in enumerate(rest, 1)]
    normed_second = send_back(normed_part[:, 0, :, half:], rest)
    weight_part = scatter_halve(
        weight_sum.reshape((3 + out_parts,) + (2,) * (nz + nx + ne) + (rows_own, head_width)), halving[:ne]
    )
    weight_part = scatter_halve(weight_part, halving[ne:]).reshape(3 + out_parts, split, rows_own, head_width)
    weight_own = [lax.dynamic_index_in_dim(weight_part, x_at ^ r, 1, keepdims=False) for r in range(split)]
    weight_own = [weight_own[0]] + [partner(weight_own[r], "x", r) for r in range(1, split)]
    normed_second, weight_own = lax.optimization_barrier((normed_second, weight_own))
    block_out = (mid + dot32(table, reorder(returned, e_at).reshape(slot_count, width))).astype(LOW)

    block_out = block_out.reshape(groups, local_len, width)
    out_w_out = sum(part[3:].astype(jnp.float32) for part in weight_own)
    out_w_out = out_w_out.transpose(1, 0, 2).reshape(rows_own, width)
    qkv_own = reorder(jnp.stack([part[:3] for part in weight_own]), x_at)
    qkv_own = qkv_own.transpose(1, 2, 0, 3).reshape(3, rows_own, hd).astype(jnp.float32)

    normed_one_grad = jnp.concatenate([normed_first, normed_second], axis=2).astype(jnp.float32).reshape(tokens, width)
    scale_one = norm_scale(inputs)
    unit_one = inputs * scale_one
    gain_one_sum = jnp.sum(normed_one_grad * unit_one, axis=0)
    block_in_grad = (mid_grad + norm_back(scale_one, unit_one, gain_one, normed_one_grad)).reshape(
        groups, local_len, width
    )

    table_sum = lax.dynamic_update_slice_in_dim(
        jnp.zeros(table_all.shape, jnp.float32), table_local, x_at * heads_here, 0
    ).reshape(-1, bias_own)
    table_sum = jnp.pad(table_sum, ((0, 0), (0, rows_own - bias_own)))[:, None, :]
    little = jnp.concatenate(
        [
            gain_one_sum.reshape(-1, 1, rows_own),
            gain_two_sum.reshape(-1, 1, rows_own),
            table_sum,
            router_sum.reshape(experts_all, -1, rows_own).transpose(1, 0, 2),
        ],
        axis=1,
    )
    little = jnp.sum(lax.all_to_all(little, ALL, split_axis=0, concat_axis=0, tiled=True), axis=0)
    return (
        block_out,
        block_in_grad,
        little[0],
        qkv_own[0],
        qkv_own[1],
        qkv_own[2],
        out_w_out,
        little[2, :bias_own],
        little[1],
        little[3:].T,
        gate_owned.astype(jnp.float32)[None],
        up_owned.astype(jnp.float32)[None],
        down_owned.astype(jnp.float32)[None],
    )


def solution(mesh):
    def run(*args):
        groups = args[0].shape[0] // mesh.shape["exp"]
        seq_count, exp_count = mesh.shape["seq"], mesh.shape["exp"]
        grid = mesh.devices.reshape(groups, seq_count // groups, exp_count)
        fine = jax.sharding.Mesh(grid, ALL)
        placed = P("exp", SEQ, None)
        whole = P(ALL)
        matrix = P(ALL, None)
        return jax.shard_map(
            per_device,
            mesh=fine,
            in_specs=(
                placed, placed, P("exp", None), placed, placed,
                whole, matrix, matrix, matrix, matrix, whole, whole, matrix,
                placed, placed, placed,
            ),
            out_specs=(
                placed, placed, whole, matrix, matrix, matrix, matrix, whole, whole, matrix,
                placed, placed, placed,
            ),
            check_vma=False,
        )(*args)

    return run
```

```python
from functools import partial

import jax
import jax.numpy as jnp
import numpy as np
from jax import lax
from jax.experimental import pallas as pl
from jax.experimental.pallas import tpu as pltpu
from jax.sharding import PartitionSpec as P

HEAD_DIM = 64
BUCKETS = 32
THRESHOLDS = (12, 16, 23, 32, 46, 64, 91)
MASKED = -1e30
TILE = 256
LANES = 128
NT = (((1,), (1,)), ((), ()))


def bucket_of(d):
    a = np.abs(d)
    extra = sum((a >= t).astype(np.int64) for t in THRESHOLDS)
    return np.where(a < 8, a, 8 + extra) + 16 * (d > 0)


def bias_rows(table_rows, tile):
    u = np.arange(2 * tile)
    x = np.where(u < tile, u, u - 2 * tile)
    ids = np.stack([bucket_of(step * tile - x) for step in (-1, 0, 1)])
    hot = (ids.reshape(-1)[None, :] == np.arange(BUCKETS)[:, None]).astype(np.float32)
    rows = jnp.dot(table_rows.astype(jnp.bfloat16), jnp.asarray(hot, jnp.bfloat16), preferred_element_type=jnp.float32)
    return rows.reshape(table_rows.shape[0], 3, 2 * tile)


def tile_ranges(segments, tile):
    blocks = segments.reshape(-1, tile)
    first, last = blocks[:, 0], blocks[:, -1]
    low = jnp.sum((last[None, :] < first[:, None]).astype(jnp.int32), axis=1)
    high = jnp.sum((first[None, :] <= last[:, None]).astype(jnp.int32), axis=1)
    return jnp.stack([low, high])


def segment_columns(segments):
    lane = jnp.arange(LANES, dtype=jnp.int32)[None, :]
    seg = segments[:, None]
    same = seg == lane
    query_side = jnp.where(same & (lane < 4), MASKED, 0.0).astype(jnp.bfloat16)
    key_side = jnp.where(lane < 4, (~same).astype(jnp.float32), (lane < 9).astype(jnp.float32)).astype(jnp.bfloat16)
    return query_side, key_side


def toeplitz(row, tile):
    wide = jnp.broadcast_to(row, (tile, row.shape[1]))
    return pltpu.roll(wide, 0, 1, stride=1, stride_axis=0)[:, :tile]


def block_at(index, own, tile):
    return pl.ds(pl.multiple_of((index ^ own[0]) * tile, tile), tile)


def fwd_kernel(ranges, ends, own, q_ref, k_ref, v_ref, qs_ref, ks_ref, rows_ref, o_ref, lse_ref, bias_ref, vt_ref):
    group, qb = pl.program_id(0), pl.program_id(1)
    tile, span = q_ref.shape
    heads = span // HEAD_DIM

    @pl.when(qb == 0)
    def _():
        for h in range(heads):
            for step in range(3):
                bias_ref[h, step] = toeplitz(rows_ref[h, step : step + 1, :], tile)
        for start in range(0, v_ref.shape[0], tile):
            vt_ref[:, start : start + tile] = v_ref[start : start + tile, :].T

    low, high = ranges[0, qb], ranges[1, qb]
    lane = lax.broadcasted_iota(jnp.int32, (tile, LANES), 1)
    q = q_ref[...] * jnp.bfloat16(HEAD_DIM**-0.5)
    qs = qs_ref[...]
    halves = []
    for h in range(heads):
        part = q[:, h // 2 * LANES : (h // 2 + 1) * LANES]
        keep = (lane < HEAD_DIM) if h % 2 == 0 else (lane >= HEAD_DIM)
        halves.append(jnp.where(keep, part, jnp.zeros_like(part)))

    def side(h, which):
        if which == 1:
            extra = qs
        else:
            value = ends[heads * group + h, which // 2].astype(jnp.bfloat16)
            extra = jnp.where(lane == 7, value, qs)
        return jnp.concatenate([halves[h], extra], axis=1)

    def visit(which):
        queries = [side(h, which) for h in range(heads)]

        def step(kb, carry):
            keys = block_at(kb, own, tile)
            ks = ks_ref[keys, :]
            scores = []
            for h in range(heads):
                kx = jnp.concatenate([k_ref[keys, h // 2 * LANES : (h // 2 + 1) * LANES], ks], axis=1)
                scores.append(lax.dot_general(kx, queries[h], NT, preferred_element_type=jnp.float32))
            kept = []
            for h in range(heads):
                peak, total, acc = carry[h]
                s = scores[h]
                if which == 1:
                    s = s + bias_ref[h, kb - qb + 1]
                new = jnp.maximum(peak, jnp.max(s, axis=0, keepdims=True))
                p = jnp.exp(s - new)
                scale = jnp.exp(peak - new)
                total = total * scale + jnp.sum(p, axis=0, keepdims=True)
                kept.append((new, total, acc, scale, p.astype(jnp.bfloat16)))
            out = []
            for h in range(heads):
                new, total, acc, scale, p = kept[h]
                vt = vt_ref[h * HEAD_DIM : (h + 1) * HEAD_DIM, keys]
                acc = acc * scale + jnp.dot(vt, p, preferred_element_type=jnp.float32)
                out.append((new, total, acc))
            return tuple(out)

        return step

    start = tuple(
        (
            jnp.full((1, tile), -3e38, jnp.float32),
            jnp.zeros((1, tile), jnp.float32),
            jnp.zeros((HEAD_DIM, tile), jnp.float32),
        )
        for _ in range(heads)
    )
    near_low, near_high = jnp.maximum(low, qb - 1), jnp.minimum(high, qb + 2)
    state = lax.fori_loop(near_low, near_high, visit(1), start)
    state = lax.fori_loop(low, near_low, visit(0), state)
    state = lax.fori_loop(near_high, high, visit(2), state)
    outs = []
    for h in range(heads):
        peak, total, acc = state[h]
        outs.append(acc / total)
        lse_ref[h // 2, h % 2 : h % 2 + 1, :] = peak + jnp.log(total)
    o_ref[...] = jnp.concatenate(outs, axis=0).T.astype(o_ref.dtype)


FWD_PAIRS = 4


def attend_forward(qkv, qs, ks, ranges, rows, ends, own, tile):
    length, width = qkv.shape[0], qkv.shape[1] // 3
    pairs = width // LANES
    together = FWD_PAIRS if pairs % FWD_PAIRS == 0 else 1
    span = together * LANES
    tiles = length // tile
    spec = pltpu.PrefetchScalarGridSpec(
        num_scalar_prefetch=3,
        grid=(pairs // together, tiles),
        in_specs=[
            pl.BlockSpec((tile, span), lambda p, i, r, e, own: (i ^ own[0], p)),
            pl.BlockSpec((length, span), lambda p, i, *_: (0, width // span + p)),
            pl.BlockSpec((length, span), lambda p, i, *_: (0, 2 * (width // span) + p)),
            pl.BlockSpec((tile, LANES), lambda p, i, r, e, own: (i ^ own[0], 0)),
            pl.BlockSpec((length, LANES), lambda p, i, *_: (0, 0)),
            pl.BlockSpec((2 * together, 3, 2 * tile), lambda p, i, *_: (p, 0, 0)),
        ],
        out_specs=[
            pl.BlockSpec((tile, span), lambda p, i, *_: (i, p)),
            pl.BlockSpec((together, 2, tile), lambda p, i, *_: (p, 0, i)),
        ],
        scratch_shapes=[
            pltpu.VMEM((2 * together, 3, tile, tile), jnp.float32),
            pltpu.VMEM((span, length), jnp.bfloat16),
        ],
    )
    return pl.pallas_call(
        fwd_kernel,
        name="attend_forward",
        out_shape=(
            jax.ShapeDtypeStruct((length, width), jnp.bfloat16),
            jax.ShapeDtypeStruct((pairs, 2, length), jnp.float32),
        ),
        grid_spec=spec,
        compiler_params=pltpu.CompilerParams(
            dimension_semantics=("arbitrary", "arbitrary"), vmem_limit_bytes=48 << 20
        ),
        cost_estimate=pl.CostEstimate(flops=length * length * width * 4, bytes_accessed=length * width * 8, transcendentals=0),
    )(ranges, ends, own, qkv, qkv, qkv, qs, ks, rows)


def pieces(row):
    high = row.astype(jnp.bfloat16).astype(jnp.float32)
    mid = (row - high).astype(jnp.bfloat16).astype(jnp.float32)
    return high, mid, row - high - mid


def bwd_kernel(ranges, ends, own, q_ref, k_ref, v_ref, do_ref, o_ref, lse_ref, qs_ref, ks_ref, rows_ref, *refs):
    (dq_ref, dk_ref, dv_ref, diag_ref, far_ref,
     qx_ref, dox_ref, kt_ref, bias_ref, dsum_ref, fsum_ref, dqt_ref, dka_ref, dva_ref) = refs[-14:]
    pair = own[1]
    length = q_ref.shape[0]
    tile = bias_ref.shape[2]
    tiles = length // tile
    for h in range(2):
        for step in range(3):
            bias_ref[h, step] = toeplitz(rows_ref[h, step : step + 1, :], tile)
    dsum_ref[...] = jnp.zeros_like(dsum_ref)
    fsum_ref[...] = jnp.zeros_like(fsum_ref)
    dqt_ref[...] = jnp.zeros_like(dqt_ref)
    lane = lax.broadcasted_iota(jnp.int32, (tile, LANES), 1)
    sub = lax.broadcasted_iota(jnp.int32, (LANES, tile), 0)
    pick = (lax.broadcasted_iota(jnp.int32, (8, LANES), 1) // HEAD_DIM == lax.broadcasted_iota(jnp.int32, (8, LANES), 0)).astype(jnp.float32)

    @pl.loop(0, tiles)
    def _(i):
        line = pl.ds(pl.multiple_of(i * tile, tile), tile)
        at = block_at(i, own, tile)
        q = q_ref[at, :] * jnp.bfloat16(HEAD_DIM**-0.5)
        do = do_ref[line, :]
        zero = jnp.zeros_like(q)
        product = do.astype(jnp.float32) * o_ref[line, :].astype(jnp.float32)
        delta = lax.dot_general(pick, product, NT, precision=lax.Precision.HIGHEST, preferred_element_type=jnp.float32)
        kt_ref[:, at] = k_ref[at, :].T
        for h in range(2):
            keep = (lane < HEAD_DIM) if h == 0 else (lane >= HEAD_DIM)
            a, b, c = pieces(-lse_ref[0, h : h + 1, line])
            extra = jnp.where(sub == 4, a, jnp.where(sub == 5, b, jnp.where(sub == 6, c, 0.0)))
            extra = extra.T.astype(jnp.bfloat16) + qs_ref[at, :]
            left, right = ends[2 * pair + h, 0].astype(jnp.bfloat16), ends[2 * pair + h, 1].astype(jnp.bfloat16)
            extra = jnp.where(lane == 7, left, jnp.where(lane == 8, right, extra))
            qx_ref[h, at, :] = jnp.concatenate([jnp.where(keep, q, zero), extra], axis=1)
            a, b, c = pieces(-delta[h : h + 1, :])
            extra = jnp.where(sub == 4, a, jnp.where(sub == 5, b, jnp.where(sub == 6, c, 0.0)))
            dox_ref[h, at, :] = jnp.concatenate([jnp.where(keep, do, zero), extra.T.astype(jnp.bfloat16)], axis=1)

    ones3 = ((lane >= 4) & (lane < 7)).astype(jnp.bfloat16)

    @pl.loop(0, tiles)
    def _(kb):
        low, high = ranges[0, kb], ranges[1, kb]
        keys = block_at(kb, own, tile)
        k, ks = k_ref[keys, :], ks_ref[keys, :]
        vx = jnp.concatenate([v_ref[keys, :], ones3], axis=1)
        nil = jnp.zeros_like(ks)
        dka_ref[...] = jnp.zeros_like(dka_ref)
        dva_ref[...] = jnp.zeros_like(dva_ref)

        def visit(which):
            if which == 0:
                extra = jnp.where(lane == 8, nil, ks)
            elif which == 2:
                extra = jnp.where(lane == 7, nil, ks)
            else:
                extra = jnp.where((lane == 7) | (lane == 8), nil, ks)
            kx = jnp.concatenate([k, extra], axis=1)

            def step(qb, carry):
                at = block_at(qb, own, tile)
                weights, grads, scores, products = [], [], [], []
                for h in range(2):
                    scores.append(lax.dot_general(kx, qx_ref[h, at, :], NT, preferred_element_type=jnp.float32))
                    products.append(lax.dot_general(vx, dox_ref[h, at, :], NT, preferred_element_type=jnp.float32))
                for h in range(2):
                    s = scores[h]
                    if which == 1:
                        s = s + bias_ref[h, kb - qb + 1]
                    p = jnp.exp(s)
                    ds = p * products[h]
                    if which == 1:
                        dsum_ref[h, kb - qb + 1] += ds
                    else:
                        fsum_ref[h, which // 2] += jnp.sum(ds.reshape(tile // 8, 8, tile), axis=0)
                    weights.append(p.astype(jnp.bfloat16))
                    grads.append(ds.astype(jnp.bfloat16))
                both_do = jnp.concatenate([dox_ref[0, at, :LANES], dox_ref[1, at, :LANES]], axis=0)
                both_q = jnp.concatenate([qx_ref[0, at, :LANES], qx_ref[1, at, :LANES]], axis=0)
                dva_ref[...] += jnp.dot(jnp.concatenate(weights, axis=1), both_do, preferred_element_type=jnp.float32)
                dka_ref[...] += jnp.dot(jnp.concatenate(grads, axis=1), both_q, preferred_element_type=jnp.float32)
                for h in range(2):
                    part = slice(h * HEAD_DIM, (h + 1) * HEAD_DIM)
                    dqt_ref[part, at] += jnp.dot(kt_ref[part, keys], grads[h], preferred_element_type=jnp.float32)
                return carry

            return step

        near_low, near_high = jnp.maximum(low, kb - 1), jnp.minimum(high, kb + 2)
        lax.fori_loop(near_low, near_high, visit(1), 0)
        lax.fori_loop(near_high, high, visit(0), 0)
        lax.fori_loop(low, near_low, visit(2), 0)
        dk_ref[keys, :] = dka_ref[...].astype(dk_ref.dtype)
        dv_ref[keys, :] = dva_ref[...].astype(dv_ref.dtype)

    @pl.loop(0, tiles)
    def _(i):
        at = pl.ds(pl.multiple_of(i * tile, tile), tile)
        dq_ref[at, :] = (dqt_ref[:, at] * HEAD_DIM**-0.5).T.astype(dq_ref.dtype)

    for h in range(2):
        for step in range(3):
            diag_ref[h, step : step + 1, :] = diagonals(dsum_ref, h, step, tile)
        for step in range(2):
            total = jnp.sum(fsum_ref[h, step], axis=0, keepdims=True)
            far_ref[h, step : step + 1, :] = total


def diagonals(dsum_ref, h, step, tile):
    width = 2 * tile
    acc = jnp.zeros((8, width), jnp.float32)
    for group in range(tile // 8):
        part = dsum_ref[h, step, group * 8 : (group + 1) * 8, :]
        part = jnp.concatenate([part, jnp.zeros((8, tile), jnp.float32)], axis=1)
        acc = acc + (pltpu.roll(part, width - 8 * group, 1) if group else part)
    row = lax.broadcasted_iota(jnp.int32, (8, width), 0)
    for bit in (1, 2, 4):
        acc = jnp.where((row & bit) != 0, pltpu.roll(acc, width - bit, 1), acc)
    return jnp.sum(acc, axis=0, keepdims=True)


def attend_backward(pair, qkv, do, o, lse, qs, ks, ranges, rows, ends, own, tile, earlier):
    length, width = do.shape
    pairs = width // LANES
    own = jnp.concatenate([own, jnp.full((1,), pair, jnp.int32)])
    column = pl.BlockSpec((length, LANES), lambda p, r, e, own: (0, own[1]))
    fixed = pl.BlockSpec((length, LANES), lambda p, *_: (0, 0))
    spec = pltpu.PrefetchScalarGridSpec(
        num_scalar_prefetch=3,
        grid=(1,),
        in_specs=[
            column,
            pl.BlockSpec((length, LANES), lambda p, r, e, own: (0, pairs + own[1])),
            pl.BlockSpec((length, LANES), lambda p, r, e, own: (0, 2 * pairs + own[1])),
            column,
            column,
            pl.BlockSpec((1, 2, length), lambda p, r, e, own: (own[1], 0, 0)),
            fixed, fixed,
            pl.BlockSpec((2, 3, 2 * tile), lambda p, r, e, own: (own[1], 0, 0)),
        ]
        + [pl.BlockSpec(memory_space=pl.ANY)] * len(earlier),
        out_specs=[
            column, column, column,
            pl.BlockSpec((2, 3, 2 * tile), lambda p, *_: (p, 0, 0)),
            pl.BlockSpec((2, 2, tile), lambda p, *_: (p, 0, 0)),
        ],
        scratch_shapes=[
            pltpu.VMEM((2, length, 2 * LANES), jnp.bfloat16),
            pltpu.VMEM((2, length, 2 * LANES), jnp.bfloat16),
            pltpu.VMEM((LANES, length), jnp.bfloat16),
            pltpu.VMEM((2, 3, tile, tile), jnp.float32),
            pltpu.VMEM((2, 3, tile, tile), jnp.float32),
            pltpu.VMEM((2, 2, 8, tile), jnp.float32),
            pltpu.VMEM((LANES, length), jnp.float32),
            pltpu.VMEM((tile, LANES), jnp.float32),
            pltpu.VMEM((tile, LANES), jnp.float32),
        ],
    )
    low = jax.ShapeDtypeStruct((length, width), jnp.bfloat16)
    return pl.pallas_call(
        bwd_kernel,
        name="attend_backward",
        out_shape=(
            low, low, low,
            jax.ShapeDtypeStruct((2, 3, 2 * tile), jnp.float32),
            jax.ShapeDtypeStruct((2, 2, tile), jnp.float32),
        ),
        grid_spec=spec,
        input_output_aliases={12 + i: i for i in range(len(earlier))},
        compiler_params=pltpu.CompilerParams(
            dimension_semantics=("arbitrary",), vmem_limit_bytes=40 << 20
        ),
        cost_estimate=pl.CostEstimate(flops=length * length * LANES * 10, bytes_accessed=length * LANES * 16, transcendentals=0),
    )(ranges, ends, own, qkv, qkv, qkv, do, o, lse, qs, ks, rows, *earlier)


def bucket_sums(diag, far, tile):
    u = np.arange(2 * tile)
    x = np.where(u < tile, u, u - 2 * tile)
    ids = np.stack([bucket_of(step * tile - x) for step in (-1, 0, 1)])
    hot = (ids.reshape(-1)[:, None] == np.arange(BUCKETS)[None, :]).astype(np.float32)
    sums = jnp.dot(diag.reshape(diag.shape[0], -1), jnp.asarray(hot), precision=lax.Precision.HIGHEST)
    outer = jnp.sum(far, axis=2)
    ends = np.zeros((2, BUCKETS), np.float32)
    ends[0, 15] = 1
    ends[1, 31] = 1
    return sums + outer[:, 0:1] * ends[0] + outer[:, 1:2] * ends[1]


GELU_A, GELU_B = 0.7978845608028654, 0.044715
FF_TILE = 256
EXTRA = 16


def expert_kernel(own_ref, x_ref, dy_ref, wg_ref, wu_ref, wd_ref, *refs):
    h_ref, dg_ref, du_ref, dx_ref, part_ref, acc_ref, gate_ref = refs[-7:]
    step = pl.program_id(0)
    rows = dy_ref.shape[0]
    chunk = rows // 2 if rows % 32 == 0 else rows

    @pl.when(step == 0)
    def _():
        acc_ref[...] = jnp.zeros_like(acc_ref)
        part_ref[...] = jnp.zeros_like(part_ref)
        lines = x_ref[rows:, :rows].astype(jnp.float32)
        gate = jnp.sum(lines, axis=0, keepdims=True)
        gate_ref[...] = jnp.broadcast_to(gate, (LANES, rows)).T

    wg, wu, wd = wg_ref[...], wu_ref[...], wd_ref[...]
    kept = []
    for start in range(0, rows, chunk):
        at = slice(start, start + chunk)
        x, dy = x_ref[at, :], dy_ref[at, :]
        g = jnp.dot(x, wg, preferred_element_type=jnp.float32)
        u = jnp.dot(x, wu, preferred_element_type=jnp.float32)
        raw = lax.dot_general(dy, wd, NT, preferred_element_type=jnp.float32)
        square = g * g
        half = 0.5 + 0.5 * jnp.tanh(g * (GELU_A + (GELU_A * GELU_B) * square))
        gelu = g * half
        slope = half + 2.0 * gelu * (1.0 - half) * (GELU_A + (3.0 * GELU_A * GELU_B) * square)
        h = gelu * u
        product = raw * h
        total = product[:, :LANES]
        for column in range(LANES, product.shape[1], LANES):
            total = total + product[:, column : column + LANES]
        part_ref[at, :] += total
        dh = raw * gate_ref[at, :1]
        du = (dh * gelu).astype(jnp.bfloat16)
        dg = (dh * u * slope).astype(jnp.bfloat16)
        h_ref[at, :] = h.astype(jnp.bfloat16)
        dg_ref[at, :] = dg
        du_ref[at, :] = du
        kept.append((at, dg, du))
    for at, dg, du in kept:
        acc_ref[at, :] += lax.dot_general(dg, wg, NT, preferred_element_type=jnp.float32) + lax.dot_general(
            du, wu, NT, preferred_element_type=jnp.float32
        )

    @pl.when(step == pl.num_programs(0) - 1)
    def _():
        dx_ref[:rows, :] = acc_ref[...].astype(dx_ref.dtype)
        sums = jnp.sum(part_ref[...].T, axis=0, keepdims=True)
        high = sums.astype(jnp.bfloat16).astype(jnp.float32)
        middle = (sums - high).astype(jnp.bfloat16).astype(jnp.float32)
        line = lax.broadcasted_iota(jnp.int32, (EXTRA, rows), 0)
        lines = jnp.where(line == 0, high, jnp.where(line == 1, middle, jnp.where(line == 2, sums - high - middle, 0.0)))
        dx_ref[rows:, :] = jnp.zeros_like(dx_ref[rows:, :])
        dx_ref[rows:, :rows] = lines.astype(dx_ref.dtype)


def expert_block(at, count, x, dy, wgu, wd, earlier):
    rows, width = dy.shape
    hidden = wd.shape[0]
    tile = FF_TILE
    whole = jax.ShapeDtypeStruct((count * rows, hidden), jnp.bfloat16)
    fixed = lambda i, *_: (0, 0)
    out_block = pl.BlockSpec((rows, tile), lambda i, *_: (at, i))
    spec = pltpu.PrefetchScalarGridSpec(
        num_scalar_prefetch=1,
        grid=(hidden // tile,),
        in_specs=[
            pl.BlockSpec((rows + EXTRA, width), fixed),
            pl.BlockSpec((rows, width), fixed),
            pl.BlockSpec((width, tile), lambda i, *_: (0, i)),
            pl.BlockSpec((width, tile), lambda i, *_: (0, hidden // tile + i)),
            pl.BlockSpec((tile, width), lambda i, *_: (i, 0)),
        ]
        + [pl.BlockSpec(memory_space=pl.ANY)] * len(earlier),
        out_specs=[
            out_block,
            out_block,
            out_block,
            pl.BlockSpec((rows + EXTRA, width), fixed),
        ],
        scratch_shapes=[
            pltpu.VMEM((rows, LANES), jnp.float32),
            pltpu.VMEM((rows, width), jnp.float32),
            pltpu.VMEM((rows, LANES), jnp.float32),
        ],
    )
    return pl.pallas_call(
        expert_kernel,
        name="expert_block",
        out_shape=(
            whole,
            whole,
            whole,
            jax.ShapeDtypeStruct((rows + EXTRA, width), jnp.bfloat16),
        ),
        grid_spec=spec,
        input_output_aliases={6 + i: i for i in range(len(earlier))},
        compiler_params=pltpu.CompilerParams(dimension_semantics=("arbitrary",), vmem_limit_bytes=40 << 20),
        cost_estimate=pl.CostEstimate(
            flops=10 * rows * width * hidden, bytes_accessed=6 * width * hidden + 6 * rows * hidden, transcendentals=0
        ),
    )(jnp.zeros((1,), jnp.int32), x, dy, wgu, wgu, wd, *earlier)


EPS = 1e-06
FULL_PRECISION = lax.Precision.HIGHEST
ALL = ("z", "x", "exp")
SEQ = ("z", "x")
LOW = jnp.bfloat16


def dot32(a, b):
    return jnp.dot(a, b, preferred_element_type=jnp.float32)


def dot_nt(a, b):
    return lax.dot_general(a, b, NT, preferred_element_type=jnp.float32)


def dot_tn(a, b):
    return lax.dot_general(a, b, (((0,), (0,)), ((), ())), preferred_element_type=jnp.float32)


def partner(value, axis, offset):
    count = lax.axis_size(axis)
    return lax.ppermute(value, axis, [(i, i ^ offset) for i in range(count)])


def bits_of(count):
    return [1 << b for b in reversed(range(count.bit_length() - 1))]


def reorder(stacked, own):
    count = stacked.shape[0]
    return jnp.stack([lax.dynamic_index_in_dim(stacked, own ^ r, 0, keepdims=False) for r in range(count)])


def gather_double(value, steps):
    for axis, bit in steps:
        other = partner(value, axis, bit)
        high = (lax.axis_index(axis) & bit) != 0
        value = jnp.stack([jnp.where(high, other, value), jnp.where(high, value, other)])
    return value


def scatter_halve(value, steps):
    gone = []
    for axis, bit, dim in steps:
        at = dim - sum(1 for d in gone if d < dim)
        gone.append(dim)
        high = (lax.axis_index(axis) & bit) != 0
        low_half = lax.index_in_dim(value, 0, at, keepdims=False)
        high_half = lax.index_in_dim(value, 1, at, keepdims=False)
        keep = jnp.where(high, high_half, low_half)
        give = jnp.where(high, low_half, high_half)
        value = (keep.astype(jnp.float32) + partner(give, axis, bit).astype(jnp.float32)).astype(LOW)
    return value


def ring_of(groups, split):
    order = []
    for x in range(split):
        line = range(groups) if x % 2 == 0 else reversed(range(groups))
        order += [z * split + x for z in line]
    place = [order.index(s) for s in range(len(order))]
    ahead = [(order[i], order[(i + 1) % len(order)]) for i in range(len(order))]
    return jnp.asarray(order, jnp.int32), jnp.asarray(place, jnp.int32), ahead


def pick(values, index):
    return lax.dynamic_index_in_dim(values, index, 0, keepdims=False)


def unwritten(shape, dtype):
    return pl.pallas_call(
        lambda out_ref: None,
        name="unwritten",
        out_shape=jax.ShapeDtypeStruct(shape, dtype),
        out_specs=pl.BlockSpec(memory_space=pl.ANY),
    )()


class RingGather:
    def __init__(self, piece, groups, split, own):
        self.order, place, self.ahead = ring_of(groups, split)
        self.count = groups * split
        self.here = pick(place, own)
        self.rows = piece.shape[0]
        self.whole = unwritten((self.count * self.rows, piece.shape[1]), piece.dtype)
        self.whole = lax.dynamic_update_slice_in_dim(self.whole, piece, own * self.rows, 0)
        self.forward = self.backward = piece
        self.round = 0
        self.waiting = []

    def step(self):
        self.settle()
        self.round += 1
        k = self.round
        self.forward = lax.ppermute(self.forward, SEQ, self.ahead)
        self.waiting.append((self.forward, -k))
        if k < self.count - self.count // 2:
            self.backward = lax.ppermute(self.backward, SEQ, [(b, a) for a, b in self.ahead])
            self.waiting.append((self.backward, k))

    def settle(self):
        for piece, k in self.waiting:
            at = pick(self.order, (self.here + k + self.count) % self.count) * self.rows
            self.whole = lax.dynamic_update_slice_in_dim(self.whole, piece, at, 0)
        self.waiting = []

    def after(self, value):
        value, self.forward, self.backward = lax.optimization_barrier((value, self.forward, self.backward))
        self.waiting = [(self.forward if k < 0 else self.backward, k) for _, k in self.waiting]
        return value

    def finish(self):
        while self.round < self.count // 2:
            self.step()
        self.settle()
        return self.whole


class RingScatter:
    def __init__(self, totals, groups, split, own):
        self.order, place, self.ahead = ring_of(groups, split)
        self.count = groups * split
        self.here = pick(place, own)
        self.rows = totals[0].shape[0] // self.count
        self.totals = totals
        self.round = 0
        self.forward = self.backward = None

    def block(self, total, offset):
        at = pick(self.order, (self.here + offset + self.count) % self.count) * self.rows
        return lax.dynamic_slice_in_dim(total, at, self.rows, 0)

    def load(self, coming, offset):
        own = [self.block(total, offset) for total in self.totals]
        if coming is None:
            return own
        return [(a.astype(jnp.float32) + b.astype(jnp.float32)).astype(LOW) for a, b in zip(own, coming)]

    def step(self):
        self.round += 1
        k, far = self.round, self.count // 2
        near = self.count - 1 - far
        if k <= far:
            parts = self.load(self.forward, far - k + 1)
            self.forward = [lax.ppermute(part, SEQ, self.ahead) for part in parts]
        if k <= near:
            parts = self.load(self.backward, k - near - 1)
            self.backward = [lax.ppermute(part, SEQ, [(b, a) for a, b in self.ahead]) for part in parts]

    def after(self, value):
        value, self.forward, self.backward = lax.optimization_barrier((value, self.forward, self.backward))
        return value

    def finish(self):
        while self.round < self.count // 2:
            self.step()
        own = [self.block(total, 0).astype(jnp.float32) for total in self.totals]
        return [
            a + b.astype(jnp.float32) + c.astype(jnp.float32) for a, b, c in zip(own, self.forward, self.backward)
        ]


def norm_scale(value):
    return lax.rsqrt(jnp.mean(value * value, axis=-1, keepdims=True) + EPS)


def norm_back(scale, normed, gain, grad):
    scaled = grad * gain
    return scale * (scaled - normed * jnp.mean(scaled * normed, axis=-1, keepdims=True))


def split3(value):
    high = value.astype(LOW)
    rest = value - high.astype(jnp.float32)
    middle = rest.astype(LOW)
    return [high, middle, (rest - middle.astype(jnp.float32)).astype(LOW)]


def per_device(
    block_in,
    cotangent,
    segment_ids,
    expert_routes,
    pair_priority,
    gain_attention,
    w_query,
    w_key,
    w_value,
    w_out,
    bias_table,
    gain_experts,
    w_router,
    w_gate,
    w_up,
    w_down,
):
    groups, local_len, width = block_in.shape
    tokens = groups * local_len
    rows_own, hd = w_query.shape
    split = lax.axis_size("x")
    exp_count = lax.axis_size("exp")
    seq_count = groups * split
    length = local_len * seq_count
    x_at, z_at, e_at = lax.axis_index("x"), lax.axis_index("z"), lax.axis_index("exp")
    s_at = z_at * split + x_at
    head_width = hd // split
    heads_here = head_width // HEAD_DIM
    experts_all = w_router.shape[1]
    bias_own = bias_table.shape[0]
    tile = min(TILE, local_len)
    own = s_at.astype(jnp.int32).reshape(1)
    z_bits, x_bits, e_bits = bits_of(groups), bits_of(split), bits_of(exp_count)

    input_r = reorder(block_in, z_at)

    arrived = [[None] * split for _ in range(groups)]
    for rz in reversed(range(groups)):
        arrived[rz][0] = partner(input_r[rz], "z", rz) if rz else input_r[0]
    small = jnp.concatenate(
        [
            gain_attention[:, None],
            gain_experts[:, None],
            jnp.pad(bias_table, (0, rows_own - bias_own))[:, None],
            w_router,
        ],
        axis=1,
    )
    small = jnp.pad(small, ((0, 0), (0, LANES - small.shape[1]))).astype(LOW)
    share = jnp.stack(
        [part.astype(LOW).reshape(rows_own, split, head_width) for part in (w_query, w_key, w_value)], axis=2
    )
    share = share.reshape(rows_own, split, 3 * head_width).transpose(1, 0, 2)
    common = jnp.concatenate([w_out.astype(LOW), small], axis=1)
    share = jnp.concatenate([share, jnp.broadcast_to(common, (split,) + common.shape)], axis=2)
    shares = [lax.dynamic_index_in_dim(share, x_at ^ r, 0, keepdims=False) for r in range(split)]
    shares = [shares[0]] + [partner(shares[r], "x", r) for r in range(1, split)]
    by_x = reorder(jnp.stack(shares), x_at)
    for rx in range(1, split):
        arrived[0][rx] = partner(arrived[0][0], "x", rx)
    packed = gather_double(by_x, [("z", b) for b in z_bits])
    near = [arrived[rz][0] for rz in range(1, groups)]
    packed, near = lax.optimization_barrier((packed, near))
    for rz in range(1, groups):
        arrived[rz][0] = near[rz - 1]
        for rx in range(1, split):
            arrived[rz][rx] = partner(arrived[rz][0], "x", rx)
    packed = gather_double(packed, [("exp", b) for b in e_bits[:-1]])
    packed, arrived = lax.optimization_barrier((packed, arrived))
    sequence = jnp.stack([block for line in arrived for block in line]).reshape(length, width)

    gate_up_own = jnp.concatenate([w_gate[0].astype(LOW), w_up[0].astype(LOW)], axis=1)
    sequence, gate_up_own, down_own = lax.optimization_barrier((sequence, gate_up_own, w_down[0].astype(LOW)))
    down_w = lax.all_gather(down_own, SEQ, axis=0, tiled=True)
    gate_up_ring = RingGather(gate_up_own, groups, split, s_at)
    gate_up_ring.step()
    packed = gather_double(packed, [("exp", b) for b in e_bits[-1:]])
    ne, nz, nx = len(e_bits), len(z_bits), len(x_bits)
    packed = packed.transpose(
        tuple(ne + i for i in reversed(range(nz))) + (ne + nz,) + tuple(reversed(range(ne))) + (ne + nz + 1, ne + nz + 2)
    ).reshape(width, 3 * head_width + width + LANES)
    qkv_w, small_all = packed[:, : 3 * head_width], packed[:, 3 * head_width + width :]
    out_w = packed[:, 3 * head_width : 3 * head_width + width]
    gain_one = small_all[:, 0].astype(jnp.float32)
    gain_two = small_all[:, 1].astype(jnp.float32)
    table_all = small_all[:, 2].reshape(-1, rows_own)[:, :bias_own].reshape(-1, BUCKETS)
    router_t = small_all[:, 3 : 3 + experts_all].T
    table_rows = lax.dynamic_slice_in_dim(table_all, x_at * heads_here, heads_here, 0)

    routes = expert_routes.reshape(tokens, -1)
    top_count = routes.shape[1]
    priority = pair_priority.reshape(-1)
    pair_experts = routes.reshape(-1)
    ahead = (pair_experts[None, :] == pair_experts[:, None]) & (priority[None, :] < priority[:, None])
    slots = jnp.sum(ahead.astype(jnp.int32), axis=1)
    capacity = (5 * top_count * tokens + 4 * experts_all - 1) // (4 * experts_all)
    slot_count = experts_all * capacity
    slot_index = jnp.where(slots < capacity, (pair_experts ^ e_at) * capacity + slots, slot_count)
    slot_index = slot_index.reshape(tokens, top_count)
    every_slot = jnp.arange(slot_count, dtype=jnp.int32)[None, :]
    table = sum((slot_index[:, k : k + 1] == every_slot).astype(LOW) for k in range(top_count))
    tables = [table[:, r * capacity : (r + 1) * capacity] for r in range(exp_count)]
    grad_low = cotangent.reshape(tokens, width)
    grad_slots = [dot_tn(part, grad_low).astype(LOW) for part in tables]

    wide = sequence.astype(jnp.float32)
    normed_one = (wide * norm_scale(wide) * gain_one).astype(LOW)
    qkv = dot32(normed_one, qkv_w).astype(LOW)
    qkv, grad_slots = lax.optimization_barrier((qkv, grad_slots))
    qkv = gate_up_ring.after(qkv)
    gate_up_ring.step()
    grad_slots = [grad_slots[0]] + [partner(grad_slots[r], "exp", r) for r in range(1, exp_count)]
    segments = lax.dynamic_index_in_dim(segment_ids, z_at, 0, keepdims=False)
    ranges = tile_ranges(segments, tile)
    seg_blocks = segments.reshape(seq_count, local_len)
    query_side, key_side = segment_columns(reorder(seg_blocks, s_at).reshape(length))
    rows = bias_rows(table_rows, tile)
    ends = jnp.stack([table_rows[:, 15], table_rows[:, 31]], axis=1).astype(jnp.float32)
    contexts, log_totals = attend_forward(qkv, query_side, key_side, ranges, rows, ends, own, tile)
    contexts = gate_up_ring.after(contexts)
    contexts, grad_slots = lax.optimization_barrier((contexts, grad_slots))
    gate_up_w = gate_up_ring.finish()

    def exchange_positions(blocks):
        return lax.all_to_all(blocks, SEQ, split_axis=0, concat_axis=0, tiled=True)

    context_local = exchange_positions(contexts.reshape(seq_count, local_len, head_width))
    context_local = (
        context_local.reshape(groups, split, local_len, head_width).transpose(0, 2, 1, 3).reshape(tokens, hd)
    )
    inputs = block_in.astype(jnp.float32).reshape(tokens, width)
    mid = inputs + dot32(context_local, out_w)
    scale_two = norm_scale(mid)
    normed_two = (mid * scale_two * gain_two).astype(LOW)

    logits = dot_nt(router_t, normed_two)
    exponent = jnp.exp(logits - jnp.max(logits, axis=0, keepdims=True))
    probabilities = exponent / jnp.sum(exponent, axis=0, keepdims=True)
    expert_ids = jnp.arange(experts_all, dtype=jnp.int32)[:, None]
    chosen = sum((routes[:, k][None, :] == expert_ids).astype(jnp.float32) for k in range(top_count))
    chosen_total = jnp.sum(probabilities * chosen, axis=0, keepdims=True)
    gates = probabilities * chosen / chosen_total
    gates_r = reorder(gates, e_at)

    gate_slots = jnp.sum(
        table.astype(jnp.float32).reshape(tokens, exp_count, capacity) * gates_r.T[:, :, None], axis=0
    )
    gate_lines = jnp.pad(jnp.stack(split3(gate_slots), axis=1), ((0, 0), (0, EXTRA - 3), (0, width - capacity)))

    def values_below(rows_):
        return jnp.sum(rows_[capacity : capacity + 3, :capacity].astype(jnp.float32), axis=0)

    sent = [None] * exp_count
    for r in reversed(range(exp_count)):
        sent[r] = jnp.concatenate([dot_tn(tables[r], normed_two).astype(LOW), gate_lines[r]], axis=0)
        if r:
            sent[r] = partner(sent[r], "exp", r)

    earlier = ()
    back = [None] * exp_count
    turns = [0] + list(range(2, exp_count)) + [1]
    for turn, r in enumerate(turns):
        if turn >= 3:
            ready = turns[turn - 2]
            sent[r], back[ready] = lax.optimization_barrier((sent[r], back[ready]))
        hidden, gate_low, up_low, dx = expert_block(
            r, exp_count, sent[r], grad_slots[r], gate_up_w, down_w, earlier
        )
        earlier = (hidden, gate_low, up_low)
        back[r] = partner(dx, "exp", r) if r else dx

    sent, hidden = lax.optimization_barrier((sent, hidden))
    slot_rows = jnp.concatenate([rows_[:capacity] for rows_ in sent], axis=0)
    slot_gates = jnp.concatenate([values_below(rows_) for rows_ in sent], axis=0)[:, None]
    slot_grads = (slot_gates * jnp.concatenate(grad_slots, axis=0).astype(jnp.float32)).astype(LOW)

    gate_grad = jnp.sum(
        table.astype(jnp.float32).reshape(tokens, exp_count, capacity) * jnp.stack([values_below(rows_) for rows_ in back])[None], axis=2
    )
    gate_grad = reorder(gate_grad.T, e_at)
    chosen_grad = chosen * (gate_grad - jnp.sum(gates * gate_grad, axis=0, keepdims=True)) / chosen_total
    logit_grad = probabilities * (chosen_grad - jnp.sum(probabilities * chosen_grad, axis=0, keepdims=True))
    logit_pieces = jnp.concatenate(split3(logit_grad), axis=0)
    router_sum = jnp.sum(dot32(logit_pieces, normed_two).reshape(3, experts_all, width), axis=0)
    normed_two_grad = dot_tn(logit_pieces, jnp.concatenate([router_t] * 3, axis=0))
    for r in range(exp_count):
        normed_two_grad = normed_two_grad + dot32(tables[r], back[r][:capacity])
    unit_two = mid * scale_two
    gain_two_sum = jnp.sum(normed_two_grad * unit_two, axis=0)
    grad_out = grad_low.astype(jnp.float32)
    mid_grad = grad_out + norm_back(scale_two, unit_two, gain_two, normed_two_grad)
    attention_grad = mid_grad.astype(LOW)
    context_grad = dot_nt(attention_grad, out_w).astype(LOW)
    context_grad, up_low, gate_low = lax.optimization_barrier((context_grad, up_low, gate_low))
    gate_sum = dot_tn(slot_rows, gate_low).astype(LOW)
    up_sum = dot_tn(slot_rows, up_low).astype(LOW)
    context_grad = (
        context_grad.reshape(groups, local_len, split, head_width)
        .transpose(0, 2, 1, 3)
        .reshape(seq_count, local_len, head_width)
    )
    context_heads = exchange_positions(context_grad).reshape(length, head_width)

    def scatter_experts(total):
        return lax.psum_scatter(total, SEQ, scatter_dimension=0, tiled=True)

    context_heads, gate_sum, up_sum = lax.optimization_barrier((context_heads, gate_sum, up_sum))

    halving = [("exp", b, 1 + nz + nx + ne - 1 - i) for i, b in enumerate(reversed(e_bits))]
    halving += [("z", b, 1 + nz - 1 - i) for i, b in enumerate(reversed(z_bits))]
    out_sum = dot_tn(context_local, attention_grad).astype(LOW)

    ring = RingScatter([gate_sum, up_sum], groups, split, s_at)
    grads, diag, far = (), [], []
    pairs = head_width // LANES
    for pair in range(pairs):
        ring.step()
        *grads, pair_diag, pair_far = attend_backward(
            pair, qkv, context_heads, contexts, log_totals, query_side, key_side, ranges, rows, ends, own, tile, tuple(grads)
        )
        grads = ring.after(grads)
        if pair == 0:
            grads, hidden = lax.optimization_barrier((grads, hidden))
            down_sum = dot_tn(hidden, slot_grads).astype(LOW)
            down_owned = scatter_experts(down_sum)
        if pair == min(1, pairs - 1):
            grads, hidden, down_sum = lax.optimization_barrier((grads, hidden, down_sum))
            expert_out = (slot_gates * dot32(hidden, down_w)).astype(LOW)
            expert_out = reorder(expert_out.reshape(exp_count, capacity, width), e_at)
            returned = lax.all_to_all(expert_out, "exp", split_axis=0, concat_axis=0, tiled=True)
        if pair == min(2, pairs - 1):
            grads, expert_out = lax.optimization_barrier((grads, expert_out))
        if pair == pairs - 1:
            grads, returned = lax.optimization_barrier((grads, returned))
        diag.append(pair_diag)
        far.append(pair_far)
    diag, far = jnp.concatenate(diag), jnp.concatenate(far)
    query_back, key_back, value_back, down_owned = lax.optimization_barrier((*grads, down_owned))
    gate_owned, up_owned = ring.finish()
    table_local = bucket_sums(diag, far, tile)

    def through(grads, part):
        return dot_nt(grads, qkv_w[:, part * head_width : (part + 1) * head_width])

    out_parts = width // head_width
    weight_sum = jnp.stack(
        [dot_tn(normed_one, grads).astype(LOW) for grads in (query_back, key_back, value_back)]
        + [out_sum[:, i * head_width : (i + 1) * head_width] for i in range(out_parts)]
    )
    weight_sum, query_back, key_back, value_back = lax.optimization_barrier(
        (weight_sum, query_back, key_back, value_back)
    )
    normed_part = through(query_back, 0) + through(key_back, 1) + through(value_back, 2)
    half = width // 2
    normed_part = normed_part.reshape(groups, split, local_len, width)

    sides = [normed_part[:, rx].astype(LOW) for rx in range(1, split)]
    first = [partner(side[:, :, :half], "x", rx) for rx, side in enumerate(sides, 1)]

    def add_up(own_part, coming):
        total = own_part + sum(part.astype(jnp.float32) for part in coming)
        return reorder(total.astype(LOW), z_at)

    def send_back(total):
        return lax.all_to_all(total, "z", split_axis=0, concat_axis=0, tiled=True)

    first = add_up(normed_part[:, 0, :, :half], first)
    first, rest = lax.optimization_barrier((first, [side[:, :, half:] for side in sides]))
    normed_first = send_back(first)
    rest = [partner(side, "x", rx) for rx, side in enumerate(rest, 1)]
    normed_second = send_back(add_up(normed_part[:, 0, :, half:], rest))
    weight_part = scatter_halve(
        weight_sum.reshape((3 + out_parts,) + (2,) * (nz + nx + ne) + (rows_own, head_width)), halving[:ne]
    )
    weight_part = scatter_halve(weight_part, halving[ne:]).reshape(3 + out_parts, split, rows_own, head_width)
    weight_own = [lax.dynamic_index_in_dim(weight_part, x_at ^ r, 1, keepdims=False) for r in range(split)]
    weight_own = [weight_own[0]] + [partner(weight_own[r], "x", r) for r in range(1, split)]
    normed_second, weight_own = lax.optimization_barrier((normed_second, weight_own))
    block_out = (mid + dot32(table, reorder(returned, e_at).reshape(slot_count, width))).astype(LOW)

    block_out = block_out.reshape(groups, local_len, width)
    out_w_out = sum(part[3:].astype(jnp.float32) for part in weight_own)
    out_w_out = out_w_out.transpose(1, 0, 2).reshape(rows_own, width)
    qkv_own = reorder(jnp.stack([part[:3] for part in weight_own]), x_at)
    qkv_own = qkv_own.transpose(1, 2, 0, 3).reshape(3, rows_own, hd).astype(jnp.float32)

    normed_one_grad = jnp.concatenate([normed_first, normed_second], axis=2).astype(jnp.float32).reshape(tokens, width)
    scale_one = norm_scale(inputs)
    unit_one = inputs * scale_one
    gain_one_sum = jnp.sum(normed_one_grad * unit_one, axis=0)
    block_in_grad = (mid_grad + norm_back(scale_one, unit_one, gain_one, normed_one_grad)).reshape(
        groups, local_len, width
    )

    table_sum = lax.dynamic_update_slice_in_dim(
        jnp.zeros(table_all.shape, jnp.float32), table_local, x_at * heads_here, 0
    ).reshape(-1, bias_own)
    table_sum = jnp.pad(table_sum, ((0, 0), (0, rows_own - bias_own)))[:, None, :]
    little = jnp.concatenate(
        [
            gain_one_sum.reshape(-1, 1, rows_own),
            gain_two_sum.reshape(-1, 1, rows_own),
            table_sum,
            router_sum.reshape(experts_all, -1, rows_own).transpose(1, 0, 2),
        ],
        axis=1,
    )
    little = jnp.sum(lax.all_to_all(little, ALL, split_axis=0, concat_axis=0, tiled=True), axis=0)
    return (
        block_out,
        block_in_grad,
        little[0],
        qkv_own[0],
        qkv_own[1],
        qkv_own[2],
        out_w_out,
        little[2, :bias_own],
        little[1],
        little[3:].T,
        gate_owned.astype(jnp.float32)[None],
        up_owned.astype(jnp.float32)[None],
        down_owned.astype(jnp.float32)[None],
    )


def solution(mesh):
    def run(*args):
        groups = args[0].shape[0] // mesh.shape["exp"]
        seq_count, exp_count = mesh.shape["seq"], mesh.shape["exp"]
        grid = mesh.devices.reshape(groups, seq_count // groups, exp_count)
        fine = jax.sharding.Mesh(grid, ALL)
        placed = P("exp", SEQ, None)
        whole = P(ALL)
        matrix = P(ALL, None)
        return jax.shard_map(
            per_device,
            mesh=fine,
            in_specs=(
                placed, placed, P("exp", None), placed, placed,
                whole, matrix, matrix, matrix, matrix, whole, whole, matrix,
                placed, placed, placed,
            ),
            out_specs=(
                placed, placed, whole, matrix, matrix, matrix, matrix, whole, whole, matrix,
                placed, placed, placed,
            ),
            check_vma=False,
        )(*args)

    return run
```
